32 devices in a mesh: wide: 8 (over z, x), narrow: 4 (over y, core).
Axes of the slice: x: 2, y: 2, z: 4, core: 2. Of those that a mesh axis runs over, the one named last changes fastest.
Arguments:
- inputs: bfloat16 [256, 14, 14, 768], P(('wide', 'narrow')), may hold values from -6 to 6
- heights: int32 [256], P(('wide', 'narrow')), may hold values from 8 to 14, as said below
- widths: int32 [256], P(('wide', 'narrow')), may hold values from 8 to 14, as said below
- conv_weight: bfloat16 [4, 9, 768], P('narrow', None, 'wide'), may hold values from -2 to 2
- conv_bias: bfloat16 [4, 768], P('narrow', 'wide'), may hold values from -0.59765625 to 0.59765625
- norm_gain: bfloat16 [4, 768], P('narrow', 'wide'), may hold values from 0.099609375 to 1.8984375
- norm_bias: bfloat16 [4, 768], P('narrow', 'wide'), may hold values from -0.59765625 to 0.59765625
- spatial_qkv: bfloat16 [2304, 768], P('wide', 'narrow'), may hold values from -0.21875 to 0.21875
- channel_qkv: bfloat16 [2304, 768], P('wide', 'narrow'), may hold values from -0.102062073 to 0.102062073
- projection: bfloat16 [2, 768, 768], P(None, 'wide', 'narrow'), may hold values from -0.875 to 0.875
- mlp_in: bfloat16 [2, 3072, 768], P(None, 'wide', 'narrow'), may hold values from -0.21875 to 0.21875
- mlp_out: bfloat16 [2, 768, 3072], P(None, 'wide', 'narrow'), may hold values from -0.15625 to 0.15625
- attn_bias: bfloat16 [5, 768], P(None, 'wide'), may hold values from -0.59765625 to 0.59765625
- hidden_bias: bfloat16 [2, 3072], P(None, 'wide'), may hold values from -3 to 3
- out_bias: bfloat16 [4, 768], P('narrow', 'wide'), may hold values from -0.59765625 to 0.59765625
- cotangent: bfloat16 [256, 14, 14, 768], P(('wide', 'narrow')), may hold values from -6 to 6
Outputs:
- block_out: bfloat16 [256, 14, 14, 768], P(('wide', 'narrow'))
- input_grad: bfloat16 [256, 14, 14, 768], P(('wide', 'narrow'))
- conv_weight_grad: float32 [4, 9, 768], P('narrow', None, 'wide')
- conv_bias_grad: float32 [4, 768], P('narrow', 'wide')
- norm_gain_grad: float32 [4, 768], P('narrow', 'wide')
- norm_bias_grad: float32 [4, 768], P('narrow', 'wide')
- spatial_qkv_grad: float32 [2304, 768], P('wide', 'narrow')
- channel_qkv_grad: float32 [2304, 768], P('wide', 'narrow')
- projection_grad: float32 [2, 768, 768], P(None, 'wide', 'narrow')
- mlp_in_grad: float32 [2, 3072, 768], P(None, 'wide', 'narrow')
- mlp_out_grad: float32 [2, 768, 3072], P(None, 'wide', 'narrow')
- attn_bias_grad: float32 [5, 768], P(None, 'wide')
- hidden_bias_grad: float32 [2, 3072], P(None, 'wide')
- out_bias_grad: float32 [4, 768], P('narrow', 'wide')
The draws below stay inside these ranges and needn't reach their ends.
Inputs may be any that keep to these rules, and one draw needn't show every extreme that they name: `heights`: every value from 8 to 14 occurs. `widths`: every value from 8 to 14 occurs.
All inputs are finite; a program needn't handle non-finite values.
Results may differ from the reference program's by a relative error of at most 0.018.
Values may be sent and summed in bfloat16 or wider, within the bound.
A program may use at most 576 MiB of HBM per device.

```python
import jax
import jax.numpy as jnp
from jax import lax

D = 768
FF = 3072
HD = 32
WIN = 7
HEADS = 24
IMAGES = 256
TILE_ROWS = 14
TILE_COLS = 14


def draw_heights(key, part):
    shuffled = jax.random.permutation(jax.random.fold_in(key, 11), IMAGES)
    return (TILE_ROWS - shuffled % WIN).astype(jnp.int32)


def draw_widths(key, part):
    shuffled = jax.random.permutation(jax.random.fold_in(key, 23), IMAGES)
    return (TILE_COLS - shuffled % WIN).astype(jnp.int32)


def draw_inputs(key, part):
    inner = jax.random.fold_in(key, 41)
    shape = (IMAGES, TILE_ROWS, TILE_COLS, D)
    raw = jnp.clip(jax.random.normal(inner, shape, jnp.float32), -6.0, 6.0)
    return raw.astype(jnp.bfloat16)


def draw_channel_qkv(key, part):
    inner = jax.random.fold_in(key, 37)
    shape = (3 * D, D)
    raw = jnp.clip(jax.random.normal(inner, shape, jnp.float32), -4.0, 4.0)
    row_ids = jnp.arange(3 * D, dtype=jnp.int32)
    row_scale = jnp.where(row_ids < 2 * D, 0.4 * float(D) ** (-0.5), (2.0 * D) ** (-0.5)).astype(jnp.float32)
    return (raw * row_scale[:, None]).astype(jnp.bfloat16)


def levels(stream_key, extent, shards, smallest, largest):
    def one(axis_at, blocks):
        steps = jax.random.uniform(jax.random.fold_in(jax.random.fold_in(stream_key, 6), axis_at), (blocks,), jnp.float32, smallest / len(shards), largest / len(shards))
        return jnp.repeat(jnp.exp(steps), extent[axis_at] // blocks).reshape((-1,) + (1,) * (len(extent) - axis_at - 1))

    loudness = one(*shards[0])
    for cut in shards[1:]:
        loudness = loudness * one(*cut)
    return loudness


def gaussian(own_key, shape, scale, limit, cuts=(), kind=jnp.bfloat16):
    values = jax.random.normal(own_key, shape, jnp.float32) * scale
    if len(cuts) > 0:
        values = levels(own_key, shape, cuts, -0.22, 0.18) * values
    return jnp.clip(values, min=-limit, max=limit).astype(kind)


def setup_inputs(seed: int = 0) -> dict:
    key_of = jax.random.split(jax.random.key(seed), 17)
    inputs = draw_inputs(jax.random.fold_in(key_of[16], 71), 0)
    heights = draw_heights(jax.random.fold_in(key_of[16], 71), 0)
    widths = draw_widths(jax.random.fold_in(key_of[16], 71), 0)
    conv_weight = gaussian(key_of[3], (4, 9, D), 9 ** -0.5, 2.0, ((0, 4), (2, 8)))
    conv_bias = gaussian(key_of[4], (4, D), 0.1, 0.59765625, ((0, 4), (1, 8)))
    norm_gain = jnp.clip(1.0 + 0.18 * jax.random.normal(key_of[5], (4, D), jnp.float32), 0.099609375, 1.8984375).astype(jnp.bfloat16)
    norm_bias = gaussian(key_of[6], (4, D), 0.1, 0.59765625, ((0, 4), (1, 8)))
    spatial_qkv = gaussian(key_of[7], (3 * D, D), D ** -0.5, 0.21875, ((0, 8), (1, 4)))
    channel_qkv = draw_channel_qkv(jax.random.fold_in(key_of[16], 71), 0)
    projection = gaussian(key_of[9], (2, D, D), (D // 16) ** -0.5, 0.875, ((1, 8), (2, 4)))
    mlp_in = gaussian(key_of[10], (2, FF, D), D ** -0.5, 0.21875, ((1, 8), (2, 4)))
    mlp_out = gaussian(key_of[11], (2, D, FF), (FF // 2) ** -0.5, 0.15625, ((1, 8), (2, 4)))
    attn_bias = gaussian(key_of[12], (5, D), 0.1, 0.59765625, ((1, 8),))
    hidden_bias = gaussian(key_of[13], (2, FF), 0.5, 3.0, ((1, 8),))
    out_bias = gaussian(key_of[14], (4, D), 0.1, 0.59765625, ((0, 4), (1, 8)))
    cotangent = gaussian(key_of[15], (IMAGES, TILE_ROWS, TILE_COLS, D), 1.0, 6.0, ((0, 32),))
    return dict(inputs=inputs, heights=heights, widths=widths, conv_weight=conv_weight, conv_bias=conv_bias, norm_gain=norm_gain, norm_bias=norm_bias, spatial_qkv=spatial_qkv, channel_qkv=channel_qkv, projection=projection, mlp_in=mlp_in, mlp_out=mlp_out, attn_bias=attn_bias, hidden_bias=hidden_bias, out_bias=out_bias, cotangent=cotangent)


@jax.custom_vjp
def low(v):
    return lax.optimization_barrier(v.astype(jnp.bfloat16)).astype(jnp.float32)

@jax.custom_vjp
def low_back(v):
    return v

def low_keep(v):
    return (low(v), None)

def low_pass(kept, grad):
    return (grad,)

def back_keep(v):
    return (v, None)

def back_low(kept, grad):
    return (low(grad),)
low.defvjp(low_keep, low_pass)
low_back.defvjp(back_keep, back_low)
epsilon = 1e-05
highest = lax.Precision.HIGHEST

def linear_map(rows_in, weight):
    return jnp.einsum('ni,oi->no', rows_in, weight, precision=highest)

def layer_norm(values, gain_row, bias_row):
    center = values - lax.optimization_barrier(jnp.mean(values, axis=-1, keepdims=True))
    spread = lax.optimization_barrier(jnp.mean(center * center, axis=-1, keepdims=True))
    return center * lax.rsqrt(spread + epsilon) * gain_row + bias_row

def depthwise(values, kernel, bias_row):
    tile_rows, tile_cols = (values.shape[1], values.shape[2])
    padded = jnp.pad(values, ((0, 0), (1, 1), (1, 1), (0, 0)))
    summed = jnp.zeros_like(values) + bias_row
    for row_step in range(3):
        for col_step in range(3):
            summed = summed + kernel[3 * row_step + col_step] * padded[:, row_step:row_step + tile_rows, col_step:col_step + tile_cols, :]
    return summed

def gelu_exact(values):
    return 0.5 * values * (1.0 + lax.erf(values * 0.7071067811865476))

def softmax_last(scores):
    row_max = lax.optimization_barrier(jnp.max(scores, axis=-1, keepdims=True))
    exponent = jnp.exp(scores - row_max)
    return exponent / lax.optimization_barrier(jnp.sum(exponent, axis=-1, keepdims=True))

def to_windows(tile_cells):
    images, tile_rows, tile_cols, features = tile_cells.shape
    blocks = tile_cells.reshape(images, tile_rows // WIN, WIN, tile_cols // WIN, WIN, features)
    return blocks.transpose(0, 1, 3, 2, 4, 5).reshape(-1, WIN * WIN, features)

def from_windows(windows, images, tile_rows, tile_cols):
    features = windows.shape[-1]
    blocks = windows.reshape(images, tile_rows // WIN, tile_cols // WIN, WIN, WIN, features)
    return blocks.transpose(0, 1, 3, 2, 4, 5).reshape(images, tile_rows, tile_cols, features)

def spatial_mix(normed, valid_cells, weight, bias_vec, proj_weight, out_row):
    images, tile_rows, tile_cols, features = normed.shape
    qkv_rows = low(low_back(linear_map(normed.reshape(-1, features), weight) + bias_vec))
    qkv_parts = to_windows(qkv_rows.reshape(images, tile_rows, tile_cols, 3 * features))
    windows_count = qkv_parts.shape[0]
    qkv_parts = qkv_parts.reshape(windows_count, WIN * WIN, 3, HEADS, HD)
    scores = jnp.einsum('wqhd,wkhd->whqk', qkv_parts[:, :, 0], qkv_parts[:, :, 1], precision=highest) * HD ** (-0.5)
    scores = low_back(scores)
    key_valid = to_windows(valid_cells[..., None])[:, :, 0]
    scores = jnp.where(key_valid[:, None, None, :], scores, -1e+30)
    attn_prob = low(softmax_last(scores))
    mixed_out = jnp.einsum('whqk,wkhd->wqhd', attn_prob, qkv_parts[:, :, 2], precision=highest)
    mixed_out = low(low_back(mixed_out.reshape(windows_count, WIN * WIN, features)))
    merged = from_windows(mixed_out, images, tile_rows, tile_cols).reshape(-1, features)
    return low_back(linear_map(merged, proj_weight) + out_row).reshape(normed.shape)

def channel_mix(normed, cell_mask, weight, bias_vec, proj_weight, out_row):
    images, tile_rows, tile_cols, features = normed.shape
    tokens = tile_rows * tile_cols
    qkv_rows = low(low_back(linear_map(normed.reshape(-1, features), weight) + bias_vec))
    qkv_parts = qkv_rows.reshape(images, tokens, 3, HEADS, HD)
    masked_keys = qkv_parts[:, :, 1] * cell_mask.reshape(images, tokens, 1, 1)
    scores = jnp.einsum('gnhd,gnhe->ghde', qkv_parts[:, :, 0], masked_keys, precision=highest) * HD ** (-0.5)
    scores = low_back(scores)
    attn_prob = low(softmax_last(scores))
    mixed_out = jnp.einsum('ghde,gnhe->gnhd', attn_prob, qkv_parts[:, :, 2], precision=highest)
    mixed_out = low(low_back(mixed_out.reshape(-1, features)))
    return low_back(linear_map(mixed_out, proj_weight) + out_row).reshape(normed.shape)

def mlp_mix(normed, in_weight, hidden_row, out_weight, out_row):
    features = normed.shape[-1]
    hidden = low_back(linear_map(normed.reshape(-1, features), in_weight) + hidden_row)
    active = low(gelu_exact(hidden))
    return low_back(linear_map(active, out_weight) + out_row).reshape(normed.shape)

def dual_block(params, images_in, cell_mask, valid_cells):
    conv_weight, conv_bias, norm_gain, norm_bias, spatial_qkv, channel_qkv, projection, mlp_in, mlp_out, attn_bias, hidden_bias, out_bias = params
    mask_cells = cell_mask[..., None]
    spatial_bias = jnp.concatenate([attn_bias[0], jnp.zeros_like(attn_bias[0]), attn_bias[1]])
    channel_bias = attn_bias[2:5].reshape(-1)
    stream = images_in + depthwise(images_in * mask_cells, conv_weight[0], conv_bias[0])
    stream = stream + spatial_mix(low(layer_norm(stream, norm_gain[0], norm_bias[0])), valid_cells, spatial_qkv, spatial_bias, projection[0], out_bias[0])
    stream = stream + depthwise(stream * mask_cells, conv_weight[1], conv_bias[1])
    stream = stream + mlp_mix(low(layer_norm(stream, norm_gain[1], norm_bias[1])), mlp_in[0], hidden_bias[0], mlp_out[0], out_bias[1])
    stream = stream + depthwise(stream * mask_cells, conv_weight[2], conv_bias[2])
    stream = stream + channel_mix(low(layer_norm(stream, norm_gain[2], norm_bias[2])), cell_mask, channel_qkv, channel_bias, projection[1], out_bias[2])
    stream = stream + depthwise(stream * mask_cells, conv_weight[3], conv_bias[3])
    stream = stream + mlp_mix(low(layer_norm(stream, norm_gain[3], norm_bias[3])), mlp_in[1], hidden_bias[1], mlp_out[1], out_bias[3])
    return stream * mask_cells

def reference(inputs, heights, widths, conv_weight, conv_bias, norm_gain, norm_bias, spatial_qkv, channel_qkv, projection, mlp_in, mlp_out, attn_bias, hidden_bias, out_bias, cotangent):
    row_ids = jnp.arange(TILE_ROWS, dtype=jnp.int32)
    col_ids = jnp.arange(TILE_COLS, dtype=jnp.int32)
    valid_cells = (row_ids[None, :, None] < heights[:, None, None]) & (col_ids[None, None, :] < widths[:, None, None])
    cell_mask = valid_cells.astype(jnp.float32)
    params = tuple((weight.astype(jnp.float32) for weight in (conv_weight, conv_bias, norm_gain, norm_bias, spatial_qkv, channel_qkv, projection, mlp_in, mlp_out, attn_bias, hidden_bias, out_bias)))
    group_size = 8
    groups = IMAGES // group_size

    def whole_block(params, images_in):

        def one_group(group_item):
            return dual_block(params, group_item[0], group_item[1], group_item[2])
        stacked = (images_in.reshape(groups, group_size, TILE_ROWS, TILE_COLS, D), cell_mask.reshape(groups, group_size, TILE_ROWS, TILE_COLS), valid_cells.reshape(groups, group_size, TILE_ROWS, TILE_COLS))
        result = lax.map(jax.checkpoint(one_group), stacked)
        return result.reshape(IMAGES, TILE_ROWS, TILE_COLS, D)
    block_out, pull_back = jax.vjp(whole_block, params, inputs.astype(jnp.float32))
    param_grads, input_grad = pull_back(cotangent.astype(jnp.float32))
    return (block_out.astype(jnp.bfloat16), input_grad.astype(jnp.bfloat16), param_grads[0], param_grads[1], param_grads[2], param_grads[3], param_grads[4], param_grads[5], param_grads[6], param_grads[7], param_grads[8], param_grads[9], param_grads[10], param_grads[11])
```

```python
import functools

import jax
import jax.numpy as jnp
from jax import lax
from jax.experimental import pallas as pl
from jax.experimental.pallas import tpu as pltpu
from jax.sharding import PartitionSpec as P

HD = 32
WIN = 7
LANES = 128
SUB = 8
GROUP = 256
WTOK = WIN * SUB
FFC = 512
SCALE = HD ** (-0.5)
EPS = 1e-05
NEG = -1e30
F32 = jnp.float32
BF16 = jnp.bfloat16
VMEM_LIMIT = 60 * 1024 * 1024
DIMS_NN = (((1,), (0,)), ((), ()))
DIMS_NT = (((1,), (1,)), ((), ()))
DIMS_TN = (((0,), (0,)), ((), ()))


def dot(a, b, dims):
    return lax.dot_general(a, b, dims, preferred_element_type=F32)


def tok(r, half):
    return ((r // WIN) * 2 + half) * WTOK + (r % WIN) * SUB


def load_cells(src, dst):
    for r in range(2 * WIN):
        row = src[0, r].astype(F32)
        dst[pl.ds(tok(r, 0), WIN), :] = row[:WIN]
        dst[pl.ds(tok(r, 1), WIN), :] = row[WIN:]


def store_cells(value_at, dst, stage):
    for r in range(2 * WIN):
        stage[pl.ds(0, SUB), :] = value_at(tok(r, 0))
        stage[pl.ds(WIN, SUB), :] = value_at(tok(r, 1))
        dst[0, r] = stage[pl.ds(0, 2 * WIN), :].astype(BF16)


def neighbours(left, right):
    last = lax.broadcasted_iota(jnp.int32, (SUB, LANES), 0) == SUB - 1
    up_right = pltpu.roll(right, SUB - 1, 0)
    up_left = pltpu.roll(jnp.where(last, up_right, left), SUB - 1, 0)
    down_left = pltpu.roll(left, 1, 0)
    down_right = pltpu.roll(jnp.where(last, down_left, right), 1, 0)
    return ((down_left, left, up_left), (down_right, right, up_right))


def masked_row(src, mask, r, lanes):
    pair = []
    for half in range(2):
        rows = pl.ds(tok(r, half), SUB)
        pair.append(src[rows, lanes] * mask[0, rows, :])
    return neighbours(*pair)


def plain_row(src, r, lanes):
    return neighbours(*[src[pl.ds(tok(r, half), SUB), lanes] for half in range(2)])


def taps(weight, lanes):
    return [jnp.broadcast_to(weight[pl.ds(k, 1), lanes], (SUB, LANES)) for k in range(9)]


def conv_forward(src, mask, weight, bias, dst):
    rows = 2 * WIN

    @pl.loop(0, src.shape[1] // LANES)
    def _(j):
        lanes = pl.ds(pl.multiple_of(j * LANES, LANES), LANES)
        w = taps(weight, lanes)
        shift = jnp.broadcast_to(bias[:, lanes], (SUB, LANES))
        window = [None, masked_row(src, mask, 0, lanes), masked_row(src, mask, 1, lanes)]
        for r in range(rows):
            for half in range(2):
                total = shift
                for a in range(3):
                    if window[a] is None:
                        continue
                    for b in range(3):
                        total = total + w[3 * a + b] * window[a][half][b]
                at = pl.ds(tok(r, half), SUB)
                dst[at, lanes] = src[at, lanes] + total
            following = masked_row(src, mask, r + 2, lanes) if r + 2 < rows else None
            window = [window[1], window[2], following]


def conv_backward(x_src, g_src, mask, weight, sums, dst):
    rows = 2 * WIN

    @pl.loop(0, x_src.shape[1] // LANES)
    def _(j):
        lanes = pl.ds(pl.multiple_of(j * LANES, LANES), LANES)
        w = taps(weight, lanes)
        g_win = [None, plain_row(g_src, 0, lanes), plain_row(g_src, 1, lanes)]
        x_win = [None, masked_row(x_src, mask, 0, lanes), masked_row(x_src, mask, 1, lanes)]
        grads = [sums[pl.ds(SUB * k, SUB), lanes] for k in range(10)]
        for r in range(rows):
            for half in range(2):
                center = g_win[1][half][1]
                total = None
                for a in range(3):
                    for b in range(3):
                        if x_win[a] is not None:
                            grads[3 * a + b] = grads[3 * a + b] + center * x_win[a][half][b]
                        if g_win[2 - a] is not None:
                            term = w[3 * a + b] * g_win[2 - a][half][2 - b]
                            total = term if total is None else total + term
                grads[9] = grads[9] + center
                at = pl.ds(tok(r, half), SUB)
                dst[at, lanes] = center + mask[0, at, :] * total
            more = r + 2 < rows
            g_win = [g_win[1], g_win[2], plain_row(g_src, r + 2, lanes) if more else None]
            x_win = [x_win[1], x_win[2], masked_row(x_src, mask, r + 2, lanes) if more else None]
        for k in range(10):
            sums[pl.ds(SUB * k, SUB), lanes] = grads[k]


def norm_forward(src, gain, bias, z_out, r_out, n_out):
    features = src.shape[1]

    @pl.loop(0, src.shape[0] // 16)
    def _(i):
        rows = pl.ds(pl.multiple_of(i * 16, 16), 16)
        x = src[rows, :]
        center = x - jnp.sum(x, axis=1, keepdims=True) * (1.0 / features)
        var = jnp.sum(center * center, axis=1, keepdims=True) * (1.0 / features)
        rstd = lax.rsqrt(var + EPS)
        z = center * rstd
        z_out[rows, :] = z
        r_out[rows, :] = jnp.broadcast_to(rstd, (16, LANES))
        n_out[rows, :] = (z * gain[...] + bias[...]).astype(BF16)


def norm_backward(dn, z_src, r_src, gain, g_src, sums, first, dst):
    features = dn.shape[1]
    gain_sum = sums[pl.ds(first, SUB), :]
    bias_sum = sums[pl.ds(first + SUB, SUB), :]

    def step(i, carry):
        gain_sum, bias_sum = carry
        rows = pl.ds(pl.multiple_of(i * SUB, SUB), SUB)
        d = dn[rows, :]
        z = z_src[rows, :]
        t = d * gain[...]
        m1 = jnp.sum(t, axis=1, keepdims=True) * (1.0 / features)
        m2 = jnp.sum(t * z, axis=1, keepdims=True) * (1.0 / features)
        dst[rows, :] = g_src[rows, :] + (t - m1 - z * m2) * r_src[rows, 0:1]
        return (gain_sum + d * z, bias_sum + d)

    gain_sum, bias_sum = lax.fori_loop(0, dn.shape[0] // SUB, step, (gain_sum, bias_sum))
    sums[pl.ds(first, SUB), :] = gain_sum
    sums[pl.ds(first + SUB, SUB), :] = bias_sum


def fold_rows(value):
    total = value[:SUB]
    for i in range(1, value.shape[0] // SUB):
        total = total + value[SUB * i : SUB * (i + 1)]
    return total


def finish_sums(sums, out):
    for k in range(sums.shape[0] // SUB):
        out[pl.ds(k, 1), :] = jnp.sum(sums[pl.ds(SUB * k, SUB), :], axis=0, keepdims=True)


def head_masks():
    lane = lax.broadcasted_iota(jnp.int32, (WTOK, GROUP), 1) // HD
    return [lane == h for h in range(GROUP // HD)]


def spread_heads(value, masks):
    return jnp.concatenate([jnp.where(m, value, 0.0) for m in masks], axis=0).astype(BF16)


def collect_heads(full, masks):
    total = full[:WTOK]
    for h in range(1, len(masks)):
        total = jnp.where(masks[h], full[WTOK * h : WTOK * (h + 1)], total)
    return total


def rounded(value):
    return value.astype(BF16).astype(F32)


def gelu_pair(h):
    cdf = 0.5 * (1.0 + lax.erf(h * 0.7071067811865476))
    pdf = jnp.exp(h * h * -0.5) * 0.3989422804014327
    return h * cdf, cdf + h * pdf


def first_step():
    return pl.program_id(0) == 0


def last_step():
    return pl.program_id(0) == pl.num_programs(0) - 1


def window_forward_kernel(
    inp, mask, conv_w, conv_b, gain, bias, wq, qb, wp, ob,
    n_out, z_out, r_out, q_out, o_out, p_out, x_out,
    x0, x1, qf, of,
):
    features = x0.shape[1]

    @pl.when(first_step())
    def _():
        x0[...] = jnp.zeros_like(x0)

    load_cells(inp, x0)
    conv_forward(x0, mask, conv_w, conv_b, x1)
    norm_forward(x1, gain, bias, z_out.at[0], r_out.at[0], n_out.at[0])
    chunk = features
    for c in range(3):
        lanes = pl.ds(c * chunk, chunk)
        part = (dot(n_out[0], wq[:, lanes], DIMS_NN) + qb[:, lanes]).astype(BF16)
        q_out[0, :, lanes] = part
        qf[:, lanes] = part.astype(F32)

    @pl.loop(0, 4)
    def _(w):
        rows = pl.ds(pl.multiple_of(w * WTOK, SUB), WTOK)
        valid = mask[0, rows, 0:1] > 0.0
        masks = head_masks()
        for g in range(features // GROUP):
            q = qf[rows, pl.ds(g * GROUP, GROUP)]
            k = qf[rows, pl.ds(features + g * GROUP, GROUP)].astype(BF16)
            v = qf[rows, pl.ds(2 * features + g * GROUP, GROUP)].astype(BF16)
            s = dot(k, spread_heads(q, masks), DIMS_NT) * SCALE
            s = jnp.where(valid, s, NEG)
            e = jnp.exp(s - jnp.max(s, axis=0, keepdims=True))
            p = (e / jnp.sum(e, axis=0, keepdims=True)).astype(BF16)
            p_out[0, w, g] = p
            of[rows, pl.ds(g * GROUP, GROUP)] = collect_heads(dot(p, v, DIMS_TN), masks)

    o_out[0] = of[...].astype(BF16)
    x_out[0] = x1[...] + (dot(o_out[0], wp[...], DIMS_NN) + ob[...])


def mlp_forward_kernel(
    x_in, mask, conv_w, conv_b, gain, bias, w_in, hb, w_out, ob,
    n_out, z_out, r_out, u_out, d_out, x_out,
    x1, acc,
):
    conv_forward(x_in.at[0], mask, conv_w, conv_b, x1)
    norm_forward(x1, gain, bias, z_out.at[0], r_out.at[0], n_out.at[0])
    for c in range(w_in.shape[1] // FFC):
        lanes = pl.ds(c * FFC, FFC)
        h = dot(n_out[0], w_in[:, lanes], DIMS_NN) + hb[:, lanes]
        u, d = gelu_pair(h)
        u = u.astype(BF16)
        u_out[0, :, lanes] = u
        d_out[0, :, lanes] = d.astype(BF16)
        y = dot(u, w_out[:, lanes], DIMS_NT)
        acc[...] = y if c == 0 else acc[...] + y
    x_out[0] = x1[...] + (acc[...] + ob[...])


def group_mask():
    row = lax.broadcasted_iota(jnp.int32, (GROUP, GROUP), 0) // HD
    col = lax.broadcasted_iota(jnp.int32, (GROUP, GROUP), 1) // HD
    return row == col


def channel_forward_kernel(
    x_in, mask, conv_w, conv_b, gain, bias, wq, qb, wp, ob,
    n_out, z_out, r_out, q_out, o_out, a_out, x_out,
    x1,
):
    features = x1.shape[1]
    conv_forward(x_in.at[0], mask, conv_w, conv_b, x1)
    norm_forward(x1, gain, bias, z_out.at[0], r_out.at[0], n_out.at[0])
    for c in range(3):
        lanes = pl.ds(c * features, features)
        part = dot(n_out[0], wq[:, lanes], DIMS_NN) + qb[:, lanes]
        if c == 1:
            part = part * mask[0, :, 0:1]
        q_out[0, :, lanes] = part.astype(BF16)
    same = group_mask()
    for g in range(features // GROUP):
        q = q_out[0, :, pl.ds(g * GROUP, GROUP)]
        k = q_out[0, :, pl.ds(features + g * GROUP, GROUP)]
        v = q_out[0, :, pl.ds(2 * features + g * GROUP, GROUP)]
        s = jnp.where(same, dot(k, q, DIMS_TN) * SCALE, -jnp.inf)
        e = jnp.exp(s - jnp.max(s, axis=0, keepdims=True))
        a = (e / jnp.sum(e, axis=0, keepdims=True)).astype(BF16)
        a_out[0, g] = a
        o_out[0, :, pl.ds(g * GROUP, GROUP)] = dot(v, a, DIMS_NN).astype(BF16)
    x_out[0] = x1[...] + (dot(o_out[0], wp[...], DIMS_NN) + ob[...])


def last_mlp_kernel(
    x_in, cot, mask, conv_w, conv_b, gain, bias, w_in, hb, w_out, ob,
    out, g_out, n_out, u_out, gy_out, gh_out, small_out, hidden_out,
    x1, z, r, acc, dn, g8, stage, sums, hsums,
):
    @pl.when(first_step())
    def _():
        g8[...] = jnp.zeros_like(g8)
        sums[...] = jnp.zeros_like(sums)
        hsums[...] = jnp.zeros_like(hsums)

    x6 = x_in.at[0]
    load_cells(cot, g8)
    conv_forward(x6, mask, conv_w, conv_b, x1)
    norm_forward(x1, gain, bias, z, r, n_out.at[0])
    g8[...] = g8[...] * mask[0, :, 0:1]
    gy_out[0] = g8[...].astype(BF16)
    sums[pl.ds(12 * SUB, SUB), :] = sums[pl.ds(12 * SUB, SUB), :] + fold_rows(gy_out[0].astype(F32))
    for c in range(w_in.shape[1] // FFC):
        lanes = pl.ds(c * FFC, FFC)
        h = dot(n_out[0], w_in[:, lanes], DIMS_NN) + hb[:, lanes]
        du = dot(gy_out[0], w_out[:, lanes], DIMS_NN)
        u, d = gelu_pair(h)
        u = u.astype(BF16)
        u_out[0, :, lanes] = u
        gh = (du * d).astype(BF16)
        gh_out[0, :, lanes] = gh
        hsums[:, lanes] = hsums[:, lanes] + fold_rows(gh.astype(F32))
        y = dot(u, w_out[:, lanes], DIMS_NT)
        dx = dot(gh, w_in[:, lanes], DIMS_NT)
        acc[...] = y if c == 0 else acc[...] + y
        dn[...] = dx if c == 0 else dn[...] + dx
    acc[...] = (x1[...] + (acc[...] + ob[...])) * mask[0, :, 0:1]
    store_cells(lambda at: acc[pl.ds(at, SUB), :], out, stage)
    norm_backward(dn, z, r, gain, g8, sums, 10 * SUB, x1)
    conv_backward(x6, x1, mask, conv_w, sums, g_out.at[0])

    @pl.when(last_step())
    def _():
        finish_sums(sums, small_out)
        finish_sums(hsums, hidden_out)


def mlp_backward_kernel(
    g_in, x_in, z_in, r_in, d_in, mask, conv_w, gain, w_in, w_out,
    g_out, gy_out, gh_out, small_out, hidden_out,
    dn, g1, sums, hsums,
):
    @pl.when(first_step())
    def _():
        sums[...] = jnp.zeros_like(sums)
        hsums[...] = jnp.zeros_like(hsums)

    gy_out[0] = g_in[0].astype(BF16)
    sums[pl.ds(12 * SUB, SUB), :] = sums[pl.ds(12 * SUB, SUB), :] + fold_rows(gy_out[0].astype(F32))
    for c in range(w_in.shape[1] // FFC):
        lanes = pl.ds(c * FFC, FFC)
        du = dot(gy_out[0], w_out[:, lanes], DIMS_NN)
        gh = (du * d_in[0, :, lanes].astype(F32)).astype(BF16)
        gh_out[0, :, lanes] = gh
        hsums[:, lanes] = hsums[:, lanes] + fold_rows(gh.astype(F32))
        dx = dot(gh, w_in[:, lanes], DIMS_NT)
        dn[...] = dx if c == 0 else dn[...] + dx
    norm_backward(dn, z_in.at[0], r_in.at[0], gain, g_in.at[0], sums, 10 * SUB, g1)
    conv_backward(x_in.at[0], g1, mask, conv_w, sums, g_out.at[0])

    @pl.when(last_step())
    def _():
        finish_sums(sums, small_out)
        finish_sums(hsums, hidden_out)


def channel_backward_kernel(
    g_in, x_in, z_in, r_in, q_in, a_in, mask, conv_w, gain, wq, wp,
    g_out, ga_out, dq_out, small_out, bias_out,
    dn, g1, sums, bsums,
):
    features = dn.shape[1]

    @pl.when(first_step())
    def _():
        sums[...] = jnp.zeros_like(sums)
        bsums[...] = jnp.zeros_like(bsums)

    ga_out[0] = g_in[0].astype(BF16)
    sums[pl.ds(12 * SUB, SUB), :] = sums[pl.ds(12 * SUB, SUB), :] + fold_rows(ga_out[0].astype(F32))
    go = dot(ga_out[0], wp[...], DIMS_NT).astype(BF16)
    for g in range(features // GROUP):
        at = [pl.ds(i * features + g * GROUP, GROUP) for i in range(3)]
        q, k, v = (q_in[0, :, lanes] for lanes in at)
        gog = go[:, g * GROUP : (g + 1) * GROUP]
        a = a_in[0, g]
        af = a.astype(F32)
        dp = dot(v, gog, DIMS_TN)
        ds = (af * (dp - jnp.sum(dp * af, axis=0, keepdims=True))).astype(BF16)
        dq_out[0, :, at[0]] = (dot(k, ds, DIMS_NN) * SCALE).astype(BF16)
        dq_out[0, :, at[1]] = (dot(q, ds, DIMS_NT) * SCALE * mask[0, :, 0:1]).astype(BF16)
        dq_out[0, :, at[2]] = dot(gog, a, DIMS_NT).astype(BF16)
    bsums[...] = bsums[...] + fold_rows(dq_out[0].astype(F32))
    dn[...] = dot(dq_out[0], wq[...], DIMS_NT)
    norm_backward(dn, z_in.at[0], r_in.at[0], gain, g_in.at[0], sums, 10 * SUB, g1)
    conv_backward(x_in.at[0], g1, mask, conv_w, sums, g_out.at[0])

    @pl.when(last_step())
    def _():
        finish_sums(sums, small_out)
        finish_sums(bsums, bias_out)


def window_backward_kernel(
    g_in, inp, z_in, r_in, q_in, p_in, mask, conv_w, gain, wq, wp,
    g_out, ga_out, dq_out, small_out, bias_out,
    x0, qf, gof, dqf, dn, g1, stage, sums, bsums,
):
    features = dn.shape[1]

    @pl.when(first_step())
    def _():
        x0[...] = jnp.zeros_like(x0)
        sums[...] = jnp.zeros_like(sums)
        bsums[...] = jnp.zeros_like(bsums)

    load_cells(inp, x0)
    ga_out[0] = g_in[0].astype(BF16)
    sums[pl.ds(12 * SUB, SUB), :] = sums[pl.ds(12 * SUB, SUB), :] + fold_rows(ga_out[0].astype(F32))
    gof[...] = rounded(dot(ga_out[0], wp[...], DIMS_NT))
    qf[...] = q_in[0].astype(F32)

    @pl.loop(0, 4)
    def _(w):
        rows = pl.ds(pl.multiple_of(w * WTOK, SUB), WTOK)
        masks = head_masks()
        for g in range(features // GROUP):
            at = [pl.ds(i * features + g * GROUP, GROUP) for i in range(3)]
            qe = spread_heads(qf[rows, at[0]], masks)
            k = qf[rows, at[1]].astype(BF16)
            v = qf[rows, at[2]].astype(BF16)
            goe = spread_heads(gof[rows, at[0]], masks)
            p = p_in[0, w, g]
            pf = p.astype(F32)
            dp = dot(v, goe, DIMS_NT)
            ds = (pf * (dp - jnp.sum(dp * pf, axis=0, keepdims=True))).astype(BF16)
            dqf[rows, at[0]] = collect_heads(dot(ds, k, DIMS_TN), masks) * SCALE
            dqf[rows, at[1]] = dot(ds, qe, DIMS_NN) * SCALE
            dqf[rows, at[2]] = dot(p, goe, DIMS_NN)

    dq_out[0] = dqf[...].astype(BF16)
    bsums[...] = bsums[...] + fold_rows(dq_out[0].astype(F32))
    dn[...] = dot(dq_out[0], wq[...], DIMS_NT)
    norm_backward(dn, z_in.at[0], r_in.at[0], gain, g_in.at[0], sums, 10 * SUB, g1)
    conv_backward(x0, g1, mask, conv_w, sums, dn)
    store_cells(lambda at: dn[pl.ds(at, SUB), :], g_out, stage)

    @pl.when(last_step())
    def _():
        finish_sums(sums, small_out)
        finish_sums(bsums, bias_out)


def per_image(shape):
    rest = (0,) * (len(shape) - 1)
    return pl.BlockSpec((1,) + tuple(shape[1:]), lambda i: (i,) + rest)


def whole(shape):
    zeros = (0,) * len(shape)
    return pl.BlockSpec(tuple(shape), lambda i: zeros, pipeline_mode=pl.Buffered(1))


def image_call(kernel, name, images, args, outs, scratch, flops):
    ins = [per_image(a.shape) if batched else whole(a.shape) for a, batched in args]
    out_specs = [
        per_image(s) if batched else pl.BlockSpec(tuple(s), lambda i, n=len(s): (0,) * n)
        for s, _, batched in outs
    ]
    size = sum(a.size * a.dtype.itemsize for a, _ in args)
    size += sum(jnp.dtype(d).itemsize * functools.reduce(lambda p, q: p * q, s) for s, d, _ in outs)
    return pl.pallas_call(
        kernel,
        grid=(images,),
        in_specs=ins,
        out_specs=out_specs,
        out_shape=[jax.ShapeDtypeStruct(s, d) for s, d, _ in outs],
        scratch_shapes=[pltpu.VMEM(s, d) for s, d in scratch],
        compiler_params=pltpu.CompilerParams(
            dimension_semantics=("arbitrary",), vmem_limit_bytes=VMEM_LIMIT
        ),
        cost_estimate=pl.CostEstimate(flops=int(flops), bytes_accessed=int(size), transcendentals=0),
        name=name,
    )(*[a for a, _ in args])


def token_mask(heights, widths):
    t = jnp.arange(4 * WTOK, dtype=jnp.int32)
    window = t // WTOK
    row = (window // 2) * WIN + (t % WTOK) // SUB
    col8 = t % SUB
    col = (window % 2) * WIN + col8
    valid = (row[None] < heights[:, None]) & (col[None] < widths[:, None]) & (col8 < WIN)[None]
    return jnp.broadcast_to(valid.astype(F32)[..., None], valid.shape + (LANES,))


def forward_window(inputs, mask, conv_w, conv_b, gain, bias, wq, qb, wp, ob):
    images, _, _, c = inputs.shape
    t = 4 * WTOK
    rows = images * t
    args = [(inputs, 1), (mask, 1)] + [(a, 0) for a in (conv_w, conv_b, gain, bias, wq, qb, wp, ob)]
    outs = [
        ((images, t, c), BF16, 1), ((images, t, c), F32, 1), ((images, t, LANES), F32, 1),
        ((images, t, 3 * c), BF16, 1), ((images, t, c), BF16, 1),
        ((images, 4, c // GROUP, WTOK, WTOK * GROUP // HD), BF16, 1), ((images, t, c), F32, 1),
    ]
    scratch = [((t, c), F32), ((t, c), F32), ((t, 3 * c), F32), ((t, c), F32)]
    return image_call(window_forward_kernel, "window_forward", images, args, outs, scratch, 10 * rows * c * c)


def forward_mlp(x, mask, conv_w, conv_b, gain, bias, w_in, hb, w_out, ob):
    images, t, c = x.shape
    ff = w_in.shape[1]
    args = [(x, 1), (mask, 1)] + [(a, 0) for a in (conv_w, conv_b, gain, bias, w_in, hb, w_out, ob)]
    outs = [
        ((images, t, c), BF16, 1), ((images, t, c), F32, 1), ((images, t, LANES), F32, 1),
        ((images, t, ff), BF16, 1), ((images, t, ff), BF16, 1), ((images, t, c), F32, 1),
    ]
    scratch = [((t, c), F32), ((t, c), F32)]
    return image_call(mlp_forward_kernel, "mlp_forward", images, args, outs, scratch, 4 * images * t * c * ff)


def forward_channel(x, mask, conv_w, conv_b, gain, bias, wq, qb, wp, ob):
    images, t, c = x.shape
    args = [(x, 1), (mask, 1)] + [(a, 0) for a in (conv_w, conv_b, gain, bias, wq, qb, wp, ob)]
    outs = [
        ((images, t, c), BF16, 1), ((images, t, c), F32, 1), ((images, t, LANES), F32, 1),
        ((images, t, 3 * c), BF16, 1), ((images, t, c), BF16, 1),
        ((images, c // GROUP, GROUP, GROUP), BF16, 1), ((images, t, c), F32, 1),
    ]
    return image_call(channel_forward_kernel, "channel_forward", images, args, outs, [((t, c), F32)], 9 * images * t * c * c)


def last_mlp(x, cot, mask, conv_w, conv_b, gain, bias, w_in, hb, w_out, ob):
    images, t, c = x.shape
    ff = w_in.shape[1]
    args = [(x, 1), (cot, 1), (mask, 1)] + [(a, 0) for a in (conv_w, conv_b, gain, bias, w_in, hb, w_out, ob)]
    outs = [
        (cot.shape, BF16, 1), ((images, t, c), F32, 1), ((images, t, c), BF16, 1), ((images, t, ff), BF16, 1),
        ((images, t, c), BF16, 1), ((images, t, ff), BF16, 1), ((13, c), F32, 0), ((1, ff), F32, 0),
    ]
    scratch = [
        ((t, c), F32), ((t, c), F32), ((t, LANES), F32), ((t, c), F32), ((t, c), F32), ((t, c), F32),
        ((16, c), F32), ((13 * SUB, c), F32), ((SUB, ff), F32),
    ]
    return image_call(last_mlp_kernel, "last_mlp", images, args, outs, scratch, 8 * images * t * c * ff)


def backward_mlp(g, x, z, r, d, mask, conv_w, gain, w_in, w_out):
    images, t, c = x.shape
    ff = w_in.shape[1]
    args = [(g, 1), (x, 1), (z, 1), (r, 1), (d, 1), (mask, 1)] + [(a, 0) for a in (conv_w, gain, w_in, w_out)]
    outs = [
        ((images, t, c), F32, 1), ((images, t, c), BF16, 1), ((images, t, ff), BF16, 1),
        ((13, c), F32, 0), ((1, ff), F32, 0),
    ]
    scratch = [((t, c), F32), ((t, c), F32), ((13 * SUB, c), F32), ((SUB, ff), F32)]
    return image_call(mlp_backward_kernel, "mlp_backward", images, args, outs, scratch, 4 * images * t * c * ff)


def backward_channel(g, x, z, r, q, a, mask, conv_w, gain, wq, wp):
    images, t, c = x.shape
    args = [(v, 1) for v in (g, x, z, r, q, a, mask)] + [(v, 0) for v in (conv_w, gain, wq, wp)]
    outs = [
        ((images, t, c), F32, 1), ((images, t, c), BF16, 1), ((images, t, 3 * c), BF16, 1),
        ((13, c), F32, 0), ((1, 3 * c), F32, 0),
    ]
    scratch = [((t, c), F32), ((t, c), F32), ((13 * SUB, c), F32), ((SUB, 3 * c), F32)]
    return image_call(channel_backward_kernel, "channel_backward", images, args, outs, scratch, 10 * images * t * c * c)


def backward_window(g, inputs, z, r, q, p, mask, conv_w, gain, wq, wp):
    images, t, c = g.shape
    args = [(v, 1) for v in (g, inputs, z, r, q, p, mask)] + [(v, 0) for v in (conv_w, gain, wq, wp)]
    outs = [
        (inputs.shape, BF16, 1), ((images, t, c), BF16, 1), ((images, t, 3 * c), BF16, 1),
        ((13, c), F32, 0), ((1, 3 * c), F32, 0),
    ]
    scratch = [
        ((t, c), F32), ((t, 3 * c), F32), ((t, c), F32), ((t, 3 * c), F32), ((t, c), F32), ((t, c), F32),
        ((16, c), F32), ((13 * SUB, c), F32), ((SUB, 3 * c), F32),
    ]
    return image_call(window_backward_kernel, "window_backward", images, args, outs, scratch, 12 * images * t * c * c)


def weight_grad(left, right):
    rows = left.shape[0] * left.shape[1]
    return dot(left.reshape(rows, -1), right.reshape(rows, -1), DIMS_TN)


BOTH = ("narrow", "wide")


def spread(pieces):
    return lax.all_gather(pieces, BOTH, axis=0, tiled=False)


def pack_small(conv_weight, conv_bias, norm_gain, norm_bias, out_bias, attn_bias, hidden_bias, lanes):
    width = conv_bias.shape[1]
    rows = [conv_weight, conv_bias, norm_gain, norm_bias, out_bias, attn_bias, hidden_bias]
    flat = jnp.concatenate([item.reshape(-1, width) for item in rows])
    return pad_rows(flat, lanes)


def pad_rows(flat, lanes):
    per_row = lanes // flat.shape[-1]
    height = -(-flat.shape[-2] // (16 * per_row)) * 16
    pad = [(0, 0)] * (flat.ndim - 2) + [(0, height * per_row - flat.shape[-2]), (0, 0)]
    return jnp.pad(flat, pad).reshape(flat.shape[:-2] + (height, lanes))


def local(wide, narrow, inputs, heights, widths, conv_weight, conv_bias, norm_gain, norm_bias, spatial_qkv,
          channel_qkv, projection, mlp_in, mlp_out, attn_bias, hidden_bias, out_bias, cotangent):
    c = inputs.shape[-1]
    ff = hidden_bias.shape[1] * wide
    layers = 4 // narrow
    cw, fw, cn = c // wide, ff // wide, c // narrow
    halves = wide // narrow

    def attention_piece(qkv, proj):
        return jnp.concatenate([qkv.T, proj.T], axis=1)

    def mlp_piece(first, second):
        second = second.reshape(cw, halves, fw).transpose(1, 0, 2).reshape(cn, fw)
        return jnp.concatenate([first.T, second], axis=0)

    def attention_full(got):
        got = got.reshape(narrow, wide, cn, 4 * cw).transpose(0, 2, 1, 3)
        wq = got[..., : 3 * cw].reshape(c, 3 * c)
        wp = got[..., 3 * cw :].reshape(c, c)
        return wq, wp

    def mlp_full(got):
        got = got.reshape(narrow, wide, 2, cn, fw)
        w_in = got[:, :, 0].transpose(0, 2, 1, 3).reshape(c, ff)
        w_out = got[:, :, 1].reshape(narrow, wide, halves, cw, fw).transpose(1, 3, 0, 2, 4).reshape(c, ff)
        return w_in, w_out

    small = pack_small(conv_weight, conv_bias, norm_gain, norm_bias, out_bias, attn_bias, hidden_bias, 4 * cw)
    first = spread(jnp.concatenate([small, attention_piece(spatial_qkv, projection[0])]))
    mlp0 = spread(mlp_piece(mlp_in[0], mlp_out[0]))
    chan = spread(attention_piece(channel_qkv, projection[1]))
    mlp1 = spread(mlp_piece(mlp_in[1], mlp_out[1]))

    srows = small.shape[0]
    sm = first[:, :srows].reshape(narrow, wide, -1, cw)
    count = 13 * layers
    by_layer = sm[:, :, :count].astype(F32)
    shared = sm[0, :, count : count + 5 + 2 * fw // cw].astype(F32)

    def layer_rows(start, size):
        part = by_layer[:, :, start * layers : (start + size) * layers]
        return part.reshape(narrow, wide, layers, size, cw).transpose(0, 2, 3, 1, 4).reshape(4, size, c)

    kernels = layer_rows(0, 9)
    shifts, gains, norm_shifts, out_shifts = (layer_rows(k, 1) for k in range(9, 13))
    attn = shared[:, :5].transpose(1, 0, 2).reshape(5, c)
    hidden = shared[:, 5:].reshape(wide, 2, fw).transpose(1, 0, 2).reshape(2, 1, ff)
    qb0 = jnp.concatenate([attn[0], jnp.zeros_like(attn[0]), attn[1]])[None]
    qb1 = attn[2:5].reshape(1, 3 * c)

    wq0, wp0 = attention_full(first[:, srows:])
    win0, wout0 = mlp_full(mlp0)
    wq1, wp1 = attention_full(chan)
    win1, wout1 = mlp_full(mlp1)

    mask = token_mask(heights, widths)
    n1, z1, r1, q1, o1, p1, x2 = forward_window(
        inputs, mask, kernels[0], shifts[0], gains[0], norm_shifts[0], wq0, qb0, wp0, out_shifts[0])
    n2, z2, r2, u1, d1, x4 = forward_mlp(
        x2, mask, kernels[1], shifts[1], gains[1], norm_shifts[1], win0, hidden[0], wout0, out_shifts[1])
    n3, z3, r3, q3, o3, a3, x6 = forward_channel(
        x4, mask, kernels[2], shifts[2], gains[2], norm_shifts[2], wq1, qb1, wp1, out_shifts[2])
    out, g6, n4, u2, gy2, gh2, small3, hid1 = last_mlp(
        x6, cotangent, mask, kernels[3], shifts[3], gains[3], norm_shifts[3], win1, hidden[1], wout1, out_shifts[3])

    def mlp_pack(n, gh, gy, u):
        g_in = weight_grad(n, gh).astype(BF16).reshape(narrow, cn, wide, fw).transpose(0, 2, 1, 3)
        g_out = weight_grad(gy, u).astype(BF16).reshape(wide, cw, narrow, halves, fw).transpose(2, 0, 3, 1, 4)
        return jnp.concatenate([g_in, g_out.reshape(narrow, wide, cn, fw)], axis=2)

    def attention_pack(n, dq, o, ga):
        g_q = weight_grad(n, dq).astype(BF16).reshape(narrow, cn, wide, 3 * cw)
        g_p = weight_grad(o, ga).astype(BF16).reshape(narrow, cn, wide, cw)
        return jnp.concatenate([g_q, g_p], axis=3).transpose(0, 2, 1, 3)

    def reduce(packed):
        flat = packed.reshape((-1, packed.shape[-1]))
        return lax.psum_scatter(flat, BOTH, scatter_dimension=0, tiled=True)

    red1 = reduce(mlp_pack(n4, gh2, gy2, u2))
    g4, ga3, dq3, small2, cb = backward_channel(
        g6, x4, z3, r3, q3, a3, mask, kernels[2], gains[2], wq1, wp1)
    redc = reduce(attention_pack(n3, dq3, o3, ga3))
    g2, gy1, gh1, small1, hid0 = backward_mlp(
        g4, x2, z2, r2, d1, mask, kernels[1], gains[1], win0, wout0)
    red0 = reduce(mlp_pack(n2, gh1, gy1, u1))
    input_grad, ga1, dq1, small0, sb = backward_window(
        g2, inputs, z1, r1, q1, p1, mask, kernels[0], gains[0], wq0, wp0)

    smalls = jnp.stack([small0, small1, small2, small3])
    per_layer = jnp.concatenate([smalls[:, a:b].reshape(narrow, layers * (b - a), wide, cw)
                                 for a, b in ((0, 9), (9, 10), (10, 11), (11, 12), (12, 13))], axis=1)
    per_layer = per_layer.transpose(0, 2, 1, 3)
    sb = sb.reshape(3, c)
    attn_grad = jnp.concatenate([sb[0:1], sb[2:3], cb.reshape(3, c)]).reshape(5, wide, cw).transpose(1, 0, 2)
    hid_grad = jnp.concatenate([hid0, hid1]).reshape(2, wide, fw).transpose(1, 0, 2).reshape(wide, -1, cw)
    common = jnp.concatenate([attn_grad, hid_grad], axis=1)
    common = jnp.broadcast_to(common[None], (narrow,) + common.shape)
    small_pack = pad_rows(jnp.concatenate([per_layer, common], axis=2), 4 * cw).astype(BF16)
    reds = reduce(jnp.concatenate([small_pack, attention_pack(n1, dq1, o1, ga1)], axis=2))

    sm = reds[:srows].reshape(-1, cw).astype(F32)
    kernel_g = sm[: 9 * layers].reshape(layers, 9, cw)
    one = [sm[k * layers : (k + 1) * layers] for k in range(9, 13)]
    attn_g = sm[count : count + 5]
    hidden_g = sm[count + 5 : count + 5 + 2 * fw // cw].reshape(2, fw)

    def attention_split(red):
        red = red.astype(F32)
        return red[:, : 3 * cw].T, red[:, 3 * cw :].T

    def mlp_split(red):
        red = red.astype(F32)
        second = red[cn:].reshape(halves, cw, fw).transpose(1, 0, 2).reshape(cw, halves * fw)
        return red[:cn].T, second

    gq0, gp0 = attention_split(reds[srows:])
    gq1, gp1 = attention_split(redc)
    gi0, go0 = mlp_split(red0)
    gi1, go1 = mlp_split(red1)
    return (
        out, input_grad, kernel_g, one[0], one[1], one[2], gq0, gq1, jnp.stack([gp0, gp1]),
        jnp.stack([gi0, gi1]), jnp.stack([go0, go1]), attn_g, hidden_g, one[3],
    )


def solution(mesh):
    matrix = P("wide", "narrow")
    cells = P(("wide", "narrow"), None, None, None)
    stacked = P(None, "wide", "narrow")
    row = P("narrow", "wide")
    shared = P(None, "wide")
    images = P(("wide", "narrow"))
    kernels = P("narrow", None, "wide")
    in_specs = (
        cells, images, images, kernels, row, row, row, matrix, matrix,
        stacked, stacked, stacked, shared, shared, row, cells,
    )
    out_specs = (
        cells, cells, kernels, row, row, row, matrix, matrix, stacked, stacked, stacked, shared, shared, row,
    )
    body = functools.partial(local, mesh.shape["wide"], mesh.shape["narrow"])
    return jax.shard_map(body, mesh=mesh, in_specs=in_specs, out_specs=out_specs, check_vma=False)
```

```python
import functools

import jax
import jax.numpy as jnp
from jax import lax
from jax.experimental import pallas as pl
from jax.experimental.pallas import tpu as pltpu
from jax.sharding import PartitionSpec as P

HD = 32
WIN = 7
LANES = 128
SUB = 8
GROUP = 256
WTOK = WIN * SUB
FFC = 1024
NROWS = 112
SCALE = HD ** (-0.5)
EPS = 1e-05
NEG = -1e30
F32 = jnp.float32
BF16 = jnp.bfloat16
VMEM_LIMIT = 60 * 1024 * 1024
DIMS_NN = (((1,), (0,)), ((), ()))
DIMS_NT = (((1,), (1,)), ((), ()))
DIMS_TN = (((0,), (0,)), ((), ()))


def dot(a, b, dims):
    return lax.dot_general(a, b, dims, preferred_element_type=F32)


def tok(r, half):
    return ((r // WIN) * 2 + half) * WTOK + (r % WIN) * SUB


def load_cells(src, dst):
    for r in range(2 * WIN):
        row = src[0, r].astype(F32)
        dst[pl.ds(tok(r, 0), WIN), :] = row[:WIN]
        dst[pl.ds(tok(r, 1), WIN), :] = row[WIN:]


def store_cells(value_at, dst, stage):
    for r in range(2 * WIN):
        stage[pl.ds(0, SUB), :] = value_at(tok(r, 0))
        stage[pl.ds(WIN, SUB), :] = value_at(tok(r, 1))
        dst[0, r] = stage[pl.ds(0, 2 * WIN), :].astype(BF16)


def neighbours(left, right):
    last = lax.broadcasted_iota(jnp.int32, (SUB, LANES), 0) == SUB - 1
    up_right = pltpu.roll(right, SUB - 1, 0)
    up_left = pltpu.roll(jnp.where(last, up_right, left), SUB - 1, 0)
    down_left = pltpu.roll(left, 1, 0)
    down_right = pltpu.roll(jnp.where(last, down_left, right), 1, 0)
    return ((down_left, left, up_left), (down_right, right, up_right))


def masked_row(src, mask, r, lanes):
    pair = []
    for half in range(2):
        rows = pl.ds(tok(r, half), SUB)
        pair.append(src[rows, lanes] * mask[0, rows, :])
    return neighbours(*pair)


def plain_row(src, r, lanes):
    return neighbours(*[src[pl.ds(tok(r, half), SUB), lanes] for half in range(2)])


def lay_row(lay, k):
    return lay[0, pl.ds(k, 1), :]


def taps(lay, lanes):
    return [jnp.broadcast_to(lay[0, pl.ds(k, 1), lanes], (SUB, LANES)) for k in range(10)]


def conv_forward(src, mask, lay, dst):
    rows = 2 * WIN

    @pl.loop(0, src.shape[1] // LANES)
    def _(j):
        lanes = pl.ds(pl.multiple_of(j * LANES, LANES), LANES)
        w = taps(lay, lanes)
        shift = w[9]
        window = [None, masked_row(src, mask, 0, lanes), masked_row(src, mask, 1, lanes)]
        for r in range(rows):
            for half in range(2):
                total = shift
                for a in range(3):
                    if window[a] is None:
                        continue
                    for b in range(3):
                        total = total + w[3 * a + b] * window[a][half][b]
                at = pl.ds(tok(r, half), SUB)
                dst[at, lanes] = src[at, lanes] + total
            following = masked_row(src, mask, r + 2, lanes) if r + 2 < rows else None
            window = [window[1], window[2], following]


def conv_backward(x_src, g_src, mask, lay, sums, dst):
    rows = 2 * WIN

    @pl.loop(0, x_src.shape[1] // LANES)
    def _(j):
        lanes = pl.ds(pl.multiple_of(j * LANES, LANES), LANES)
        w = taps(lay, lanes)
        g_win = [None, plain_row(g_src, 0, lanes), plain_row(g_src, 1, lanes)]
        x_win = [None, masked_row(x_src, mask, 0, lanes), masked_row(x_src, mask, 1, lanes)]
        grads = [sums[pl.ds(SUB * k, SUB), lanes] for k in range(10)]
        for r in range(rows):
            for half in range(2):
                center = g_win[1][half][1]
                total = None
                for a in range(3):
                    for b in range(3):
                        if x_win[a] is not None:
                            grads[3 * a + b] = grads[3 * a + b] + center * x_win[a][half][b]
                        if g_win[2 - a] is not None:
                            term = w[3 * a + b] * g_win[2 - a][half][2 - b]
                            total = term if total is None else total + term
                grads[9] = grads[9] + center
                at = pl.ds(tok(r, half), SUB)
                dst[at, lanes] = center + mask[0, at, :] * total
            more = r + 2 < rows
            g_win = [g_win[1], g_win[2], plain_row(g_src, r + 2, lanes) if more else None]
            x_win = [x_win[1], x_win[2], masked_row(x_src, mask, r + 2, lanes) if more else None]
        for k in range(10):
            sums[pl.ds(SUB * k, SUB), lanes] = grads[k]


def norm_forward(src, lay, z_out, r_out, n_out):
    features = src.shape[1]

    @pl.loop(0, src.shape[0] // (2 * NROWS))
    def _(i):
        for j in range(2):
            rows = pl.ds(pl.multiple_of(i * (2 * NROWS) + j * NROWS, NROWS), NROWS)
            x = src[rows, :]
            center = x - jnp.sum(x, axis=1, keepdims=True) * (1.0 / features)
            var = jnp.sum(center * center, axis=1, keepdims=True) * (1.0 / features)
            rstd = lax.rsqrt(var + EPS)
            z = center * rstd
            z_out[rows, :] = z
            r_out[rows, :] = jnp.broadcast_to(rstd, (NROWS, LANES))
            n_out[rows, :] = (z * lay_row(lay, 10) + lay_row(lay, 11)).astype(BF16)


def norm_backward(dn, z_src, r_src, lay, g_src, sums, first, dst):
    features = dn.shape[1]

    @pl.loop(0, dn.shape[0] // (2 * NROWS))
    def _(i):
        for j in range(2):
            rows = pl.ds(pl.multiple_of(i * (2 * NROWS) + j * NROWS, NROWS), NROWS)
            d = dn[rows, :]
            z = z_src[rows, :]
            t = d * lay_row(lay, 10)
            m1 = jnp.sum(t, axis=1, keepdims=True) * (1.0 / features)
            m2 = jnp.sum(t * z, axis=1, keepdims=True) * (1.0 / features)
            dst[rows, :] = g_src[rows, :] + (t - m1 - z * m2) * r_src[rows, 0:1]
            at = pl.ds(first, SUB)
            sums[at, :] = sums[at, :] + fold_rows(d * z)
            at = pl.ds(first + SUB, SUB)
            sums[at, :] = sums[at, :] + fold_rows(d)


def fold_rows(value):
    total = value[:SUB]
    for i in range(1, value.shape[0] // SUB):
        total = total + value[SUB * i : SUB * (i + 1)]
    return total


def finish_sums(sums, out):
    for k in range(sums.shape[0] // SUB):
        out[pl.ds(k, 1), :] = jnp.sum(sums[pl.ds(SUB * k, SUB), :], axis=0, keepdims=True)


def head_masks():
    lane = lax.broadcasted_iota(jnp.int32, (WTOK, GROUP), 1) // HD
    return [lane == h for h in range(GROUP // HD)]


def spread_heads(value, masks):
    return jnp.concatenate([jnp.where(m, value, 0.0) for m in masks], axis=0).astype(BF16)


def collect_heads(full, masks):
    total = full[:WTOK]
    for h in range(1, len(masks)):
        total = jnp.where(masks[h], full[WTOK * h : WTOK * (h + 1)], total)
    return total


def rounded(value):
    return value.astype(BF16).astype(F32)


def gelu_pair(h):
    cdf = 0.5 * (1.0 + lax.erf(h * 0.7071067811865476))
    pdf = jnp.exp(h * h * -0.5) * 0.3989422804014327
    return h * cdf, cdf + h * pdf


def first_step():
    return pl.program_id(0) == 0


def last_step():
    return pl.program_id(0) == pl.num_programs(0) - 1


def window_forward_kernel(
    inp, mask, lay, sh, watt,
    n_out, z_out, r_out, q_out, o_out, p_out, x_out,
    x0, x1, qf, of,
):
    features = x0.shape[1]

    @pl.when(first_step())
    def _():
        x0[...] = jnp.zeros_like(x0)

    load_cells(inp, x0)
    conv_forward(x0, mask, lay, x1)
    norm_forward(x1, lay, z_out.at[0], r_out.at[0], n_out.at[0])
    chunk = features
    for c in range(3):
        lanes = pl.ds(c * chunk, chunk)
        part = dot(n_out[0], watt[:, lanes], DIMS_NN)
        if c != 1:
            part = part + sh[pl.ds(c // 2, 1), :]
        part = part.astype(BF16)
        q_out[0, :, lanes] = part
        qf[:, lanes] = part.astype(F32)

    @pl.loop(0, 4)
    def _(w):
        rows = pl.ds(pl.multiple_of(w * WTOK, SUB), WTOK)
        valid = mask[0, rows, 0:1] > 0.0
        masks = head_masks()
        for g in range(features // GROUP):
            q = qf[rows, pl.ds(g * GROUP, GROUP)]
            k = qf[rows, pl.ds(features + g * GROUP, GROUP)].astype(BF16)
            v = qf[rows, pl.ds(2 * features + g * GROUP, GROUP)].astype(BF16)
            s = dot(k, spread_heads(q, masks), DIMS_NT) * SCALE
            s = jnp.where(valid, s, NEG)
            e = jnp.exp(s - jnp.max(s, axis=0, keepdims=True))
            p = (e / jnp.sum(e, axis=0, keepdims=True)).astype(BF16)
            p_out[0, w, g] = p
            of[rows, pl.ds(g * GROUP, GROUP)] = collect_heads(dot(p, v, DIMS_TN), masks)

    o_out[0] = of[...].astype(BF16)
    x_out[0] = x1[...] + (dot(o_out[0], watt[:, pl.ds(3 * features, features)], DIMS_NN) + lay_row(lay, 12))


def mlp_forward_kernel(
    x_in, mask, lay, hb, w_in, w_out,
    n_out, z_out, r_out, u_out, d_out, x_out,
    x1, acc,
):
    conv_forward(x_in.at[0], mask, lay, x1)
    norm_forward(x1, lay, z_out.at[0], r_out.at[0], n_out.at[0])
    for c in range(w_in.shape[1] // FFC):
        lanes = pl.ds(c * FFC, FFC)
        h = dot(n_out[0], w_in[:, lanes], DIMS_NN) + hb[0, :, lanes]
        u, d = gelu_pair(h)
        u = u.astype(BF16)
        u_out[0, :, lanes] = u
        d_out[0, :, lanes] = d.astype(BF16)
        y = dot(u, w_out[:, lanes], DIMS_NT)
        acc[...] = y if c == 0 else acc[...] + y
    x_out[0] = x1[...] + (acc[...] + lay_row(lay, 12))


def group_mask():
    row = lax.broadcasted_iota(jnp.int32, (GROUP, GROUP), 0) // HD
    col = lax.broadcasted_iota(jnp.int32, (GROUP, GROUP), 1) // HD
    return row == col


def channel_forward_kernel(
    x_in, mask, lay, sh, watt,
    n_out, z_out, r_out, q_out, o_out, a_out, x_out,
    x1,
):
    features = x1.shape[1]
    conv_forward(x_in.at[0], mask, lay, x1)
    norm_forward(x1, lay, z_out.at[0], r_out.at[0], n_out.at[0])
    for c in range(3):
        lanes = pl.ds(c * features, features)
        part = dot(n_out[0], watt[:, lanes], DIMS_NN) + sh[pl.ds(2 + c, 1), :]
        if c == 1:
            part = part * mask[0, :, 0:1]
        q_out[0, :, lanes] = part.astype(BF16)
    same = group_mask()
    for g in range(features // GROUP):
        q = q_out[0, :, pl.ds(g * GROUP, GROUP)]
        k = q_out[0, :, pl.ds(features + g * GROUP, GROUP)]
        v = q_out[0, :, pl.ds(2 * features + g * GROUP, GROUP)]
        s = jnp.where(same, dot(k, q, DIMS_TN) * SCALE, -jnp.inf)
        e = jnp.exp(s - jnp.max(s, axis=0, keepdims=True))
        a = (e / jnp.sum(e, axis=0, keepdims=True)).astype(BF16)
        a_out[0, g] = a
        o_out[0, :, pl.ds(g * GROUP, GROUP)] = dot(v, a, DIMS_NN).astype(BF16)
    x_out[0] = x1[...] + (dot(o_out[0], watt[:, pl.ds(3 * features, features)], DIMS_NN) + lay_row(lay, 12))


def last_mlp_kernel(
    x_in, cot, mask, lay, hb, w_in, w_out,
    out, g_out, n_out, u_out, gy_out, gh_out, small_out, hidden_out,
    x1, z, r, acc, dn, g8, stage, sums, hsums,
):
    @pl.when(first_step())
    def _():
        g8[...] = jnp.zeros_like(g8)
        sums[...] = jnp.zeros_like(sums)
        hsums[...] = jnp.zeros_like(hsums)

    x6 = x_in.at[0]
    load_cells(cot, g8)
    conv_forward(x6, mask, lay, x1)
    norm_forward(x1, lay, z, r, n_out.at[0])
    g8[...] = g8[...] * mask[0, :, 0:1]
    gy_out[0] = g8[...].astype(BF16)
    sums[pl.ds(12 * SUB, SUB), :] = sums[pl.ds(12 * SUB, SUB), :] + fold_rows(gy_out[0].astype(F32))
    for c in range(w_in.shape[1] // FFC):
        lanes = pl.ds(c * FFC, FFC)
        h = dot(n_out[0], w_in[:, lanes], DIMS_NN) + hb[0, :, lanes]
        du = dot(gy_out[0], w_out[:, lanes], DIMS_NN)
        u, d = gelu_pair(h)
        u = u.astype(BF16)
        u_out[0, :, lanes] = u
        gh = (du * d).astype(BF16)
        gh_out[0, :, lanes] = gh
        hsums[:, lanes] = hsums[:, lanes] + fold_rows(gh.astype(F32))
        y = dot(u, w_out[:, lanes], DIMS_NT)
        dx = dot(gh, w_in[:, lanes], DIMS_NT)
        acc[...] = y if c == 0 else acc[...] + y
        dn[...] = dx if c == 0 else dn[...] + dx
    acc[...] = (x1[...] + (acc[...] + lay_row(lay, 12))) * mask[0, :, 0:1]
    store_cells(lambda at: acc[pl.ds(at, SUB), :], out, stage)
    norm_backward(dn, z, r, lay, g8, sums, 10 * SUB, x1)
    conv_backward(x6, x1, mask, lay, sums, g_out.at[0])

    @pl.when(last_step())
    def _():
        finish_sums(sums, small_out)
        finish_sums(hsums, hidden_out)


def mlp_backward_kernel(
    g_in, x_in, z_in, r_in, d_in, mask, lay, w_in, w_out,
    g_out, gy_out, gh_out, small_out, hidden_out,
    dn, g1, sums, hsums,
):
    @pl.when(first_step())
    def _():
        sums[...] = jnp.zeros_like(sums)
        hsums[...] = jnp.zeros_like(hsums)

    gy_out[0] = g_in[0].astype(BF16)
    sums[pl.ds(12 * SUB, SUB), :] = sums[pl.ds(12 * SUB, SUB), :] + fold_rows(gy_out[0].astype(F32))
    for c in range(w_in.shape[1] // FFC):
        lanes = pl.ds(c * FFC, FFC)
        du = dot(gy_out[0], w_out[:, lanes], DIMS_NN)
        gh = (du * d_in[0, :, lanes].astype(F32)).astype(BF16)
        gh_out[0, :, lanes] = gh
        hsums[:, lanes] = hsums[:, lanes] + fold_rows(gh.astype(F32))
        dx = dot(gh, w_in[:, lanes], DIMS_NT)
        dn[...] = dx if c == 0 else dn[...] + dx
    norm_backward(dn, z_in.at[0], r_in.at[0], lay, g_in.at[0], sums, 10 * SUB, g1)
    conv_backward(x_in.at[0], g1, mask, lay, sums, g_out.at[0])

    @pl.when(last_step())
    def _():
        finish_sums(sums, small_out)
        finish_sums(hsums, hidden_out)


def channel_backward_kernel(
    g_in, x_in, z_in, r_in, q_in, a_in, mask, lay, watt,
    g_out, ga_out, dq_out, small_out, bias_out,
    dn, g1, sums, bsums,
):
    features = dn.shape[1]

    @pl.when(first_step())
    def _():
        sums[...] = jnp.zeros_like(sums)
        bsums[...] = jnp.zeros_like(bsums)

    ga_out[0] = g_in[0].astype(BF16)
    sums[pl.ds(12 * SUB, SUB), :] = sums[pl.ds(12 * SUB, SUB), :] + fold_rows(ga_out[0].astype(F32))
    go = dot(ga_out[0], watt[:, pl.ds(3 * features, features)], DIMS_NT).astype(BF16)
    for g in range(features // GROUP):
        at = [pl.ds(i * features + g * GROUP, GROUP) for i in range(3)]
        q, k, v = (q_in[0, :, lanes] for lanes in at)
        gog = go[:, g * GROUP : (g + 1) * GROUP]
        a = a_in[0, g]
        af = a.astype(F32)
        dp = dot(v, gog, DIMS_TN)
        ds = (af * (dp - jnp.sum(dp * af, axis=0, keepdims=True))).astype(BF16)
        dq_out[0, :, at[0]] = (dot(k, ds, DIMS_NN) * SCALE).astype(BF16)
        dq_out[0, :, at[1]] = (dot(q, ds, DIMS_NT) * SCALE * mask[0, :, 0:1]).astype(BF16)
        dq_out[0, :, at[2]] = dot(gog, a, DIMS_NT).astype(BF16)
    bsums[...] = bsums[...] + fold_rows(dq_out[0].astype(F32))
    dn[...] = dot(dq_out[0], watt[:, pl.ds(0, 3 * features)], DIMS_NT)
    norm_backward(dn, z_in.at[0], r_in.at[0], lay, g_in.at[0], sums, 10 * SUB, g1)
    conv_backward(x_in.at[0], g1, mask, lay, sums, g_out.at[0])

    @pl.when(last_step())
    def _():
        finish_sums(sums, small_out)
        finish_sums(bsums, bias_out)


def window_backward_kernel(
    g_in, inp, z_in, r_in, q_in, p_in, mask, lay, watt,
    g_out, ga_out, dq_out, small_out, bias_out,
    x0, qf, gof, dqf, dn, g1, stage, sums, bsums,
):
    features = dn.shape[1]

    @pl.when(first_step())
    def _():
        x0[...] = jnp.zeros_like(x0)
        sums[...] = jnp.zeros_like(sums)
        bsums[...] = jnp.zeros_like(bsums)

    load_cells(inp, x0)
    ga_out[0] = g_in[0].astype(BF16)
    sums[pl.ds(12 * SUB, SUB), :] = sums[pl.ds(12 * SUB, SUB), :] + fold_rows(ga_out[0].astype(F32))
    gof[...] = rounded(dot(ga_out[0], watt[:, pl.ds(3 * features, features)], DIMS_NT))
    qf[...] = q_in[0].astype(F32)

    @pl.loop(0, 4)
    def _(w):
        rows = pl.ds(pl.multiple_of(w * WTOK, SUB), WTOK)
        masks = head_masks()
        for g in range(features // GROUP):
            at = [pl.ds(i * features + g * GROUP, GROUP) for i in range(3)]
            qe = spread_heads(qf[rows, at[0]], masks)
            k = qf[rows, at[1]].astype(BF16)
            v = qf[rows, at[2]].astype(BF16)
            goe = spread_heads(gof[rows, at[0]], masks)
            p = p_in[0, w, g]
            pf = p.astype(F32)
            dp = dot(v, goe, DIMS_NT)
            ds = (pf * (dp - jnp.sum(dp * pf, axis=0, keepdims=True))).astype(BF16)
            dqf[rows, at[0]] = collect_heads(dot(ds, k, DIMS_TN), masks) * SCALE
            dqf[rows, at[1]] = dot(ds, qe, DIMS_NN) * SCALE
            dqf[rows, at[2]] = dot(p, goe, DIMS_NN)

    dq_out[0] = dqf[...].astype(BF16)
    bsums[...] = bsums[...] + fold_rows(dq_out[0].astype(F32))
    dn[...] = dot(dq_out[0], watt[:, pl.ds(0, 3 * features)], DIMS_NT)
    norm_backward(dn, z_in.at[0], r_in.at[0], lay, g_in.at[0], sums, 10 * SUB, g1)
    conv_backward(x0, g1, mask, lay, sums, dn)
    store_cells(lambda at: dn[pl.ds(at, SUB), :], g_out, stage)

    @pl.when(last_step())
    def _():
        finish_sums(sums, small_out)
        finish_sums(bsums, bias_out)


def per_image(shape):
    rest = (0,) * (len(shape) - 1)
    return pl.BlockSpec((1,) + tuple(shape[1:]), lambda i: (i,) + rest)


def whole(shape):
    zeros = (0,) * len(shape)
    return pl.BlockSpec(tuple(shape), lambda i: zeros, pipeline_mode=pl.Buffered(1))


def one_layer(shape, layer):
    return pl.BlockSpec((1,) + tuple(shape[1:]), lambda i: (layer, 0, 0), pipeline_mode=pl.Buffered(1))


def cost(flops, arrays):
    size = sum(jnp.dtype(d).itemsize * functools.reduce(lambda p, q: p * q, s) for s, d in arrays)
    return pl.CostEstimate(flops=int(flops), bytes_accessed=int(size), transcendentals=0)


def params():
    return pltpu.CompilerParams(dimension_semantics=("arbitrary",), vmem_limit_bytes=VMEM_LIMIT)


def image_call(kernel, name, layer, batched, lay, shared, outs, sums, scratch, flops):
    images = batched[0].shape[0]
    ins = [per_image(a.shape) for a in batched] + [one_layer(lay.shape, layer)]
    args = list(batched) + [lay]
    for item in shared:
        if isinstance(item, tuple):
            ins.append(one_layer(item[0].shape, item[1]))
            args.append(item[0])
        else:
            ins.append(whole(item.shape))
            args.append(item)
    out_specs = [per_image(s) for s, _ in outs]
    out_specs += [pl.BlockSpec(tuple(s), lambda i: (0, 0)) for s, _ in sums]
    arrays = [(a.shape, a.dtype) for a in args] + outs + sums
    return pl.pallas_call(
        kernel,
        grid=(images,),
        in_specs=ins,
        out_specs=out_specs,
        out_shape=[jax.ShapeDtypeStruct(s, d) for s, d in outs + sums],
        scratch_shapes=[pltpu.VMEM(s, d) for s, d in scratch],
        compiler_params=params(),
        cost_estimate=cost(flops, arrays),
        name=name,
    )(*args)


def token_mask(heights, widths):
    t = jnp.arange(4 * WTOK, dtype=jnp.int32)
    window = t // WTOK
    row = (window // 2) * WIN + (t % WTOK) // SUB
    col8 = t % SUB
    col = (window % 2) * WIN + col8
    valid = (row[None] < heights[:, None]) & (col[None] < widths[:, None]) & (col8 < WIN)[None]
    return jnp.broadcast_to(valid.astype(F32)[..., None], valid.shape + (LANES,))


def forward_window(inputs, mask, lay, sh, watt):
    images, _, _, c = inputs.shape
    t = 4 * WTOK
    outs = [
        ((images, t, c), BF16), ((images, t, c), F32), ((images, t, LANES), F32),
        ((images, t, 3 * c), BF16), ((images, t, c), BF16),
        ((images, 4, c // GROUP, WTOK, WTOK * GROUP // HD), BF16), ((images, t, c), F32),
    ]
    scratch = [((t, c), F32), ((t, c), F32), ((t, 3 * c), F32), ((t, c), F32)]
    return image_call(window_forward_kernel, "window_forward", 0, [inputs, mask], lay, [sh, watt],
                      outs, [], scratch, 10 * images * t * c * c)


def forward_mlp(x, mask, lay, hid, w_in, w_out):
    images, t, c = x.shape
    ff = w_in.shape[1]
    outs = [
        ((images, t, c), BF16), ((images, t, c), F32), ((images, t, LANES), F32),
        ((images, t, ff), BF16), ((images, t, ff), BF16), ((images, t, c), F32),
    ]
    scratch = [((t, c), F32), ((t, c), F32)]
    return image_call(mlp_forward_kernel, "mlp_forward", 1, [x, mask], lay, [(hid, 0), w_in, w_out],
                      outs, [], scratch, 4 * images * t * c * ff)


def forward_channel(x, mask, lay, sh, watt):
    images, t, c = x.shape
    outs = [
        ((images, t, c), BF16), ((images, t, c), F32), ((images, t, LANES), F32),
        ((images, t, 3 * c), BF16), ((images, t, c), BF16),
        ((images, c // GROUP, GROUP, GROUP), BF16), ((images, t, c), F32),
    ]
    return image_call(channel_forward_kernel, "channel_forward", 2, [x, mask], lay, [sh, watt],
                      outs, [], [((t, c), F32)], 9 * images * t * c * c)


def last_mlp(x, cot, mask, lay, hid, w_in, w_out):
    images, t, c = x.shape
    ff = w_in.shape[1]
    outs = [
        (cot.shape, BF16), ((images, t, c), F32), ((images, t, c), BF16), ((images, t, ff), BF16),
        ((images, t, c), BF16), ((images, t, ff), BF16),
    ]
    scratch = [
        ((t, c), F32), ((t, c), F32), ((t, LANES), F32), ((t, c), F32), ((t, c), F32), ((t, c), F32),
        ((16, c), F32), ((16 * SUB, c), F32), ((SUB, ff), F32),
    ]
    return image_call(last_mlp_kernel, "last_mlp", 3, [x, cot, mask], lay, [(hid, 1), w_in, w_out],
                      outs, [((16, c), F32), ((1, ff), F32)], scratch, 8 * images * t * c * ff)


def backward_mlp(g, x, z, r, d, mask, lay, w_in, w_out):
    images, t, c = x.shape
    ff = w_in.shape[1]
    outs = [((images, t, c), F32), ((images, t, c), BF16), ((images, t, ff), BF16)]
    scratch = [((t, c), F32), ((t, c), F32), ((16 * SUB, c), F32), ((SUB, ff), F32)]
    return image_call(mlp_backward_kernel, "mlp_backward", 1, [g, x, z, r, d, mask], lay, [w_in, w_out],
                      outs, [((16, c), F32), ((1, ff), F32)], scratch, 4 * images * t * c * ff)


def backward_channel(g, x, z, r, q, a, mask, lay, watt):
    images, t, c = x.shape
    outs = [((images, t, c), F32), ((images, t, c), BF16), ((images, t, 3 * c), BF16)]
    scratch = [((t, c), F32), ((t, c), F32), ((16 * SUB, c), F32), ((SUB, 3 * c), F32)]
    return image_call(channel_backward_kernel, "channel_backward", 2, [g, x, z, r, q, a, mask], lay, [watt],
                      outs, [((16, c), F32), ((1, 3 * c), F32)], scratch, 10 * images * t * c * c)


def backward_window(g, inputs, z, r, q, p, mask, lay, watt):
    images, t, c = g.shape
    outs = [(inputs.shape, BF16), ((images, t, c), BF16), ((images, t, 3 * c), BF16)]
    scratch = [
        ((t, c), F32), ((t, 3 * c), F32), ((t, c), F32), ((t, 3 * c), F32), ((t, c), F32), ((t, c), F32),
        ((16, c), F32), ((16 * SUB, c), F32), ((SUB, 3 * c), F32),
    ]
    return image_call(window_backward_kernel, "window_backward", 0, [g, inputs, z, r, q, p, mask], lay, [watt],
                      outs, [((16, c), F32), ((1, 3 * c), F32)], scratch, 12 * images * t * c * c)


def grad_pair_kernel(first, left0, right0, left1, right1, out0, out1):
    step = pl.program_id(0)

    @pl.when(step < first)
    def _():
        out0[...] = dot(left0[...], right0[...], DIMS_TN).astype(BF16)

    @pl.when(step >= first)
    def _():
        out1[...] = dot(left1[...], right1[...], DIMS_TN).astype(BF16)


def grad_pair(name, left0, right0, left1, right1):
    flat = [a.reshape(-1, a.shape[-1]) for a in (left0, right0, left1, right1)]
    rows, c = flat[0].shape
    first, second = flat[1].shape[1] // c, flat[3].shape[1] // c

    def at_first(i):
        return (0, jnp.minimum(i, first - 1))

    def at_second(i):
        return (0, jnp.maximum(i - first, 0))

    outs = [((c, flat[1].shape[1]), BF16), ((c, flat[3].shape[1]), BF16)]
    return pl.pallas_call(
        functools.partial(grad_pair_kernel, first),
        grid=(first + second,),
        in_specs=[
            whole((rows, c)), pl.BlockSpec((rows, c), at_first),
            whole((rows, c)), pl.BlockSpec((rows, c), at_second),
        ],
        out_specs=[pl.BlockSpec((c, c), at_first), pl.BlockSpec((c, c), at_second)],
        out_shape=[jax.ShapeDtypeStruct(s, d) for s, d in outs],
        compiler_params=params(),
        cost_estimate=cost(2 * rows * c * c * (first + second), [(a.shape, BF16) for a in flat] + outs),
        name=name,
    )(*flat)


WIDE = 8
NARROW = 4
BOTH = ("narrow", "wide")
AXES = (("wide", 2), ("wide", 4), ("wide", 1), ("narrow", 2), ("narrow", 1))
ORDERS = ((0, 1, 2, 3), (0, 1, 3, 2))
MESH_ID = pl.DeviceIdType.MESH
STAGES = (0, 4, 8, 12, 1, 5, 9, 13, 2, 6, 10, 14, 3, 7, 11, 15)


def flip(value, bit):
    return value + bit - 2 * bit * ((value // bit) % 2)


def place(order, rel):
    at = {"narrow": lax.axis_index("narrow"), "wide": lax.axis_index("wide")}
    for i, axis in enumerate(tuple(ORDERS[order]) + (4,)):
        if rel & (1 << i):
            name, bit = AXES[axis]
            at[name] = flip(at[name], bit)
    return at


def highest(rel):
    return rel.bit_length() - 1


def meet():
    barrier = pltpu.get_barrier_semaphore()
    for axis in range(5):
        order = (axis, axis, axis, axis)
        name, bit = AXES[axis]
        at = {"narrow": lax.axis_index("narrow"), "wide": lax.axis_index("wide")}
        at[name] = flip(at[name], bit)
        pl.semaphore_signal(barrier, inc=1, device_id=at, device_id_type=MESH_ID)
    pl.semaphore_wait(barrier, 5)


class Gather:
    def __init__(self, index, order, own, view, send, recv, keep):
        self.index, self.order, self.own, self.view = index, order, own, view
        self.send, self.recv, self.keep = send, recv, keep

    def ref(self, rel):
        at = place(self.order, rel)
        return self.view(at["narrow"], at["wide"])

    def copy(self, rel, axis, slot):
        target = self.ref(rel)
        return pltpu.make_async_remote_copy(
            src_ref=self.own if rel == 0 else target,
            dst_ref=target,
            send_sem=self.send.at[self.index, slot],
            recv_sem=self.recv.at[self.index, rel | (1 << axis)],
            device_id=place(self.order, 1 << axis),
            device_id_type=MESH_ID,
        )

    def arrival(self, rel):
        target = self.ref(rel)
        return pltpu.make_async_remote_copy(
            src_ref=target, dst_ref=target, send_sem=self.send.at[self.index, 0],
            recv_sem=self.recv.at[self.index, rel], device_id=place(self.order, 1), device_id_type=MESH_ID,
        )

    def sends(self, rel):
        first = highest(rel) + 1
        return [(axis, rel | (1 << axis)) for axis in range(first, 5)][::-1]

    def stage(self, rel):
        if rel == 0:
            pltpu.make_async_copy(self.own, self.ref(0), self.keep.at[self.index]).start()
        else:
            self.arrival(rel).wait_recv()
        for axis, slot in self.sends(rel):
            self.copy(rel, axis, slot).start()

    def finish(self):
        for rel in range(16, 32):
            self.arrival(rel).wait_recv()
        for rel in range(16):
            for axis, slot in self.sends(rel):
                self.copy(rel, axis, slot).wait_send()
        pltpu.make_async_copy(self.own, self.ref(0), self.keep.at[self.index]).wait()


def slot_view(ref, start, size):
    return lambda n, w: ref.at[n * WIDE + w, pl.ds(start, size), :]


def in_view(ref, rows, cols):
    return lambda n, w: ref.at[pl.ds(pl.multiple_of(n * rows, rows), rows), pl.ds(pl.multiple_of(w * cols, cols), cols)]


def out_view(ref, rows, cols):
    return lambda n, w: ref.at[pl.ds(pl.multiple_of(w * rows, rows), rows), pl.ds(pl.multiple_of(n * cols, cols), cols)]


def gather_items(pieces, firsts, seconds, wholes, in_mats, out_mats, send, recv, keep):
    items = []
    for piece, dest in zip(pieces, wholes):
        half = piece.shape[0] // 32 * 16
        rest = piece.shape[0] - half
        items.append((0, piece.at[pl.ds(0, half)], slot_view(dest, 0, half)))
        items.append((1, piece.at[pl.ds(half, rest)], slot_view(dest, half, rest)))
    for own, dest in zip(firsts, in_mats):
        items.append((0, own, in_view(dest, *own.shape)))
    for own, dest in zip(seconds, out_mats):
        items.append((1, own, out_view(dest, *own.shape)))
    return [Gather(i, order, own, view, send, recv, keep) for i, (order, own, view) in enumerate(items)]


def gather_kernel(np_, nm, *refs):
    pieces, refs = refs[:np_], refs[np_:]
    firsts, refs = refs[:nm], refs[nm:]
    seconds, refs = refs[:nm], refs[nm:]
    wholes, refs = refs[:np_], refs[np_:]
    in_mats, refs = refs[:nm], refs[nm:]
    out_mats, refs = refs[:nm], refs[nm:]
    items = gather_items(pieces, firsts, seconds, wholes, in_mats, out_mats, *refs)
    meet()
    for rel in STAGES:
        for item in items:
            item.stage(rel)
    for item in items:
        item.finish()


def gather(name, ident, pieces, firsts, seconds):
    count = 2 * len(pieces) + len(firsts) + len(seconds)
    outs = [jax.ShapeDtypeStruct((WIDE * NARROW,) + p.shape, p.dtype) for p in pieces]
    outs += [jax.ShapeDtypeStruct((NARROW * f.shape[0], WIDE * f.shape[1]), f.dtype) for f in firsts]
    outs += [jax.ShapeDtypeStruct((WIDE * s.shape[0], NARROW * s.shape[1]), s.dtype) for s in seconds]
    args = list(pieces) + list(firsts) + list(seconds)
    arrays = [(o.shape, o.dtype) for o in outs]
    return pl.pallas_call(
        functools.partial(gather_kernel, len(pieces), len(firsts)),
        in_specs=[pl.BlockSpec(memory_space=pl.ANY)] * len(args),
        out_specs=[pl.BlockSpec(memory_space=pl.ANY)] * len(outs),
        out_shape=outs,
        scratch_shapes=[
            pltpu.SemaphoreType.DMA((count, 32)), pltpu.SemaphoreType.DMA((count, 32)),
            pltpu.SemaphoreType.DMA((count,)),
        ],
        compiler_params=pltpu.CompilerParams(collective_id=ident, has_side_effects=True, vmem_limit_bytes=VMEM_LIMIT),
        cost_estimate=cost(0, arrays),
        name=name,
    )(*args)


class Reduce:
    def __init__(self, index, order, view, acc, mate, inbox, out, sems):
        self.index, self.order, self.view = index, order, view
        self.acc, self.mate, self.inbox, self.out = acc, mate, inbox, out
        self.load_sem, self.send_sem, self.mate_sem, self.recv_sem = sems

    def ref(self, rel):
        at = place(self.order, rel)
        return self.view(at["narrow"], at["wide"])

    def load(self, rel):
        return pltpu.make_async_copy(self.ref(rel), self.acc.at[rel], self.load_sem.at[self.index, rel])

    def to_mate(self, rel):
        return pltpu.make_async_remote_copy(
            src_ref=self.ref(rel | 16), dst_ref=self.mate.at[rel], send_sem=self.send_sem.at[self.index, 16 + rel],
            recv_sem=self.mate_sem.at[self.index, rel], device_id=place(self.order, 16), device_id_type=MESH_ID,
        )

    def onward(self, rel):
        return pltpu.make_async_remote_copy(
            src_ref=self.acc.at[rel], dst_ref=self.inbox.at[rel - 1], send_sem=self.send_sem.at[self.index, rel],
            recv_sem=self.recv_sem.at[self.index, rel], device_id=place(self.order, 1 << highest(rel)),
            device_id_type=MESH_ID,
        )

    def begin(self, rel):
        self.to_mate(rel).start()
        self.load(rel).start()

    def stage(self, rel):
        self.load(rel).wait()
        self.to_mate(rel).wait_recv()
        total = self.acc[rel].astype(F32) + self.mate[rel].astype(F32)
        for axis in range(highest(rel) + 1, 4):
            came = rel | (1 << axis)
            self.onward(came).wait_recv()
            total = total + self.inbox[came - 1].astype(F32)
        if rel == 0:
            self.out[...] = total
        else:
            self.acc[rel] = total.astype(BF16)
            self.onward(rel).start()

    def finish(self):
        for rel in range(16):
            self.to_mate(rel).wait_send()
            if rel:
                self.onward(rel).wait_send()


def reduce_kernel(shapes, np_, nm, *refs):
    pieces, refs = refs[:np_], refs[np_:]
    in_mats, refs = refs[:nm], refs[nm:]
    out_mats, refs = refs[:nm], refs[nm:]
    count = len(shapes)
    outs, refs = refs[:count], refs[count:]
    bufs, sems = refs[: 3 * count], refs[3 * count :]
    views = []
    for k, piece in enumerate(pieces):
        half = shapes[2 * k][0]
        views += [(0, slot_view(piece, 0, half)), (1, slot_view(piece, half, shapes[2 * k + 1][0]))]
    for k, mat in enumerate(in_mats):
        views.append((0, in_view(mat, *shapes[2 * np_ + k])))
    for k, mat in enumerate(out_mats):
        views.append((1, out_view(mat, *shapes[2 * np_ + nm + k])))
    items = [
        Reduce(i, order, view, *bufs[3 * i : 3 * i + 3], outs[i], sems) for i, (order, view) in enumerate(views)
    ]
    meet()
    for rel in reversed(STAGES):
        for item in items:
            item.begin(rel)
    for rel in reversed(STAGES):
        for item in items:
            item.stage(rel)
    for item in items:
        item.finish()


def reduce_all(name, ident, pieces, in_mats, out_mats):
    shapes = []
    for p in pieces:
        half = p.shape[1] // 32 * 16
        shapes += [(half, p.shape[2]), (p.shape[1] - half, p.shape[2])]
    shapes += [(m.shape[0] // NARROW, m.shape[1] // WIDE) for m in in_mats]
    shapes += [(m.shape[0] // WIDE, m.shape[1] // NARROW) for m in out_mats]
    count = len(shapes)
    args = list(pieces) + list(in_mats) + list(out_mats)
    scratch = []
    for s in shapes:
        scratch += [pltpu.VMEM((16,) + s, BF16), pltpu.VMEM((16,) + s, BF16), pltpu.VMEM((15,) + s, BF16)]
    scratch += [
        pltpu.SemaphoreType.DMA((count, 16)), pltpu.SemaphoreType.DMA((count, 32)),
        pltpu.SemaphoreType.DMA((count, 16)), pltpu.SemaphoreType.DMA((count, 16)),
    ]
    return pl.pallas_call(
        functools.partial(reduce_kernel, tuple(shapes), len(pieces), len(in_mats)),
        in_specs=[pl.BlockSpec(memory_space=pl.ANY)] * len(args),
        out_specs=[pl.BlockSpec(memory_space=pltpu.VMEM)] * count,
        out_shape=[jax.ShapeDtypeStruct(s, F32) for s in shapes],
        scratch_shapes=scratch,
        compiler_params=pltpu.CompilerParams(collective_id=ident, has_side_effects=True, vmem_limit_bytes=VMEM_LIMIT),
        cost_estimate=cost(0, [(a.shape, a.dtype) for a in args]),
        name=name,
    )(*args)


def copy_attention(src, start, dst):
    cn = dst.shape[0]
    cw = src.shape[2] // 4
    c = WIDE * cw
    for w in range(WIDE):
        dst[:, pl.ds(3 * cw * w, 3 * cw)] = src[w, pl.ds(start, cn), pl.ds(0, 3 * cw)]
        dst[:, pl.ds(3 * c + cw * w, cw)] = src[w, pl.ds(start, cn), pl.ds(3 * cw, cw)]


def unpack_first_kernel(got, watt, lay, sh, hid):
    copy_attention(got, 16, watt)
    cw = got.shape[2] // 4
    for w in range(WIDE):
        lay[0, :, pl.ds(cw * w, cw)] = got[w, pl.ds(0, 16), pl.ds(0, cw)].astype(F32)

    @pl.when(pl.program_id(0) == 0)
    def _():
        for w in range(WIDE):
            part = got[w, pl.ds(0, 16), pl.ds(LANES, cw)].astype(F32)
            sh[:, pl.ds(cw * w, cw)] = part
            for j in range(2):
                for q in range(4):
                    row = 5 + 4 * j + q
                    hid[j, :, pl.ds(4 * cw * w + cw * q, cw)] = part[row : row + 1]


def unpack_first(got):
    rows, lanes = got.shape[1:]
    c = 2 * lanes
    cn = c // NARROW
    outs = [((c, 4 * c), BF16), ((NARROW, 16, c), F32), ((16, c), F32), ((2, 1, 4 * c), F32)]
    return pl.pallas_call(
        unpack_first_kernel,
        grid=(NARROW,),
        in_specs=[pl.BlockSpec((WIDE, rows, lanes), lambda n: (n, 0, 0))],
        out_specs=[
            pl.BlockSpec((cn, 4 * c), lambda n: (n, 0)), pl.BlockSpec((1, 16, c), lambda n: (n, 0, 0)),
            pl.BlockSpec((16, c), lambda n: (0, 0)), pl.BlockSpec((2, 1, 4 * c), lambda n: (0, 0, 0)),
        ],
        out_shape=[jax.ShapeDtypeStruct(s, d) for s, d in outs],
        compiler_params=params(),
        cost_estimate=cost(0, [(got.shape, BF16)] + outs),
        name="unpack_first",
    )(got)


def unpack_rest_kernel(got, watt, w_in, w_out):
    cn = watt.shape[0]
    lanes = got.shape[2]
    cw = lanes // 4
    copy_attention(got, 0, watt)
    for w in range(WIDE):
        w_in[:, pl.ds(lanes * w, lanes)] = got[w, pl.ds(cn, cn), :]
        for h in range(2):
            w_out[pl.ds(cw * w, cw), pl.ds(lanes * h, lanes)] = got[w, pl.ds(2 * cn + cw * h, cw), :]


def rest_specs(rows, lanes):
    c = 2 * lanes
    cn = c // NARROW
    packed = pl.BlockSpec((WIDE, rows, lanes), lambda n: (n, 0, 0))
    flat = pl.BlockSpec((cn, 4 * c), lambda n: (n, 0))
    return packed, [flat, flat, pl.BlockSpec((c, c), lambda n: (0, n))], (c, 4 * c)


def unpack_rest(got):
    packed, mats, shape = rest_specs(*got.shape[1:])
    return pl.pallas_call(
        unpack_rest_kernel,
        grid=(NARROW,),
        in_specs=[packed],
        out_specs=mats,
        out_shape=[jax.ShapeDtypeStruct(shape, BF16)] * 3,
        compiler_params=params(),
        cost_estimate=cost(0, [(got.shape, BF16)] * 2),
        name="unpack_rest",
    )(got)


def gather_attention(gq, gp, start, dst):
    cn = gq.shape[0]
    cw = dst.shape[2] // 4
    for w in range(WIDE):
        dst[w, pl.ds(start, cn), pl.ds(0, 3 * cw)] = gq[:, pl.ds(3 * cw * w, 3 * cw)]
        dst[w, pl.ds(start, cn), pl.ds(3 * cw, cw)] = gp[:, pl.ds(cw * w, cw)]


def pack_rest_kernel(gq, gp, g_in, g_out, out):
    cn = gq.shape[0]
    lanes = out.shape[2]
    cw = lanes // 4
    gather_attention(gq, gp, 0, out)
    for w in range(WIDE):
        out[w, pl.ds(cn, cn), :] = g_in[:, pl.ds(lanes * w, lanes)]
        for h in range(2):
            out[w, pl.ds(2 * cn + cw * h, cw), :] = g_out[pl.ds(cw * w, cw), pl.ds(lanes * h, lanes)]


def pack_rest(gq, gp, g_in, g_out):
    c = gp.shape[0]
    cn, lanes = c // NARROW, c // 2
    rows = 3 * cn
    packed, mats, _ = rest_specs(rows, lanes)
    shape = (WIDE * NARROW, rows, lanes)
    return pl.pallas_call(
        pack_rest_kernel,
        grid=(NARROW,),
        in_specs=[pl.BlockSpec((cn, 3 * c), lambda n: (n, 0)), pl.BlockSpec((cn, c), lambda n: (n, 0)), mats[1], mats[2]],
        out_specs=packed,
        out_shape=jax.ShapeDtypeStruct(shape, BF16),
        compiler_params=params(),
        cost_estimate=cost(0, [(shape, BF16)] * 2),
        name="pack_rest",
    )(gq, gp, g_in, g_out)


def pack_first_kernel(gq, gp, small, sb, cb, hid0, hid1, out, shared):
    gather_attention(gq, gp, 16, out)
    c = gp.shape[1]
    cw = c // WIDE

    @pl.when(pl.program_id(0) == 0)
    def _():
        shared[...] = jnp.zeros_like(shared)
        shared[pl.ds(0, 1), :] = sb[:, pl.ds(0, c)]
        shared[pl.ds(1, 1), :] = sb[:, pl.ds(2 * c, c)]
        for k in range(3):
            shared[pl.ds(2 + k, 1), :] = cb[:, pl.ds(k * c, c)]
        for j, hid in enumerate((hid0, hid1)):
            for w in range(WIDE):
                for q in range(4):
                    shared[pl.ds(5 + 4 * j + q, 1), pl.ds(cw * w, cw)] = hid[:, pl.ds(4 * cw * w + cw * q, cw)]

    out[:, pl.ds(0, 16), :] = jnp.zeros((WIDE, 16, out.shape[2]), BF16)
    for w in range(WIDE):
        out[w, pl.ds(0, 16), pl.ds(0, cw)] = small[0, :, pl.ds(cw * w, cw)].astype(BF16)
        out[w, pl.ds(0, 16), pl.ds(LANES, cw)] = shared[:, pl.ds(cw * w, cw)].astype(BF16)


def pack_first(gq, gp, small, sb, cb, hid0, hid1):
    c = gp.shape[0]
    cn, lanes = c // NARROW, c // 2
    rows = cn + 16
    shape = (WIDE * NARROW, rows, lanes)
    return pl.pallas_call(
        pack_first_kernel,
        grid=(NARROW,),
        in_specs=[
            pl.BlockSpec((cn, 3 * c), lambda n: (n, 0)), pl.BlockSpec((cn, c), lambda n: (n, 0)),
            pl.BlockSpec((1, 16, c), lambda n: (n, 0, 0)),
        ] + [whole(a.shape) for a in (sb, cb, hid0, hid1)],
        out_specs=pl.BlockSpec((WIDE, rows, lanes), lambda n: (n, 0, 0)),
        out_shape=jax.ShapeDtypeStruct(shape, BF16),
        scratch_shapes=[pltpu.VMEM((16, c), F32)],
        compiler_params=params(),
        cost_estimate=cost(0, [(shape, BF16)] * 2),
        name="pack_first",
    )(gq, gp, small, sb, cb, hid0, hid1)


def attention_piece(qkv, proj):
    return jnp.concatenate([qkv.T, proj.T], axis=1)


def halves_piece(second, rows, lanes):
    return second.reshape(second.shape[0], -1, lanes).transpose(1, 0, 2).reshape(rows, lanes)


def pad_to(item, rows, lanes):
    return jnp.pad(item, ((0, rows - item.shape[0]), (0, lanes - item.shape[1])))


def small_rows(conv_weight, conv_bias, norm_gain, norm_bias, out_bias):
    return jnp.concatenate([conv_weight[0], conv_bias, norm_gain, norm_bias, out_bias])


def shared_rows(attn_bias, hidden_bias):
    return jnp.concatenate([attn_bias, hidden_bias.reshape(-1, attn_bias.shape[1])])


class Direct:
    def __init__(self, p):
        lanes = p["spatial_qkv"].shape[0] * 4 // 3
        small = pad_to(small_rows(p["conv_weight"], p["conv_bias"], p["norm_gain"], p["norm_bias"], p["out_bias"]), 16, LANES)
        shared = pad_to(shared_rows(p["attn_bias"], p["hidden_bias"]), 16, LANES)
        head = pad_to(jnp.concatenate([small, shared], axis=1), 16, lanes)
        first = jnp.concatenate([head, attention_piece(p["spatial_qkv"], p["projection"][0])])
        rows = p["spatial_qkv"].shape[1]
        rest = jnp.concatenate([
            attention_piece(p["channel_qkv"], p["projection"][1]), p["mlp_in"][1].T,
            halves_piece(p["mlp_out"][1], rows, lanes),
        ])
        rest = lax.all_gather(rest, BOTH, axis=0, tiled=False)
        got, win0, wout0 = gather("gather_first", 1, [first], [p["mlp_in"][0].T], [p["mlp_out"][0]])
        watt0, self.lay, self.sh, self.hid = unpack_first(got)
        watt1, win1, wout1 = unpack_rest(rest)
        self.watt, self.w_in, self.w_out = (watt0, watt1), (win0, win1), (wout0, wout1)

    def reduce_rest(self, gq, gp, g_in, g_out):
        packed = pack_rest(gq, gp, g_in, g_out)
        packed = packed.reshape(-1, packed.shape[2])
        self.rest = lax.psum_scatter(packed, BOTH, scatter_dimension=0, tiled=True)

    def reduce_first(self, gq, gp, g_in, g_out, smalls, sb, cb, hid0, hid1):
        c = gp.shape[0]
        cn, lanes, cw = c // NARROW, c // 2, c // WIDE
        packed = pack_first(gq, gp, jnp.stack(smalls), sb, cb, hid0, hid1)
        low, high, gi0, go0 = reduce_all("reduce_first", 2, [packed], [g_in], [g_out])
        att0 = jnp.concatenate([low[16:], high])
        rest = self.rest.astype(F32)
        att1, gi1 = rest[:cn], rest[cn : 2 * cn]
        go1 = rest[2 * cn :].reshape(2, cw, lanes).transpose(1, 0, 2).reshape(cw, 2 * lanes)
        small, shared = low[:16, :cw], low[:16, LANES : LANES + cw]
        proj = jnp.stack([att0[:, 3 * cw :].T, att1[:, 3 * cw :].T])
        return (
            small[None, :9], small[9:10], small[10:11], small[11:12], att0[:, : 3 * cw].T, att1[:, : 3 * cw].T,
            proj, jnp.stack([gi0.T, gi1.T]), jnp.stack([go0, go1]), shared[:5], shared[5:13].reshape(2, lanes),
            small[12:13],
        )


class Plain:
    def __init__(self, p):
        self.layers, self.cw = p["conv_bias"].shape
        wide = p["attn_bias"].shape
        self.narrow = 4 // self.layers
        self.cn = p["spatial_qkv"].shape[1]
        self.c = self.cn * self.narrow
        self.wide = self.c // self.cw
        self.fw = p["hidden_bias"].shape[1]
        c, cn, cw, fw, n, w = self.c, self.cn, self.cw, self.fw, self.narrow, self.wide

        def spread(v):
            return lax.all_gather(v, BOTH, axis=0, tiled=False).reshape((n, w) + v.shape)

        def attention(qkv, proj):
            got = spread(attention_piece(qkv, proj)).transpose(0, 2, 1, 3)
            return jnp.concatenate([got[..., : 3 * cw].reshape(c, 3 * c), got[..., 3 * cw :].reshape(c, c)], axis=1)

        self.watt = tuple(attention(p[k], p["projection"][i]) for i, k in enumerate(("spatial_qkv", "channel_qkv")))
        self.w_in = tuple(spread(p["mlp_in"][i].T).transpose(0, 2, 1, 3).reshape(c, -1) for i in range(2))
        self.w_out = tuple(spread(p["mlp_out"][i]).transpose(1, 2, 0, 3).reshape(c, -1) for i in range(2))

        def layer(v):
            return spread(v).transpose(0, 2, 3, 1, 4).reshape(4, -1, c)

        rows = [layer(p["conv_weight"])]
        rows += [layer(p[k][:, None]) for k in ("conv_bias", "norm_gain", "norm_bias", "out_bias")]
        self.lay = jnp.pad(jnp.concatenate(rows, axis=1).astype(F32), ((0, 0), (0, 3), (0, 0)))
        attn = spread(p["attn_bias"])[0].transpose(1, 0, 2).reshape(5, c)
        self.sh = jnp.pad(attn.astype(F32), ((0, 11), (0, 0)))
        self.hid = spread(p["hidden_bias"])[0].transpose(1, 0, 2).reshape(2, 1, -1).astype(F32)

    def matrix(self, grad, rows_wide):
        n, w = self.narrow, self.wide
        a, b = (w, n) if rows_wide else (n, w)
        grad = grad.reshape(a, grad.shape[0] // a, b, grad.shape[1] // b)
        grad = grad.transpose(2, 0, 1, 3) if rows_wide else grad.transpose(0, 2, 1, 3)
        grad = grad.astype(BF16).reshape(n * w * grad.shape[2], grad.shape[3])
        return lax.psum_scatter(grad, BOTH, scatter_dimension=0, tiled=True).astype(F32)

    def reduce_rest(self, gq, gp, g_in, g_out):
        self.rest = (self.matrix(gq, False), self.matrix(gp, False), self.matrix(g_in, False), self.matrix(g_out, True))

    def reduce_first(self, gq, gp, g_in, g_out, smalls, sb, cb, hid0, hid1):
        c, cw, fw, n, w = self.c, self.cw, self.fw, self.narrow, self.wide
        first = (self.matrix(gq, False), self.matrix(gp, False), self.matrix(g_in, False), self.matrix(g_out, True))
        small = jnp.stack(smalls).reshape(n, self.layers * 16, w, cw).transpose(0, 2, 1, 3)
        attn = jnp.concatenate([sb[:, :c], sb[:, 2 * c :], cb.reshape(3, c)]).reshape(5, w, cw).transpose(1, 0, 2)
        hid = jnp.concatenate([hid0, hid1]).reshape(2, w, fw).transpose(1, 0, 2).reshape(w, -1, cw)
        common = jnp.concatenate([attn, hid], axis=1)
        common = jnp.broadcast_to(common[None], (n,) + common.shape)
        flat = jnp.concatenate([small, common], axis=2).astype(BF16).reshape(-1, cw)
        got = lax.psum_scatter(flat, BOTH, scatter_dimension=0, tiled=True).astype(F32)
        small = got[: self.layers * 16].reshape(self.layers, 16, cw)
        shared = got[self.layers * 16 :]
        rest = self.rest
        return (
            small[:, :9], small[:, 9], small[:, 10], small[:, 11], first[0].T, rest[0].T,
            jnp.stack([first[1].T, rest[1].T]), jnp.stack([first[2].T, rest[2].T]), jnp.stack([first[3], rest[3]]),
            shared[:5], shared[5:].reshape(2, fw), small[:, 12],
        )


NAMES = (
    "conv_weight", "conv_bias", "norm_gain", "norm_bias", "spatial_qkv", "channel_qkv", "projection", "mlp_in",
    "mlp_out", "attn_bias", "hidden_bias", "out_bias",
)


def local(plan, inputs, heights, widths, *rest):
    weights = plan(dict(zip(NAMES, rest[:-1])))
    cotangent = rest[-1]
    lay, sh, hid = weights.lay, weights.sh, weights.hid
    mask = token_mask(heights, widths)
    n1, z1, r1, q1, o1, p1, x2 = forward_window(inputs, mask, lay, sh, weights.watt[0])
    n2, z2, r2, u1, d1, x4 = forward_mlp(x2, mask, lay, hid, weights.w_in[0], weights.w_out[0])
    n3, z3, r3, q3, o3, a3, x6 = forward_channel(x4, mask, lay, sh, weights.watt[1])
    out, g6, n4, u2, gy2, gh2, small3, hid1 = last_mlp(
        x6, cotangent, mask, lay, hid, weights.w_in[1], weights.w_out[1])
    gi1, go1 = grad_pair("last_mlp_grads", n4, gh2, gy2, u2)
    g4, ga3, dq3, small2, cb = backward_channel(g6, x4, z3, r3, q3, a3, mask, lay, weights.watt[1])
    gq1, gp1 = grad_pair("channel_grads", n3, dq3, o3, ga3)
    weights.reduce_rest(gq1, gp1, gi1, go1)
    g2, gy1, gh1, small1, hid0 = backward_mlp(g4, x2, z2, r2, d1, mask, lay, weights.w_in[0], weights.w_out[0])
    gi0, go0 = grad_pair("mlp_grads", n2, gh1, gy1, u1)
    input_grad, ga1, dq1, small0, sb = backward_window(g2, inputs, z1, r1, q1, p1, mask, lay, weights.watt[0])
    gq0, gp0 = grad_pair("window_grads", n1, dq1, o1, ga1)
    grads = weights.reduce_first(gq0, gp0, gi0, go0, (small0, small1, small2, small3), sb, cb, hid0, hid1)
    return (out, input_grad) + grads


def solution(mesh):
    matrix = P("wide", "narrow")
    cells = P(("wide", "narrow"), None, None, None)
    stacked = P(None, "wide", "narrow")
    row = P("narrow", "wide")
    shared = P(None, "wide")
    images = P(("wide", "narrow"))
    kernels = P("narrow", None, "wide")
    in_specs = (
        cells, images, images, kernels, row, row, row, matrix, matrix,
        stacked, stacked, stacked, shared, shared, row, cells,
    )
    out_specs = (
        cells, cells, kernels, row, row, row, matrix, matrix, stacked, stacked, stacked, shared, shared, row,
    )
    plan = Direct if (mesh.shape["wide"], mesh.shape["narrow"]) == (WIDE, NARROW) else Plain
    body = functools.partial(local, plan)
    return jax.shard_map(body, mesh=mesh, in_specs=in_specs, out_specs=out_specs, check_vma=False)
```

```python
import functools

import jax
import jax.numpy as jnp
from jax import lax
from jax.experimental import pallas as pl
from jax.experimental.pallas import tpu as pltpu
from jax.sharding import PartitionSpec as P

HD = 32
WIN = 7
LANES = 128
SUB = 8
GROUP = 256
WTOK = WIN * SUB
FFC = 1024
NROWS = 112
SCALE = HD ** (-0.5)
EPS = 1e-05
NEG = -1e30
F32 = jnp.float32
BF16 = jnp.bfloat16
VMEM_LIMIT = 60 * 1024 * 1024
DIMS_NN = (((1,), (0,)), ((), ()))
DIMS_NT = (((1,), (1,)), ((), ()))
DIMS_TN = (((0,), (0,)), ((), ()))


def dot(a, b, dims):
    return lax.dot_general(a, b, dims, preferred_element_type=F32)


def tok(r, half):
    return ((r // WIN) * 2 + half) * WTOK + (r % WIN) * SUB


def load_cells(src, dst):
    for r in range(2 * WIN):
        row = src[0, r].astype(F32)
        dst[pl.ds(tok(r, 0), WIN), :] = row[:WIN]
        dst[pl.ds(tok(r, 1), WIN), :] = row[WIN:]


def store_cells(value_at, dst, stage):
    for r in range(2 * WIN):
        stage[pl.ds(0, SUB), :] = value_at(tok(r, 0))
        stage[pl.ds(WIN, SUB), :] = value_at(tok(r, 1))
        dst[0, r] = stage[pl.ds(0, 2 * WIN), :].astype(BF16)


def neighbours(left, right):
    last = lax.broadcasted_iota(jnp.int32, (SUB, LANES), 0) == SUB - 1
    up_right = pltpu.roll(right, SUB - 1, 0)
    up_left = pltpu.roll(jnp.where(last, up_right, left), SUB - 1, 0)
    down_left = pltpu.roll(left, 1, 0)
    down_right = pltpu.roll(jnp.where(last, down_left, right), 1, 0)
    return ((down_left, left, up_left), (down_right, right, up_right))


def masked_row(src, mask, r, lanes):
    pair = []
    for half in range(2):
        rows = pl.ds(tok(r, half), SUB)
        pair.append(src[rows, lanes] * mask[0, rows, :])
    return neighbours(*pair)


def plain_row(src, r, lanes):
    return neighbours(*[src[pl.ds(tok(r, half), SUB), lanes] for half in range(2)])


def lay_row(lay, k):
    return lay[0, pl.ds(k, 1), :]


def taps(lay, lanes):
    return [jnp.broadcast_to(lay[0, pl.ds(k, 1), lanes], (SUB, LANES)) for k in range(10)]


def conv_forward(src, mask, lay, dst):
    rows = 2 * WIN

    @pl.loop(0, src.shape[1] // LANES)
    def _(j):
        lanes = pl.ds(pl.multiple_of(j * LANES, LANES), LANES)
        w = taps(lay, lanes)
        shift = w[9]
        window = [None, masked_row(src, mask, 0, lanes), masked_row(src, mask, 1, lanes)]
        for r in range(rows):
            for half in range(2):
                total = shift
                for a in range(3):
                    if window[a] is None:
                        continue
                    for b in range(3):
                        total = total + w[3 * a + b] * window[a][half][b]
                at = pl.ds(tok(r, half), SUB)
                dst[at, lanes] = src[at, lanes] + total
            following = masked_row(src, mask, r + 2, lanes) if r + 2 < rows else None
            window = [window[1], window[2], following]


def conv_backward(x_src, g_src, mask, lay, sums, dst):
    rows = 2 * WIN

    @pl.loop(0, x_src.shape[1] // LANES)
    def _(j):
        lanes = pl.ds(pl.multiple_of(j * LANES, LANES), LANES)
        w = taps(lay, lanes)
        g_win = [None, plain_row(g_src, 0, lanes), plain_row(g_src, 1, lanes)]
        x_win = [None, masked_row(x_src, mask, 0, lanes), masked_row(x_src, mask, 1, lanes)]
        grads = [sums[pl.ds(SUB * k, SUB), lanes] for k in range(10)]
        for r in range(rows):
            for half in range(2):
                center = g_win[1][half][1]
                total = None
                for a in range(3):
                    for b in range(3):
                        if x_win[a] is not None:
                            grads[3 * a + b] = grads[3 * a + b] + center * x_win[a][half][b]
                        if g_win[2 - a] is not None:
                            term = w[3 * a + b] * g_win[2 - a][half][2 - b]
                            total = term if total is None else total + term
                grads[9] = grads[9] + center
                at = pl.ds(tok(r, half), SUB)
                dst[at, lanes] = center + mask[0, at, :] * total
            more = r + 2 < rows
            g_win = [g_win[1], g_win[2], plain_row(g_src, r + 2, lanes) if more else None]
            x_win = [x_win[1], x_win[2], masked_row(x_src, mask, r + 2, lanes) if more else None]
        for k in range(10):
            sums[pl.ds(SUB * k, SUB), lanes] = grads[k]


def norm_forward(src, lay, z_out, r_out, n_out):
    features = src.shape[1]

    @pl.loop(0, src.shape[0] // (2 * NROWS))
    def _(i):
        for j in range(2):
            rows = pl.ds(pl.multiple_of(i * (2 * NROWS) + j * NROWS, NROWS), NROWS)
            x = src[rows, :]
            center = x - jnp.sum(x, axis=1, keepdims=True) * (1.0 / features)
            var = jnp.sum(center * center, axis=1, keepdims=True) * (1.0 / features)
            rstd = lax.rsqrt(var + EPS)
            z = center * rstd
            z_out[rows, :] = z
            r_out[rows, :] = jnp.broadcast_to(rstd, (NROWS, LANES))
            n_out[rows, :] = (z * lay_row(lay, 10) + lay_row(lay, 11)).astype(BF16)


def norm_backward(dn, z_src, r_src, lay, g_src, sums, first, dst):
    features = dn.shape[1]

    @pl.loop(0, dn.shape[0] // (2 * NROWS))
    def _(i):
        for j in range(2):
            rows = pl.ds(pl.multiple_of(i * (2 * NROWS) + j * NROWS, NROWS), NROWS)
            d = dn[rows, :]
            z = z_src[rows, :]
            t = d * lay_row(lay, 10)
            m1 = jnp.sum(t, axis=1, keepdims=True) * (1.0 / features)
            m2 = jnp.sum(t * z, axis=1, keepdims=True) * (1.0 / features)
            dst[rows, :] = g_src[rows, :] + (t - m1 - z * m2) * r_src[rows, 0:1]
            at = pl.ds(first, SUB)
            sums[at, :] = sums[at, :] + fold_rows(d * z)
            at = pl.ds(first + SUB, SUB)
            sums[at, :] = sums[at, :] + fold_rows(d)


def fold_rows(value):
    total = value[:SUB]
    for i in range(1, value.shape[0] // SUB):
        total = total + value[SUB * i : SUB * (i + 1)]
    return total


def finish_sums(sums, out):
    for k in range(sums.shape[0] // SUB):
        out[pl.ds(k, 1), :] = jnp.sum(sums[pl.ds(SUB * k, SUB), :], axis=0, keepdims=True)


def head_masks():
    lane = lax.broadcasted_iota(jnp.int32, (WTOK, GROUP), 1) // HD
    return [lane == h for h in range(GROUP // HD)]


def spread_heads(value, masks):
    return jnp.concatenate([jnp.where(m, value, 0.0) for m in masks], axis=0).astype(BF16)


def collect_heads(full, masks):
    total = full[:WTOK]
    for h in range(1, len(masks)):
        total = jnp.where(masks[h], full[WTOK * h : WTOK * (h + 1)], total)
    return total


def rounded(value):
    return value.astype(BF16).astype(F32)


def gelu_pair(h):
    cdf = 0.5 * (1.0 + lax.erf(h * 0.7071067811865476))
    pdf = jnp.exp(h * h * -0.5) * 0.3989422804014327
    return h * cdf, cdf + h * pdf


def first_step():
    return pl.program_id(0) == 0


def last_step():
    return pl.program_id(0) == pl.num_programs(0) - 1


def window_forward_kernel(
    inp, mask, lay, sh, watt,
    n_out, z_out, r_out, q_out, o_out, p_out, x_out,
    x0, x1, qf, of,
):
    features = x0.shape[1]

    @pl.when(first_step())
    def _():
        x0[...] = jnp.zeros_like(x0)

    load_cells(inp, x0)
    conv_forward(x0, mask, lay, x1)
    norm_forward(x1, lay, z_out.at[0], r_out.at[0], n_out.at[0])
    chunk = features
    for c in range(3):
        lanes = pl.ds(c * chunk, chunk)
        part = dot(n_out[0], watt[:, lanes], DIMS_NN)
        if c != 1:
            part = part + sh[pl.ds(c // 2, 1), :]
        part = part.astype(BF16)
        q_out[0, :, lanes] = part
        qf[:, lanes] = part.astype(F32)

    @pl.loop(0, 4)
    def _(w):
        rows = pl.ds(pl.multiple_of(w * WTOK, SUB), WTOK)
        valid = mask[0, rows, 0:1] > 0.0
        masks = head_masks()
        for g in range(features // GROUP):
            q = qf[rows, pl.ds(g * GROUP, GROUP)]
            k = qf[rows, pl.ds(features + g * GROUP, GROUP)].astype(BF16)
            v = qf[rows, pl.ds(2 * features + g * GROUP, GROUP)].astype(BF16)
            s = dot(k, spread_heads(q, masks), DIMS_NT) * SCALE
            s = jnp.where(valid, s, NEG)
            e = jnp.exp(s - jnp.max(s, axis=0, keepdims=True))
            p = (e / jnp.sum(e, axis=0, keepdims=True)).astype(BF16)
            p_out[0, w, g] = p
            of[rows, pl.ds(g * GROUP, GROUP)] = collect_heads(dot(p, v, DIMS_TN), masks)

    o_out[0] = of[...].astype(BF16)
    x_out[0] = x1[...] + (dot(o_out[0], watt[:, pl.ds(3 * features, features)], DIMS_NN) + lay_row(lay, 12))


def mlp_forward_kernel(
    x_in, mask, lay, hb, w_in, w_out,
    n_out, z_out, r_out, u_out, d_out, x_out,
    x1, acc,
):
    conv_forward(x_in.at[0], mask, lay, x1)
    norm_forward(x1, lay, z_out.at[0], r_out.at[0], n_out.at[0])
    for c in range(w_in.shape[1] // FFC):
        lanes = pl.ds(c * FFC, FFC)
        h = dot(n_out[0], w_in[:, lanes], DIMS_NN) + hb[0, :, lanes]
        u, d = gelu_pair(h)
        u = u.astype(BF16)
        u_out[0, :, lanes] = u
        d_out[0, :, lanes] = d.astype(BF16)
        y = dot(u, w_out[:, lanes], DIMS_NT)
        acc[...] = y if c == 0 else acc[...] + y
    x_out[0] = x1[...] + (acc[...] + lay_row(lay, 12))


def group_mask():
    row = lax.broadcasted_iota(jnp.int32, (GROUP, GROUP), 0) // HD
    col = lax.broadcasted_iota(jnp.int32, (GROUP, GROUP), 1) // HD
    return row == col


def channel_forward_kernel(
    x_in, mask, lay, sh, watt,
    n_out, z_out, r_out, q_out, o_out, a_out, x_out,
    x1,
):
    features = x1.shape[1]
    conv_forward(x_in.at[0], mask, lay, x1)
    norm_forward(x1, lay, z_out.at[0], r_out.at[0], n_out.at[0])
    for c in range(3):
        lanes = pl.ds(c * features, features)
        part = dot(n_out[0], watt[:, lanes], DIMS_NN) + sh[pl.ds(2 + c, 1), :]
        if c == 1:
            part = part * mask[0, :, 0:1]
        q_out[0, :, lanes] = part.astype(BF16)
    same = group_mask()
    for g in range(features // GROUP):
        q = q_out[0, :, pl.ds(g * GROUP, GROUP)]
        k = q_out[0, :, pl.ds(features + g * GROUP, GROUP)]
        v = q_out[0, :, pl.ds(2 * features + g * GROUP, GROUP)]
        s = jnp.where(same, dot(k, q, DIMS_TN) * SCALE, -jnp.inf)
        e = jnp.exp(s - jnp.max(s, axis=0, keepdims=True))
        a = (e / jnp.sum(e, axis=0, keepdims=True)).astype(BF16)
        a_out[0, g] = a
        o_out[0, :, pl.ds(g * GROUP, GROUP)] = dot(v, a, DIMS_NN).astype(BF16)
    x_out[0] = x1[...] + (dot(o_out[0], watt[:, pl.ds(3 * features, features)], DIMS_NN) + lay_row(lay, 12))


def last_mlp_kernel(
    x_in, cot, mask, lay, hb, w_in, w_out,
    out, g_out, n_out, u_out, gy_out, gh_out, small_out, hidden_out,
    x1, z, r, acc, dn, g8, stage, sums, hsums,
):
    @pl.when(first_step())
    def _():
        g8[...] = jnp.zeros_like(g8)
        sums[...] = jnp.zeros_like(sums)
        hsums[...] = jnp.zeros_like(hsums)

    x6 = x_in.at[0]
    load_cells(cot, g8)
    conv_forward(x6, mask, lay, x1)
    norm_forward(x1, lay, z, r, n_out.at[0])
    g8[...] = g8[...] * mask[0, :, 0:1]
    gy_out[0] = g8[...].astype(BF16)
    sums[pl.ds(12 * SUB, SUB), :] = sums[pl.ds(12 * SUB, SUB), :] + fold_rows(gy_out[0].astype(F32))
    for c in range(w_in.shape[1] // FFC):
        lanes = pl.ds(c * FFC, FFC)
        h = dot(n_out[0], w_in[:, lanes], DIMS_NN) + hb[0, :, lanes]
        du = dot(gy_out[0], w_out[:, lanes], DIMS_NN)
        u, d = gelu_pair(h)
        u = u.astype(BF16)
        u_out[0, :, lanes] = u
        gh = (du * d).astype(BF16)
        gh_out[0, :, lanes] = gh
        hsums[:, lanes] = hsums[:, lanes] + fold_rows(gh.astype(F32))
        y = dot(u, w_out[:, lanes], DIMS_NT)
        dx = dot(gh, w_in[:, lanes], DIMS_NT)
        acc[...] = y if c == 0 else acc[...] + y
        dn[...] = dx if c == 0 else dn[...] + dx
    acc[...] = (x1[...] + (acc[...] + lay_row(lay, 12))) * mask[0, :, 0:1]
    store_cells(lambda at: acc[pl.ds(at, SUB), :], out, stage)
    norm_backward(dn, z, r, lay, g8, sums, 10 * SUB, x1)
    conv_backward(x6, x1, mask, lay, sums, g_out.at[0])

    @pl.when(last_step())
    def _():
        finish_sums(sums, small_out)
        finish_sums(hsums, hidden_out)


def mlp_backward_kernel(
    g_in, x_in, z_in, r_in, d_in, mask, lay, w_in, w_out,
    g_out, gy_out, gh_out, small_out, hidden_out,
    dn, g1, sums, hsums,
):
    @pl.when(first_step())
    def _():
        sums[...] = jnp.zeros_like(sums)
        hsums[...] = jnp.zeros_like(hsums)

    gy_out[0] = g_in[0].astype(BF16)
    sums[pl.ds(12 * SUB, SUB), :] = sums[pl.ds(12 * SUB, SUB), :] + fold_rows(gy_out[0].astype(F32))
    for c in range(w_in.shape[1] // FFC):
        lanes = pl.ds(c * FFC, FFC)
        du = dot(gy_out[0], w_out[:, lanes], DIMS_NN)
        gh = (du * d_in[0, :, lanes].astype(F32)).astype(BF16)
        gh_out[0, :, lanes] = gh
        hsums[:, lanes] = hsums[:, lanes] + fold_rows(gh.astype(F32))
        dx = dot(gh, w_in[:, lanes], DIMS_NT)
        dn[...] = dx if c == 0 else dn[...] + dx
    norm_backward(dn, z_in.at[0], r_in.at[0], lay, g_in.at[0], sums, 10 * SUB, g1)
    conv_backward(x_in.at[0], g1, mask, lay, sums, g_out.at[0])

    @pl.when(last_step())
    def _():
        finish_sums(sums, small_out)
        finish_sums(hsums, hidden_out)


def channel_backward_kernel(
    g_in, x_in, z_in, r_in, q_in, a_in, mask, lay, watt,
    g_out, ga_out, dq_out, small_out, bias_out,
    dn, g1, sums, bsums,
):
    features = dn.shape[1]

    @pl.when(first_step())
    def _():
        sums[...] = jnp.zeros_like(sums)
        bsums[...] = jnp.zeros_like(bsums)

    ga_out[0] = g_in[0].astype(BF16)
    sums[pl.ds(12 * SUB, SUB), :] = sums[pl.ds(12 * SUB, SUB), :] + fold_rows(ga_out[0].astype(F32))
    go = dot(ga_out[0], watt[:, pl.ds(3 * features, features)], DIMS_NT).astype(BF16)
    for g in range(features // GROUP):
        at = [pl.ds(i * features + g * GROUP, GROUP) for i in range(3)]
        q, k, v = (q_in[0, :, lanes] for lanes in at)
        gog = go[:, g * GROUP : (g + 1) * GROUP]
        a = a_in[0, g]
        af = a.astype(F32)
        dp = dot(v, gog, DIMS_TN)
        ds = (af * (dp - jnp.sum(dp * af, axis=0, keepdims=True))).astype(BF16)
        dq_out[0, :, at[0]] = (dot(k, ds, DIMS_NN) * SCALE).astype(BF16)
        dq_out[0, :, at[1]] = (dot(q, ds, DIMS_NT) * SCALE * mask[0, :, 0:1]).astype(BF16)
        dq_out[0, :, at[2]] = dot(gog, a, DIMS_NT).astype(BF16)
    bsums[...] = bsums[...] + fold_rows(dq_out[0].astype(F32))
    dn[...] = dot(dq_out[0], watt[:, pl.ds(0, 3 * features)], DIMS_NT)
    norm_backward(dn, z_in.at[0], r_in.at[0], lay, g_in.at[0], sums, 10 * SUB, g1)
    conv_backward(x_in.at[0], g1, mask, lay, sums, g_out.at[0])

    @pl.when(last_step())
    def _():
        finish_sums(sums, small_out)
        finish_sums(bsums, bias_out)


def window_backward_kernel(
    g_in, inp, z_in, r_in, q_in, p_in, mask, lay, watt,
    g_out, ga_out, dq_out, small_out, bias_out,
    x0, qf, gof, dqf, dn, g1, stage, sums, bsums,
):
    features = dn.shape[1]

    @pl.when(first_step())
    def _():
        x0[...] = jnp.zeros_like(x0)
        sums[...] = jnp.zeros_like(sums)
        bsums[...] = jnp.zeros_like(bsums)

    load_cells(inp, x0)
    ga_out[0] = g_in[0].astype(BF16)
    sums[pl.ds(12 * SUB, SUB), :] = sums[pl.ds(12 * SUB, SUB), :] + fold_rows(ga_out[0].astype(F32))
    gof[...] = rounded(dot(ga_out[0], watt[:, pl.ds(3 * features, features)], DIMS_NT))
    qf[...] = q_in[0].astype(F32)

    @pl.loop(0, 4)
    def _(w):
        rows = pl.ds(pl.multiple_of(w * WTOK, SUB), WTOK)
        masks = head_masks()
        for g in range(features // GROUP):
            at = [pl.ds(i * features + g * GROUP, GROUP) for i in range(3)]
            qe = spread_heads(qf[rows, at[0]], masks)
            k = qf[rows, at[1]].astype(BF16)
            v = qf[rows, at[2]].astype(BF16)
            goe = spread_heads(gof[rows, at[0]], masks)
            p = p_in[0, w, g]
            pf = p.astype(F32)
            dp = dot(v, goe, DIMS_NT)
            ds = (pf * (dp - jnp.sum(dp * pf, axis=0, keepdims=True))).astype(BF16)
            dqf[rows, at[0]] = collect_heads(dot(ds, k, DIMS_TN), masks) * SCALE
            dqf[rows, at[1]] = dot(ds, qe, DIMS_NN) * SCALE
            dqf[rows, at[2]] = dot(p, goe, DIMS_NN)

    dq_out[0] = dqf[...].astype(BF16)
    bsums[...] = bsums[...] + fold_rows(dq_out[0].astype(F32))
    dn[...] = dot(dq_out[0], watt[:, pl.ds(0, 3 * features)], DIMS_NT)
    norm_backward(dn, z_in.at[0], r_in.at[0], lay, g_in.at[0], sums, 10 * SUB, g1)
    conv_backward(x0, g1, mask, lay, sums, dn)
    store_cells(lambda at: dn[pl.ds(at, SUB), :], g_out, stage)

    @pl.when(last_step())
    def _():
        finish_sums(sums, small_out)
        finish_sums(bsums, bias_out)


def per_image(shape):
    rest = (0,) * (len(shape) - 1)
    return pl.BlockSpec((1,) + tuple(shape[1:]), lambda i: (i,) + rest)


def whole(shape):
    zeros = (0,) * len(shape)
    return pl.BlockSpec(tuple(shape), lambda i: zeros, pipeline_mode=pl.Buffered(1))


def one_layer(shape, layer):
    return pl.BlockSpec((1,) + tuple(shape[1:]), lambda i: (layer, 0, 0), pipeline_mode=pl.Buffered(1))


def cost(flops, arrays):
    size = sum(jnp.dtype(d).itemsize * functools.reduce(lambda p, q: p * q, s) for s, d in arrays)
    return pl.CostEstimate(flops=int(flops), bytes_accessed=int(size), transcendentals=0)


def params():
    return pltpu.CompilerParams(dimension_semantics=("arbitrary",), vmem_limit_bytes=VMEM_LIMIT)


def carrier(kernel, carry, ins, outs, scratch, refs):
    extra_in, extra_out = len(carry.args), len(carry.outs)
    base_in, refs = refs[:ins], refs[ins:]
    carry_in, refs = refs[:extra_in], refs[extra_in:]
    base_out, refs = refs[:outs], refs[outs:]
    carry_out, refs = refs[:extra_out], refs[extra_out:]
    base_scratch, carry_scratch = refs[:scratch], refs[scratch:]
    carry.run(carry_in, carry_out, carry_scratch)
    kernel(*base_in, *base_out, *base_scratch)
    carry.end(carry_in, carry_out, carry_scratch)


def image_call(kernel, name, layer, batched, lay, shared, outs, sums, scratch, flops, carry=None):
    images = batched[0].shape[0]
    ins = [per_image(a.shape) for a in batched] + [one_layer(lay.shape, layer)]
    args = list(batched) + [lay]
    for item in shared:
        if isinstance(item, tuple):
            ins.append(one_layer(item[0].shape, item[1]))
            args.append(item[0])
        else:
            ins.append(whole(item.shape))
            args.append(item)
    out_specs = [per_image(s) for s, _ in outs]
    out_specs += [pl.BlockSpec(tuple(s), lambda i: (0, 0)) for s, _ in sums]
    results = outs + sums
    buffers = [pltpu.VMEM(s, d) for s, d in scratch]
    options = params()
    body = kernel
    if carry is not None:
        counts = (len(args), len(results), len(scratch))

        def body(*refs):
            carrier(kernel, carry, *counts, refs)

        args = args + carry.args
        ins = ins + [pl.BlockSpec(memory_space=pl.ANY)] * len(carry.args)
        out_specs += [carry.out_spec or pl.BlockSpec(tuple(s), lambda i: (0, 0)) for s, _ in carry.outs]
        results = results + carry.outs
        buffers += carry.scratch
        options = pltpu.CompilerParams(
            dimension_semantics=("arbitrary",), vmem_limit_bytes=VMEM_LIMIT, collective_id=carry.ident,
            has_side_effects=True,
        )
    arrays = [(a.shape, a.dtype) for a in args] + results
    return pl.pallas_call(
        body,
        grid=(images,),
        in_specs=ins,
        out_specs=out_specs,
        out_shape=[jax.ShapeDtypeStruct(s, d) for s, d in results],
        scratch_shapes=buffers,
        compiler_params=options,
        cost_estimate=cost(flops, arrays),
        name=name,
    )(*args)


def token_mask(heights, widths):
    t = jnp.arange(4 * WTOK, dtype=jnp.int32)
    window = t // WTOK
    row = (window // 2) * WIN + (t % WTOK) // SUB
    col8 = t % SUB
    col = (window % 2) * WIN + col8
    valid = (row[None] < heights[:, None]) & (col[None] < widths[:, None]) & (col8 < WIN)[None]
    return jnp.broadcast_to(valid.astype(F32)[..., None], valid.shape + (LANES,))


def forward_window(inputs, mask, lay, sh, watt, carry=None):
    images, _, _, c = inputs.shape
    t = 4 * WTOK
    outs = [
        ((images, t, c), BF16), ((images, t, c), F32), ((images, t, LANES), F32),
        ((images, t, 3 * c), BF16), ((images, t, c), BF16),
        ((images, 4, c // GROUP, WTOK, WTOK * GROUP // HD), BF16), ((images, t, c), F32),
    ]
    scratch = [((t, c), F32), ((t, c), F32), ((t, 3 * c), F32), ((t, c), F32)]
    return image_call(window_forward_kernel, "window_forward", 0, [inputs, mask], lay, [sh, watt],
                      outs, [], scratch, 10 * images * t * c * c, carry)


def forward_mlp(x, mask, lay, hid, w_in, w_out):
    images, t, c = x.shape
    ff = w_in.shape[1]
    outs = [
        ((images, t, c), BF16), ((images, t, c), F32), ((images, t, LANES), F32),
        ((images, t, ff), BF16), ((images, t, ff), BF16), ((images, t, c), F32),
    ]
    scratch = [((t, c), F32), ((t, c), F32)]
    return image_call(mlp_forward_kernel, "mlp_forward", 1, [x, mask], lay, [(hid, 0), w_in, w_out],
                      outs, [], scratch, 4 * images * t * c * ff)


def forward_channel(x, mask, lay, sh, watt):
    images, t, c = x.shape
    outs = [
        ((images, t, c), BF16), ((images, t, c), F32), ((images, t, LANES), F32),
        ((images, t, 3 * c), BF16), ((images, t, c), BF16),
        ((images, c // GROUP, GROUP, GROUP), BF16), ((images, t, c), F32),
    ]
    return image_call(channel_forward_kernel, "channel_forward", 2, [x, mask], lay, [sh, watt],
                      outs, [], [((t, c), F32)], 9 * images * t * c * c)


def last_mlp(x, cot, mask, lay, hid, w_in, w_out):
    images, t, c = x.shape
    ff = w_in.shape[1]
    outs = [
        (cot.shape, BF16), ((images, t, c), F32), ((images, t, c), BF16), ((images, t, ff), BF16),
        ((images, t, c), BF16), ((images, t, ff), BF16),
    ]
    scratch = [
        ((t, c), F32), ((t, c), F32), ((t, LANES), F32), ((t, c), F32), ((t, c), F32), ((t, c), F32),
        ((16, c), F32), ((16 * SUB, c), F32), ((SUB, ff), F32),
    ]
    return image_call(last_mlp_kernel, "last_mlp", 3, [x, cot, mask], lay, [(hid, 1), w_in, w_out],
                      outs, [((16, c), F32), ((1, ff), F32)], scratch, 8 * images * t * c * ff)


def backward_mlp(g, x, z, r, d, mask, lay, w_in, w_out):
    images, t, c = x.shape
    ff = w_in.shape[1]
    outs = [((images, t, c), F32), ((images, t, c), BF16), ((images, t, ff), BF16)]
    scratch = [((t, c), F32), ((t, c), F32), ((16 * SUB, c), F32), ((SUB, ff), F32)]
    return image_call(mlp_backward_kernel, "mlp_backward", 1, [g, x, z, r, d, mask], lay, [w_in, w_out],
                      outs, [((16, c), F32), ((1, ff), F32)], scratch, 4 * images * t * c * ff)


def backward_channel(g, x, z, r, q, a, mask, lay, watt):
    images, t, c = x.shape
    outs = [((images, t, c), F32), ((images, t, c), BF16), ((images, t, 3 * c), BF16)]
    scratch = [((t, c), F32), ((t, c), F32), ((16 * SUB, c), F32), ((SUB, 3 * c), F32)]
    return image_call(channel_backward_kernel, "channel_backward", 2, [g, x, z, r, q, a, mask], lay, [watt],
                      outs, [((16, c), F32), ((1, 3 * c), F32)], scratch, 10 * images * t * c * c)


def backward_window(g, inputs, z, r, q, p, mask, lay, watt, carry=None):
    images, t, c = g.shape
    outs = [(inputs.shape, BF16), ((images, t, c), BF16), ((images, t, 3 * c), BF16)]
    scratch = [
        ((t, c), F32), ((t, 3 * c), F32), ((t, c), F32), ((t, 3 * c), F32), ((t, c), F32), ((t, c), F32),
        ((16, c), F32), ((16 * SUB, c), F32), ((SUB, 3 * c), F32),
    ]
    return image_call(window_backward_kernel, "window_backward", 0, [g, inputs, z, r, q, p, mask], lay, [watt],
                      outs, [((16, c), F32), ((1, 3 * c), F32)], scratch, 12 * images * t * c * c, carry)


def grad_pair_kernel(first, left0, right0, left1, right1, out0, out1):
    step = pl.program_id(0)

    @pl.when(step < first)
    def _():
        out0[...] = dot(left0[...], right0[...], DIMS_TN).astype(BF16)

    @pl.when(step >= first)
    def _():
        out1[...] = dot(left1[...], right1[...], DIMS_TN).astype(BF16)


def grad_pair(name, left0, right0, left1, right1):
    flat = [a.reshape(-1, a.shape[-1]) for a in (left0, right0, left1, right1)]
    rows, c = flat[0].shape
    first, second = flat[1].shape[1] // c, flat[3].shape[1] // c

    def at_first(i):
        return (0, jnp.minimum(i, first - 1))

    def at_second(i):
        return (0, jnp.maximum(i - first, 0))

    outs = [((c, flat[1].shape[1]), BF16), ((c, flat[3].shape[1]), BF16)]
    return pl.pallas_call(
        functools.partial(grad_pair_kernel, first),
        grid=(first + second,),
        in_specs=[
            whole((rows, c)), pl.BlockSpec((rows, c), at_first),
            whole((rows, c)), pl.BlockSpec((rows, c), at_second),
        ],
        out_specs=[pl.BlockSpec((c, c), at_first), pl.BlockSpec((c, c), at_second)],
        out_shape=[jax.ShapeDtypeStruct(s, d) for s, d in outs],
        compiler_params=params(),
        cost_estimate=cost(2 * rows * c * c * (first + second), [(a.shape, BF16) for a in flat] + outs),
        name=name,
    )(*flat)


WIDE = 8
NARROW = 4
BOTH = ("narrow", "wide")
AXES = (("wide", 2), ("wide", 4), ("wide", 1), ("narrow", 2), ("narrow", 1))
ORDERS = ((0, 1, 2, 3), (0, 1, 3, 2))
MESH_ID = pl.DeviceIdType.MESH
STAGES = (0, 4, 8, 12, 1, 5, 9, 13, 2, 6, 10, 14, 3, 7, 11, 15)


def flip(value, bit):
    return value + bit - 2 * bit * ((value // bit) % 2)


def place(order, rel):
    at = {"narrow": lax.axis_index("narrow"), "wide": lax.axis_index("wide")}
    for i, axis in enumerate(tuple(ORDERS[order]) + (4,)):
        if rel & (1 << i):
            name, bit = AXES[axis]
            at[name] = flip(at[name], bit)
    return at


def highest(rel):
    return rel.bit_length() - 1


def meet():
    barrier = pltpu.get_barrier_semaphore()
    for axis in range(5):
        order = (axis, axis, axis, axis)
        name, bit = AXES[axis]
        at = {"narrow": lax.axis_index("narrow"), "wide": lax.axis_index("wide")}
        at[name] = flip(at[name], bit)
        pl.semaphore_signal(barrier, inc=1, device_id=at, device_id_type=MESH_ID)
    pl.semaphore_wait(barrier, 5)


class Gather:
    def __init__(self, index, order, own, view, send, recv, keep):
        self.index, self.order, self.own, self.view = index, order, own, view
        self.send, self.recv, self.keep = send, recv, keep

    def ref(self, rel):
        at = place(self.order, rel)
        return self.view(at["narrow"], at["wide"])

    def copy(self, rel, axis, slot):
        target = self.ref(rel)
        return pltpu.make_async_remote_copy(
            src_ref=self.own if rel == 0 else target,
            dst_ref=target,
            send_sem=self.send.at[self.index, slot],
            recv_sem=self.recv.at[self.index, rel | (1 << axis)],
            device_id=place(self.order, 1 << axis),
            device_id_type=MESH_ID,
        )

    def arrival(self, rel):
        target = self.ref(rel)
        return pltpu.make_async_remote_copy(
            src_ref=target, dst_ref=target, send_sem=self.send.at[self.index, 0],
            recv_sem=self.recv.at[self.index, rel], device_id=place(self.order, 1), device_id_type=MESH_ID,
        )

    def sends(self, rel):
        first = highest(rel) + 1
        return [(axis, rel | (1 << axis)) for axis in range(first, 5)][::-1]

    def stage(self, rel):
        if rel == 0:
            pltpu.make_async_copy(self.own, self.ref(0), self.keep.at[self.index]).start()
        else:
            self.arrival(rel).wait_recv()
        for axis, slot in self.sends(rel):
            self.copy(rel, axis, slot).start()

    def finish(self):
        for rel in range(16, 32):
            self.arrival(rel).wait_recv()
        for rel in range(16):
            for axis, slot in self.sends(rel):
                self.copy(rel, axis, slot).wait_send()
        pltpu.make_async_copy(self.own, self.ref(0), self.keep.at[self.index]).wait()


def slot_view(ref, start, size):
    return lambda n, w: ref.at[n * WIDE + w, pl.ds(start, size), :]


def in_view(ref, rows, cols):
    return lambda n, w: ref.at[pl.ds(pl.multiple_of(n * rows, rows), rows), pl.ds(pl.multiple_of(w * cols, cols), cols)]


def out_view(ref, rows, cols):
    return lambda n, w: ref.at[pl.ds(pl.multiple_of(w * rows, rows), rows), pl.ds(pl.multiple_of(n * cols, cols), cols)]


def gather_items(pieces, firsts, seconds, wholes, in_mats, out_mats, send, recv, keep):
    items = []
    for piece, dest in zip(pieces, wholes):
        half = piece.shape[0] // 32 * 16
        rest = piece.shape[0] - half
        items.append((0, piece.at[pl.ds(0, half)], slot_view(dest, 0, half)))
        items.append((1, piece.at[pl.ds(half, rest)], slot_view(dest, half, rest)))
    for own, dest in zip(firsts, in_mats):
        items.append((0, own, in_view(dest, *own.shape)))
    for own, dest in zip(seconds, out_mats):
        items.append((1, own, out_view(dest, *own.shape)))
    return [Gather(i, order, own, view, send, recv, keep) for i, (order, own, view) in enumerate(items)]


def gather_kernel(np_, nm, *refs):
    pieces, refs = refs[:np_], refs[np_:]
    firsts, refs = refs[:nm], refs[nm:]
    seconds, refs = refs[:nm], refs[nm:]
    wholes, refs = refs[:np_], refs[np_:]
    in_mats, refs = refs[:nm], refs[nm:]
    out_mats, refs = refs[:nm], refs[nm:]
    items = gather_items(pieces, firsts, seconds, wholes, in_mats, out_mats, *refs)
    meet()
    for rel in STAGES:
        for item in items:
            item.stage(rel)
    for item in items:
        item.finish()


GATHER_STEPS = ((0,), (1, 2, 4, 8), (5, 12, 9), (3, 6, 10), (13, 7), (14, 11), (15,))
REDUCE_STEPS = ((), (15, 11), (7, 14, 10), (3, 6, 13), (2, 9), (5, 12), (1, 8, 4), (0,))


class Beside:
    def __init__(self, ident, first, second):
        self.ident = ident
        self.args = [first, second]
        self.outs = [
            ((NARROW * first.shape[0], WIDE * first.shape[1]), BF16),
            ((WIDE * second.shape[0], NARROW * second.shape[1]), BF16),
        ]
        self.out_spec = pl.BlockSpec(memory_space=pl.ANY)
        self.scratch = [
            pltpu.SemaphoreType.DMA((2, 32)), pltpu.SemaphoreType.DMA((2, 32)), pltpu.SemaphoreType.DMA((2,)),
        ]

    def run(self, ins, outs, scratch):
        items = gather_items([], ins[:1], ins[1:], [], outs[:1], outs[1:], *scratch)
        for s, rels in enumerate(GATHER_STEPS):

            @pl.when(pl.program_id(0) == s)
            def _(s=s, rels=rels):
                if s == 0:
                    meet()
                for rel in rels:
                    for item in items:
                        item.stage(rel)

    def end(self, ins, outs, scratch):
        items = gather_items([], ins[:1], ins[1:], [], outs[:1], outs[1:], *scratch)

        @pl.when(last_step())
        def _():
            for item in items:
                item.finish()


class Behind:
    def __init__(self, ident, g_in, g_out):
        self.ident = ident
        self.args = [g_in, g_out]
        self.shapes = [
            (g_in.shape[0] // NARROW, g_in.shape[1] // WIDE), (g_out.shape[0] // WIDE, g_out.shape[1] // NARROW),
        ]
        self.outs = [(s, F32) for s in self.shapes]
        self.out_spec = None
        self.scratch = []
        for s in self.shapes:
            self.scratch += [pltpu.VMEM((16,) + s, BF16), pltpu.VMEM((16,) + s, BF16), pltpu.VMEM((15,) + s, BF16)]
        self.scratch += [
            pltpu.SemaphoreType.DMA((2, 16)), pltpu.SemaphoreType.DMA((2, 32)),
            pltpu.SemaphoreType.DMA((2, 16)), pltpu.SemaphoreType.DMA((2, 16)),
        ]

    def items(self, ins, outs, scratch):
        views = [(0, in_view(ins[0], *self.shapes[0])), (1, out_view(ins[1], *self.shapes[1]))]
        return [
            Reduce(i, order, view, *scratch[3 * i : 3 * i + 3], outs[i], scratch[6:])
            for i, (order, view) in enumerate(views)
        ]

    def run(self, ins, outs, scratch):
        items = self.items(ins, outs, scratch)
        for s, rels in enumerate(REDUCE_STEPS):

            @pl.when(pl.program_id(0) == s)
            def _(s=s, rels=rels):
                if s == 0:
                    meet()
                    for rel in reversed(STAGES):
                        for item in items:
                            item.begin(rel)
                for rel in rels:
                    for item in items:
                        item.stage(rel)

    def end(self, ins, outs, scratch):
        @pl.when(last_step())
        def _():
            for item in self.items(ins, outs, scratch):
                item.finish()


def gather(name, ident, pieces, firsts, seconds):
    count = 2 * len(pieces) + len(firsts) + len(seconds)
    outs = [jax.ShapeDtypeStruct((WIDE * NARROW,) + p.shape, p.dtype) for p in pieces]
    outs += [jax.ShapeDtypeStruct((NARROW * f.shape[0], WIDE * f.shape[1]), f.dtype) for f in firsts]
    outs += [jax.ShapeDtypeStruct((WIDE * s.shape[0], NARROW * s.shape[1]), s.dtype) for s in seconds]
    args = list(pieces) + list(firsts) + list(seconds)
    arrays = [(o.shape, o.dtype) for o in outs]
    return pl.pallas_call(
        functools.partial(gather_kernel, len(pieces), len(firsts)),
        in_specs=[pl.BlockSpec(memory_space=pl.ANY)] * len(args),
        out_specs=[pl.BlockSpec(memory_space=pl.ANY)] * len(outs),
        out_shape=outs,
        scratch_shapes=[
            pltpu.SemaphoreType.DMA((count, 32)), pltpu.SemaphoreType.DMA((count, 32)),
            pltpu.SemaphoreType.DMA((count,)),
        ],
        compiler_params=pltpu.CompilerParams(collective_id=ident, has_side_effects=True, vmem_limit_bytes=VMEM_LIMIT),
        cost_estimate=cost(0, arrays),
        name=name,
    )(*args)


class Reduce:
    def __init__(self, index, order, view, acc, mate, inbox, out, sems):
        self.index, self.order, self.view = index, order, view
        self.acc, self.mate, self.inbox, self.out = acc, mate, inbox, out
        self.load_sem, self.send_sem, self.mate_sem, self.recv_sem = sems

    def ref(self, rel):
        at = place(self.order, rel)
        return self.view(at["narrow"], at["wide"])

    def load(self, rel):
        return pltpu.make_async_copy(self.ref(rel), self.acc.at[rel], self.load_sem.at[self.index, rel])

    def to_mate(self, rel):
        return pltpu.make_async_remote_copy(
            src_ref=self.ref(rel | 16), dst_ref=self.mate.at[rel], send_sem=self.send_sem.at[self.index, 16 + rel],
            recv_sem=self.mate_sem.at[self.index, rel], device_id=place(self.order, 16), device_id_type=MESH_ID,
        )

    def onward(self, rel):
        return pltpu.make_async_remote_copy(
            src_ref=self.acc.at[rel], dst_ref=self.inbox.at[rel - 1], send_sem=self.send_sem.at[self.index, rel],
            recv_sem=self.recv_sem.at[self.index, rel], device_id=place(self.order, 1 << highest(rel)),
            device_id_type=MESH_ID,
        )

    def begin(self, rel):
        self.to_mate(rel).start()
        self.load(rel).start()

    def stage(self, rel):
        self.load(rel).wait()
        self.to_mate(rel).wait_recv()
        total = self.acc[rel].astype(F32) + self.mate[rel].astype(F32)
        for axis in range(highest(rel) + 1, 4):
            came = rel | (1 << axis)
            self.onward(came).wait_recv()
            total = total + self.inbox[came - 1].astype(F32)
        if rel == 0:
            self.out[...] = total
        else:
            self.acc[rel] = total.astype(BF16)
            self.onward(rel).start()

    def finish(self):
        for rel in range(16):
            self.to_mate(rel).wait_send()
            if rel:
                self.onward(rel).wait_send()


def reduce_kernel(shapes, np_, nm, *refs):
    pieces, refs = refs[:np_], refs[np_:]
    in_mats, refs = refs[:nm], refs[nm:]
    out_mats, refs = refs[:nm], refs[nm:]
    count = len(shapes)
    outs, refs = refs[:count], refs[count:]
    bufs, sems = refs[: 3 * count], refs[3 * count :]
    views = []
    for k, piece in enumerate(pieces):
        half = shapes[2 * k][0]
        views += [(0, slot_view(piece, 0, half)), (1, slot_view(piece, half, shapes[2 * k + 1][0]))]
    for k, mat in enumerate(in_mats):
        views.append((0, in_view(mat, *shapes[2 * np_ + k])))
    for k, mat in enumerate(out_mats):
        views.append((1, out_view(mat, *shapes[2 * np_ + nm + k])))
    items = [
        Reduce(i, order, view, *bufs[3 * i : 3 * i + 3], outs[i], sems) for i, (order, view) in enumerate(views)
    ]
    meet()
    for rel in reversed(STAGES):
        for item in items:
            item.begin(rel)
    for rel in reversed(STAGES):
        for item in items:
            item.stage(rel)
    for item in items:
        item.finish()


def reduce_all(name, ident, pieces, in_mats, out_mats):
    shapes = []
    for p in pieces:
        half = p.shape[1] // 32 * 16
        shapes += [(half, p.shape[2]), (p.shape[1] - half, p.shape[2])]
    shapes += [(m.shape[0] // NARROW, m.shape[1] // WIDE) for m in in_mats]
    shapes += [(m.shape[0] // WIDE, m.shape[1] // NARROW) for m in out_mats]
    count = len(shapes)
    args = list(pieces) + list(in_mats) + list(out_mats)
    scratch = []
    for s in shapes:
        scratch += [pltpu.VMEM((16,) + s, BF16), pltpu.VMEM((16,) + s, BF16), pltpu.VMEM((15,) + s, BF16)]
    scratch += [
        pltpu.SemaphoreType.DMA((count, 16)), pltpu.SemaphoreType.DMA((count, 32)),
        pltpu.SemaphoreType.DMA((count, 16)), pltpu.SemaphoreType.DMA((count, 16)),
    ]
    return pl.pallas_call(
        functools.partial(reduce_kernel, tuple(shapes), len(pieces), len(in_mats)),
        in_specs=[pl.BlockSpec(memory_space=pl.ANY)] * len(args),
        out_specs=[pl.BlockSpec(memory_space=pltpu.VMEM)] * count,
        out_shape=[jax.ShapeDtypeStruct(s, F32) for s in shapes],
        scratch_shapes=scratch,
        compiler_params=pltpu.CompilerParams(collective_id=ident, has_side_effects=True, vmem_limit_bytes=VMEM_LIMIT),
        cost_estimate=cost(0, [(a.shape, a.dtype) for a in args]),
        name=name,
    )(*args)


def copy_attention(src, start, dst):
    cn = dst.shape[0]
    cw = src.shape[2] // 4
    c = WIDE * cw
    for w in range(WIDE):
        dst[:, pl.ds(3 * cw * w, 3 * cw)] = src[w, pl.ds(start, cn), pl.ds(0, 3 * cw)]
        dst[:, pl.ds(3 * c + cw * w, cw)] = src[w, pl.ds(start, cn), pl.ds(3 * cw, cw)]


def unpack_first_kernel(got, watt, lay, sh, hid):
    copy_attention(got, 16, watt)
    cw = got.shape[2] // 4
    for w in range(WIDE):
        lay[0, :, pl.ds(cw * w, cw)] = got[w, pl.ds(0, 16), pl.ds(0, cw)].astype(F32)

    @pl.when(pl.program_id(0) == 0)
    def _():
        for w in range(WIDE):
            part = got[w, pl.ds(0, 16), pl.ds(LANES, cw)].astype(F32)
            sh[:, pl.ds(cw * w, cw)] = part
            for j in range(2):
                for q in range(4):
                    row = 5 + 4 * j + q
                    hid[j, :, pl.ds(4 * cw * w + cw * q, cw)] = part[row : row + 1]


def unpack_first(got):
    rows, lanes = got.shape[1:]
    c = 2 * lanes
    cn = c // NARROW
    outs = [((c, 4 * c), BF16), ((NARROW, 16, c), F32), ((16, c), F32), ((2, 1, 4 * c), F32)]
    return pl.pallas_call(
        unpack_first_kernel,
        grid=(NARROW,),
        in_specs=[pl.BlockSpec((WIDE, rows, lanes), lambda n: (n, 0, 0))],
        out_specs=[
            pl.BlockSpec((cn, 4 * c), lambda n: (n, 0)), pl.BlockSpec((1, 16, c), lambda n: (n, 0, 0)),
            pl.BlockSpec((16, c), lambda n: (0, 0)), pl.BlockSpec((2, 1, 4 * c), lambda n: (0, 0, 0)),
        ],
        out_shape=[jax.ShapeDtypeStruct(s, d) for s, d in outs],
        compiler_params=params(),
        cost_estimate=cost(0, [(got.shape, BF16)] + outs),
        name="unpack_first",
    )(got)


def unpack_rest_kernel(got, watt, w_in, w_out):
    cn = watt.shape[0]
    lanes = got.shape[2]
    cw = lanes // 4
    copy_attention(got, 0, watt)
    for w in range(WIDE):
        w_in[:, pl.ds(lanes * w, lanes)] = got[w, pl.ds(cn, cn), :]
        for h in range(2):
            w_out[pl.ds(cw * w, cw), pl.ds(lanes * h, lanes)] = got[w, pl.ds(2 * cn + cw * h, cw), :]


def rest_specs(rows, lanes):
    c = 2 * lanes
    cn = c // NARROW
    packed = pl.BlockSpec((WIDE, rows, lanes), lambda n: (n, 0, 0))
    flat = pl.BlockSpec((cn, 4 * c), lambda n: (n, 0))
    return packed, [flat, flat, pl.BlockSpec((c, c), lambda n: (0, n))], (c, 4 * c)


def unpack_rest(got):
    packed, mats, shape = rest_specs(*got.shape[1:])
    return pl.pallas_call(
        unpack_rest_kernel,
        grid=(NARROW,),
        in_specs=[packed],
        out_specs=mats,
        out_shape=[jax.ShapeDtypeStruct(shape, BF16)] * 3,
        compiler_params=params(),
        cost_estimate=cost(0, [(got.shape, BF16)] * 2),
        name="unpack_rest",
    )(got)


def gather_attention(gq, gp, start, dst):
    cn = gq.shape[0]
    cw = dst.shape[2] // 4
    for w in range(WIDE):
        dst[w, pl.ds(start, cn), pl.ds(0, 3 * cw)] = gq[:, pl.ds(3 * cw * w, 3 * cw)]
        dst[w, pl.ds(start, cn), pl.ds(3 * cw, cw)] = gp[:, pl.ds(cw * w, cw)]


def pack_rest_kernel(gq, gp, g_in, g_out, out):
    cn = gq.shape[0]
    lanes = out.shape[2]
    cw = lanes // 4
    gather_attention(gq, gp, 0, out)
    for w in range(WIDE):
        out[w, pl.ds(cn, cn), :] = g_in[:, pl.ds(lanes * w, lanes)]
        for h in range(2):
            out[w, pl.ds(2 * cn + cw * h, cw), :] = g_out[pl.ds(cw * w, cw), pl.ds(lanes * h, lanes)]


def pack_rest(gq, gp, g_in, g_out):
    c = gp.shape[0]
    cn, lanes = c // NARROW, c // 2
    rows = 3 * cn
    packed, mats, _ = rest_specs(rows, lanes)
    shape = (WIDE * NARROW, rows, lanes)
    return pl.pallas_call(
        pack_rest_kernel,
        grid=(NARROW,),
        in_specs=[pl.BlockSpec((cn, 3 * c), lambda n: (n, 0)), pl.BlockSpec((cn, c), lambda n: (n, 0)), mats[1], mats[2]],
        out_specs=packed,
        out_shape=jax.ShapeDtypeStruct(shape, BF16),
        compiler_params=params(),
        cost_estimate=cost(0, [(shape, BF16)] * 2),
        name="pack_rest",
    )(gq, gp, g_in, g_out)


def pack_first_kernel(gq, gp, small, sb, cb, hid0, hid1, out, shared):
    gather_attention(gq, gp, 16, out)
    c = gp.shape[1]
    cw = c // WIDE

    @pl.when(pl.program_id(0) == 0)
    def _():
        shared[...] = jnp.zeros_like(shared)
        shared[pl.ds(0, 1), :] = sb[:, pl.ds(0, c)]
        shared[pl.ds(1, 1), :] = sb[:, pl.ds(2 * c, c)]
        for k in range(3):
            shared[pl.ds(2 + k, 1), :] = cb[:, pl.ds(k * c, c)]
        for j, hid in enumerate((hid0, hid1)):
            for w in range(WIDE):
                for q in range(4):
                    shared[pl.ds(5 + 4 * j + q, 1), pl.ds(cw * w, cw)] = hid[:, pl.ds(4 * cw * w + cw * q, cw)]

    out[:, pl.ds(0, 16), :] = jnp.zeros((WIDE, 16, out.shape[2]), BF16)
    for w in range(WIDE):
        out[w, pl.ds(0, 16), pl.ds(0, cw)] = small[0, :, pl.ds(cw * w, cw)].astype(BF16)
        out[w, pl.ds(0, 16), pl.ds(LANES, cw)] = shared[:, pl.ds(cw * w, cw)].astype(BF16)


def pack_first(gq, gp, small, sb, cb, hid0, hid1):
    c = gp.shape[0]
    cn, lanes = c // NARROW, c // 2
    rows = cn + 16
    shape = (WIDE * NARROW, rows, lanes)
    return pl.pallas_call(
        pack_first_kernel,
        grid=(NARROW,),
        in_specs=[
            pl.BlockSpec((cn, 3 * c), lambda n: (n, 0)), pl.BlockSpec((cn, c), lambda n: (n, 0)),
            pl.BlockSpec((1, 16, c), lambda n: (n, 0, 0)),
        ] + [whole(a.shape) for a in (sb, cb, hid0, hid1)],
        out_specs=pl.BlockSpec((WIDE, rows, lanes), lambda n: (n, 0, 0)),
        out_shape=jax.ShapeDtypeStruct(shape, BF16),
        scratch_shapes=[pltpu.VMEM((16, c), F32)],
        compiler_params=params(),
        cost_estimate=cost(0, [(shape, BF16)] * 2),
        name="pack_first",
    )(gq, gp, small, sb, cb, hid0, hid1)


def attention_piece(qkv, proj):
    return jnp.concatenate([qkv.T, proj.T], axis=1)


def halves_piece(second, rows, lanes):
    return second.reshape(second.shape[0], -1, lanes).transpose(1, 0, 2).reshape(rows, lanes)


def pad_to(item, rows, lanes):
    return jnp.pad(item, ((0, rows - item.shape[0]), (0, lanes - item.shape[1])))


def small_rows(conv_weight, conv_bias, norm_gain, norm_bias, out_bias):
    return jnp.concatenate([conv_weight[0], conv_bias, norm_gain, norm_bias, out_bias])


def shared_rows(attn_bias, hidden_bias):
    return jnp.concatenate([attn_bias, hidden_bias.reshape(-1, attn_bias.shape[1])])


class Direct:
    def __init__(self, p):
        lanes = p["spatial_qkv"].shape[0] * 4 // 3
        small = pad_to(small_rows(p["conv_weight"], p["conv_bias"], p["norm_gain"], p["norm_bias"], p["out_bias"]), 16, LANES)
        shared = pad_to(shared_rows(p["attn_bias"], p["hidden_bias"]), 16, LANES)
        head = pad_to(jnp.concatenate([small, shared], axis=1), 16, lanes)
        first = jnp.concatenate([head, attention_piece(p["spatial_qkv"], p["projection"][0])])
        rows = p["spatial_qkv"].shape[1]
        rest = jnp.concatenate([
            attention_piece(p["channel_qkv"], p["projection"][1]), p["mlp_in"][1].T,
            halves_piece(p["mlp_out"][1], rows, lanes),
        ])
        rest = lax.all_gather(rest, BOTH, axis=0, tiled=False)
        (got,) = gather("gather_first", 1, [first], [], [])
        watt0, self.lay, self.sh, self.hid = unpack_first(got)
        watt1, win1, wout1 = unpack_rest(rest)
        self.watt, self.w_in, self.w_out = (watt0, watt1), [None, win1], [None, wout1]
        self.own = (p["mlp_in"][0].T, p["mlp_out"][0])

    def forward_window(self, *args):
        *outs, self.w_in[0], self.w_out[0] = forward_window(*args, carry=Beside(3, *self.own))
        return outs

    def backward_window(self, g_in, g_out, *args):
        *outs, self.gi0, self.go0 = backward_window(*args, carry=Behind(4, g_in, g_out))
        return outs

    def reduce_rest(self, gq, gp, g_in, g_out):
        packed = pack_rest(gq, gp, g_in, g_out)
        packed = packed.reshape(-1, packed.shape[2])
        self.rest = lax.psum_scatter(packed, BOTH, scatter_dimension=0, tiled=True)

    def reduce_first(self, gq, gp, smalls, sb, cb, hid0, hid1):
        c = gp.shape[0]
        cn, lanes, cw = c // NARROW, c // 2, c // WIDE
        packed = pack_first(gq, gp, jnp.stack(smalls), sb, cb, hid0, hid1)
        low, high = reduce_all("reduce_first", 2, [packed], [], [])
        gi0, go0 = self.gi0, self.go0
        att0 = jnp.concatenate([low[16:], high])
        rest = self.rest.astype(F32)
        att1, gi1 = rest[:cn], rest[cn : 2 * cn]
        go1 = rest[2 * cn :].reshape(2, cw, lanes).transpose(1, 0, 2).reshape(cw, 2 * lanes)
        small, shared = low[:16, :cw], low[:16, LANES : LANES + cw]
        proj = jnp.stack([att0[:, 3 * cw :].T, att1[:, 3 * cw :].T])
        return (
            small[None, :9], small[9:10], small[10:11], small[11:12], att0[:, : 3 * cw].T, att1[:, : 3 * cw].T,
            proj, jnp.stack([gi0.T, gi1.T]), jnp.stack([go0, go1]), shared[:5], shared[5:13].reshape(2, lanes),
            small[12:13],
        )


class Plain:
    def __init__(self, p):
        self.layers, self.cw = p["conv_bias"].shape
        wide = p["attn_bias"].shape
        self.narrow = 4 // self.layers
        self.cn = p["spatial_qkv"].shape[1]
        self.c = self.cn * self.narrow
        self.wide = self.c // self.cw
        self.fw = p["hidden_bias"].shape[1]
        c, cn, cw, fw, n, w = self.c, self.cn, self.cw, self.fw, self.narrow, self.wide

        def spread(v):
            return lax.all_gather(v, BOTH, axis=0, tiled=False).reshape((n, w) + v.shape)

        def attention(qkv, proj):
            got = spread(attention_piece(qkv, proj)).transpose(0, 2, 1, 3)
            return jnp.concatenate([got[..., : 3 * cw].reshape(c, 3 * c), got[..., 3 * cw :].reshape(c, c)], axis=1)

        self.watt = tuple(attention(p[k], p["projection"][i]) for i, k in enumerate(("spatial_qkv", "channel_qkv")))
        self.w_in = tuple(spread(p["mlp_in"][i].T).transpose(0, 2, 1, 3).reshape(c, -1) for i in range(2))
        self.w_out = tuple(spread(p["mlp_out"][i]).transpose(1, 2, 0, 3).reshape(c, -1) for i in range(2))

        def layer(v):
            return spread(v).transpose(0, 2, 3, 1, 4).reshape(4, -1, c)

        rows = [layer(p["conv_weight"])]
        rows += [layer(p[k][:, None]) for k in ("conv_bias", "norm_gain", "norm_bias", "out_bias")]
        self.lay = jnp.pad(jnp.concatenate(rows, axis=1).astype(F32), ((0, 0), (0, 3), (0, 0)))
        attn = spread(p["attn_bias"])[0].transpose(1, 0, 2).reshape(5, c)
        self.sh = jnp.pad(attn.astype(F32), ((0, 11), (0, 0)))
        self.hid = spread(p["hidden_bias"])[0].transpose(1, 0, 2).reshape(2, 1, -1).astype(F32)

    def forward_window(self, *args):
        return forward_window(*args)

    def backward_window(self, g_in, g_out, *args):
        self.pair = (self.matrix(g_in, False), self.matrix(g_out, True))
        return backward_window(*args)

    def matrix(self, grad, rows_wide):
        n, w = self.narrow, self.wide
        a, b = (w, n) if rows_wide else (n, w)
        grad = grad.reshape(a, grad.shape[0] // a, b, grad.shape[1] // b)
        grad = grad.transpose(2, 0, 1, 3) if rows_wide else grad.transpose(0, 2, 1, 3)
        grad = grad.astype(BF16).reshape(n * w * grad.shape[2], grad.shape[3])
        return lax.psum_scatter(grad, BOTH, scatter_dimension=0, tiled=True).astype(F32)

    def reduce_rest(self, gq, gp, g_in, g_out):
        self.rest = (self.matrix(gq, False), self.matrix(gp, False), self.matrix(g_in, False), self.matrix(g_out, True))

    def reduce_first(self, gq, gp, smalls, sb, cb, hid0, hid1):
        c, cw, fw, n, w = self.c, self.cw, self.fw, self.narrow, self.wide
        first = (self.matrix(gq, False), self.matrix(gp, False)) + self.pair
        small = jnp.stack(smalls).reshape(n, self.layers * 16, w, cw).transpose(0, 2, 1, 3)
        attn = jnp.concatenate([sb[:, :c], sb[:, 2 * c :], cb.reshape(3, c)]).reshape(5, w, cw).transpose(1, 0, 2)
        hid = jnp.concatenate([hid0, hid1]).reshape(2, w, fw).transpose(1, 0, 2).reshape(w, -1, cw)
        common = jnp.concatenate([attn, hid], axis=1)
        common = jnp.broadcast_to(common[None], (n,) + common.shape)
        flat = jnp.concatenate([small, common], axis=2).astype(BF16).reshape(-1, cw)
        got = lax.psum_scatter(flat, BOTH, scatter_dimension=0, tiled=True).astype(F32)
        small = got[: self.layers * 16].reshape(self.layers, 16, cw)
        shared = got[self.layers * 16 :]
        rest = self.rest
        return (
            small[:, :9], small[:, 9], small[:, 10], small[:, 11], first[0].T, rest[0].T,
            jnp.stack([first[1].T, rest[1].T]), jnp.stack([first[2].T, rest[2].T]), jnp.stack([first[3], rest[3]]),
            shared[:5], shared[5:].reshape(2, fw), small[:, 12],
        )


NAMES = (
    "conv_weight", "conv_bias", "norm_gain", "norm_bias", "spatial_qkv", "channel_qkv", "projection", "mlp_in",
    "mlp_out", "attn_bias", "hidden_bias", "out_bias",
)


def local(plan, inputs, heights, widths, *rest):
    if inputs.shape[0] != len(REDUCE_STEPS):
        plan = Plain
    weights = plan(dict(zip(NAMES, rest[:-1])))
    cotangent = rest[-1]
    lay, sh, hid = weights.lay, weights.sh, weights.hid
    mask = token_mask(heights, widths)
    n1, z1, r1, q1, o1, p1, x2 = weights.forward_window(inputs, mask, lay, sh, weights.watt[0])
    n2, z2, r2, u1, d1, x4 = forward_mlp(x2, mask, lay, hid, weights.w_in[0], weights.w_out[0])
    n3, z3, r3, q3, o3, a3, x6 = forward_channel(x4, mask, lay, sh, weights.watt[1])
    out, g6, n4, u2, gy2, gh2, small3, hid1 = last_mlp(
        x6, cotangent, mask, lay, hid, weights.w_in[1], weights.w_out[1])
    gi1, go1 = grad_pair("last_mlp_grads", n4, gh2, gy2, u2)
    g4, ga3, dq3, small2, cb = backward_channel(g6, x4, z3, r3, q3, a3, mask, lay, weights.watt[1])
    gq1, gp1 = grad_pair("channel_grads", n3, dq3, o3, ga3)
    weights.reduce_rest(gq1, gp1, gi1, go1)
    g2, gy1, gh1, small1, hid0 = backward_mlp(g4, x2, z2, r2, d1, mask, lay, weights.w_in[0], weights.w_out[0])
    gi0, go0 = grad_pair("mlp_grads", n2, gh1, gy1, u1)
    input_grad, ga1, dq1, small0, sb = weights.backward_window(
        gi0, go0, g2, inputs, z1, r1, q1, p1, mask, lay, weights.watt[0])
    gq0, gp0 = grad_pair("window_grads", n1, dq1, o1, ga1)
    grads = weights.reduce_first(gq0, gp0, (small0, small1, small2, small3), sb, cb, hid0, hid1)
    return (out, input_grad) + grads


def solution(mesh):
    matrix = P("wide", "narrow")
    cells = P(("wide", "narrow"), None, None, None)
    stacked = P(None, "wide", "narrow")
    row = P("narrow", "wide")
    shared = P(None, "wide")
    images = P(("wide", "narrow"))
    kernels = P("narrow", None, "wide")
    in_specs = (
        cells, images, images, kernels, row, row, row, matrix, matrix,
        stacked, stacked, stacked, shared, shared, row, cells,
    )
    out_specs = (
        cells, cells, kernels, row, row, row, matrix, matrix, stacked, stacked, stacked, shared, shared, row,
    )
    plan = Direct if (mesh.shape["wide"], mesh.shape["narrow"]) == (WIDE, NARROW) else Plain
    body = functools.partial(local, plan)
    return jax.shard_map(body, mesh=mesh, in_specs=in_specs, out_specs=out_specs, check_vma=False)
```

```python
import functools

import jax
import jax.numpy as jnp
from jax import lax
from jax.experimental import pallas as pl
from jax.experimental.pallas import tpu as pltpu
from jax.sharding import PartitionSpec as P

HD = 32
WIN = 7
LANES = 128
SUB = 8
GROUP = 256
WTOK = WIN * SUB
FFC = 1024
NROWS = 112
SCALE = HD ** (-0.5)
EPS = 1e-05
NEG = -1e30
F32 = jnp.float32
BF16 = jnp.bfloat16
VMEM_LIMIT = 60 * 1024 * 1024
DIMS_NN = (((1,), (0,)), ((), ()))
DIMS_NT = (((1,), (1,)), ((), ()))
DIMS_TN = (((0,), (0,)), ((), ()))


def dot(a, b, dims):
    return lax.dot_general(a, b, dims, preferred_element_type=F32)


def tok(r, half):
    return ((r // WIN) * 2 + half) * WTOK + (r % WIN) * SUB


def load_cells(src, dst):
    for r in range(2 * WIN):
        row = src[0, r].astype(F32)
        dst[pl.ds(tok(r, 0), WIN), :] = row[:WIN]
        dst[pl.ds(tok(r, 1), WIN), :] = row[WIN:]


def store_cells(value_at, dst, stage):
    for r in range(2 * WIN):
        stage[pl.ds(0, SUB), :] = value_at(tok(r, 0))
        stage[pl.ds(WIN, SUB), :] = value_at(tok(r, 1))
        dst[0, r] = stage[pl.ds(0, 2 * WIN), :].astype(BF16)


def neighbours(left, right):
    last = lax.broadcasted_iota(jnp.int32, (SUB, LANES), 0) == SUB - 1
    up_right = pltpu.roll(right, SUB - 1, 0)
    up_left = pltpu.roll(jnp.where(last, up_right, left), SUB - 1, 0)
    down_left = pltpu.roll(left, 1, 0)
    down_right = pltpu.roll(jnp.where(last, down_left, right), 1, 0)
    return ((down_left, left, up_left), (down_right, right, up_right))


def masked_row(src, mask, r, lanes):
    pair = []
    for half in range(2):
        rows = pl.ds(tok(r, half), SUB)
        pair.append(src[rows, lanes] * mask[0, rows, :])
    return neighbours(*pair)


def plain_row(src, r, lanes):
    return neighbours(*[src[pl.ds(tok(r, half), SUB), lanes] for half in range(2)])


def lay_row(lay, k):
    return lay[0, pl.ds(k, 1), :]


def taps(lay, lanes):
    return [jnp.broadcast_to(lay[0, pl.ds(k, 1), lanes], (SUB, LANES)) for k in range(10)]


def conv_forward(src, mask, lay, dst):
    rows = 2 * WIN

    @pl.loop(0, src.shape[1] // LANES)
    def _(j):
        lanes = pl.ds(pl.multiple_of(j * LANES, LANES), LANES)
        w = taps(lay, lanes)
        shift = w[9]
        window = [None, masked_row(src, mask, 0, lanes), masked_row(src, mask, 1, lanes)]
        for r in range(rows):
            for half in range(2):
                total = shift
                for a in range(3):
                    if window[a] is None:
                        continue
                    for b in range(3):
                        total = total + w[3 * a + b] * window[a][half][b]
                at = pl.ds(tok(r, half), SUB)
                dst[at, lanes] = src[at, lanes] + total
            following = masked_row(src, mask, r + 2, lanes) if r + 2 < rows else None
            window = [window[1], window[2], following]


def conv_backward(x_src, g_src, mask, lay, sums, dst):
    rows = 2 * WIN

    @pl.loop(0, x_src.shape[1] // LANES)
    def _(j):
        lanes = pl.ds(pl.multiple_of(j * LANES, LANES), LANES)
        w = taps(lay, lanes)
        g_win = [None, plain_row(g_src, 0, lanes), plain_row(g_src, 1, lanes)]
        x_win = [None, masked_row(x_src, mask, 0, lanes), masked_row(x_src, mask, 1, lanes)]
        grads = [sums[pl.ds(SUB * k, SUB), lanes] for k in range(10)]
        for r in range(rows):
            for half in range(2):
                center = g_win[1][half][1]
                total = None
                for a in range(3):
                    for b in range(3):
                        if x_win[a] is not None:
                            grads[3 * a + b] = grads[3 * a + b] + center * x_win[a][half][b]
                        if g_win[2 - a] is not None:
                            term = w[3 * a + b] * g_win[2 - a][half][2 - b]
                            total = term if total is None else total + term
                grads[9] = grads[9] + center
                at = pl.ds(tok(r, half), SUB)
                dst[at, lanes] = center + mask[0, at, :] * total
            more = r + 2 < rows
            g_win = [g_win[1], g_win[2], plain_row(g_src, r + 2, lanes) if more else None]
            x_win = [x_win[1], x_win[2], masked_row(x_src, mask, r + 2, lanes) if more else None]
        for k in range(10):
            sums[pl.ds(SUB * k, SUB), lanes] = grads[k]


def norm_forward(src, lay, z_out, r_out, n_out):
    features = src.shape[1]

    @pl.loop(0, src.shape[0] // (2 * NROWS))
    def _(i):
        for j in range(2):
            rows = pl.ds(pl.multiple_of(i * (2 * NROWS) + j * NROWS, NROWS), NROWS)
            x = src[rows, :]
            center = x - jnp.sum(x, axis=1, keepdims=True) * (1.0 / features)
            var = jnp.sum(center * center, axis=1, keepdims=True) * (1.0 / features)
            rstd = lax.rsqrt(var + EPS)
            z = center * rstd
            z_out[rows, :] = z
            r_out[rows, :] = jnp.broadcast_to(rstd, (NROWS, LANES))
            n_out[rows, :] = (z * lay_row(lay, 10) + lay_row(lay, 11)).astype(BF16)


def norm_backward(dn, z_src, r_src, lay, g_src, sums, first, dst):
    features = dn.shape[1]

    @pl.loop(0, dn.shape[0] // (2 * NROWS))
    def _(i):
        for j in range(2):
            rows = pl.ds(pl.multiple_of(i * (2 * NROWS) + j * NROWS, NROWS), NROWS)
            d = dn[rows, :]
            z = z_src[rows, :]
            t = d * lay_row(lay, 10)
            m1 = jnp.sum(t, axis=1, keepdims=True) * (1.0 / features)
            m2 = jnp.sum(t * z, axis=1, keepdims=True) * (1.0 / features)
            dst[rows, :] = g_src[rows, :] + (t - m1 - z * m2) * r_src[rows, 0:1]
            at = pl.ds(first, SUB)
            sums[at, :] = sums[at, :] + fold_rows(d * z)
            at = pl.ds(first + SUB, SUB)
            sums[at, :] = sums[at, :] + fold_rows(d)


def fold_rows(value):
    total = value[:SUB]
    for i in range(1, value.shape[0] // SUB):
        total = total + value[SUB * i : SUB * (i + 1)]
    return total


def finish_sums(sums, out):
    for k in range(sums.shape[0] // SUB):
        out[pl.ds(k, 1), :] = jnp.sum(sums[pl.ds(SUB * k, SUB), :], axis=0, keepdims=True)


def head_masks():
    lane = lax.broadcasted_iota(jnp.int32, (WTOK, GROUP), 1) // HD
    return [lane == h for h in range(GROUP // HD)]


def spread_heads(value, masks):
    return jnp.concatenate([jnp.where(m, value, 0.0) for m in masks], axis=0).astype(BF16)


def collect_heads(full, masks):
    total = full[:WTOK]
    for h in range(1, len(masks)):
        total = jnp.where(masks[h], full[WTOK * h : WTOK * (h + 1)], total)
    return total


def rounded(value):
    return value.astype(BF16).astype(F32)


def gelu_pair(h):
    cdf = 0.5 * (1.0 + lax.erf(h * 0.7071067811865476))
    pdf = jnp.exp(h * h * -0.5) * 0.3989422804014327
    return h * cdf, cdf + h * pdf


def first_step():
    return pl.program_id(0) == 0


def last_step():
    return pl.program_id(0) == pl.num_programs(0) - 1


def window_forward_kernel(
    inp, mask, lay, sh, watt,
    n_out, z_out, r_out, q_out, o_out, p_out, x_out,
    x0, x1, qf, of,
):
    features = x0.shape[1]

    @pl.when(first_step())
    def _():
        x0[...] = jnp.zeros_like(x0)

    load_cells(inp, x0)
    conv_forward(x0, mask, lay, x1)
    norm_forward(x1, lay, z_out.at[0], r_out.at[0], n_out.at[0])
    chunk = features
    for c in range(3):
        lanes = pl.ds(c * chunk, chunk)
        part = dot(n_out[0], watt[:, lanes], DIMS_NN)
        if c != 1:
            part = part + sh[pl.ds(c // 2, 1), :]
        part = part.astype(BF16)
        q_out[0, :, lanes] = part
        qf[:, lanes] = part.astype(F32)

    @pl.loop(0, 4)
    def _(w):
        rows = pl.ds(pl.multiple_of(w * WTOK, SUB), WTOK)
        valid = mask[0, rows, 0:1] > 0.0
        masks = head_masks()
        for g in range(features // GROUP):
            q = qf[rows, pl.ds(g * GROUP, GROUP)]
            k = qf[rows, pl.ds(features + g * GROUP, GROUP)].astype(BF16)
            v = qf[rows, pl.ds(2 * features + g * GROUP, GROUP)].astype(BF16)
            s = dot(k, spread_heads(q, masks), DIMS_NT) * SCALE
            s = jnp.where(valid, s, NEG)
            e = jnp.exp(s - jnp.max(s, axis=0, keepdims=True))
            p = (e / jnp.sum(e, axis=0, keepdims=True)).astype(BF16)
            p_out[0, w, g] = p
            of[rows, pl.ds(g * GROUP, GROUP)] = collect_heads(dot(p, v, DIMS_TN), masks)

    o_out[0] = of[...].astype(BF16)
    x_out[0] = x1[...] + (dot(o_out[0], watt[:, pl.ds(3 * features, features)], DIMS_NN) + lay_row(lay, 12))


def mlp_forward_kernel(
    x_in, mask, lay, hb, w_in, w_out,
    n_out, z_out, r_out, u_out, d_out, x_out,
    x1, acc,
):
    conv_forward(x_in.at[0], mask, lay, x1)
    norm_forward(x1, lay, z_out.at[0], r_out.at[0], n_out.at[0])
    for c in range(w_in.shape[1] // FFC):
        lanes = pl.ds(c * FFC, FFC)
        h = dot(n_out[0], w_in[:, lanes], DIMS_NN) + hb[0, :, lanes]
        u, d = gelu_pair(h)
        u = u.astype(BF16)
        u_out[0, :, lanes] = u
        d_out[0, :, lanes] = d.astype(BF16)
        y = dot(u, w_out[:, lanes], DIMS_NT)
        acc[...] = y if c == 0 else acc[...] + y
    x_out[0] = x1[...] + (acc[...] + lay_row(lay, 12))


def group_mask():
    row = lax.broadcasted_iota(jnp.int32, (GROUP, GROUP), 0) // HD
    col = lax.broadcasted_iota(jnp.int32, (GROUP, GROUP), 1) // HD
    return row == col


def channel_forward_kernel(
    x_in, mask, lay, sh, watt,
    n_out, z_out, r_out, q_out, o_out, a_out, x_out,
    x1,
):
    features = x1.shape[1]
    conv_forward(x_in.at[0], mask, lay, x1)
    norm_forward(x1, lay, z_out.at[0], r_out.at[0], n_out.at[0])
    for c in range(3):
        lanes = pl.ds(c * features, features)
        part = dot(n_out[0], watt[:, lanes], DIMS_NN) + sh[pl.ds(2 + c, 1), :]
        if c == 1:
            part = part * mask[0, :, 0:1]
        q_out[0, :, lanes] = part.astype(BF16)
    same = group_mask()
    for g in range(features // GROUP):
        q = q_out[0, :, pl.ds(g * GROUP, GROUP)]
        k = q_out[0, :, pl.ds(features + g * GROUP, GROUP)]
        v = q_out[0, :, pl.ds(2 * features + g * GROUP, GROUP)]
        s = jnp.where(same, dot(k, q, DIMS_TN) * SCALE, -jnp.inf)
        e = jnp.exp(s - jnp.max(s, axis=0, keepdims=True))
        a = (e / jnp.sum(e, axis=0, keepdims=True)).astype(BF16)
        a_out[0, g] = a
        o_out[0, :, pl.ds(g * GROUP, GROUP)] = dot(v, a, DIMS_NN).astype(BF16)
    x_out[0] = x1[...] + (dot(o_out[0], watt[:, pl.ds(3 * features, features)], DIMS_NN) + lay_row(lay, 12))


def last_mlp_kernel(
    x_in, cot, mask, lay, hb, w_in, w_out,
    out, g_out, n_out, u_out, gy_out, gh_out, small_out, hidden_out,
    x1, z, r, acc, dn, g8, stage, sums, hsums,
):
    @pl.when(first_step())
    def _():
        g8[...] = jnp.zeros_like(g8)
        sums[...] = jnp.zeros_like(sums)
        hsums[...] = jnp.zeros_like(hsums)

    x6 = x_in.at[0]
    load_cells(cot, g8)
    conv_forward(x6, mask, lay, x1)
    norm_forward(x1, lay, z, r, n_out.at[0])
    g8[...] = g8[...] * mask[0, :, 0:1]
    gy_out[0] = g8[...].astype(BF16)
    sums[pl.ds(12 * SUB, SUB), :] = sums[pl.ds(12 * SUB, SUB), :] + fold_rows(gy_out[0].astype(F32))
    for c in range(w_in.shape[1] // FFC):
        lanes = pl.ds(c * FFC, FFC)
        h = dot(n_out[0], w_in[:, lanes], DIMS_NN) + hb[0, :, lanes]
        du = dot(gy_out[0], w_out[:, lanes], DIMS_NN)
        u, d = gelu_pair(h)
        u = u.astype(BF16)
        u_out[0, :, lanes] = u
        gh = (du * d).astype(BF16)
        gh_out[0, :, lanes] = gh
        hsums[:, lanes] = hsums[:, lanes] + fold_rows(gh.astype(F32))
        y = dot(u, w_out[:, lanes], DIMS_NT)
        dx = dot(gh, w_in[:, lanes], DIMS_NT)
        acc[...] = y if c == 0 else acc[...] + y
        dn[...] = dx if c == 0 else dn[...] + dx
    acc[...] = (x1[...] + (acc[...] + lay_row(lay, 12))) * mask[0, :, 0:1]
    store_cells(lambda at: acc[pl.ds(at, SUB), :], out, stage)
    norm_backward(dn, z, r, lay, g8, sums, 10 * SUB, x1)
    conv_backward(x6, x1, mask, lay, sums, g_out.at[0])

    @pl.when(last_step())
    def _():
        finish_sums(sums, small_out)
        finish_sums(hsums, hidden_out)


def mlp_backward_kernel(
    g_in, x_in, z_in, r_in, d_in, mask, lay, w_in, w_out,
    g_out, gy_out, gh_out, small_out, hidden_out,
    dn, g1, sums, hsums,
):
    @pl.when(first_step())
    def _():
        sums[...] = jnp.zeros_like(sums)
        hsums[...] = jnp.zeros_like(hsums)

    gy_out[0] = g_in[0].astype(BF16)
    sums[pl.ds(12 * SUB, SUB), :] = sums[pl.ds(12 * SUB, SUB), :] + fold_rows(gy_out[0].astype(F32))
    for c in range(w_in.shape[1] // FFC):
        lanes = pl.ds(c * FFC, FFC)
        du = dot(gy_out[0], w_out[:, lanes], DIMS_NN)
        gh = (du * d_in[0, :, lanes].astype(F32)).astype(BF16)
        gh_out[0, :, lanes] = gh
        hsums[:, lanes] = hsums[:, lanes] + fold_rows(gh.astype(F32))
        dx = dot(gh, w_in[:, lanes], DIMS_NT)
        dn[...] = dx if c == 0 else dn[...] + dx
    norm_backward(dn, z_in.at[0], r_in.at[0], lay, g_in.at[0], sums, 10 * SUB, g1)
    conv_backward(x_in.at[0], g1, mask, lay, sums, g_out.at[0])

    @pl.when(last_step())
    def _():
        finish_sums(sums, small_out)
        finish_sums(hsums, hidden_out)


def channel_backward_kernel(
    g_in, x_in, z_in, r_in, q_in, a_in, mask, lay, watt,
    g_out, ga_out, dq_out, small_out, bias_out,
    dn, g1, sums, bsums,
):
    features = dn.shape[1]

    @pl.when(first_step())
    def _():
        sums[...] = jnp.zeros_like(sums)
        bsums[...] = jnp.zeros_like(bsums)

    ga_out[0] = g_in[0].astype(BF16)
    sums[pl.ds(12 * SUB, SUB), :] = sums[pl.ds(12 * SUB, SUB), :] + fold_rows(ga_out[0].astype(F32))
    go = dot(ga_out[0], watt[:, pl.ds(3 * features, features)], DIMS_NT).astype(BF16)
    for g in range(features // GROUP):
        at = [pl.ds(i * features + g * GROUP, GROUP) for i in range(3)]
        q, k, v = (q_in[0, :, lanes] for lanes in at)
        gog = go[:, g * GROUP : (g + 1) * GROUP]
        a = a_in[0, g]
        af = a.astype(F32)
        dp = dot(v, gog, DIMS_TN)
        ds = (af * (dp - jnp.sum(dp * af, axis=0, keepdims=True))).astype(BF16)
        dq_out[0, :, at[0]] = (dot(k, ds, DIMS_NN) * SCALE).astype(BF16)
        dq_out[0, :, at[1]] = (dot(q, ds, DIMS_NT) * SCALE * mask[0, :, 0:1]).astype(BF16)
        dq_out[0, :, at[2]] = dot(gog, a, DIMS_NT).astype(BF16)
    bsums[...] = bsums[...] + fold_rows(dq_out[0].astype(F32))
    dn[...] = dot(dq_out[0], watt[:, pl.ds(0, 3 * features)], DIMS_NT)
    norm_backward(dn, z_in.at[0], r_in.at[0], lay, g_in.at[0], sums, 10 * SUB, g1)
    conv_backward(x_in.at[0], g1, mask, lay, sums, g_out.at[0])

    @pl.when(last_step())
    def _():
        finish_sums(sums, small_out)
        finish_sums(bsums, bias_out)


def window_backward_kernel(
    g_in, inp, z_in, r_in, q_in, p_in, mask, lay, watt,
    g_out, ga_out, dq_out, small_out, bias_out,
    x0, qf, gof, dqf, dn, g1, stage, sums, bsums,
):
    features = dn.shape[1]

    @pl.when(first_step())
    def _():
        x0[...] = jnp.zeros_like(x0)
        sums[...] = jnp.zeros_like(sums)
        bsums[...] = jnp.zeros_like(bsums)

    load_cells(inp, x0)
    ga_out[0] = g_in[0].astype(BF16)
    sums[pl.ds(12 * SUB, SUB), :] = sums[pl.ds(12 * SUB, SUB), :] + fold_rows(ga_out[0].astype(F32))
    gof[...] = rounded(dot(ga_out[0], watt[:, pl.ds(3 * features, features)], DIMS_NT))
    qf[...] = q_in[0].astype(F32)

    @pl.loop(0, 4)
    def _(w):
        rows = pl.ds(pl.multiple_of(w * WTOK, SUB), WTOK)
        masks = head_masks()
        for g in range(features // GROUP):
            at = [pl.ds(i * features + g * GROUP, GROUP) for i in range(3)]
            qe = spread_heads(qf[rows, at[0]], masks)
            k = qf[rows, at[1]].astype(BF16)
            v = qf[rows, at[2]].astype(BF16)
            goe = spread_heads(gof[rows, at[0]], masks)
            p = p_in[0, w, g]
            pf = p.astype(F32)
            dp = dot(v, goe, DIMS_NT)
            ds = (pf * (dp - jnp.sum(dp * pf, axis=0, keepdims=True))).astype(BF16)
            dqf[rows, at[0]] = collect_heads(dot(ds, k, DIMS_TN), masks) * SCALE
            dqf[rows, at[1]] = dot(ds, qe, DIMS_NN) * SCALE
            dqf[rows, at[2]] = dot(p, goe, DIMS_NN)

    dq_out[0] = dqf[...].astype(BF16)
    bsums[...] = bsums[...] + fold_rows(dq_out[0].astype(F32))
    dn[...] = dot(dq_out[0], watt[:, pl.ds(0, 3 * features)], DIMS_NT)
    norm_backward(dn, z_in.at[0], r_in.at[0], lay, g_in.at[0], sums, 10 * SUB, g1)
    conv_backward(x0, g1, mask, lay, sums, dn)
    store_cells(lambda at: dn[pl.ds(at, SUB), :], g_out, stage)

    @pl.when(last_step())
    def _():
        finish_sums(sums, small_out)
        finish_sums(bsums, bias_out)


def per_image(shape):
    rest = (0,) * (len(shape) - 1)
    return pl.BlockSpec((1,) + tuple(shape[1:]), lambda i: (i,) + rest)


def whole(shape):
    zeros = (0,) * len(shape)
    return pl.BlockSpec(tuple(shape), lambda i: zeros, pipeline_mode=pl.Buffered(1))


def one_layer(shape, layer):
    return pl.BlockSpec((1,) + tuple(shape[1:]), lambda i: (layer, 0, 0), pipeline_mode=pl.Buffered(1))


def cost(flops, arrays):
    size = sum(jnp.dtype(d).itemsize * functools.reduce(lambda p, q: p * q, s) for s, d in arrays)
    return pl.CostEstimate(flops=int(flops), bytes_accessed=int(size), transcendentals=0)


def params():
    return pltpu.CompilerParams(dimension_semantics=("arbitrary",), vmem_limit_bytes=VMEM_LIMIT)


def carrier(kernel, carry, ins, outs, scratch, refs):
    extra_in, extra_out = len(carry.args), len(carry.outs)
    base_in, refs = refs[:ins], refs[ins:]
    carry_in, refs = refs[:extra_in], refs[extra_in:]
    base_out, refs = refs[:outs], refs[outs:]
    carry_out, refs = refs[:extra_out], refs[extra_out:]
    base_scratch, carry_scratch = refs[:scratch], refs[scratch:]
    carry.run(carry_in, carry_out, carry_scratch)
    kernel(*base_in, *base_out, *base_scratch)
    carry.end(carry_in, carry_out, carry_scratch)


def image_call(kernel, name, layer, batched, lay, shared, outs, sums, scratch, flops, carry=None):
    images = batched[0].shape[0]
    ins = [per_image(a.shape) for a in batched] + [one_layer(lay.shape, layer)]
    args = list(batched) + [lay]
    for item in shared:
        if isinstance(item, tuple):
            ins.append(one_layer(item[0].shape, item[1]))
            args.append(item[0])
        else:
            ins.append(whole(item.shape))
            args.append(item)
    out_specs = [per_image(s) for s, _ in outs]
    out_specs += [pl.BlockSpec(tuple(s), lambda i: (0, 0)) for s, _ in sums]
    results = outs + sums
    buffers = [pltpu.VMEM(s, d) for s, d in scratch]
    options = params()
    body = kernel
    if carry is not None:
        counts = (len(args), len(results), len(scratch))

        def body(*refs):
            carrier(kernel, carry, *counts, refs)

        args = args + carry.args
        ins = ins + [pl.BlockSpec(memory_space=pl.ANY)] * len(carry.args)
        out_specs += [carry.out_spec or pl.BlockSpec(tuple(s), lambda i: (0, 0)) for s, _ in carry.outs]
        results = results + carry.outs
        buffers += carry.scratch
        options = pltpu.CompilerParams(
            dimension_semantics=("arbitrary",), vmem_limit_bytes=VMEM_LIMIT, collective_id=carry.ident,
            has_side_effects=True,
        )
    arrays = [(a.shape, a.dtype) for a in args] + results
    return pl.pallas_call(
        body,
        grid=(images,),
        in_specs=ins,
        out_specs=out_specs,
        out_shape=[jax.ShapeDtypeStruct(s, d) for s, d in results],
        scratch_shapes=buffers,
        compiler_params=options,
        cost_estimate=cost(flops, arrays),
        name=name,
    )(*args)


def token_mask(heights, widths):
    t = jnp.arange(4 * WTOK, dtype=jnp.int32)
    window = t // WTOK
    row = (window // 2) * WIN + (t % WTOK) // SUB
    col8 = t % SUB
    col = (window % 2) * WIN + col8
    valid = (row[None] < heights[:, None]) & (col[None] < widths[:, None]) & (col8 < WIN)[None]
    return jnp.broadcast_to(valid.astype(F32)[..., None], valid.shape + (LANES,))


def forward_window(inputs, mask, lay, sh, watt, carry=None):
    images, _, _, c = inputs.shape
    t = 4 * WTOK
    outs = [
        ((images, t, c), BF16), ((images, t, c), F32), ((images, t, LANES), F32),
        ((images, t, 3 * c), BF16), ((images, t, c), BF16),
        ((images, 4, c // GROUP, WTOK, WTOK * GROUP // HD), BF16), ((images, t, c), F32),
    ]
    scratch = [((t, c), F32), ((t, c), F32), ((t, 3 * c), F32), ((t, c), F32)]
    return image_call(window_forward_kernel, "window_forward", 0, [inputs, mask], lay, [sh, watt],
                      outs, [], scratch, 10 * images * t * c * c, carry)


def forward_mlp(x, mask, lay, hid, w_in, w_out, carry=None):
    images, t, c = x.shape
    ff = w_in.shape[1]
    outs = [
        ((images, t, c), BF16), ((images, t, c), F32), ((images, t, LANES), F32),
        ((images, t, ff), BF16), ((images, t, ff), BF16), ((images, t, c), F32),
    ]
    scratch = [((t, c), F32), ((t, c), F32)]
    return image_call(mlp_forward_kernel, "mlp_forward", 1, [x, mask], lay, [(hid, 0), w_in, w_out],
                      outs, [], scratch, 4 * images * t * c * ff, carry)


def forward_channel(x, mask, lay, sh, watt, carry=None):
    images, t, c = x.shape
    outs = [
        ((images, t, c), BF16), ((images, t, c), F32), ((images, t, LANES), F32),
        ((images, t, 3 * c), BF16), ((images, t, c), BF16),
        ((images, c // GROUP, GROUP, GROUP), BF16), ((images, t, c), F32),
    ]
    return image_call(channel_forward_kernel, "channel_forward", 2, [x, mask], lay, [sh, watt],
                      outs, [], [((t, c), F32)], 9 * images * t * c * c, carry)


def last_mlp(x, cot, mask, lay, hid, w_in, w_out):
    images, t, c = x.shape
    ff = w_in.shape[1]
    outs = [
        (cot.shape, BF16), ((images, t, c), F32), ((images, t, c), BF16), ((images, t, ff), BF16),
        ((images, t, c), BF16), ((images, t, ff), BF16),
    ]
    scratch = [
        ((t, c), F32), ((t, c), F32), ((t, LANES), F32), ((t, c), F32), ((t, c), F32), ((t, c), F32),
        ((16, c), F32), ((16 * SUB, c), F32), ((SUB, ff), F32),
    ]
    return image_call(last_mlp_kernel, "last_mlp", 3, [x, cot, mask], lay, [(hid, 1), w_in, w_out],
                      outs, [((16, c), F32), ((1, ff), F32)], scratch, 8 * images * t * c * ff)


def backward_mlp(g, x, z, r, d, mask, lay, w_in, w_out, carry=None):
    images, t, c = x.shape
    ff = w_in.shape[1]
    outs = [((images, t, c), F32), ((images, t, c), BF16), ((images, t, ff), BF16)]
    scratch = [((t, c), F32), ((t, c), F32), ((16 * SUB, c), F32), ((SUB, ff), F32)]
    return image_call(mlp_backward_kernel, "mlp_backward", 1, [g, x, z, r, d, mask], lay, [w_in, w_out],
                      outs, [((16, c), F32), ((1, ff), F32)], scratch, 4 * images * t * c * ff, carry)


def backward_channel(g, x, z, r, q, a, mask, lay, watt, carry=None):
    images, t, c = x.shape
    outs = [((images, t, c), F32), ((images, t, c), BF16), ((images, t, 3 * c), BF16)]
    scratch = [((t, c), F32), ((t, c), F32), ((16 * SUB, c), F32), ((SUB, 3 * c), F32)]
    return image_call(channel_backward_kernel, "channel_backward", 2, [g, x, z, r, q, a, mask], lay, [watt],
                      outs, [((16, c), F32), ((1, 3 * c), F32)], scratch, 10 * images * t * c * c, carry)


def backward_window(g, inputs, z, r, q, p, mask, lay, watt, carry=None):
    images, t, c = g.shape
    outs = [(inputs.shape, BF16), ((images, t, c), BF16), ((images, t, 3 * c), BF16)]
    scratch = [
        ((t, c), F32), ((t, 3 * c), F32), ((t, c), F32), ((t, 3 * c), F32), ((t, c), F32), ((t, c), F32),
        ((16, c), F32), ((16 * SUB, c), F32), ((SUB, 3 * c), F32),
    ]
    return image_call(window_backward_kernel, "window_backward", 0, [g, inputs, z, r, q, p, mask], lay, [watt],
                      outs, [((16, c), F32), ((1, 3 * c), F32)], scratch, 12 * images * t * c * c, carry)


def grad_pair_kernel(first, left0, right0, left1, right1, out0, out1):
    step = pl.program_id(0)

    @pl.when(step < first)
    def _():
        out0[...] = dot(left0[...], right0[...], DIMS_TN).astype(BF16)

    @pl.when(step >= first)
    def _():
        out1[...] = dot(left1[...], right1[...], DIMS_TN).astype(BF16)


def grad_pair(name, left0, right0, left1, right1):
    flat = [a.reshape(-1, a.shape[-1]) for a in (left0, right0, left1, right1)]
    rows, c = flat[0].shape
    first, second = flat[1].shape[1] // c, flat[3].shape[1] // c

    def at_first(i):
        return (0, jnp.minimum(i, first - 1))

    def at_second(i):
        return (0, jnp.maximum(i - first, 0))

    outs = [((c, flat[1].shape[1]), BF16), ((c, flat[3].shape[1]), BF16)]
    return pl.pallas_call(
        functools.partial(grad_pair_kernel, first),
        grid=(first + second,),
        in_specs=[
            whole((rows, c)), pl.BlockSpec((rows, c), at_first),
            whole((rows, c)), pl.BlockSpec((rows, c), at_second),
        ],
        out_specs=[pl.BlockSpec((c, c), at_first), pl.BlockSpec((c, c), at_second)],
        out_shape=[jax.ShapeDtypeStruct(s, d) for s, d in outs],
        compiler_params=params(),
        cost_estimate=cost(2 * rows * c * c * (first + second), [(a.shape, BF16) for a in flat] + outs),
        name=name,
    )(*flat)


WIDE = 8
NARROW = 4
BOTH = ("narrow", "wide")
AXES = (("wide", 2), ("wide", 4), ("wide", 1), ("narrow", 2), ("narrow", 1))
ORDERS = ((0, 1, 2, 3), (0, 1, 3, 2))
MESH_ID = pl.DeviceIdType.MESH
STAGES = (0, 4, 8, 12, 1, 5, 9, 13, 2, 6, 10, 14, 3, 7, 11, 15)
GATHER_STEPS = ((0,), (1, 2, 4, 8), (5, 12, 9), (3, 6, 10), (13, 7), (14, 11), (15,))
REDUCE_STEPS = ((), (15, 11), (7, 14, 10), (3, 6, 13), (2, 9), (5, 12), (1, 8, 4), (0,))


def flip(value, bit):
    return value + bit - 2 * bit * ((value // bit) % 2)


def place(order, rel):
    at = {"narrow": lax.axis_index("narrow"), "wide": lax.axis_index("wide")}
    for i, axis in enumerate(tuple(ORDERS[order]) + (4,)):
        if rel & (1 << i):
            name, bit = AXES[axis]
            at[name] = flip(at[name], bit)
    return at


def highest(rel):
    return rel.bit_length() - 1


def meet():
    barrier = pltpu.get_barrier_semaphore()
    for name, bit in AXES:
        at = {"narrow": lax.axis_index("narrow"), "wide": lax.axis_index("wide")}
        at[name] = flip(at[name], bit)
        pl.semaphore_signal(barrier, inc=1, device_id=at, device_id_type=MESH_ID)
    pl.semaphore_wait(barrier, 5)


class Part:
    def __init__(self, operand, kind, shape, start, size, order):
        self.operand, self.kind, self.shape, self.start, self.size, self.order = operand, kind, shape, start, size, order

    def whole(self):
        rows, cols = self.shape
        return {
            "slot": (WIDE * NARROW, rows, cols), "in": (NARROW * rows, WIDE * cols), "out": (WIDE * rows, NARROW * cols),
        }[self.kind]

    def view(self, ref, n, w):
        rows, cols = self.shape
        if self.kind == "slot":
            return ref.at[n * WIDE + w, pl.ds(self.start, self.size), :]
        a, b = (n, w) if self.kind == "in" else (w, n)
        step = 16
        while step < 128 and rows % (2 * step) == 0 and self.start % (2 * step) == 0:
            step *= 2
        at = pl.multiple_of(a * rows + self.start, step)
        return ref.at[pl.ds(at, self.size), pl.ds(pl.multiple_of(b * cols, cols), cols)]

    def of(self, ref, rel):
        at = place(self.order, rel)
        return self.view(ref, at["narrow"], at["wide"])


def halves(operand, kind, shape):
    low = shape[0] // 32 * 16
    return [Part(operand, kind, shape, 0, low, 0), Part(operand, kind, shape, low, shape[0] - low, 1)]


def pair(first, second, shape_in, shape_out):
    return [Part(first, "in", shape_in, 0, shape_in[0], 0), Part(second, "out", shape_out, 0, shape_out[0], 1)]


class Gather:
    def __init__(self, index, part, own, dest, sems):
        self.index, self.part, self.dest = index, part, dest
        self.own = own.at[pl.ds(part.start, part.size), :]
        self.send, self.recv, self.keep = sems

    def copy(self, rel, axis):
        target = self.part.of(self.dest, rel)
        slot = rel | (1 << axis)
        return pltpu.make_async_remote_copy(
            src_ref=self.own if rel == 0 else target, dst_ref=target, send_sem=self.send.at[self.index, slot],
            recv_sem=self.recv.at[self.index, slot], device_id=place(self.part.order, 1 << axis), device_id_type=MESH_ID,
        )

    def arrival(self, rel):
        target = self.part.of(self.dest, rel)
        return pltpu.make_async_remote_copy(
            src_ref=target, dst_ref=target, send_sem=self.send.at[self.index, 0],
            recv_sem=self.recv.at[self.index, rel], device_id=place(self.part.order, 1), device_id_type=MESH_ID,
        )

    def stay(self):
        return pltpu.make_async_copy(self.own, self.part.of(self.dest, 0), self.keep.at[self.index])

    def stage(self, rel):
        if rel == 0:
            self.stay().start()
        else:
            self.arrival(rel).wait_recv()
        for axis in reversed(range(highest(rel) + 1, 5)):
            self.copy(rel, axis).start()

    def finish(self):
        for rel in range(16, 32):
            self.arrival(rel).wait_recv()
        for rel in range(16):
            for axis in range(highest(rel) + 1, 5):
                self.copy(rel, axis).wait_send()
        self.stay().wait()


def gather_sems(count):
    return [pltpu.SemaphoreType.DMA((count, 32)), pltpu.SemaphoreType.DMA((count, 32)), pltpu.SemaphoreType.DMA((count,))]


class Beside:
    def __init__(self, ident, args, parts, pick=None):
        self.ident, self.args, self.parts = ident, list(args), parts
        self.pick = pick or {}
        shapes = {p.operand: p.whole() for p in parts}
        self.outs = [(shapes[k], BF16) for k in range(len(self.args))]
        self.out_spec = pl.BlockSpec(memory_space=pl.ANY)
        self.scratch = gather_sems(len(parts))

    def items(self, ins, outs, scratch):
        ins = [ref.at[self.pick[k]] if k in self.pick else ref for k, ref in enumerate(ins)]
        return [Gather(i, p, ins[p.operand], outs[p.operand], scratch) for i, p in enumerate(self.parts)]

    def run(self, ins, outs, scratch):
        items = self.items(ins, outs, scratch)
        for s, rels in enumerate(GATHER_STEPS):

            @pl.when(pl.program_id(0) == s)
            def _(s=s, rels=rels):
                if s == 0:
                    meet()
                for rel in rels:
                    for item in items:
                        item.stage(rel)

    def end(self, ins, outs, scratch):
        @pl.when(last_step())
        def _():
            for item in self.items(ins, outs, scratch):
                item.finish()


class Reduce:
    def __init__(self, index, part, src, out, bufs, sems):
        self.index, self.part, self.src, self.out = index, part, src, out
        self.acc, self.mate, self.inbox = bufs
        self.load_sem, self.send_sem, self.mate_sem, self.recv_sem = sems

    def load(self, rel):
        return pltpu.make_async_copy(self.part.of(self.src, rel), self.acc.at[rel], self.load_sem.at[self.index, rel])

    def to_mate(self, rel):
        return pltpu.make_async_remote_copy(
            src_ref=self.part.of(self.src, rel | 16), dst_ref=self.mate.at[rel],
            send_sem=self.send_sem.at[self.index, 16 + rel], recv_sem=self.mate_sem.at[self.index, rel],
            device_id=place(self.part.order, 16), device_id_type=MESH_ID,
        )

    def onward(self, rel):
        return pltpu.make_async_remote_copy(
            src_ref=self.acc.at[rel], dst_ref=self.inbox.at[rel - 1], send_sem=self.send_sem.at[self.index, rel],
            recv_sem=self.recv_sem.at[self.index, rel], device_id=place(self.part.order, 1 << highest(rel)),
            device_id_type=MESH_ID,
        )

    def begin(self, rel):
        self.to_mate(rel).start()
        self.load(rel).start()

    def stage(self, rel):
        self.load(rel).wait()
        self.to_mate(rel).wait_recv()
        total = self.acc[rel].astype(F32) + self.mate[rel].astype(F32)
        for axis in range(highest(rel) + 1, 4):
            came = rel | (1 << axis)
            self.onward(came).wait_recv()
            total = total + self.inbox[came - 1].astype(F32)
        if rel == 0:
            self.out[pl.ds(self.part.start, self.part.size), :] = total
        else:
            self.acc[rel] = total.astype(BF16)
            self.onward(rel).start()

    def finish(self):
        for rel in range(16):
            self.to_mate(rel).wait_send()
            if rel:
                self.onward(rel).wait_send()


class Behind:
    def __init__(self, ident, args, parts):
        self.ident, self.args, self.parts = ident, list(args), parts
        shapes = {p.operand: p.shape for p in parts}
        self.outs = [(shapes[k], F32) for k in range(len(self.args))]
        self.out_spec = None
        self.scratch = []
        for p in parts:
            block = (p.size, p.shape[1])
            self.scratch += [pltpu.VMEM((16,) + block, BF16), pltpu.VMEM((16,) + block, BF16), pltpu.VMEM((15,) + block, BF16)]
        count = len(parts)
        self.scratch += [
            pltpu.SemaphoreType.DMA((count, 16)), pltpu.SemaphoreType.DMA((count, 32)),
            pltpu.SemaphoreType.DMA((count, 16)), pltpu.SemaphoreType.DMA((count, 16)),
        ]

    def items(self, ins, outs, scratch):
        bufs, sems = scratch[: 3 * len(self.parts)], scratch[3 * len(self.parts) :]
        return [
            Reduce(i, p, ins[p.operand], outs[p.operand], bufs[3 * i : 3 * i + 3], sems)
            for i, p in enumerate(self.parts)
        ]

    def run(self, ins, outs, scratch):
        items = self.items(ins, outs, scratch)
        for s, rels in enumerate(REDUCE_STEPS):

            @pl.when(pl.program_id(0) == s)
            def _(s=s, rels=rels):
                if s == 0:
                    meet()
                    for rel in reversed(STAGES):
                        for item in items:
                            item.begin(rel)
                for rel in rels:
                    for item in items:
                        item.stage(rel)

    def end(self, ins, outs, scratch):
        @pl.when(last_step())
        def _():
            for item in self.items(ins, outs, scratch):
                item.finish()


def reduce_kernel(plan, *refs):
    ins, refs = refs[: len(plan.args)], refs[len(plan.args) :]
    outs, scratch = refs[: len(plan.outs)], refs[len(plan.outs) :]
    items = plan.items(ins, outs, scratch)
    meet()
    for rel in reversed(STAGES):
        for item in items:
            item.begin(rel)
    for rel in reversed(STAGES):
        for item in items:
            item.stage(rel)
    for item in items:
        item.finish()


def reduce_now(name, plan):
    return pl.pallas_call(
        functools.partial(reduce_kernel, plan),
        in_specs=[pl.BlockSpec(memory_space=pl.ANY)] * len(plan.args),
        out_specs=[pl.BlockSpec(memory_space=pltpu.VMEM)] * len(plan.outs),
        out_shape=[jax.ShapeDtypeStruct(s, d) for s, d in plan.outs],
        scratch_shapes=plan.scratch,
        compiler_params=pltpu.CompilerParams(
            collective_id=plan.ident, has_side_effects=True, vmem_limit_bytes=VMEM_LIMIT
        ),
        cost_estimate=cost(0, [(a.shape, a.dtype) for a in plan.args]),
        name=name,
    )(*plan.args)


def copy_attention(src, start, dst):
    cn = dst.shape[0]
    cw = src.shape[2] // 4
    c = WIDE * cw
    for w in range(WIDE):
        dst[:, pl.ds(3 * cw * w, 3 * cw)] = src[w, pl.ds(start, cn), pl.ds(0, 3 * cw)]
        dst[:, pl.ds(3 * c + cw * w, cw)] = src[w, pl.ds(start, cn), pl.ds(3 * cw, cw)]


def unpack_first_kernel(got, watt, lay, sh, hid):
    copy_attention(got, 16, watt)
    cw = got.shape[2] // 4
    for w in range(WIDE):
        lay[0, :, pl.ds(cw * w, cw)] = got[w, pl.ds(0, 16), pl.ds(0, cw)].astype(F32)

    @pl.when(pl.program_id(0) == 0)
    def _():
        for w in range(WIDE):
            part = got[w, pl.ds(0, 16), pl.ds(LANES, cw)].astype(F32)
            sh[:, pl.ds(cw * w, cw)] = part
            for j in range(2):
                for q in range(4):
                    row = 5 + 4 * j + q
                    hid[j, :, pl.ds(4 * cw * w + cw * q, cw)] = part[row : row + 1]


def unpack_first(got):
    rows, lanes = got.shape[1:]
    c = 2 * lanes
    cn = c // NARROW
    outs = [((c, 4 * c), BF16), ((NARROW, 16, c), F32), ((16, c), F32), ((2, 1, 4 * c), F32)]
    return pl.pallas_call(
        unpack_first_kernel,
        grid=(NARROW,),
        in_specs=[pl.BlockSpec((WIDE, rows, lanes), lambda n: (n, 0, 0))],
        out_specs=[
            pl.BlockSpec((cn, 4 * c), lambda n: (n, 0)), pl.BlockSpec((1, 16, c), lambda n: (n, 0, 0)),
            pl.BlockSpec((16, c), lambda n: (0, 0)), pl.BlockSpec((2, 1, 4 * c), lambda n: (0, 0, 0)),
        ],
        out_shape=[jax.ShapeDtypeStruct(s, d) for s, d in outs],
        compiler_params=params(),
        cost_estimate=cost(0, [(got.shape, BF16)] + outs),
        name="unpack_first",
    )(got)


def unpack_attention_kernel(got, watt):
    copy_attention(got, 0, watt)


def unpack_attention(got):
    rows, lanes = got.shape[1:]
    c = 2 * lanes
    shape = (c, 4 * c)
    return pl.pallas_call(
        unpack_attention_kernel,
        grid=(NARROW,),
        in_specs=[pl.BlockSpec((WIDE, rows, lanes), lambda n: (n, 0, 0))],
        out_specs=pl.BlockSpec((c // NARROW, 4 * c), lambda n: (n, 0)),
        out_shape=jax.ShapeDtypeStruct(shape, BF16),
        compiler_params=params(),
        cost_estimate=cost(0, [(shape, BF16)] * 2),
        name="unpack_attention",
    )(got)


def gather_attention(gq, gp, start, dst):
    cn = gq.shape[0]
    cw = dst.shape[2] // 4
    for w in range(WIDE):
        dst[w, pl.ds(start, cn), pl.ds(0, 3 * cw)] = gq[:, pl.ds(3 * cw * w, 3 * cw)]
        dst[w, pl.ds(start, cn), pl.ds(3 * cw, cw)] = gp[:, pl.ds(cw * w, cw)]


def pack_attention_kernel(gq, gp, out):
    gather_attention(gq, gp, 0, out)


def pack_attention(gq, gp):
    c = gp.shape[0]
    cn, lanes = c // NARROW, c // 2
    shape = (WIDE * NARROW, cn, lanes)
    return pl.pallas_call(
        pack_attention_kernel,
        grid=(NARROW,),
        in_specs=[pl.BlockSpec((cn, 3 * c), lambda n: (n, 0)), pl.BlockSpec((cn, c), lambda n: (n, 0))],
        out_specs=pl.BlockSpec((WIDE, cn, lanes), lambda n: (n, 0, 0)),
        out_shape=jax.ShapeDtypeStruct(shape, BF16),
        compiler_params=params(),
        cost_estimate=cost(0, [(shape, BF16)] * 2),
        name="pack_attention",
    )(gq, gp)


def pack_first_kernel(gq, gp, small, sb, cb, hid0, hid1, out, shared):
    gather_attention(gq, gp, 16, out)
    c = gp.shape[1]
    cw = c // WIDE

    @pl.when(pl.program_id(0) == 0)
    def _():
        shared[...] = jnp.zeros_like(shared)
        shared[pl.ds(0, 1), :] = sb[:, pl.ds(0, c)]
        shared[pl.ds(1, 1), :] = sb[:, pl.ds(2 * c, c)]
        for k in range(3):
            shared[pl.ds(2 + k, 1), :] = cb[:, pl.ds(k * c, c)]
        for j, hid in enumerate((hid0, hid1)):
            for w in range(WIDE):
                for q in range(4):
                    shared[pl.ds(5 + 4 * j + q, 1), pl.ds(cw * w, cw)] = hid[:, pl.ds(4 * cw * w + cw * q, cw)]

    out[:, pl.ds(0, 16), :] = jnp.zeros((WIDE, 16, out.shape[2]), BF16)
    for w in range(WIDE):
        out[w, pl.ds(0, 16), pl.ds(0, cw)] = small[0, :, pl.ds(cw * w, cw)].astype(BF16)
        out[w, pl.ds(0, 16), pl.ds(LANES, cw)] = shared[:, pl.ds(cw * w, cw)].astype(BF16)


def pack_first(gq, gp, small, sb, cb, hid0, hid1):
    c = gp.shape[0]
    cn, lanes = c // NARROW, c // 2
    rows = cn + 16
    shape = (WIDE * NARROW, rows, lanes)
    return pl.pallas_call(
        pack_first_kernel,
        grid=(NARROW,),
        in_specs=[
            pl.BlockSpec((cn, 3 * c), lambda n: (n, 0)), pl.BlockSpec((cn, c), lambda n: (n, 0)),
            pl.BlockSpec((1, 16, c), lambda n: (n, 0, 0)),
        ] + [whole(a.shape) for a in (sb, cb, hid0, hid1)],
        out_specs=pl.BlockSpec((WIDE, rows, lanes), lambda n: (n, 0, 0)),
        out_shape=jax.ShapeDtypeStruct(shape, BF16),
        scratch_shapes=[pltpu.VMEM((16, c), F32)],
        compiler_params=params(),
        cost_estimate=cost(0, [(shape, BF16)] * 2),
        name="pack_first",
    )(gq, gp, small, sb, cb, hid0, hid1)


def attention_piece(qkv, proj):
    return jnp.concatenate([qkv.T, proj.T], axis=1)


def turned(value):
    return value.astype(F32).T.astype(BF16)


def gather_first_kernel(
    plan, conv_weight, conv_bias, norm_gain, norm_bias, qkv0, qkv1, proj, mlp_in, attn_bias, hidden_bias, out_bias,
    got, chan, in0, in1, piece, *sems,
):
    cw = conv_bias.shape[1]
    cn = qkv0.shape[1]
    piece[pl.ds(0, 16), :] = jnp.zeros((16, piece.shape[1]), BF16)
    taps_now = conv_weight[0].astype(F32)
    rows = [taps_now] + [r[...].astype(F32) for r in (conv_bias, norm_gain, norm_bias, out_bias)]
    rows.append(jnp.zeros((3, cw), F32))
    piece[pl.ds(0, 16), pl.ds(0, cw)] = jnp.concatenate(rows, axis=0).astype(BF16)
    hidden = hidden_bias[...].astype(F32)
    rows = [attn_bias[...].astype(F32)]
    rows += [hidden[j : j + 1, cw * q : cw * (q + 1)] for j in range(2) for q in range(4)]
    rows.append(jnp.zeros((3, cw), F32))
    piece[pl.ds(0, 16), pl.ds(LANES, cw)] = jnp.concatenate(rows, axis=0).astype(BF16)
    piece[pl.ds(16, cn), pl.ds(0, 3 * cw)] = turned(qkv0[...])
    piece[pl.ds(16, cn), pl.ds(3 * cw, cw)] = turned(proj[0])
    items = plan.items([piece], [got], sems)
    meet()
    for item in items:
        item.stage(0)
    in0[...] = turned(mlp_in[0])
    in1[...] = turned(mlp_in[1])
    chan[:, pl.ds(0, 3 * cw)] = turned(qkv1[...])
    chan[:, pl.ds(3 * cw, cw)] = turned(proj[1])
    for rel in STAGES[1:]:
        for item in items:
            item.stage(rel)
    for item in items:
        item.finish()


def gather_first(p):
    rows, cn = p["spatial_qkv"].shape
    lanes = rows * 4 // 3
    shape = (16 + cn, lanes)
    plan = Beside(1, [None], halves(0, "slot", shape))
    outs = plan.outs + [((cn, lanes), BF16)] * 3
    args = [p[k] for k in NAMES if k != "mlp_out"]
    vmem = pl.BlockSpec(memory_space=pltpu.VMEM)
    return pl.pallas_call(
        functools.partial(gather_first_kernel, plan),
        in_specs=[vmem] * len(args),
        out_specs=[plan.out_spec] + [vmem] * 3,
        out_shape=[jax.ShapeDtypeStruct(s, d) for s, d in outs],
        scratch_shapes=[pltpu.VMEM(shape, BF16)] + plan.scratch,
        compiler_params=pltpu.CompilerParams(collective_id=1, has_side_effects=True, vmem_limit_bytes=VMEM_LIMIT),
        cost_estimate=cost(0, outs),
        name="gather_first",
    )(*args)


def finish_kernel(
    att0, att1, in0, in1, out0, out1,
    conv_weight, conv_bias, norm_gain, norm_bias, qkv0, qkv1, proj, mlp_in, mlp_out, attn_bias, hidden_bias, out_bias,
):
    cw = conv_bias.shape[1]
    cn = qkv0.shape[1]
    conv_weight[0] = att0[pl.ds(0, 9), pl.ds(0, cw)]
    for k, row in enumerate((conv_bias, norm_gain, norm_bias, out_bias)):
        row[...] = att0[pl.ds(9 + k, 1), pl.ds(0, cw)]
    attn_bias[...] = att0[pl.ds(0, 5), pl.ds(LANES, cw)]
    for j in range(2):
        for q in range(4):
            hidden_bias[pl.ds(j, 1), pl.ds(cw * q, cw)] = att0[pl.ds(5 + 4 * j + q, 1), pl.ds(LANES, cw)]
    qkv0[...] = att0[pl.ds(16, cn), pl.ds(0, 3 * cw)].T
    proj[0] = att0[pl.ds(16, cn), pl.ds(3 * cw, cw)].T
    qkv1[...] = att1[:, pl.ds(0, 3 * cw)].T
    proj[1] = att1[:, pl.ds(3 * cw, cw)].T
    mlp_in[0] = in0[...].T
    mlp_in[1] = in1[...].T
    mlp_out[0] = out0[...]
    mlp_out[1] = out1[...]


def finish(*reduced):
    att0 = reduced[0]
    cn, lanes = att0.shape[0] - 16, att0.shape[1]
    cw = lanes // 4
    row = (1, cw)
    shapes = [
        (1, 9, cw), row, row, row, (3 * cw, cn), (3 * cw, cn), (2, cw, cn), (2, lanes, cn), (2, cw, 2 * lanes),
        (5, cw), (2, lanes), row,
    ]
    vmem = pl.BlockSpec(memory_space=pltpu.VMEM)
    return pl.pallas_call(
        finish_kernel,
        in_specs=[vmem] * 6,
        out_specs=[vmem] * len(shapes),
        out_shape=[jax.ShapeDtypeStruct(s, F32) for s in shapes],
        compiler_params=pltpu.CompilerParams(vmem_limit_bytes=VMEM_LIMIT),
        cost_estimate=cost(0, [(s, F32) for s in shapes]),
        name="finish",
    )(*reduced)


class Direct:
    def __init__(self, p):
        got, self.chan, self.in0, self.in1 = gather_first(p)
        self.second = p["mlp_out"]
        watt0, self.lay, self.sh, self.hid = unpack_first(got)
        self.watt, self.w_in, self.w_out = [watt0, None], [None, None], [None, None]

    def forward_window(self, *args):
        parts = pair(0, 1, self.in0.shape, self.second.shape[1:])
        carry = Beside(3, [self.in0, self.second], parts, {1: 0})
        *outs, self.w_in[0], self.w_out[0] = forward_window(*args, carry=carry)
        return outs

    def forward_mlp(self, *args):
        parts = halves(0, "slot", self.chan.shape) + halves(1, "in", self.in1.shape)
        *outs, chan, self.w_in[1] = forward_mlp(*args, carry=Beside(4, [self.chan, self.in1], parts))
        self.watt[1] = unpack_attention(chan)
        return outs

    def forward_channel(self, *args):
        parts = halves(0, "out", self.second.shape[1:])
        *outs, self.w_out[1] = forward_channel(*args, carry=Beside(5, [self.second], parts, {0: 1}))
        return outs

    def backward_channel(self, grads, *args):
        self.go1 = grads[1]
        parts = halves(0, "in", self.in1.shape)
        *outs, self.gi1 = backward_channel(*args, carry=Behind(6, grads[:1], parts))
        return outs

    def backward_mlp(self, grads, *args):
        self.att1 = pack_attention(*grads)
        parts = halves(0, "out", self.second.shape[1:])
        *outs, self.go1 = backward_mlp(*args, carry=Behind(7, [self.go1], parts))
        return outs

    def backward_window(self, grads, *args):
        parts = pair(0, 1, self.in0.shape, self.second.shape[1:]) + halves(2, "slot", self.chan.shape)
        *outs, self.gi0, self.go0, self.att1 = backward_window(*args, carry=Behind(8, list(grads) + [self.att1], parts))
        return outs

    def reduce_last(self, grads, smalls, sb, cb, hid0, hid1):
        packed = pack_first(*grads, jnp.stack(smalls), sb, cb, hid0, hid1)
        (att0,) = reduce_now("reduce_last", Behind(2, [packed], halves(0, "slot", packed.shape[1:])))
        return tuple(finish(att0, self.att1, self.gi0, self.gi1, self.go0, self.go1))


class Plain:
    def __init__(self, p):
        self.layers, self.cw = p["conv_bias"].shape
        wide = p["attn_bias"].shape
        self.narrow = 4 // self.layers
        self.cn = p["spatial_qkv"].shape[1]
        self.c = self.cn * self.narrow
        self.wide = self.c // self.cw
        self.fw = p["hidden_bias"].shape[1]
        c, cn, cw, fw, n, w = self.c, self.cn, self.cw, self.fw, self.narrow, self.wide

        def spread(v):
            return lax.all_gather(v, BOTH, axis=0, tiled=False).reshape((n, w) + v.shape)

        def attention(qkv, proj):
            got = spread(attention_piece(qkv, proj)).transpose(0, 2, 1, 3)
            return jnp.concatenate([got[..., : 3 * cw].reshape(c, 3 * c), got[..., 3 * cw :].reshape(c, c)], axis=1)

        self.watt = tuple(attention(p[k], p["projection"][i]) for i, k in enumerate(("spatial_qkv", "channel_qkv")))
        self.w_in = tuple(spread(p["mlp_in"][i].T).transpose(0, 2, 1, 3).reshape(c, -1) for i in range(2))
        self.w_out = tuple(spread(p["mlp_out"][i]).transpose(1, 2, 0, 3).reshape(c, -1) for i in range(2))

        def layer(v):
            return spread(v).transpose(0, 2, 3, 1, 4).reshape(4, -1, c)

        rows = [layer(p["conv_weight"])]
        rows += [layer(p[k][:, None]) for k in ("conv_bias", "norm_gain", "norm_bias", "out_bias")]
        self.lay = jnp.pad(jnp.concatenate(rows, axis=1).astype(F32), ((0, 0), (0, 3), (0, 0)))
        attn = spread(p["attn_bias"])[0].transpose(1, 0, 2).reshape(5, c)
        self.sh = jnp.pad(attn.astype(F32), ((0, 11), (0, 0)))
        self.hid = spread(p["hidden_bias"])[0].transpose(1, 0, 2).reshape(2, 1, -1).astype(F32)

    def forward_window(self, *args):
        return forward_window(*args)

    def forward_mlp(self, *args):
        return forward_mlp(*args)

    def forward_channel(self, *args):
        return forward_channel(*args)

    def backward_channel(self, grads, *args):
        self.mlp1 = (self.matrix(grads[0], False), self.matrix(grads[1], True))
        return backward_channel(*args)

    def backward_mlp(self, grads, *args):
        self.att1 = (self.matrix(grads[0], False), self.matrix(grads[1], False))
        return backward_mlp(*args)

    def backward_window(self, grads, *args):
        self.mlp0 = (self.matrix(grads[0], False), self.matrix(grads[1], True))
        return backward_window(*args)

    def matrix(self, grad, rows_wide):
        n, w = self.narrow, self.wide
        a, b = (w, n) if rows_wide else (n, w)
        grad = grad.reshape(a, grad.shape[0] // a, b, grad.shape[1] // b)
        grad = grad.transpose(2, 0, 1, 3) if rows_wide else grad.transpose(0, 2, 1, 3)
        grad = grad.astype(BF16).reshape(n * w * grad.shape[2], grad.shape[3])
        return lax.psum_scatter(grad, BOTH, scatter_dimension=0, tiled=True).astype(F32)

    def reduce_last(self, grads, smalls, sb, cb, hid0, hid1):
        c, cw, fw, n, w = self.c, self.cw, self.fw, self.narrow, self.wide
        first = (self.matrix(grads[0], False), self.matrix(grads[1], False)) + self.mlp0
        rest = self.att1 + self.mlp1
        small = jnp.stack(smalls).reshape(n, self.layers * 16, w, cw).transpose(0, 2, 1, 3)
        attn = jnp.concatenate([sb[:, :c], sb[:, 2 * c :], cb.reshape(3, c)]).reshape(5, w, cw).transpose(1, 0, 2)
        hid = jnp.concatenate([hid0, hid1]).reshape(2, w, fw).transpose(1, 0, 2).reshape(w, -1, cw)
        common = jnp.concatenate([attn, hid], axis=1)
        common = jnp.broadcast_to(common[None], (n,) + common.shape)
        flat = jnp.concatenate([small, common], axis=2).astype(BF16).reshape(-1, cw)
        got = lax.psum_scatter(flat, BOTH, scatter_dimension=0, tiled=True).astype(F32)
        small = got[: self.layers * 16].reshape(self.layers, 16, cw)
        shared = got[self.layers * 16 :]
        return (
            small[:, :9], small[:, 9], small[:, 10], small[:, 11], first[0].T, rest[0].T,
            jnp.stack([first[1].T, rest[1].T]), jnp.stack([first[2].T, rest[2].T]), jnp.stack([first[3], rest[3]]),
            shared[:5], shared[5:].reshape(2, fw), small[:, 12],
        )


NAMES = (
    "conv_weight", "conv_bias", "norm_gain", "norm_bias", "spatial_qkv", "channel_qkv", "projection", "mlp_in",
    "mlp_out", "attn_bias", "hidden_bias", "out_bias",
)


def local(plan, inputs, heights, widths, *rest):
    if inputs.shape[0] != len(REDUCE_STEPS):
        plan = Plain
    weights = plan(dict(zip(NAMES, rest[:-1])))
    cotangent = rest[-1]
    lay, sh, hid = weights.lay, weights.sh, weights.hid
    mask = token_mask(heights, widths)
    n1, z1, r1, q1, o1, p1, x2 = weights.forward_window(inputs, mask, lay, sh, weights.watt[0])
    n2, z2, r2, u1, d1, x4 = weights.forward_mlp(x2, mask, lay, hid, weights.w_in[0], weights.w_out[0])
    n3, z3, r3, q3, o3, a3, x6 = weights.forward_channel(x4, mask, lay, sh, weights.watt[1])
    out, g6, n4, u2, gy2, gh2, small3, hid1 = last_mlp(
        x6, cotangent, mask, lay, hid, weights.w_in[1], weights.w_out[1])
    grads = grad_pair("last_mlp_grads", n4, gh2, gy2, u2)
    g4, ga3, dq3, small2, cb = weights.backward_channel(
        grads, g6, x4, z3, r3, q3, a3, mask, lay, weights.watt[1])
    grads = grad_pair("channel_grads", n3, dq3, o3, ga3)
    g2, gy1, gh1, small1, hid0 = weights.backward_mlp(
        grads, g4, x2, z2, r2, d1, mask, lay, weights.w_in[0], weights.w_out[0])
    grads = grad_pair("mlp_grads", n2, gh1, gy1, u1)
    input_grad, ga1, dq1, small0, sb = weights.backward_window(
        grads, g2, inputs, z1, r1, q1, p1, mask, lay, weights.watt[0])
    grads = grad_pair("window_grads", n1, dq1, o1, ga1)
    last = weights.reduce_last(grads, (small0, small1, small2, small3), sb, cb, hid0, hid1)
    return (out, input_grad) + tuple(last)


def solution(mesh):
    matrix = P("wide", "narrow")
    cells = P(("wide", "narrow"), None, None, None)
    stacked = P(None, "wide", "narrow")
    row = P("narrow", "wide")
    shared = P(None, "wide")
    images = P(("wide", "narrow"))
    kernels = P("narrow", None, "wide")
    in_specs = (
        cells, images, images, kernels, row, row, row, matrix, matrix,
        stacked, stacked, stacked, shared, shared, row, cells,
    )
    out_specs = (
        cells, cells, kernels, row, row, row, matrix, matrix, stacked, stacked, stacked, shared, shared, row,
    )
    plan = Direct if (mesh.shape["wide"], mesh.shape["narrow"]) == (WIDE, NARROW) else Plain
    body = functools.partial(local, plan)
    return jax.shard_map(body, mesh=mesh, in_specs=in_specs, out_specs=out_specs, check_vma=False)
```

```python
import functools

import jax
import jax.numpy as jnp
from jax import lax
from jax.experimental import pallas as pl
from jax.experimental.pallas import tpu as pltpu
from jax.sharding import PartitionSpec as P

HD = 32
WIN = 7
LANES = 128
SUB = 8
GROUP = 256
WTOK = WIN * SUB
FFC = 1024
NROWS = 112
SCALE = HD ** (-0.5)
EPS = 1e-05
NEG = -1e30
F32 = jnp.float32
BF16 = jnp.bfloat16
VMEM_LIMIT = 60 * 1024 * 1024
DIMS_NN = (((1,), (0,)), ((), ()))
DIMS_NT = (((1,), (1,)), ((), ()))
DIMS_TN = (((0,), (0,)), ((), ()))


def dot(a, b, dims):
    return lax.dot_general(a, b, dims, preferred_element_type=F32)


def tok(r, half):
    return ((r // WIN) * 2 + half) * WTOK + (r % WIN) * SUB


def load_cells(src, dst):
    for r in range(2 * WIN):
        row = src[0, r].astype(F32)
        dst[pl.ds(tok(r, 0), WIN), :] = row[:WIN]
        dst[pl.ds(tok(r, 1), WIN), :] = row[WIN:]


def store_cells(value_at, dst, stage):
    for r in range(2 * WIN):
        stage[pl.ds(0, SUB), :] = value_at(tok(r, 0))
        stage[pl.ds(WIN, SUB), :] = value_at(tok(r, 1))
        dst[0, r] = stage[pl.ds(0, 2 * WIN), :].astype(BF16)


def neighbours(left, right):
    last = lax.broadcasted_iota(jnp.int32, (SUB, LANES), 0) == SUB - 1
    up_right = pltpu.roll(right, SUB - 1, 0)
    up_left = pltpu.roll(jnp.where(last, up_right, left), SUB - 1, 0)
    down_left = pltpu.roll(left, 1, 0)
    down_right = pltpu.roll(jnp.where(last, down_left, right), 1, 0)
    return ((down_left, left, up_left), (down_right, right, up_right))


def masked_row(src, mask, r, lanes):
    pair = []
    for half in range(2):
        rows = pl.ds(tok(r, half), SUB)
        pair.append(src[rows, lanes] * mask[0, rows, :])
    return neighbours(*pair)


def plain_row(src, r, lanes):
    return neighbours(*[src[pl.ds(tok(r, half), SUB), lanes] for half in range(2)])


def lay_row(lay, k):
    return lay[0, pl.ds(k, 1), :]


def taps(lay, lanes):
    return [jnp.broadcast_to(lay[0, pl.ds(k, 1), lanes], (SUB, LANES)) for k in range(10)]


def conv_forward(src, mask, lay, dst):
    rows = 2 * WIN

    @pl.loop(0, src.shape[1] // LANES)
    def _(j):
        lanes = pl.ds(pl.multiple_of(j * LANES, LANES), LANES)
        w = taps(lay, lanes)
        shift = w[9]
        window = [None, masked_row(src, mask, 0, lanes), masked_row(src, mask, 1, lanes)]
        for r in range(rows):
            for half in range(2):
                total = shift
                for a in range(3):
                    if window[a] is None:
                        continue
                    for b in range(3):
                        total = total + w[3 * a + b] * window[a][half][b]
                at = pl.ds(tok(r, half), SUB)
                dst[at, lanes] = src[at, lanes] + total
            following = masked_row(src, mask, r + 2, lanes) if r + 2 < rows else None
            window = [window[1], window[2], following]


def conv_backward(x_src, g_src, mask, lay, sums, dst):
    rows = 2 * WIN

    @pl.loop(0, x_src.shape[1] // LANES)
    def _(j):
        lanes = pl.ds(pl.multiple_of(j * LANES, LANES), LANES)
        w = taps(lay, lanes)
        g_win = [None, plain_row(g_src, 0, lanes), plain_row(g_src, 1, lanes)]
        x_win = [None, masked_row(x_src, mask, 0, lanes), masked_row(x_src, mask, 1, lanes)]
        grads = [sums[pl.ds(SUB * k, SUB), lanes] for k in range(10)]
        for r in range(rows):
            for half in range(2):
                center = g_win[1][half][1]
                total = None
                for a in range(3):
                    for b in range(3):
                        if x_win[a] is not None:
                            grads[3 * a + b] = grads[3 * a + b] + center * x_win[a][half][b]
                        if g_win[2 - a] is not None:
                            term = w[3 * a + b] * g_win[2 - a][half][2 - b]
                            total = term if total is None else total + term
                grads[9] = grads[9] + center
                at = pl.ds(tok(r, half), SUB)
                dst[at, lanes] = center + mask[0, at, :] * total
            more = r + 2 < rows
            g_win = [g_win[1], g_win[2], plain_row(g_src, r + 2, lanes) if more else None]
            x_win = [x_win[1], x_win[2], masked_row(x_src, mask, r + 2, lanes) if more else None]
        for k in range(10):
            sums[pl.ds(SUB * k, SUB), lanes] = grads[k]


def norm_forward(src, lay, z_out, r_out, n_out):
    features = src.shape[1]

    @pl.loop(0, src.shape[0] // (2 * NROWS))
    def _(i):
        for j in range(2):
            rows = pl.ds(pl.multiple_of(i * (2 * NROWS) + j * NROWS, NROWS), NROWS)
            x = src[rows, :]
            center = x - jnp.sum(x, axis=1, keepdims=True) * (1.0 / features)
            var = jnp.sum(center * center, axis=1, keepdims=True) * (1.0 / features)
            rstd = lax.rsqrt(var + EPS)
            z = center * rstd
            z_out[rows, :] = z
            r_out[rows, :] = jnp.broadcast_to(rstd, (NROWS, LANES))
            n_out[rows, :] = (z * lay_row(lay, 10) + lay_row(lay, 11)).astype(BF16)


def norm_backward(dn, z_src, r_src, lay, g_src, sums, first, dst):
    features = dn.shape[1]

    @pl.loop(0, dn.shape[0] // (2 * NROWS))
    def _(i):
        for j in range(2):
            rows = pl.ds(pl.multiple_of(i * (2 * NROWS) + j * NROWS, NROWS), NROWS)
            d = dn[rows, :]
            z = z_src[rows, :]
            t = d * lay_row(lay, 10)
            m1 = jnp.sum(t, axis=1, keepdims=True) * (1.0 / features)
            m2 = jnp.sum(t * z, axis=1, keepdims=True) * (1.0 / features)
            dst[rows, :] = g_src[rows, :] + (t - m1 - z * m2) * r_src[rows, 0:1]
            at = pl.ds(first, SUB)
            sums[at, :] = sums[at, :] + fold_rows(d * z)
            at = pl.ds(first + SUB, SUB)
            sums[at, :] = sums[at, :] + fold_rows(d)


def fold_rows(value):
    total = value[:SUB]
    for i in range(1, value.shape[0] // SUB):
        total = total + value[SUB * i : SUB * (i + 1)]
    return total


def finish_sums(sums, out):
    for k in range(sums.shape[0] // SUB):
        out[pl.ds(k, 1), :] = jnp.sum(sums[pl.ds(SUB * k, SUB), :], axis=0, keepdims=True)


def head_masks():
    lane = lax.broadcasted_iota(jnp.int32, (WTOK, GROUP), 1) // HD
    return [lane == h for h in range(GROUP // HD)]


def spread_heads(value, masks):
    return jnp.concatenate([jnp.where(m, value, 0.0) for m in masks], axis=0).astype(BF16)


def collect_heads(full, masks):
    total = full[:WTOK]
    for h in range(1, len(masks)):
        total = jnp.where(masks[h], full[WTOK * h : WTOK * (h + 1)], total)
    return total


def rounded(value):
    return value.astype(BF16).astype(F32)


def gelu_pair(h):
    cdf = 0.5 * (1.0 + lax.erf(h * 0.7071067811865476))
    pdf = jnp.exp(h * h * -0.5) * 0.3989422804014327
    return h * cdf, cdf + h * pdf


def first_step():
    return pl.program_id(0) == 0


def last_step():
    return pl.program_id(0) == pl.num_programs(0) - 1


def window_forward_kernel(
    inp, mask, lay, sh, watt,
    n_out, z_out, r_out, q_out, o_out, p_out, x_out,
    x0, x1, qf, of,
):
    features = x0.shape[1]

    @pl.when(first_step())
    def _():
        x0[...] = jnp.zeros_like(x0)

    load_cells(inp, x0)
    conv_forward(x0, mask, lay, x1)
    norm_forward(x1, lay, z_out.at[0], r_out.at[0], n_out.at[0])
    chunk = features
    for c in range(3):
        lanes = pl.ds(c * chunk, chunk)
        part = dot(n_out[0], watt[:, lanes], DIMS_NN)
        if c != 1:
            part = part + sh[pl.ds(c // 2, 1), :]
        part = part.astype(BF16)
        q_out[0, :, lanes] = part
        qf[:, lanes] = part.astype(F32)

    @pl.loop(0, 4)
    def _(w):
        rows = pl.ds(pl.multiple_of(w * WTOK, SUB), WTOK)
        valid = mask[0, rows, 0:1] > 0.0
        masks = head_masks()
        for g in range(features // GROUP):
            q = qf[rows, pl.ds(g * GROUP, GROUP)]
            k = qf[rows, pl.ds(features + g * GROUP, GROUP)].astype(BF16)
            v = qf[rows, pl.ds(2 * features + g * GROUP, GROUP)].astype(BF16)
            s = dot(k, spread_heads(q, masks), DIMS_NT) * SCALE
            s = jnp.where(valid, s, NEG)
            e = jnp.exp(s - jnp.max(s, axis=0, keepdims=True))
            p = (e / jnp.sum(e, axis=0, keepdims=True)).astype(BF16)
            p_out[0, w, g] = p
            of[rows, pl.ds(g * GROUP, GROUP)] = collect_heads(dot(p, v, DIMS_TN), masks)

    o_out[0] = of[...].astype(BF16)
    x_out[0] = x1[...] + (dot(o_out[0], watt[:, pl.ds(3 * features, features)], DIMS_NN) + lay_row(lay, 12))


def mlp_forward_kernel(
    x_in, mask, lay, hb, w_in, w_out,
    n_out, z_out, r_out, u_out, d_out, x_out,
    x1, acc,
):
    conv_forward(x_in.at[0], mask, lay, x1)
    norm_forward(x1, lay, z_out.at[0], r_out.at[0], n_out.at[0])
    for c in range(w_in.shape[1] // FFC):
        lanes = pl.ds(c * FFC, FFC)
        h = dot(n_out[0], w_in[:, lanes], DIMS_NN) + hb[0, :, lanes]
        u, d = gelu_pair(h)
        u = u.astype(BF16)
        u_out[0, :, lanes] = u
        d_out[0, :, lanes] = d.astype(BF16)
        y = dot(u, w_out[:, lanes], DIMS_NT)
        acc[...] = y if c == 0 else acc[...] + y
    x_out[0] = x1[...] + (acc[...] + lay_row(lay, 12))


def group_mask():
    row = lax.broadcasted_iota(jnp.int32, (GROUP, GROUP), 0) // HD
    col = lax.broadcasted_iota(jnp.int32, (GROUP, GROUP), 1) // HD
    return row == col


def channel_forward_kernel(
    x_in, mask, lay, sh, watt,
    n_out, z_out, r_out, q_out, o_out, a_out, x_out,
    x1,
):
    features = x1.shape[1]
    conv_forward(x_in.at[0], mask, lay, x1)
    norm_forward(x1, lay, z_out.at[0], r_out.at[0], n_out.at[0])
    for c in range(3):
        lanes = pl.ds(c * features, features)
        part = dot(n_out[0], watt[:, lanes], DIMS_NN) + sh[pl.ds(2 + c, 1), :]
        if c == 1:
            part = part * mask[0, :, 0:1]
        q_out[0, :, lanes] = part.astype(BF16)
    same = group_mask()
    for g in range(features // GROUP):
        q = q_out[0, :, pl.ds(g * GROUP, GROUP)]
        k = q_out[0, :, pl.ds(features + g * GROUP, GROUP)]
        v = q_out[0, :, pl.ds(2 * features + g * GROUP, GROUP)]
        s = jnp.where(same, dot(k, q, DIMS_TN) * SCALE, -jnp.inf)
        e = jnp.exp(s - jnp.max(s, axis=0, keepdims=True))
        a = (e / jnp.sum(e, axis=0, keepdims=True)).astype(BF16)
        a_out[0, g] = a
        o_out[0, :, pl.ds(g * GROUP, GROUP)] = dot(v, a, DIMS_NN).astype(BF16)
    x_out[0] = x1[...] + (dot(o_out[0], watt[:, pl.ds(3 * features, features)], DIMS_NN) + lay_row(lay, 12))


def last_mlp_kernel(
    x_in, cot, mask, lay, hb, w_in, w_out,
    out, g_out, n_out, u_out, gy_out, gh_out, small_out, hidden_out,
    x1, z, r, acc, dn, g8, stage, sums, hsums,
):
    @pl.when(first_step())
    def _():
        g8[...] = jnp.zeros_like(g8)
        sums[...] = jnp.zeros_like(sums)
        hsums[...] = jnp.zeros_like(hsums)

    x6 = x_in.at[0]
    load_cells(cot, g8)
    conv_forward(x6, mask, lay, x1)
    norm_forward(x1, lay, z, r, n_out.at[0])
    g8[...] = g8[...] * mask[0, :, 0:1]
    gy_out[0] = g8[...].astype(BF16)
    sums[pl.ds(12 * SUB, SUB), :] = sums[pl.ds(12 * SUB, SUB), :] + fold_rows(gy_out[0].astype(F32))
    for c in range(w_in.shape[1] // FFC):
        lanes = pl.ds(c * FFC, FFC)
        h = dot(n_out[0], w_in[:, lanes], DIMS_NN) + hb[0, :, lanes]
        du = dot(gy_out[0], w_out[:, lanes], DIMS_NN)
        u, d = gelu_pair(h)
        u = u.astype(BF16)
        u_out[0, :, lanes] = u
        gh = (du * d).astype(BF16)
        gh_out[0, :, lanes] = gh
        hsums[:, lanes] = hsums[:, lanes] + fold_rows(gh.astype(F32))
        y = dot(u, w_out[:, lanes], DIMS_NT)
        dx = dot(gh, w_in[:, lanes], DIMS_NT)
        acc[...] = y if c == 0 else acc[...] + y
        dn[...] = dx if c == 0 else dn[...] + dx
    acc[...] = (x1[...] + (acc[...] + lay_row(lay, 12))) * mask[0, :, 0:1]
    store_cells(lambda at: acc[pl.ds(at, SUB), :], out, stage)
    norm_backward(dn, z, r, lay, g8, sums, 10 * SUB, x1)
    conv_backward(x6, x1, mask, lay, sums, g_out.at[0])

    @pl.when(last_step())
    def _():
        finish_sums(sums, small_out)
        finish_sums(hsums, hidden_out)


def mlp_backward_kernel(
    g_in, x_in, z_in, r_in, d_in, mask, lay, w_in, w_out,
    g_out, gy_out, gh_out, small_out, hidden_out,
    dn, g1, sums, hsums,
):
    @pl.when(first_step())
    def _():
        sums[...] = jnp.zeros_like(sums)
        hsums[...] = jnp.zeros_like(hsums)

    gy_out[0] = g_in[0].astype(BF16)
    sums[pl.ds(12 * SUB, SUB), :] = sums[pl.ds(12 * SUB, SUB), :] + fold_rows(gy_out[0].astype(F32))
    for c in range(w_in.shape[1] // FFC):
        lanes = pl.ds(c * FFC, FFC)
        du = dot(gy_out[0], w_out[:, lanes], DIMS_NN)
        gh = (du * d_in[0, :, lanes].astype(F32)).astype(BF16)
        gh_out[0, :, lanes] = gh
        hsums[:, lanes] = hsums[:, lanes] + fold_rows(gh.astype(F32))
        dx = dot(gh, w_in[:, lanes], DIMS_NT)
        dn[...] = dx if c == 0 else dn[...] + dx
    norm_backward(dn, z_in.at[0], r_in.at[0], lay, g_in.at[0], sums, 10 * SUB, g1)
    conv_backward(x_in.at[0], g1, mask, lay, sums, g_out.at[0])

    @pl.when(last_step())
    def _():
        finish_sums(sums, small_out)
        finish_sums(hsums, hidden_out)


def channel_backward_kernel(
    g_in, x_in, z_in, r_in, q_in, a_in, mask, lay, watt,
    g_out, ga_out, dq_out, small_out, bias_out,
    dn, g1, sums, bsums,
):
    features = dn.shape[1]

    @pl.when(first_step())
    def _():
        sums[...] = jnp.zeros_like(sums)
        bsums[...] = jnp.zeros_like(bsums)

    ga_out[0] = g_in[0].astype(BF16)
    sums[pl.ds(12 * SUB, SUB), :] = sums[pl.ds(12 * SUB, SUB), :] + fold_rows(ga_out[0].astype(F32))
    go = dot(ga_out[0], watt[:, pl.ds(3 * features, features)], DIMS_NT).astype(BF16)
    for g in range(features // GROUP):
        at = [pl.ds(i * features + g * GROUP, GROUP) for i in range(3)]
        q, k, v = (q_in[0, :, lanes] for lanes in at)
        gog = go[:, g * GROUP : (g + 1) * GROUP]
        a = a_in[0, g]
        af = a.astype(F32)
        dp = dot(v, gog, DIMS_TN)
        ds = (af * (dp - jnp.sum(dp * af, axis=0, keepdims=True))).astype(BF16)
        dq_out[0, :, at[0]] = (dot(k, ds, DIMS_NN) * SCALE).astype(BF16)
        dq_out[0, :, at[1]] = (dot(q, ds, DIMS_NT) * SCALE * mask[0, :, 0:1]).astype(BF16)
        dq_out[0, :, at[2]] = dot(gog, a, DIMS_NT).astype(BF16)
    bsums[...] = bsums[...] + fold_rows(dq_out[0].astype(F32))
    dn[...] = dot(dq_out[0], watt[:, pl.ds(0, 3 * features)], DIMS_NT)
    norm_backward(dn, z_in.at[0], r_in.at[0], lay, g_in.at[0], sums, 10 * SUB, g1)
    conv_backward(x_in.at[0], g1, mask, lay, sums, g_out.at[0])

    @pl.when(last_step())
    def _():
        finish_sums(sums, small_out)
        finish_sums(bsums, bias_out)


def window_backward_kernel(
    g_in, inp, z_in, r_in, q_in, p_in, mask, lay, watt,
    g_out, ga_out, dq_out, small_out, bias_out,
    x0, qf, gof, dqf, dn, g1, stage, sums, bsums,
):
    features = dn.shape[1]

    @pl.when(first_step())
    def _():
        x0[...] = jnp.zeros_like(x0)
        sums[...] = jnp.zeros_like(sums)
        bsums[...] = jnp.zeros_like(bsums)

    load_cells(inp, x0)
    ga_out[0] = g_in[0].astype(BF16)
    sums[pl.ds(12 * SUB, SUB), :] = sums[pl.ds(12 * SUB, SUB), :] + fold_rows(ga_out[0].astype(F32))
    gof[...] = rounded(dot(ga_out[0], watt[:, pl.ds(3 * features, features)], DIMS_NT))
    qf[...] = q_in[0].astype(F32)

    @pl.loop(0, 4)
    def _(w):
        rows = pl.ds(pl.multiple_of(w * WTOK, SUB), WTOK)
        masks = head_masks()
        for g in range(features // GROUP):
            at = [pl.ds(i * features + g * GROUP, GROUP) for i in range(3)]
            qe = spread_heads(qf[rows, at[0]], masks)
            k = qf[rows, at[1]].astype(BF16)
            v = qf[rows, at[2]].astype(BF16)
            goe = spread_heads(gof[rows, at[0]], masks)
            p = p_in[0, w, g]
            pf = p.astype(F32)
            dp = dot(v, goe, DIMS_NT)
            ds = (pf * (dp - jnp.sum(dp * pf, axis=0, keepdims=True))).astype(BF16)
            dqf[rows, at[0]] = collect_heads(dot(ds, k, DIMS_TN), masks) * SCALE
            dqf[rows, at[1]] = dot(ds, qe, DIMS_NN) * SCALE
            dqf[rows, at[2]] = dot(p, goe, DIMS_NN)

    dq_out[0] = dqf[...].astype(BF16)
    bsums[...] = bsums[...] + fold_rows(dq_out[0].astype(F32))
    dn[...] = dot(dq_out[0], watt[:, pl.ds(0, 3 * features)], DIMS_NT)
    norm_backward(dn, z_in.at[0], r_in.at[0], lay, g_in.at[0], sums, 10 * SUB, g1)
    conv_backward(x0, g1, mask, lay, sums, dn)
    store_cells(lambda at: dn[pl.ds(at, SUB), :], g_out, stage)

    @pl.when(last_step())
    def _():
        finish_sums(sums, small_out)
        finish_sums(bsums, bias_out)


def per_image(shape):
    rest = (0,) * (len(shape) - 1)
    return pl.BlockSpec((1,) + tuple(shape[1:]), lambda i: (i,) + rest)


def whole(shape):
    zeros = (0,) * len(shape)
    return pl.BlockSpec(tuple(shape), lambda i: zeros, pipeline_mode=pl.Buffered(1))


def one_layer(shape, layer):
    return pl.BlockSpec((1,) + tuple(shape[1:]), lambda i: (layer, 0, 0), pipeline_mode=pl.Buffered(1))


def cost(flops, arrays):
    size = sum(jnp.dtype(d).itemsize * functools.reduce(lambda p, q: p * q, s) for s, d in arrays)
    return pl.CostEstimate(flops=int(flops), bytes_accessed=int(size), transcendentals=0)


def params():
    return pltpu.CompilerParams(dimension_semantics=("arbitrary",), vmem_limit_bytes=VMEM_LIMIT)


def carrier(kernel, carry, ins, outs, scratch, refs):
    extra_in, extra_out = len(carry.args), len(carry.outs)
    base_in, refs = refs[:ins], refs[ins:]
    carry_in, refs = refs[:extra_in], refs[extra_in:]
    base_out, refs = refs[:outs], refs[outs:]
    carry_out, refs = refs[:extra_out], refs[extra_out:]
    base_scratch, carry_scratch = refs[:scratch], refs[scratch:]
    carry.run(carry_in, carry_out, carry_scratch)
    kernel(*base_in, *base_out, *base_scratch)
    carry.end(carry_in, carry_out, carry_scratch)


def image_call(kernel, name, layer, batched, lay, shared, outs, sums, scratch, flops, carry=None):
    images = batched[0].shape[0]
    ins = [per_image(a.shape) for a in batched] + [one_layer(lay.shape, layer)]
    args = list(batched) + [lay]
    for item in shared:
        if isinstance(item, tuple):
            ins.append(one_layer(item[0].shape, item[1]))
            args.append(item[0])
        else:
            ins.append(whole(item.shape))
            args.append(item)
    out_specs = [per_image(s) for s, _ in outs]
    out_specs += [pl.BlockSpec(tuple(s), lambda i: (0, 0)) for s, _ in sums]
    results = outs + sums
    buffers = [pltpu.VMEM(s, d) for s, d in scratch]
    options = params()
    body = kernel
    if carry is not None:
        counts = (len(args), len(results), len(scratch))

        def body(*refs):
            carrier(kernel, carry, *counts, refs)

        args = args + carry.args
        ins = ins + [pl.BlockSpec(memory_space=pl.ANY)] * len(carry.args)
        out_specs += [carry.out_spec or pl.BlockSpec(tuple(s), lambda i: (0, 0)) for s, _ in carry.outs]
        results = results + carry.outs
        buffers += carry.scratch
        options = pltpu.CompilerParams(
            dimension_semantics=("arbitrary",), vmem_limit_bytes=VMEM_LIMIT, collective_id=carry.ident,
            has_side_effects=True,
        )
    arrays = [(a.shape, a.dtype) for a in args] + results
    return pl.pallas_call(
        body,
        grid=(images,),
        in_specs=ins,
        out_specs=out_specs,
        out_shape=[jax.ShapeDtypeStruct(s, d) for s, d in results],
        scratch_shapes=buffers,
        compiler_params=options,
        cost_estimate=cost(flops, arrays),
        name=name,
    )(*args)


def token_mask(heights, widths):
    t = jnp.arange(4 * WTOK, dtype=jnp.int32)
    window = t // WTOK
    row = (window // 2) * WIN + (t % WTOK) // SUB
    col8 = t % SUB
    col = (window % 2) * WIN + col8
    valid = (row[None] < heights[:, None]) & (col[None] < widths[:, None]) & (col8 < WIN)[None]
    return jnp.broadcast_to(valid.astype(F32)[..., None], valid.shape + (LANES,))


def forward_window(inputs, mask, lay, sh, watt, carry=None):
    images, _, _, c = inputs.shape
    t = 4 * WTOK
    outs = [
        ((images, t, c), BF16), ((images, t, c), F32), ((images, t, LANES), F32),
        ((images, t, 3 * c), BF16), ((images, t, c), BF16),
        ((images, 4, c // GROUP, WTOK, WTOK * GROUP // HD), BF16), ((images, t, c), F32),
    ]
    scratch = [((t, c), F32), ((t, c), F32), ((t, 3 * c), F32), ((t, c), F32)]
    return image_call(window_forward_kernel, "window_forward", 0, [inputs, mask], lay, [sh, watt],
                      outs, [], scratch, 10 * images * t * c * c, carry)


def forward_mlp(x, mask, lay, hid, w_in, w_out, carry=None):
    images, t, c = x.shape
    ff = w_in.shape[1]
    outs = [
        ((images, t, c), BF16), ((images, t, c), F32), ((images, t, LANES), F32),
        ((images, t, ff), BF16), ((images, t, ff), BF16), ((images, t, c), F32),
    ]
    scratch = [((t, c), F32), ((t, c), F32)]
    return image_call(mlp_forward_kernel, "mlp_forward", 1, [x, mask], lay, [(hid, 0), w_in, w_out],
                      outs, [], scratch, 4 * images * t * c * ff, carry)


def forward_channel(x, mask, lay, sh, watt, carry=None):
    images, t, c = x.shape
    outs = [
        ((images, t, c), BF16), ((images, t, c), F32), ((images, t, LANES), F32),
        ((images, t, 3 * c), BF16), ((images, t, c), BF16),
        ((images, c // GROUP, GROUP, GROUP), BF16), ((images, t, c), F32),
    ]
    return image_call(channel_forward_kernel, "channel_forward", 2, [x, mask], lay, [sh, watt],
                      outs, [], [((t, c), F32)], 9 * images * t * c * c, carry)


def last_mlp(x, cot, mask, lay, hid, w_in, w_out):
    images, t, c = x.shape
    ff = w_in.shape[1]
    outs = [
        (cot.shape, BF16), ((images, t, c), F32), ((images, t, c), BF16), ((images, t, ff), BF16),
        ((images, t, c), BF16), ((images, t, ff), BF16),
    ]
    scratch = [
        ((t, c), F32), ((t, c), F32), ((t, LANES), F32), ((t, c), F32), ((t, c), F32), ((t, c), F32),
        ((16, c), F32), ((16 * SUB, c), F32), ((SUB, ff), F32),
    ]
    return image_call(last_mlp_kernel, "last_mlp", 3, [x, cot, mask], lay, [(hid, 1), w_in, w_out],
                      outs, [((16, c), F32), ((1, ff), F32)], scratch, 8 * images * t * c * ff)


def backward_mlp(g, x, z, r, d, mask, lay, w_in, w_out, carry=None):
    images, t, c = x.shape
    ff = w_in.shape[1]
    outs = [((images, t, c), F32), ((images, t, c), BF16), ((images, t, ff), BF16)]
    scratch = [((t, c), F32), ((t, c), F32), ((16 * SUB, c), F32), ((SUB, ff), F32)]
    return image_call(mlp_backward_kernel, "mlp_backward", 1, [g, x, z, r, d, mask], lay, [w_in, w_out],
                      outs, [((16, c), F32), ((1, ff), F32)], scratch, 4 * images * t * c * ff, carry)


def backward_channel(g, x, z, r, q, a, mask, lay, watt, carry=None):
    images, t, c = x.shape
    outs = [((images, t, c), F32), ((images, t, c), BF16), ((images, t, 3 * c), BF16)]
    scratch = [((t, c), F32), ((t, c), F32), ((16 * SUB, c), F32), ((SUB, 3 * c), F32)]
    return image_call(channel_backward_kernel, "channel_backward", 2, [g, x, z, r, q, a, mask], lay, [watt],
                      outs, [((16, c), F32), ((1, 3 * c), F32)], scratch, 10 * images * t * c * c, carry)


def backward_window(g, inputs, z, r, q, p, mask, lay, watt, carry=None):
    images, t, c = g.shape
    outs = [(inputs.shape, BF16), ((images, t, c), BF16), ((images, t, 3 * c), BF16)]
    scratch = [
        ((t, c), F32), ((t, 3 * c), F32), ((t, c), F32), ((t, 3 * c), F32), ((t, c), F32), ((t, c), F32),
        ((16, c), F32), ((16 * SUB, c), F32), ((SUB, 3 * c), F32),
    ]
    return image_call(window_backward_kernel, "window_backward", 0, [g, inputs, z, r, q, p, mask], lay, [watt],
                      outs, [((16, c), F32), ((1, 3 * c), F32)], scratch, 12 * images * t * c * c, carry)


def grad_pair_kernel(first, left0, right0, left1, right1, out0, out1):
    step = pl.program_id(0)

    @pl.when(step < first)
    def _():
        out0[...] = dot(left0[...], right0[...], DIMS_TN).astype(BF16)

    @pl.when(step >= first)
    def _():
        out1[...] = dot(left1[...], right1[...], DIMS_TN).astype(BF16)


def grad_pair(name, left0, right0, left1, right1):
    flat = [a.reshape(-1, a.shape[-1]) for a in (left0, right0, left1, right1)]
    rows, c = flat[0].shape
    first, second = flat[1].shape[1] // c, flat[3].shape[1] // c

    def at_first(i):
        return (0, jnp.minimum(i, first - 1))

    def at_second(i):
        return (0, jnp.maximum(i - first, 0))

    outs = [((c, flat[1].shape[1]), BF16), ((c, flat[3].shape[1]), BF16)]
    return pl.pallas_call(
        functools.partial(grad_pair_kernel, first),
        grid=(first + second,),
        in_specs=[
            whole((rows, c)), pl.BlockSpec((rows, c), at_first),
            whole((rows, c)), pl.BlockSpec((rows, c), at_second),
        ],
        out_specs=[pl.BlockSpec((c, c), at_first), pl.BlockSpec((c, c), at_second)],
        out_shape=[jax.ShapeDtypeStruct(s, d) for s, d in outs],
        compiler_params=params(),
        cost_estimate=cost(2 * rows * c * c * (first + second), [(a.shape, BF16) for a in flat] + outs),
        name=name,
    )(*flat)


WIDE = 8
NARROW = 4
BOTH = ("narrow", "wide")
MESH_ID = pl.DeviceIdType.MESH
RING = (0, 1, -1, 2, -2, 3, -3, 4)
AFAR = RING[::-1]
GATHER_STEPS = (((0,), ()), ((1, -1), (0,)), ((2, -2), (1, -1)), ((3, -3), (2, -2)), ((4,), (3, -3)), ((), (4,)))
REDUCE_STEPS = ((), (15, 11), (7, 14, 10), (3, 6, 13), (2, 9), (5, 12), (1, 8, 4), (0,))
STAGES = (0, 4, 8, 12, 1, 5, 9, 13, 2, 6, 10, 14, 3, 7, 11, 15)
CARRY_STEPS = 8


def whole_part(condition):
    return jnp.where(condition, jnp.int32(1), jnp.int32(0))


def place(order, ring, cross=0, core=0):
    n, w = lax.axis_index("narrow"), lax.axis_index("wide")
    z = whole_part(w >= 2) + whole_part(w >= 4) + whole_part(w >= 6)
    y = whole_part(n >= 2)
    x, c = w - 2 * z, n - 2 * y
    a, b = (x, y) if order == 0 else (y, x)
    if ring:
        at = z + a * (7 - 2 * z) + ring
        at = at - 8 * whole_part(at >= 8) if ring > 0 else at + 8 * whole_part(at < 0)
        a = whole_part(at >= 4)
        z = at + a * (7 - 2 * at)
    if cross:
        b = 1 - b
    if core:
        c = 1 - c
    x, y = (a, b) if order == 0 else (b, a)
    return {"narrow": 2 * y + c, "wide": 2 * z + x}


def chip(order, rel):
    n, w = lax.axis_index("narrow"), lax.axis_index("wide")
    z1 = whole_part(w >= 4)
    z0 = whole_part(w - 4 * z1 >= 2)
    y = whole_part(n >= 2)
    x, c = w - 4 * z1 - 2 * z0, n - 2 * y
    first, second = (4, 8) if order == 0 else (8, 4)
    bits = (1, 2, first, second, 16)
    z0, z1, x, y, c = (1 - v if rel & bit else v for v, bit in zip((z0, z1, x, y, c), bits))
    return {"narrow": 2 * y + c, "wide": 4 * z1 + 2 * z0 + x}


def highest(rel):
    return rel.bit_length() - 1


def number(ring, cross=0, core=0):
    return ring % 8 + 8 * cross + 16 * core


def ring_peers():
    return [place(0, 1), place(0, -1), place(1, 1), place(1, -1), place(0, 0, 1), place(1, 0, 1), place(0, 0, 0, 1)]


def chip_peers():
    return [chip(0, 1 << k) for k in range(5)]


def meet(peers):
    barrier = pltpu.get_barrier_semaphore()
    for at in peers:
        pl.semaphore_signal(barrier, inc=1, device_id=at, device_id_type=MESH_ID)
    pl.semaphore_wait(barrier, len(peers))


class Part:
    def __init__(self, operand, kind, shape, start, size, order):
        self.operand, self.kind, self.shape, self.start, self.size, self.order = operand, kind, shape, start, size, order

    def whole(self):
        rows, cols = self.shape
        return {
            "slot": (WIDE * NARROW, rows, cols), "in": (NARROW * rows, WIDE * cols), "out": (WIDE * rows, NARROW * cols),
        }[self.kind]

    def view(self, ref, n, w):
        rows, cols = self.shape
        if self.kind == "slot":
            return ref.at[n * WIDE + w, pl.ds(self.start, self.size), :]
        a, b = (n, w) if self.kind == "in" else (w, n)
        step = 16
        while step < 128 and rows % (2 * step) == 0 and self.start % (2 * step) == 0:
            step *= 2
        at = pl.multiple_of(a * rows + self.start, step)
        return ref.at[pl.ds(at, self.size), pl.ds(pl.multiple_of(b * cols, cols), cols)]

    def of(self, ref, *where):
        at = place(self.order, *where)
        return self.view(ref, at["narrow"], at["wide"])


    def of_chip(self, ref, rel):
        at = chip(self.order, rel)
        return self.view(ref, at["narrow"], at["wide"])


def halves(operand, kind, shape):
    low = shape[0] // 32 * 16
    return [Part(operand, kind, shape, 0, low, 0), Part(operand, kind, shape, low, shape[0] - low, 1)]


def pair(first, second, shape_in, shape_out):
    return [Part(first, "in", shape_in, 0, shape_in[0], 0), Part(second, "out", shape_out, 0, shape_out[0], 1)]


class Gather:
    def __init__(self, index, part, own, dest, sems):
        self.index, self.part, self.dest = index, part, dest
        self.own = own.at[pl.ds(part.start, part.size), :]
        self.send, self.recv, self.keep = sems

    def copy(self, ring, cross, step):
        target = self.part.of(self.dest, ring, cross)
        if step is None:
            to, slot = place(self.part.order, 0, 0, 1), number(ring, cross, 1)
        elif step == 0:
            to, slot = place(self.part.order, 0, 1), number(ring, 1)
        else:
            to, slot = place(self.part.order, step), number(ring - step)
        return pltpu.make_async_remote_copy(
            src_ref=self.own if ring == 0 and cross == 0 else target, dst_ref=target,
            send_sem=self.send.at[self.index, slot], recv_sem=self.recv.at[self.index, slot],
            device_id=to, device_id_type=MESH_ID,
        )

    def arrival(self, ring, cross=0, core=0):
        target = self.part.of(self.dest, ring, cross, core)
        return pltpu.make_async_remote_copy(
            src_ref=target, dst_ref=target, send_sem=self.send.at[self.index, 0],
            recv_sem=self.recv.at[self.index, number(ring, cross, core)], device_id=place(self.part.order, 1),
            device_id_type=MESH_ID,
        )

    def stay(self):
        return pltpu.make_async_copy(self.own, self.part.of(self.dest, 0), self.keep.at[self.index])

    def sends(self, ring):
        steps = []
        if 0 <= ring < 4:
            steps.append(-1)
        if -3 < ring <= 0:
            steps.append(1)
        return steps + [0, None]

    def stage(self, ring):
        if ring == 0:
            self.stay().start()
        else:
            self.arrival(ring).wait_recv()
        for step in self.sends(ring):
            self.copy(ring, 0, step).start()

    def crossed(self, ring):
        self.arrival(ring, 1).wait_recv()
        self.copy(ring, 1, None).start()

    def finish(self):
        for ring in RING:
            self.arrival(ring, 0, 1).wait_recv()
            self.arrival(ring, 1, 1).wait_recv()
        for ring in RING:
            for step in self.sends(ring):
                self.copy(ring, 0, step).wait_send()
            self.copy(ring, 1, None).wait_send()
        self.stay().wait()


def gather_step(items, rings, crosses):
    for ring in rings:
        for item in items:
            item.stage(ring)
    for ring in crosses:
        for item in items:
            item.crossed(ring)


def gather_sems(count):
    return [pltpu.SemaphoreType.DMA((count, 32)), pltpu.SemaphoreType.DMA((count, 32)), pltpu.SemaphoreType.DMA((count,))]


class Beside:
    def __init__(self, ident, args, parts, pick=None):
        self.ident, self.args, self.parts = ident, list(args), parts
        self.pick = pick or {}
        shapes = {p.operand: p.whole() for p in parts}
        self.outs = [(shapes[k], BF16) for k in range(len(self.args))]
        self.out_spec = pl.BlockSpec(memory_space=pl.ANY)
        self.scratch = gather_sems(len(parts))

    def items(self, ins, outs, scratch):
        ins = [ref.at[self.pick[k]] if k in self.pick else ref for k, ref in enumerate(ins)]
        return [Gather(i, p, ins[p.operand], outs[p.operand], scratch) for i, p in enumerate(self.parts)]

    def run(self, ins, outs, scratch):
        items = self.items(ins, outs, scratch)
        for s, (rings, crosses) in enumerate(GATHER_STEPS):

            @pl.when(pl.program_id(0) == s)
            def _(s=s, rings=rings, crosses=crosses):
                if s == 0:
                    meet(ring_peers())
                gather_step(items, rings, crosses)

    def end(self, ins, outs, scratch):
        @pl.when(last_step())
        def _():
            for item in self.items(ins, outs, scratch):
                item.finish()


class Reduce:
    def __init__(self, index, part, src, out, bufs, sems):
        self.index, self.part, self.src, self.out = index, part, src, out
        self.acc, self.mate, self.inbox = bufs
        self.load_sem, self.send_sem, self.mate_sem, self.recv_sem = sems

    def load(self, rel):
        return pltpu.make_async_copy(self.part.of_chip(self.src, rel), self.acc.at[rel], self.load_sem.at[self.index, rel])

    def to_mate(self, rel):
        return pltpu.make_async_remote_copy(
            src_ref=self.part.of_chip(self.src, rel | 16), dst_ref=self.mate.at[rel],
            send_sem=self.send_sem.at[self.index, 16 + rel], recv_sem=self.mate_sem.at[self.index, rel],
            device_id=chip(self.part.order, 16), device_id_type=MESH_ID,
        )

    def onward(self, rel):
        return pltpu.make_async_remote_copy(
            src_ref=self.acc.at[rel], dst_ref=self.inbox.at[rel - 1], send_sem=self.send_sem.at[self.index, rel],
            recv_sem=self.recv_sem.at[self.index, rel], device_id=chip(self.part.order, 1 << highest(rel)),
            device_id_type=MESH_ID,
        )

    def begin(self, rel):
        self.to_mate(rel).start()
        self.load(rel).start()

    def stage(self, rel):
        self.load(rel).wait()
        self.to_mate(rel).wait_recv()
        total = self.acc[rel].astype(F32) + self.mate[rel].astype(F32)
        for axis in range(highest(rel) + 1, 4):
            came = rel | (1 << axis)
            self.onward(came).wait_recv()
            total = total + self.inbox[came - 1].astype(F32)
        if rel == 0:
            self.out[pl.ds(self.part.start, self.part.size), :] = total
        else:
            self.acc[rel] = total.astype(BF16)
            self.onward(rel).start()

    def finish(self):
        for rel in range(16):
            self.to_mate(rel).wait_send()
            if rel:
                self.onward(rel).wait_send()


class Behind:
    def __init__(self, ident, args, parts):
        self.ident, self.args, self.parts = ident, list(args), parts
        shapes = {p.operand: p.shape for p in parts}
        self.outs = [(shapes[k], F32) for k in range(len(self.args))]
        self.out_spec = None
        self.scratch = []
        for p in parts:
            block = (p.size, p.shape[1])
            self.scratch += [pltpu.VMEM((16,) + block, BF16), pltpu.VMEM((16,) + block, BF16), pltpu.VMEM((15,) + block, BF16)]
        count = len(parts)
        self.scratch += [
            pltpu.SemaphoreType.DMA((count, 16)), pltpu.SemaphoreType.DMA((count, 32)),
            pltpu.SemaphoreType.DMA((count, 16)), pltpu.SemaphoreType.DMA((count, 16)),
        ]

    def items(self, ins, outs, scratch):
        bufs, sems = scratch[: 3 * len(self.parts)], scratch[3 * len(self.parts) :]
        return [
            Reduce(i, p, ins[p.operand], outs[p.operand], bufs[3 * i : 3 * i + 3], sems)
            for i, p in enumerate(self.parts)
        ]

    def run(self, ins, outs, scratch):
        items = self.items(ins, outs, scratch)
        for s, rels in enumerate(REDUCE_STEPS):

            @pl.when(pl.program_id(0) == s)
            def _(s=s, rels=rels):
                if s == 0:
                    meet(chip_peers())
                    for rel in reversed(STAGES):
                        for item in items:
                            item.begin(rel)
                for rel in rels:
                    for item in items:
                        item.stage(rel)

    def end(self, ins, outs, scratch):
        @pl.when(last_step())
        def _():
            for item in self.items(ins, outs, scratch):
                item.finish()


def reduce_kernel(plan, *refs):
    ins, refs = refs[: len(plan.args)], refs[len(plan.args) :]
    outs, scratch = refs[: len(plan.outs)], refs[len(plan.outs) :]
    items = plan.items(ins, outs, scratch)
    meet(chip_peers())
    for rel in reversed(STAGES):
        for item in items:
            item.begin(rel)
    for rel in reversed(STAGES):
        for item in items:
            item.stage(rel)
    for item in items:
        item.finish()


def reduce_now(name, plan):
    return pl.pallas_call(
        functools.partial(reduce_kernel, plan),
        in_specs=[pl.BlockSpec(memory_space=pl.ANY)] * len(plan.args),
        out_specs=[pl.BlockSpec(memory_space=pltpu.VMEM)] * len(plan.outs),
        out_shape=[jax.ShapeDtypeStruct(s, d) for s, d in plan.outs],
        scratch_shapes=plan.scratch,
        compiler_params=pltpu.CompilerParams(
            collective_id=plan.ident, has_side_effects=True, vmem_limit_bytes=VMEM_LIMIT
        ),
        cost_estimate=cost(0, [(a.shape, a.dtype) for a in plan.args]),
        name=name,
    )(*plan.args)


def copy_attention(src, start, dst):
    cn = dst.shape[0]
    cw = src.shape[2] // 4
    c = WIDE * cw
    for w in range(WIDE):
        dst[:, pl.ds(3 * cw * w, 3 * cw)] = src[w, pl.ds(start, cn), pl.ds(0, 3 * cw)]
        dst[:, pl.ds(3 * c + cw * w, cw)] = src[w, pl.ds(start, cn), pl.ds(3 * cw, cw)]


def unpack_first_kernel(got, watt, lay, sh, hid):
    copy_attention(got, 16, watt)
    cw = got.shape[2] // 4
    for w in range(WIDE):
        lay[0, :, pl.ds(cw * w, cw)] = got[w, pl.ds(0, 16), pl.ds(0, cw)].astype(F32)

    @pl.when(pl.program_id(0) == 0)
    def _():
        for w in range(WIDE):
            part = got[w, pl.ds(0, 16), pl.ds(LANES, cw)].astype(F32)
            sh[:, pl.ds(cw * w, cw)] = part
            for j in range(2):
                for q in range(4):
                    row = 5 + 4 * j + q
                    hid[j, :, pl.ds(4 * cw * w + cw * q, cw)] = part[row : row + 1]


def unpack_first(got):
    rows, lanes = got.shape[1:]
    c = 2 * lanes
    cn = c // NARROW
    outs = [((c, 4 * c), BF16), ((NARROW, 16, c), F32), ((16, c), F32), ((2, 1, 4 * c), F32)]
    return pl.pallas_call(
        unpack_first_kernel,
        grid=(NARROW,),
        in_specs=[pl.BlockSpec((WIDE, rows, lanes), lambda n: (n, 0, 0))],
        out_specs=[
            pl.BlockSpec((cn, 4 * c), lambda n: (n, 0)), pl.BlockSpec((1, 16, c), lambda n: (n, 0, 0)),
            pl.BlockSpec((16, c), lambda n: (0, 0)), pl.BlockSpec((2, 1, 4 * c), lambda n: (0, 0, 0)),
        ],
        out_shape=[jax.ShapeDtypeStruct(s, d) for s, d in outs],
        compiler_params=params(),
        cost_estimate=cost(0, [(got.shape, BF16)] + outs),
        name="unpack_first",
    )(got)


def unpack_attention_kernel(got, watt):
    copy_attention(got, 0, watt)


def unpack_attention(got):
    rows, lanes = got.shape[1:]
    c = 2 * lanes
    shape = (c, 4 * c)
    return pl.pallas_call(
        unpack_attention_kernel,
        grid=(NARROW,),
        in_specs=[pl.BlockSpec((WIDE, rows, lanes), lambda n: (n, 0, 0))],
        out_specs=pl.BlockSpec((c // NARROW, 4 * c), lambda n: (n, 0)),
        out_shape=jax.ShapeDtypeStruct(shape, BF16),
        compiler_params=params(),
        cost_estimate=cost(0, [(shape, BF16)] * 2),
        name="unpack_attention",
    )(got)


def gather_attention(gq, gp, start, dst):
    cn = gq.shape[0]
    cw = dst.shape[2] // 4
    for w in range(WIDE):
        dst[w, pl.ds(start, cn), pl.ds(0, 3 * cw)] = gq[:, pl.ds(3 * cw * w, 3 * cw)]
        dst[w, pl.ds(start, cn), pl.ds(3 * cw, cw)] = gp[:, pl.ds(cw * w, cw)]


def pack_attention_kernel(gq, gp, out):
    gather_attention(gq, gp, 0, out)


def pack_attention(gq, gp):
    c = gp.shape[0]
    cn, lanes = c // NARROW, c // 2
    shape = (WIDE * NARROW, cn, lanes)
    return pl.pallas_call(
        pack_attention_kernel,
        grid=(NARROW,),
        in_specs=[pl.BlockSpec((cn, 3 * c), lambda n: (n, 0)), pl.BlockSpec((cn, c), lambda n: (n, 0))],
        out_specs=pl.BlockSpec((WIDE, cn, lanes), lambda n: (n, 0, 0)),
        out_shape=jax.ShapeDtypeStruct(shape, BF16),
        compiler_params=params(),
        cost_estimate=cost(0, [(shape, BF16)] * 2),
        name="pack_attention",
    )(gq, gp)


def pack_first_kernel(gq, gp, small, sb, cb, hid0, hid1, out, shared):
    gather_attention(gq, gp, 16, out)
    c = gp.shape[1]
    cw = c // WIDE

    @pl.when(pl.program_id(0) == 0)
    def _():
        shared[...] = jnp.zeros_like(shared)
        shared[pl.ds(0, 1), :] = sb[:, pl.ds(0, c)]
        shared[pl.ds(1, 1), :] = sb[:, pl.ds(2 * c, c)]
        for k in range(3):
            shared[pl.ds(2 + k, 1), :] = cb[:, pl.ds(k * c, c)]
        for j, hid in enumerate((hid0, hid1)):
            for w in range(WIDE):
                for q in range(4):
                    shared[pl.ds(5 + 4 * j + q, 1), pl.ds(cw * w, cw)] = hid[:, pl.ds(4 * cw * w + cw * q, cw)]

    out[:, pl.ds(0, 16), :] = jnp.zeros((WIDE, 16, out.shape[2]), BF16)
    for w in range(WIDE):
        out[w, pl.ds(0, 16), pl.ds(0, cw)] = small[0, :, pl.ds(cw * w, cw)].astype(BF16)
        out[w, pl.ds(0, 16), pl.ds(LANES, cw)] = shared[:, pl.ds(cw * w, cw)].astype(BF16)


def pack_first(gq, gp, small, sb, cb, hid0, hid1):
    c = gp.shape[0]
    cn, lanes = c // NARROW, c // 2
    rows = cn + 16
    shape = (WIDE * NARROW, rows, lanes)
    return pl.pallas_call(
        pack_first_kernel,
        grid=(NARROW,),
        in_specs=[
            pl.BlockSpec((cn, 3 * c), lambda n: (n, 0)), pl.BlockSpec((cn, c), lambda n: (n, 0)),
            pl.BlockSpec((1, 16, c), lambda n: (n, 0, 0)),
        ] + [whole(a.shape) for a in (sb, cb, hid0, hid1)],
        out_specs=pl.BlockSpec((WIDE, rows, lanes), lambda n: (n, 0, 0)),
        out_shape=jax.ShapeDtypeStruct(shape, BF16),
        scratch_shapes=[pltpu.VMEM((16, c), F32)],
        compiler_params=params(),
        cost_estimate=cost(0, [(shape, BF16)] * 2),
        name="pack_first",
    )(gq, gp, small, sb, cb, hid0, hid1)


def attention_piece(qkv, proj):
    return jnp.concatenate([qkv.T, proj.T], axis=1)


def turned(value):
    return value.astype(F32).T.astype(BF16)


def gather_first_kernel(
    plan, conv_weight, conv_bias, norm_gain, norm_bias, qkv0, qkv1, proj, mlp_in, attn_bias, hidden_bias, out_bias,
    got, chan, in0, in1, piece, *sems,
):
    cw = conv_bias.shape[1]
    cn = qkv0.shape[1]
    piece[pl.ds(0, 16), :] = jnp.zeros((16, piece.shape[1]), BF16)
    taps_now = conv_weight[0].astype(F32)
    rows = [taps_now] + [r[...].astype(F32) for r in (conv_bias, norm_gain, norm_bias, out_bias)]
    rows.append(jnp.zeros((3, cw), F32))
    piece[pl.ds(0, 16), pl.ds(0, cw)] = jnp.concatenate(rows, axis=0).astype(BF16)
    hidden = hidden_bias[...].astype(F32)
    rows = [attn_bias[...].astype(F32)]
    rows += [hidden[j : j + 1, cw * q : cw * (q + 1)] for j in range(2) for q in range(4)]
    rows.append(jnp.zeros((3, cw), F32))
    piece[pl.ds(0, 16), pl.ds(LANES, cw)] = jnp.concatenate(rows, axis=0).astype(BF16)
    piece[pl.ds(16, cn), pl.ds(0, 3 * cw)] = turned(qkv0[...])
    piece[pl.ds(16, cn), pl.ds(3 * cw, cw)] = turned(proj[0])
    items = plan.items([piece], [got], sems)
    meet(ring_peers())
    gather_step(items, (0,), ())
    in0[...] = turned(mlp_in[0])
    in1[...] = turned(mlp_in[1])
    chan[:, pl.ds(0, 3 * cw)] = turned(qkv1[...])
    chan[:, pl.ds(3 * cw, cw)] = turned(proj[1])
    for rings, crosses in GATHER_STEPS[1:]:
        gather_step(items, rings, crosses)
    for item in items:
        item.finish()


def gather_first(p):
    rows, cn = p["spatial_qkv"].shape
    lanes = rows * 4 // 3
    shape = (16 + cn, lanes)
    plan = Beside(1, [None], halves(0, "slot", shape))
    outs = plan.outs + [((cn, lanes), BF16)] * 3
    args = [p[k] for k in NAMES if k != "mlp_out"]
    vmem = pl.BlockSpec(memory_space=pltpu.VMEM)
    return pl.pallas_call(
        functools.partial(gather_first_kernel, plan),
        in_specs=[vmem] * len(args),
        out_specs=[plan.out_spec] + [vmem] * 3,
        out_shape=[jax.ShapeDtypeStruct(s, d) for s, d in outs],
        scratch_shapes=[pltpu.VMEM(shape, BF16)] + plan.scratch,
        compiler_params=pltpu.CompilerParams(collective_id=1, has_side_effects=True, vmem_limit_bytes=VMEM_LIMIT),
        cost_estimate=cost(0, outs),
        name="gather_first",
    )(*args)


def finish_kernel(
    att0, att1, in0, in1, out0, out1,
    conv_weight, conv_bias, norm_gain, norm_bias, qkv0, qkv1, proj, mlp_in, mlp_out, attn_bias, hidden_bias, out_bias,
):
    cw = conv_bias.shape[1]
    cn = qkv0.shape[1]
    conv_weight[0] = att0[pl.ds(0, 9), pl.ds(0, cw)]
    for k, row in enumerate((conv_bias, norm_gain, norm_bias, out_bias)):
        row[...] = att0[pl.ds(9 + k, 1), pl.ds(0, cw)]
    attn_bias[...] = att0[pl.ds(0, 5), pl.ds(LANES, cw)]
    for j in range(2):
        for q in range(4):
            hidden_bias[pl.ds(j, 1), pl.ds(cw * q, cw)] = att0[pl.ds(5 + 4 * j + q, 1), pl.ds(LANES, cw)]
    qkv0[...] = att0[pl.ds(16, cn), pl.ds(0, 3 * cw)].T
    proj[0] = att0[pl.ds(16, cn), pl.ds(3 * cw, cw)].T
    qkv1[...] = att1[:, pl.ds(0, 3 * cw)].T
    proj[1] = att1[:, pl.ds(3 * cw, cw)].T
    mlp_in[0] = in0[...].T
    mlp_in[1] = in1[...].T
    mlp_out[0] = out0[...]
    mlp_out[1] = out1[...]


def finish(*reduced):
    att0 = reduced[0]
    cn, lanes = att0.shape[0] - 16, att0.shape[1]
    cw = lanes // 4
    row = (1, cw)
    shapes = [
        (1, 9, cw), row, row, row, (3 * cw, cn), (3 * cw, cn), (2, cw, cn), (2, lanes, cn), (2, cw, 2 * lanes),
        (5, cw), (2, lanes), row,
    ]
    vmem = pl.BlockSpec(memory_space=pltpu.VMEM)
    return pl.pallas_call(
        finish_kernel,
        in_specs=[vmem] * 6,
        out_specs=[vmem] * len(shapes),
        out_shape=[jax.ShapeDtypeStruct(s, F32) for s in shapes],
        compiler_params=pltpu.CompilerParams(vmem_limit_bytes=VMEM_LIMIT),
        cost_estimate=cost(0, [(s, F32) for s in shapes]),
        name="finish",
    )(*reduced)


class Direct:
    def __init__(self, p):
        got, self.chan, self.in0, self.in1 = gather_first(p)
        self.second = p["mlp_out"]
        watt0, self.lay, self.sh, self.hid = unpack_first(got)
        self.watt, self.w_in, self.w_out = [watt0, None], [None, None], [None, None]

    def forward_window(self, *args):
        parts = pair(0, 1, self.in0.shape, self.second.shape[1:])
        carry = Beside(3, [self.in0, self.second], parts, {1: 0})
        *outs, self.w_in[0], self.w_out[0] = forward_window(*args, carry=carry)
        return outs

    def forward_mlp(self, *args):
        parts = halves(0, "slot", self.chan.shape) + halves(1, "in", self.in1.shape)
        *outs, chan, self.w_in[1] = forward_mlp(*args, carry=Beside(4, [self.chan, self.in1], parts))
        self.watt[1] = unpack_attention(chan)
        return outs

    def forward_channel(self, *args):
        parts = halves(0, "out", self.second.shape[1:])
        *outs, self.w_out[1] = forward_channel(*args, carry=Beside(5, [self.second], parts, {0: 1}))
        return outs

    def backward_channel(self, grads, *args):
        self.go1 = grads[1]
        parts = halves(0, "in", self.in1.shape)
        *outs, self.gi1 = backward_channel(*args, carry=Behind(6, grads[:1], parts))
        return outs

    def backward_mlp(self, grads, *args):
        self.att1 = pack_attention(*grads)
        parts = halves(0, "out", self.second.shape[1:])
        *outs, self.go1 = backward_mlp(*args, carry=Behind(7, [self.go1], parts))
        return outs

    def backward_window(self, grads, *args):
        parts = pair(0, 1, self.in0.shape, self.second.shape[1:]) + halves(2, "slot", self.chan.shape)
        *outs, self.gi0, self.go0, self.att1 = backward_window(*args, carry=Behind(8, list(grads) + [self.att1], parts))
        return outs

    def reduce_last(self, grads, smalls, sb, cb, hid0, hid1):
        packed = pack_first(*grads, jnp.stack(smalls), sb, cb, hid0, hid1)
        (att0,) = reduce_now("reduce_last", Behind(2, [packed], halves(0, "slot", packed.shape[1:])))
        return tuple(finish(att0, self.att1, self.gi0, self.gi1, self.go0, self.go1))


class Plain:
    def __init__(self, p):
        self.layers, self.cw = p["conv_bias"].shape
        wide = p["attn_bias"].shape
        self.narrow = 4 // self.layers
        self.cn = p["spatial_qkv"].shape[1]
        self.c = self.cn * self.narrow
        self.wide = self.c // self.cw
        self.fw = p["hidden_bias"].shape[1]
        c, cn, cw, fw, n, w = self.c, self.cn, self.cw, self.fw, self.narrow, self.wide

        def spread(v):
            return lax.all_gather(v, BOTH, axis=0, tiled=False).reshape((n, w) + v.shape)

        def attention(qkv, proj):
            got = spread(attention_piece(qkv, proj)).transpose(0, 2, 1, 3)
            return jnp.concatenate([got[..., : 3 * cw].reshape(c, 3 * c), got[..., 3 * cw :].reshape(c, c)], axis=1)

        self.watt = tuple(attention(p[k], p["projection"][i]) for i, k in enumerate(("spatial_qkv", "channel_qkv")))
        self.w_in = tuple(spread(p["mlp_in"][i].T).transpose(0, 2, 1, 3).reshape(c, -1) for i in range(2))
        self.w_out = tuple(spread(p["mlp_out"][i]).transpose(1, 2, 0, 3).reshape(c, -1) for i in range(2))

        def layer(v):
            return spread(v).transpose(0, 2, 3, 1, 4).reshape(4, -1, c)

        rows = [layer(p["conv_weight"])]
        rows += [layer(p[k][:, None]) for k in ("conv_bias", "norm_gain", "norm_bias", "out_bias")]
        self.lay = jnp.pad(jnp.concatenate(rows, axis=1).astype(F32), ((0, 0), (0, 3), (0, 0)))
        attn = spread(p["attn_bias"])[0].transpose(1, 0, 2).reshape(5, c)
        self.sh = jnp.pad(attn.astype(F32), ((0, 11), (0, 0)))
        self.hid = spread(p["hidden_bias"])[0].transpose(1, 0, 2).reshape(2, 1, -1).astype(F32)

    def forward_window(self, *args):
        return forward_window(*args)

    def forward_mlp(self, *args):
        return forward_mlp(*args)

    def forward_channel(self, *args):
        return forward_channel(*args)

    def backward_channel(self, grads, *args):
        self.mlp1 = (self.matrix(grads[0], False), self.matrix(grads[1], True))
        return backward_channel(*args)

    def backward_mlp(self, grads, *args):
        self.att1 = (self.matrix(grads[0], False), self.matrix(grads[1], False))
        return backward_mlp(*args)

    def backward_window(self, grads, *args):
        self.mlp0 = (self.matrix(grads[0], False), self.matrix(grads[1], True))
        return backward_window(*args)

    def matrix(self, grad, rows_wide):
        n, w = self.narrow, self.wide
        a, b = (w, n) if rows_wide else (n, w)
        grad = grad.reshape(a, grad.shape[0] // a, b, grad.shape[1] // b)
        grad = grad.transpose(2, 0, 1, 3) if rows_wide else grad.transpose(0, 2, 1, 3)
        grad = grad.astype(BF16).reshape(n * w * grad.shape[2], grad.shape[3])
        return lax.psum_scatter(grad, BOTH, scatter_dimension=0, tiled=True).astype(F32)

    def reduce_last(self, grads, smalls, sb, cb, hid0, hid1):
        c, cw, fw, n, w = self.c, self.cw, self.fw, self.narrow, self.wide
        first = (self.matrix(grads[0], False), self.matrix(grads[1], False)) + self.mlp0
        rest = self.att1 + self.mlp1
        small = jnp.stack(smalls).reshape(n, self.layers * 16, w, cw).transpose(0, 2, 1, 3)
        attn = jnp.concatenate([sb[:, :c], sb[:, 2 * c :], cb.reshape(3, c)]).reshape(5, w, cw).transpose(1, 0, 2)
        hid = jnp.concatenate([hid0, hid1]).reshape(2, w, fw).transpose(1, 0, 2).reshape(w, -1, cw)
        common = jnp.concatenate([attn, hid], axis=1)
        common = jnp.broadcast_to(common[None], (n,) + common.shape)
        flat = jnp.concatenate([small, common], axis=2).astype(BF16).reshape(-1, cw)
        got = lax.psum_scatter(flat, BOTH, scatter_dimension=0, tiled=True).astype(F32)
        small = got[: self.layers * 16].reshape(self.layers, 16, cw)
        shared = got[self.layers * 16 :]
        return (
            small[:, :9], small[:, 9], small[:, 10], small[:, 11], first[0].T, rest[0].T,
            jnp.stack([first[1].T, rest[1].T]), jnp.stack([first[2].T, rest[2].T]), jnp.stack([first[3], rest[3]]),
            shared[:5], shared[5:].reshape(2, fw), small[:, 12],
        )


NAMES = (
    "conv_weight", "conv_bias", "norm_gain", "norm_bias", "spatial_qkv", "channel_qkv", "projection", "mlp_in",
    "mlp_out", "attn_bias", "hidden_bias", "out_bias",
)


def local(plan, inputs, heights, widths, *rest):
    if inputs.shape[0] != CARRY_STEPS:
        plan = Plain
    weights = plan(dict(zip(NAMES, rest[:-1])))
    cotangent = rest[-1]
    lay, sh, hid = weights.lay, weights.sh, weights.hid
    mask = token_mask(heights, widths)
    n1, z1, r1, q1, o1, p1, x2 = weights.forward_window(inputs, mask, lay, sh, weights.watt[0])
    n2, z2, r2, u1, d1, x4 = weights.forward_mlp(x2, mask, lay, hid, weights.w_in[0], weights.w_out[0])
    n3, z3, r3, q3, o3, a3, x6 = weights.forward_channel(x4, mask, lay, sh, weights.watt[1])
    out, g6, n4, u2, gy2, gh2, small3, hid1 = last_mlp(
        x6, cotangent, mask, lay, hid, weights.w_in[1], weights.w_out[1])
    grads = grad_pair("last_mlp_grads", n4, gh2, gy2, u2)
    g4, ga3, dq3, small2, cb = weights.backward_channel(
        grads, g6, x4, z3, r3, q3, a3, mask, lay, weights.watt[1])
    grads = grad_pair("channel_grads", n3, dq3, o3, ga3)
    g2, gy1, gh1, small1, hid0 = weights.backward_mlp(
        grads, g4, x2, z2, r2, d1, mask, lay, weights.w_in[0], weights.w_out[0])
    grads = grad_pair("mlp_grads", n2, gh1, gy1, u1)
    input_grad, ga1, dq1, small0, sb = weights.backward_window(
        grads, g2, inputs, z1, r1, q1, p1, mask, lay, weights.watt[0])
    grads = grad_pair("window_grads", n1, dq1, o1, ga1)
    last = weights.reduce_last(grads, (small0, small1, small2, small3), sb, cb, hid0, hid1)
    return (out, input_grad) + tuple(last)


def solution(mesh):
    matrix = P("wide", "narrow")
    cells = P(("wide", "narrow"), None, None, None)
    stacked = P(None, "wide", "narrow")
    row = P("narrow", "wide")
    shared = P(None, "wide")
    images = P(("wide", "narrow"))
    kernels = P("narrow", None, "wide")
    in_specs = (
        cells, images, images, kernels, row, row, row, matrix, matrix,
        stacked, stacked, stacked, shared, shared, row, cells,
    )
    out_specs = (
        cells, cells, kernels, row, row, row, matrix, matrix, stacked, stacked, stacked, shared, shared, row,
    )
    plan = Direct if (mesh.shape["wide"], mesh.shape["narrow"]) == (WIDE, NARROW) else Plain
    body = functools.partial(local, plan)
    return jax.shard_map(body, mesh=mesh, in_specs=in_specs, out_specs=out_specs, check_vma=False)
```

```python
import functools

import jax
import jax.numpy as jnp
from jax import lax
from jax.experimental import pallas as pl
from jax.experimental.pallas import tpu as pltpu
from jax.sharding import PartitionSpec as P

HD = 32
WIN = 7
LANES = 128
SUB = 8
GROUP = 256
WTOK = WIN * SUB
FFC = 1024
NROWS = 112
SCALE = HD ** (-0.5)
EPS = 1e-05
NEG = -1e30
F32 = jnp.float32
BF16 = jnp.bfloat16
VMEM_LIMIT = 60 * 1024 * 1024
DIMS_NN = (((1,), (0,)), ((), ()))
DIMS_NT = (((1,), (1,)), ((), ()))
DIMS_TN = (((0,), (0,)), ((), ()))


def dot(a, b, dims):
    return lax.dot_general(a, b, dims, preferred_element_type=F32)


def tok(r, half):
    return ((r // WIN) * 2 + half) * WTOK + (r % WIN) * SUB


def fill_cells(src, cells):
    for j in range(cells.shape[0]):
        cells[j] = src[:, pl.ds(j * LANES, LANES)].astype(F32)


def drain_cells(cells, dst):
    for j in range(cells.shape[0]):
        dst[:, pl.ds(j * LANES, LANES)] = cells[j].astype(BF16)


def cell_rows(cells, r, half):
    images = cells.shape[1] // (4 * WIN * WIN)
    start = (r * 2 * WIN + WIN * half) * images
    if images == 1:
        return pl.ds(start, WIN)
    return pl.ds(start + pl.program_id(0), WIN, stride=images)


def load_cells(cells, dst):
    for r in range(2 * WIN):
        for half in range(2):
            for j in range(cells.shape[0]):
                dst[pl.ds(tok(r, half), WIN), pl.ds(j * LANES, LANES)] = cells.at[j][cell_rows(cells, r, half), :]


def store_cells(src, cells):
    for r in range(2 * WIN):
        for half in range(2):
            for j in range(cells.shape[0]):
                cells.at[j][cell_rows(cells, r, half), :] = src[pl.ds(tok(r, half), WIN), pl.ds(j * LANES, LANES)]


def cells_first(images):
    return images.transpose(1, 2, 0, 3).reshape(-1, images.shape[3])


def images_first(cells):
    return cells.reshape(2 * WIN, 2 * WIN, -1, cells.shape[1]).transpose(2, 0, 1, 3)


def neighbours(left, right):
    last = lax.broadcasted_iota(jnp.int32, (SUB, LANES), 0) == SUB - 1
    up_right = pltpu.roll(right, SUB - 1, 0)
    up_left = pltpu.roll(jnp.where(last, up_right, left), SUB - 1, 0)
    down_left = pltpu.roll(left, 1, 0)
    down_right = pltpu.roll(jnp.where(last, down_left, right), 1, 0)
    return ((down_left, left, up_left), (down_right, right, up_right))


def masked_row(src, mask, r, lanes):
    pair = []
    for half in range(2):
        rows = pl.ds(tok(r, half), SUB)
        pair.append(src[rows, lanes] * mask[0, rows, :])
    return neighbours(*pair)


def plain_row(src, r, lanes):
    return neighbours(*[src[pl.ds(tok(r, half), SUB), lanes] for half in range(2)])


def lay_row(lay, k):
    return lay[0, pl.ds(k, 1), :]


def taps(lay, lanes):
    return [jnp.broadcast_to(lay[0, pl.ds(k, 1), lanes], (SUB, LANES)) for k in range(10)]


def conv_forward(src, mask, lay, dst):
    rows = 2 * WIN

    @pl.loop(0, src.shape[1] // LANES)
    def _(j):
        lanes = pl.ds(pl.multiple_of(j * LANES, LANES), LANES)
        w = taps(lay, lanes)
        shift = w[9]
        window = [None, masked_row(src, mask, 0, lanes), masked_row(src, mask, 1, lanes)]
        for r in range(rows):
            for half in range(2):
                total = shift
                for a in range(3):
                    if window[a] is None:
                        continue
                    for b in range(3):
                        total = total + w[3 * a + b] * window[a][half][b]
                at = pl.ds(tok(r, half), SUB)
                dst[at, lanes] = src[at, lanes] + total
            following = masked_row(src, mask, r + 2, lanes) if r + 2 < rows else None
            window = [window[1], window[2], following]


def conv_backward(x_src, g_src, mask, lay, sums, dst):
    rows = 2 * WIN

    @pl.loop(0, x_src.shape[1] // LANES)
    def _(j):
        lanes = pl.ds(pl.multiple_of(j * LANES, LANES), LANES)
        w = taps(lay, lanes)
        g_win = [None, plain_row(g_src, 0, lanes), plain_row(g_src, 1, lanes)]
        x_win = [None, masked_row(x_src, mask, 0, lanes), masked_row(x_src, mask, 1, lanes)]
        grads = [sums[pl.ds(SUB * k, SUB), lanes] for k in range(10)]
        for r in range(rows):
            for half in range(2):
                center = g_win[1][half][1]
                total = None
                for a in range(3):
                    for b in range(3):
                        if x_win[a] is not None:
                            grads[3 * a + b] = grads[3 * a + b] + center * x_win[a][half][b]
                        if g_win[2 - a] is not None:
                            term = w[3 * a + b] * g_win[2 - a][half][2 - b]
                            total = term if total is None else total + term
                grads[9] = grads[9] + center
                at = pl.ds(tok(r, half), SUB)
                dst[at, lanes] = center + mask[0, at, :] * total
            more = r + 2 < rows
            g_win = [g_win[1], g_win[2], plain_row(g_src, r + 2, lanes) if more else None]
            x_win = [x_win[1], x_win[2], masked_row(x_src, mask, r + 2, lanes) if more else None]
        for k in range(10):
            sums[pl.ds(SUB * k, SUB), lanes] = grads[k]


def norm_forward(src, lay, z_out, r_out, n_out):
    features = src.shape[1]

    @pl.loop(0, src.shape[0] // (2 * NROWS))
    def _(i):
        for j in range(2):
            rows = pl.ds(pl.multiple_of(i * (2 * NROWS) + j * NROWS, NROWS), NROWS)
            x = src[rows, :]
            center = x - jnp.sum(x, axis=1, keepdims=True) * (1.0 / features)
            var = jnp.sum(center * center, axis=1, keepdims=True) * (1.0 / features)
            rstd = lax.rsqrt(var + EPS)
            z = center * rstd
            z_out[rows, :] = z
            r_out[rows, :] = jnp.broadcast_to(rstd, (NROWS, LANES))
            n_out[rows, :] = (z * lay_row(lay, 10) + lay_row(lay, 11)).astype(BF16)


def norm_backward(dn, z_src, r_src, lay, g_src, sums, first, dst):
    features = dn.shape[1]

    @pl.loop(0, dn.shape[0] // (2 * NROWS))
    def _(i):
        for j in range(2):
            rows = pl.ds(pl.multiple_of(i * (2 * NROWS) + j * NROWS, NROWS), NROWS)
            d = dn[rows, :]
            z = z_src[rows, :]
            t = d * lay_row(lay, 10)
            m1 = jnp.sum(t, axis=1, keepdims=True) * (1.0 / features)
            m2 = jnp.sum(t * z, axis=1, keepdims=True) * (1.0 / features)
            dst[rows, :] = g_src[rows, :] + (t - m1 - z * m2) * r_src[rows, 0:1]
            at = pl.ds(first, SUB)
            sums[at, :] = sums[at, :] + fold_rows(d * z)
            at = pl.ds(first + SUB, SUB)
            sums[at, :] = sums[at, :] + fold_rows(d)


def fold_rows(value):
    total = value[:SUB]
    for i in range(1, value.shape[0] // SUB):
        total = total + value[SUB * i : SUB * (i + 1)]
    return total


def finish_sums(sums, out):
    for k in range(sums.shape[0] // SUB):
        out[pl.ds(k, 1), :] = jnp.sum(sums[pl.ds(SUB * k, SUB), :], axis=0, keepdims=True)


def head_masks():
    lane = lax.broadcasted_iota(jnp.int32, (WTOK, GROUP), 1) // HD
    return [lane == h for h in range(GROUP // HD)]


def spread_heads(value, masks):
    return jnp.concatenate([jnp.where(m, value, 0.0) for m in masks], axis=0).astype(BF16)


def collect_heads(full, masks):
    total = full[:WTOK]
    for h in range(1, len(masks)):
        total = jnp.where(masks[h], full[WTOK * h : WTOK * (h + 1)], total)
    return total


def rounded(value):
    return value.astype(BF16).astype(F32)


def gelu_pair(h):
    cdf = 0.5 * (1.0 + lax.erf(h * 0.7071067811865476))
    pdf = jnp.exp(h * h * -0.5) * 0.3989422804014327
    return h * cdf, cdf + h * pdf


def first_step():
    return pl.program_id(0) == 0


def last_step():
    return pl.program_id(0) == pl.num_programs(0) - 1


def window_forward_kernel(
    inp, mask, lay, sh, watt,
    n_out, z_out, r_out, q_out, o_out, p_out, x_out,
    cells, x0, x1, qf, of,
):
    features = x0.shape[1]

    @pl.when(first_step())
    def _():
        x0[...] = jnp.zeros_like(x0)
        fill_cells(inp, cells)

    load_cells(cells, x0)
    conv_forward(x0, mask, lay, x1)
    norm_forward(x1, lay, z_out.at[0], r_out.at[0], n_out.at[0])
    chunk = features
    for c in range(3):
        lanes = pl.ds(c * chunk, chunk)
        part = dot(n_out[0], watt[:, lanes], DIMS_NN)
        if c != 1:
            part = part + sh[pl.ds(c // 2, 1), :]
        part = part.astype(BF16)
        q_out[0, :, lanes] = part
        qf[:, lanes] = part.astype(F32)

    @pl.loop(0, 4)
    def _(w):
        rows = pl.ds(pl.multiple_of(w * WTOK, SUB), WTOK)
        valid = mask[0, rows, 0:1] > 0.0
        masks = head_masks()
        for g in range(features // GROUP):
            q = qf[rows, pl.ds(g * GROUP, GROUP)]
            k = qf[rows, pl.ds(features + g * GROUP, GROUP)].astype(BF16)
            v = qf[rows, pl.ds(2 * features + g * GROUP, GROUP)].astype(BF16)
            s = dot(k, spread_heads(q, masks), DIMS_NT) * SCALE
            s = jnp.where(valid, s, NEG)
            e = jnp.exp(s - jnp.max(s, axis=0, keepdims=True))
            p = (e / jnp.sum(e, axis=0, keepdims=True)).astype(BF16)
            p_out[0, w, g] = p
            of[rows, pl.ds(g * GROUP, GROUP)] = collect_heads(dot(p, v, DIMS_TN), masks)

    o_out[0] = of[...].astype(BF16)
    x_out[0] = x1[...] + (dot(o_out[0], watt[:, pl.ds(3 * features, features)], DIMS_NN) + lay_row(lay, 12))


def mlp_forward_kernel(
    x_in, mask, lay, hb, w_in, w_out,
    n_out, z_out, r_out, u_out, d_out, x_out,
    x1, acc,
):
    conv_forward(x_in.at[0], mask, lay, x1)
    norm_forward(x1, lay, z_out.at[0], r_out.at[0], n_out.at[0])
    for c in range(w_in.shape[1] // FFC):
        lanes = pl.ds(c * FFC, FFC)
        h = dot(n_out[0], w_in[:, lanes], DIMS_NN) + hb[0, :, lanes]
        u, d = gelu_pair(h)
        u = u.astype(BF16)
        u_out[0, :, lanes] = u
        d_out[0, :, lanes] = d.astype(BF16)
        y = dot(u, w_out[:, lanes], DIMS_NT)
        acc[...] = y if c == 0 else acc[...] + y
    x_out[0] = x1[...] + (acc[...] + lay_row(lay, 12))


def group_mask():
    row = lax.broadcasted_iota(jnp.int32, (GROUP, GROUP), 0) // HD
    col = lax.broadcasted_iota(jnp.int32, (GROUP, GROUP), 1) // HD
    return row == col


def channel_forward_kernel(
    x_in, mask, lay, sh, watt,
    n_out, z_out, r_out, q_out, o_out, a_out, x_out,
    x1,
):
    features = x1.shape[1]
    conv_forward(x_in.at[0], mask, lay, x1)
    norm_forward(x1, lay, z_out.at[0], r_out.at[0], n_out.at[0])
    for c in range(3):
        lanes = pl.ds(c * features, features)
        part = dot(n_out[0], watt[:, lanes], DIMS_NN) + sh[pl.ds(2 + c, 1), :]
        if c == 1:
            part = part * mask[0, :, 0:1]
        q_out[0, :, lanes] = part.astype(BF16)
    same = group_mask()
    for g in range(features // GROUP):
        q = q_out[0, :, pl.ds(g * GROUP, GROUP)]
        k = q_out[0, :, pl.ds(features + g * GROUP, GROUP)]
        v = q_out[0, :, pl.ds(2 * features + g * GROUP, GROUP)]
        s = jnp.where(same, dot(k, q, DIMS_TN) * SCALE, -jnp.inf)
        e = jnp.exp(s - jnp.max(s, axis=0, keepdims=True))
        a = (e / jnp.sum(e, axis=0, keepdims=True)).astype(BF16)
        a_out[0, g] = a
        o_out[0, :, pl.ds(g * GROUP, GROUP)] = dot(v, a, DIMS_NN).astype(BF16)
    x_out[0] = x1[...] + (dot(o_out[0], watt[:, pl.ds(3 * features, features)], DIMS_NN) + lay_row(lay, 12))


def last_mlp_kernel(
    x_in, cot, mask, lay, hb, w_in, w_out,
    out, g_out, n_out, u_out, gy_out, gh_out, small_out, hidden_out,
    cells, x1, z, r, acc, dn, g8, sums, hsums,
):
    @pl.when(first_step())
    def _():
        g8[...] = jnp.zeros_like(g8)
        sums[...] = jnp.zeros_like(sums)
        hsums[...] = jnp.zeros_like(hsums)
        fill_cells(cot, cells)

    x6 = x_in.at[0]
    load_cells(cells, g8)
    conv_forward(x6, mask, lay, x1)
    norm_forward(x1, lay, z, r, n_out.at[0])
    g8[...] = g8[...] * mask[0, :, 0:1]
    gy_out[0] = g8[...].astype(BF16)
    sums[pl.ds(12 * SUB, SUB), :] = sums[pl.ds(12 * SUB, SUB), :] + fold_rows(gy_out[0].astype(F32))
    for c in range(w_in.shape[1] // FFC):
        lanes = pl.ds(c * FFC, FFC)
        h = dot(n_out[0], w_in[:, lanes], DIMS_NN) + hb[0, :, lanes]
        du = dot(gy_out[0], w_out[:, lanes], DIMS_NN)
        u, d = gelu_pair(h)
        u = u.astype(BF16)
        u_out[0, :, lanes] = u
        gh = (du * d).astype(BF16)
        gh_out[0, :, lanes] = gh
        hsums[:, lanes] = hsums[:, lanes] + fold_rows(gh.astype(F32))
        y = dot(u, w_out[:, lanes], DIMS_NT)
        dx = dot(gh, w_in[:, lanes], DIMS_NT)
        acc[...] = y if c == 0 else acc[...] + y
        dn[...] = dx if c == 0 else dn[...] + dx
    acc[...] = (x1[...] + (acc[...] + lay_row(lay, 12))) * mask[0, :, 0:1]
    store_cells(acc, cells)
    norm_backward(dn, z, r, lay, g8, sums, 10 * SUB, x1)
    conv_backward(x6, x1, mask, lay, sums, g_out.at[0])

    @pl.when(last_step())
    def _():
        drain_cells(cells, out)
        finish_sums(sums, small_out)
        finish_sums(hsums, hidden_out)


def mlp_backward_kernel(
    g_in, x_in, z_in, r_in, d_in, mask, lay, w_in, w_out,
    g_out, gy_out, gh_out, small_out, hidden_out,
    dn, g1, sums, hsums,
):
    @pl.when(first_step())
    def _():
        sums[...] = jnp.zeros_like(sums)
        hsums[...] = jnp.zeros_like(hsums)

    gy_out[0] = g_in[0].astype(BF16)
    sums[pl.ds(12 * SUB, SUB), :] = sums[pl.ds(12 * SUB, SUB), :] + fold_rows(gy_out[0].astype(F32))
    for c in range(w_in.shape[1] // FFC):
        lanes = pl.ds(c * FFC, FFC)
        du = dot(gy_out[0], w_out[:, lanes], DIMS_NN)
        gh = (du * d_in[0, :, lanes].astype(F32)).astype(BF16)
        gh_out[0, :, lanes] = gh
        hsums[:, lanes] = hsums[:, lanes] + fold_rows(gh.astype(F32))
        dx = dot(gh, w_in[:, lanes], DIMS_NT)
        dn[...] = dx if c == 0 else dn[...] + dx
    norm_backward(dn, z_in.at[0], r_in.at[0], lay, g_in.at[0], sums, 10 * SUB, g1)
    conv_backward(x_in.at[0], g1, mask, lay, sums, g_out.at[0])

    @pl.when(last_step())
    def _():
        finish_sums(sums, small_out)
        finish_sums(hsums, hidden_out)


def channel_backward_kernel(
    g_in, x_in, z_in, r_in, q_in, a_in, mask, lay, watt,
    g_out, ga_out, dq_out, small_out, bias_out,
    dn, g1, sums, bsums,
):
    features = dn.shape[1]

    @pl.when(first_step())
    def _():
        sums[...] = jnp.zeros_like(sums)
        bsums[...] = jnp.zeros_like(bsums)

    ga_out[0] = g_in[0].astype(BF16)
    sums[pl.ds(12 * SUB, SUB), :] = sums[pl.ds(12 * SUB, SUB), :] + fold_rows(ga_out[0].astype(F32))
    go = dot(ga_out[0], watt[:, pl.ds(3 * features, features)], DIMS_NT).astype(BF16)
    for g in range(features // GROUP):
        at = [pl.ds(i * features + g * GROUP, GROUP) for i in range(3)]
        q, k, v = (q_in[0, :, lanes] for lanes in at)
        gog = go[:, g * GROUP : (g + 1) * GROUP]
        a = a_in[0, g]
        af = a.astype(F32)
        dp = dot(v, gog, DIMS_TN)
        ds = (af * (dp - jnp.sum(dp * af, axis=0, keepdims=True))).astype(BF16)
        dq_out[0, :, at[0]] = (dot(k, ds, DIMS_NN) * SCALE).astype(BF16)
        dq_out[0, :, at[1]] = (dot(q, ds, DIMS_NT) * SCALE * mask[0, :, 0:1]).astype(BF16)
        dq_out[0, :, at[2]] = dot(gog, a, DIMS_NT).astype(BF16)
    bsums[...] = bsums[...] + fold_rows(dq_out[0].astype(F32))
    dn[...] = dot(dq_out[0], watt[:, pl.ds(0, 3 * features)], DIMS_NT)
    norm_backward(dn, z_in.at[0], r_in.at[0], lay, g_in.at[0], sums, 10 * SUB, g1)
    conv_backward(x_in.at[0], g1, mask, lay, sums, g_out.at[0])

    @pl.when(last_step())
    def _():
        finish_sums(sums, small_out)
        finish_sums(bsums, bias_out)


def window_backward_kernel(
    g_in, inp, z_in, r_in, q_in, p_in, mask, lay, watt,
    g_out, ga_out, dq_out, small_out, bias_out,
    cells, x0, qf, gof, dqf, dn, g1, sums, bsums,
):
    features = dn.shape[1]

    @pl.when(first_step())
    def _():
        x0[...] = jnp.zeros_like(x0)
        sums[...] = jnp.zeros_like(sums)
        bsums[...] = jnp.zeros_like(bsums)
        fill_cells(inp, cells)

    load_cells(cells, x0)
    ga_out[0] = g_in[0].astype(BF16)
    sums[pl.ds(12 * SUB, SUB), :] = sums[pl.ds(12 * SUB, SUB), :] + fold_rows(ga_out[0].astype(F32))
    gof[...] = rounded(dot(ga_out[0], watt[:, pl.ds(3 * features, features)], DIMS_NT))
    qf[...] = q_in[0].astype(F32)

    @pl.loop(0, 4)
    def _(w):
        rows = pl.ds(pl.multiple_of(w * WTOK, SUB), WTOK)
        masks = head_masks()
        for g in range(features // GROUP):
            at = [pl.ds(i * features + g * GROUP, GROUP) for i in range(3)]
            qe = spread_heads(qf[rows, at[0]], masks)
            k = qf[rows, at[1]].astype(BF16)
            v = qf[rows, at[2]].astype(BF16)
            goe = spread_heads(gof[rows, at[0]], masks)
            p = p_in[0, w, g]
            pf = p.astype(F32)
            dp = dot(v, goe, DIMS_NT)
            ds = (pf * (dp - jnp.sum(dp * pf, axis=0, keepdims=True))).astype(BF16)
            dqf[rows, at[0]] = collect_heads(dot(ds, k, DIMS_TN), masks) * SCALE
            dqf[rows, at[1]] = dot(ds, qe, DIMS_NN) * SCALE
            dqf[rows, at[2]] = dot(p, goe, DIMS_NN)

    dq_out[0] = dqf[...].astype(BF16)
    bsums[...] = bsums[...] + fold_rows(dq_out[0].astype(F32))
    dn[...] = dot(dq_out[0], watt[:, pl.ds(0, 3 * features)], DIMS_NT)
    norm_backward(dn, z_in.at[0], r_in.at[0], lay, g_in.at[0], sums, 10 * SUB, g1)
    conv_backward(x0, g1, mask, lay, sums, dn)
    store_cells(dn, cells)

    @pl.when(last_step())
    def _():
        drain_cells(cells, g_out)
        finish_sums(sums, small_out)
        finish_sums(bsums, bias_out)


def per_image(shape):
    if len(shape) == 2:
        return whole(shape)
    rest = (0,) * (len(shape) - 1)
    return pl.BlockSpec((1,) + tuple(shape[1:]), lambda i: (i,) + rest)


def whole(shape):
    zeros = (0,) * len(shape)
    return pl.BlockSpec(tuple(shape), lambda i: zeros, pipeline_mode=pl.Buffered(1))


def one_layer(shape, layer):
    return pl.BlockSpec((1,) + tuple(shape[1:]), lambda i: (layer, 0, 0), pipeline_mode=pl.Buffered(1))


def cost(flops, arrays):
    size = sum(jnp.dtype(d).itemsize * functools.reduce(lambda p, q: p * q, s) for s, d in arrays)
    return pl.CostEstimate(flops=int(flops), bytes_accessed=int(size), transcendentals=0)


def params():
    return pltpu.CompilerParams(dimension_semantics=("arbitrary",), vmem_limit_bytes=VMEM_LIMIT)


def carrier(kernel, carry, ins, outs, scratch, refs):
    extra_in, extra_out = len(carry.args), len(carry.outs)
    base_in, refs = refs[:ins], refs[ins:]
    carry_in, refs = refs[:extra_in], refs[extra_in:]
    base_out, refs = refs[:outs], refs[outs:]
    carry_out, refs = refs[:extra_out], refs[extra_out:]
    base_scratch, carry_scratch = refs[:scratch], refs[scratch:]
    carry.run(carry_in, carry_out, carry_scratch)
    kernel(*base_in, *base_out, *base_scratch)
    carry.end(carry_in, carry_out, carry_scratch)


def image_call(kernel, name, layer, batched, lay, shared, outs, sums, scratch, flops, carry=None):
    images = next(a.shape[0] for a in batched if a.ndim > 2)
    ins = [per_image(a.shape) for a in batched] + [one_layer(lay.shape, layer)]
    args = list(batched) + [lay]
    for item in shared:
        if isinstance(item, tuple):
            ins.append(one_layer(item[0].shape, item[1]))
            args.append(item[0])
        else:
            ins.append(whole(item.shape))
            args.append(item)
    out_specs = [per_image(s) for s, _ in outs]
    out_specs += [pl.BlockSpec(tuple(s), lambda i: (0, 0)) for s, _ in sums]
    results = outs + sums
    buffers = [pltpu.VMEM(s, d) for s, d in scratch]
    options = params()
    body = kernel
    if carry is not None:
        counts = (len(args), len(results), len(scratch))

        def body(*refs):
            carrier(kernel, carry, *counts, refs)

        args = args + carry.args
        ins = ins + [pl.BlockSpec(memory_space=pl.ANY)] * len(carry.args)
        out_specs += [carry.out_spec or pl.BlockSpec(tuple(s), lambda i: (0, 0)) for s, _ in carry.outs]
        results = results + carry.outs
        buffers += carry.scratch
        options = pltpu.CompilerParams(
            dimension_semantics=("arbitrary",), vmem_limit_bytes=VMEM_LIMIT, collective_id=carry.ident,
            has_side_effects=True,
        )
    arrays = [(a.shape, a.dtype) for a in args] + results
    return pl.pallas_call(
        body,
        grid=(images,),
        in_specs=ins,
        out_specs=out_specs,
        out_shape=[jax.ShapeDtypeStruct(s, d) for s, d in results],
        scratch_shapes=buffers,
        compiler_params=options,
        cost_estimate=cost(flops, arrays),
        name=name,
    )(*args)


def token_mask(heights, widths):
    t = jnp.arange(4 * WTOK, dtype=jnp.int32)
    window = t // WTOK
    row = (window // 2) * WIN + (t % WTOK) // SUB
    col8 = t % SUB
    col = (window % 2) * WIN + col8
    valid = (row[None] < heights[:, None]) & (col[None] < widths[:, None]) & (col8 < WIN)[None]
    return jnp.broadcast_to(valid.astype(F32)[..., None], valid.shape + (LANES,))


def forward_window(inputs, mask, lay, sh, watt, carry=None):
    (rows, c), images, t = inputs.shape, mask.shape[0], mask.shape[1]
    outs = [
        ((images, t, c), BF16), ((images, t, c), F32), ((images, t, LANES), F32),
        ((images, t, 3 * c), BF16), ((images, t, c), BF16),
        ((images, 4, c // GROUP, WTOK, WTOK * GROUP // HD), BF16), ((images, t, c), F32),
    ]
    scratch = [((c // LANES, rows, LANES), F32), ((t, c), F32), ((t, c), F32), ((t, 3 * c), F32), ((t, c), F32)]
    return image_call(window_forward_kernel, "window_forward", 0, [inputs, mask], lay, [sh, watt],
                      outs, [], scratch, 10 * images * t * c * c, carry)


def forward_mlp(x, mask, lay, hid, w_in, w_out, carry=None):
    images, t, c = x.shape
    ff = w_in.shape[1]
    outs = [
        ((images, t, c), BF16), ((images, t, c), F32), ((images, t, LANES), F32),
        ((images, t, ff), BF16), ((images, t, ff), BF16), ((images, t, c), F32),
    ]
    scratch = [((t, c), F32), ((t, c), F32)]
    return image_call(mlp_forward_kernel, "mlp_forward", 1, [x, mask], lay, [(hid, 0), w_in, w_out],
                      outs, [], scratch, 4 * images * t * c * ff, carry)


def forward_channel(x, mask, lay, sh, watt, carry=None):
    images, t, c = x.shape
    outs = [
        ((images, t, c), BF16), ((images, t, c), F32), ((images, t, LANES), F32),
        ((images, t, 3 * c), BF16), ((images, t, c), BF16),
        ((images, c // GROUP, GROUP, GROUP), BF16), ((images, t, c), F32),
    ]
    return image_call(channel_forward_kernel, "channel_forward", 2, [x, mask], lay, [sh, watt],
                      outs, [], [((t, c), F32)], 9 * images * t * c * c, carry)


def last_mlp(x, cot, mask, lay, hid, w_in, w_out):
    images, t, c = x.shape
    ff = w_in.shape[1]
    outs = [
        (cot.shape, BF16), ((images, t, c), F32), ((images, t, c), BF16), ((images, t, ff), BF16),
        ((images, t, c), BF16), ((images, t, ff), BF16),
    ]
    scratch = [
        ((c // LANES, cot.shape[0], LANES), F32), ((t, c), F32), ((t, c), F32), ((t, LANES), F32), ((t, c), F32),
        ((t, c), F32), ((t, c), F32), ((16 * SUB, c), F32), ((SUB, ff), F32),
    ]
    return image_call(last_mlp_kernel, "last_mlp", 3, [x, cot, mask], lay, [(hid, 1), w_in, w_out],
                      outs, [((16, c), F32), ((1, ff), F32)], scratch, 8 * images * t * c * ff)


def backward_mlp(g, x, z, r, d, mask, lay, w_in, w_out, carry=None):
    images, t, c = x.shape
    ff = w_in.shape[1]
    outs = [((images, t, c), F32), ((images, t, c), BF16), ((images, t, ff), BF16)]
    scratch = [((t, c), F32), ((t, c), F32), ((16 * SUB, c), F32), ((SUB, ff), F32)]
    return image_call(mlp_backward_kernel, "mlp_backward", 1, [g, x, z, r, d, mask], lay, [w_in, w_out],
                      outs, [((16, c), F32), ((1, ff), F32)], scratch, 4 * images * t * c * ff, carry)


def backward_channel(g, x, z, r, q, a, mask, lay, watt, carry=None):
    images, t, c = x.shape
    outs = [((images, t, c), F32), ((images, t, c), BF16), ((images, t, 3 * c), BF16)]
    scratch = [((t, c), F32), ((t, c), F32), ((16 * SUB, c), F32), ((SUB, 3 * c), F32)]
    return image_call(channel_backward_kernel, "channel_backward", 2, [g, x, z, r, q, a, mask], lay, [watt],
                      outs, [((16, c), F32), ((1, 3 * c), F32)], scratch, 10 * images * t * c * c, carry)


def backward_window(g, inputs, z, r, q, p, mask, lay, watt, carry=None):
    images, t, c = g.shape
    outs = [(inputs.shape, BF16), ((images, t, c), BF16), ((images, t, 3 * c), BF16)]
    scratch = [
        ((c // LANES, inputs.shape[0], LANES), F32), ((t, c), F32), ((t, 3 * c), F32), ((t, c), F32),
        ((t, 3 * c), F32), ((t, c), F32), ((t, c), F32), ((16 * SUB, c), F32), ((SUB, 3 * c), F32),
    ]
    return image_call(window_backward_kernel, "window_backward", 0, [g, inputs, z, r, q, p, mask], lay, [watt],
                      outs, [((16, c), F32), ((1, 3 * c), F32)], scratch, 12 * images * t * c * c, carry)


def grad_pair_kernel(first, left0, right0, left1, right1, out0, out1):
    step = pl.program_id(0)

    @pl.when(step < first)
    def _():
        out0[...] = dot(left0[...], right0[...], DIMS_TN).astype(BF16)

    @pl.when(step >= first)
    def _():
        out1[...] = dot(left1[...], right1[...], DIMS_TN).astype(BF16)


def grad_pair(name, left0, right0, left1, right1):
    flat = [a.reshape(-1, a.shape[-1]) for a in (left0, right0, left1, right1)]
    rows, c = flat[0].shape
    first, second = flat[1].shape[1] // c, flat[3].shape[1] // c

    def at_first(i):
        return (0, jnp.minimum(i, first - 1))

    def at_second(i):
        return (0, jnp.maximum(i - first, 0))

    outs = [((c, flat[1].shape[1]), BF16), ((c, flat[3].shape[1]), BF16)]
    return pl.pallas_call(
        functools.partial(grad_pair_kernel, first),
        grid=(first + second,),
        in_specs=[
            whole((rows, c)), pl.BlockSpec((rows, c), at_first),
            whole((rows, c)), pl.BlockSpec((rows, c), at_second),
        ],
        out_specs=[pl.BlockSpec((c, c), at_first), pl.BlockSpec((c, c), at_second)],
        out_shape=[jax.ShapeDtypeStruct(s, d) for s, d in outs],
        compiler_params=params(),
        cost_estimate=cost(2 * rows * c * c * (first + second), [(a.shape, BF16) for a in flat] + outs),
        name=name,
    )(*flat)


WIDE = 8
NARROW = 4
BOTH = ("narrow", "wide")
MESH_ID = pl.DeviceIdType.MESH
RING = (0, 1, -1, 2, -2, 3, -3, 4)
AFAR = RING[::-1]
GATHER_STEPS = (((0,), ()), ((1, -1), (0,)), ((2, -2), (1, -1)), ((3, -3), (2, -2)), ((4,), (3, -3)), ((), (4,)))
REDUCE_STEPS = ((), (15, 11), (7, 14, 10), (3, 6, 13), (2, 9), (5, 12), (1, 8, 4), (0,))
STAGES = (0, 4, 8, 12, 1, 5, 9, 13, 2, 6, 10, 14, 3, 7, 11, 15)
CARRY_STEPS = 8


def whole_part(condition):
    return jnp.where(condition, jnp.int32(1), jnp.int32(0))


def place(order, ring, cross=0, core=0):
    n, w = lax.axis_index("narrow"), lax.axis_index("wide")
    z = whole_part(w >= 2) + whole_part(w >= 4) + whole_part(w >= 6)
    y = whole_part(n >= 2)
    x, c = w - 2 * z, n - 2 * y
    a, b = (x, y) if order == 0 else (y, x)
    if ring:
        at = z + a * (7 - 2 * z) + ring
        at = at - 8 * whole_part(at >= 8) if ring > 0 else at + 8 * whole_part(at < 0)
        a = whole_part(at >= 4)
        z = at + a * (7 - 2 * at)
    if cross:
        b = 1 - b
    if core:
        c = 1 - c
    x, y = (a, b) if order == 0 else (b, a)
    return {"narrow": 2 * y + c, "wide": 2 * z + x}


def chip(order, rel):
    n, w = lax.axis_index("narrow"), lax.axis_index("wide")
    z1 = whole_part(w >= 4)
    z0 = whole_part(w - 4 * z1 >= 2)
    y = whole_part(n >= 2)
    x, c = w - 4 * z1 - 2 * z0, n - 2 * y
    first, second = (4, 8) if order == 0 else (8, 4)
    bits = (1, 2, first, second, 16)
    z0, z1, x, y, c = (1 - v if rel & bit else v for v, bit in zip((z0, z1, x, y, c), bits))
    return {"narrow": 2 * y + c, "wide": 4 * z1 + 2 * z0 + x}


def highest(rel):
    return rel.bit_length() - 1


def number(ring, cross=0, core=0):
    return ring % 8 + 8 * cross + 16 * core


def ring_peers():
    return [place(0, 1), place(0, -1), place(1, 1), place(1, -1), place(0, 0, 1), place(1, 0, 1), place(0, 0, 0, 1)]


def chip_peers():
    return [chip(0, 1 << k) for k in range(5)]


def meet(peers):
    barrier = pltpu.get_barrier_semaphore()
    for at in peers:
        pl.semaphore_signal(barrier, inc=1, device_id=at, device_id_type=MESH_ID)
    pl.semaphore_wait(barrier, len(peers))


class Part:
    def __init__(self, operand, kind, shape, start, size, order):
        self.operand, self.kind, self.shape, self.start, self.size, self.order = operand, kind, shape, start, size, order

    def whole(self):
        rows, cols = self.shape
        return {
            "slot": (WIDE * NARROW, rows, cols), "in": (NARROW * rows, WIDE * cols), "out": (WIDE * rows, NARROW * cols),
        }[self.kind]

    def view(self, ref, n, w):
        rows, cols = self.shape
        if self.kind == "slot":
            return ref.at[n * WIDE + w, pl.ds(self.start, self.size), :]
        a, b = (n, w) if self.kind == "in" else (w, n)
        step = 16
        while step < 128 and rows % (2 * step) == 0 and self.start % (2 * step) == 0:
            step *= 2
        at = pl.multiple_of(a * rows + self.start, step)
        return ref.at[pl.ds(at, self.size), pl.ds(pl.multiple_of(b * cols, cols), cols)]

    def of(self, ref, *where):
        at = place(self.order, *where)
        return self.view(ref, at["narrow"], at["wide"])


    def of_chip(self, ref, rel):
        at = chip(self.order, rel)
        return self.view(ref, at["narrow"], at["wide"])


def halves(operand, kind, shape):
    low = shape[0] // 32 * 16
    return [Part(operand, kind, shape, 0, low, 0), Part(operand, kind, shape, low, shape[0] - low, 1)]


def pair(first, second, shape_in, shape_out):
    return [Part(first, "in", shape_in, 0, shape_in[0], 0), Part(second, "out", shape_out, 0, shape_out[0], 1)]


class Gather:
    def __init__(self, index, part, own, dest, sems):
        self.index, self.part, self.dest = index, part, dest
        self.own = own.at[pl.ds(part.start, part.size), :]
        self.send, self.recv, self.keep = sems

    def copy(self, ring, cross, step):
        target = self.part.of(self.dest, ring, cross)
        if step is None:
            to, slot = place(self.part.order, 0, 0, 1), number(ring, cross, 1)
        elif step == 0:
            to, slot = place(self.part.order, 0, 1), number(ring, 1)
        else:
            to, slot = place(self.part.order, step), number(ring - step)
        return pltpu.make_async_remote_copy(
            src_ref=self.own if ring == 0 and cross == 0 else target, dst_ref=target,
            send_sem=self.send.at[self.index, slot], recv_sem=self.recv.at[self.index, slot],
            device_id=to, device_id_type=MESH_ID,
        )

    def arrival(self, ring, cross=0, core=0):
        target = self.part.of(self.dest, ring, cross, core)
        return pltpu.make_async_remote_copy(
            src_ref=target, dst_ref=target, send_sem=self.send.at[self.index, 0],
            recv_sem=self.recv.at[self.index, number(ring, cross, core)], device_id=place(self.part.order, 1),
            device_id_type=MESH_ID,
        )

    def stay(self):
        return pltpu.make_async_copy(self.own, self.part.of(self.dest, 0), self.keep.at[self.index])

    def sends(self, ring):
        steps = []
        if 0 <= ring < 4:
            steps.append(-1)
        if -3 < ring <= 0:
            steps.append(1)
        return steps + [0, None]

    def stage(self, ring):
        if ring == 0:
            self.stay().start()
        else:
            self.arrival(ring).wait_recv()
        for step in self.sends(ring):
            self.copy(ring, 0, step).start()

    def crossed(self, ring):
        self.arrival(ring, 1).wait_recv()
        self.copy(ring, 1, None).start()

    def finish(self):
        for ring in RING:
            self.arrival(ring, 0, 1).wait_recv()
            self.arrival(ring, 1, 1).wait_recv()
        for ring in RING:
            for step in self.sends(ring):
                self.copy(ring, 0, step).wait_send()
            self.copy(ring, 1, None).wait_send()
        self.stay().wait()


def gather_step(items, rings, crosses):
    for ring in rings:
        for item in items:
            item.stage(ring)
    for ring in crosses:
        for item in items:
            item.crossed(ring)


def gather_sems(count):
    return [pltpu.SemaphoreType.DMA((count, 32)), pltpu.SemaphoreType.DMA((count, 32)), pltpu.SemaphoreType.DMA((count,))]


class Beside:
    def __init__(self, ident, args, parts, pick=None):
        self.ident, self.args, self.parts = ident, list(args), parts
        self.pick = pick or {}
        shapes = {p.operand: p.whole() for p in parts}
        self.outs = [(shapes[k], BF16) for k in range(len(self.args))]
        self.out_spec = pl.BlockSpec(memory_space=pl.ANY)
        self.scratch = gather_sems(len(parts))

    def items(self, ins, outs, scratch):
        ins = [ref.at[self.pick[k]] if k in self.pick else ref for k, ref in enumerate(ins)]
        return [Gather(i, p, ins[p.operand], outs[p.operand], scratch) for i, p in enumerate(self.parts)]

    def run(self, ins, outs, scratch):
        items = self.items(ins, outs, scratch)
        for s, (rings, crosses) in enumerate(GATHER_STEPS):

            @pl.when(pl.program_id(0) == s)
            def _(s=s, rings=rings, crosses=crosses):
                if s == 0:
                    meet(ring_peers())
                gather_step(items, rings, crosses)

    def end(self, ins, outs, scratch):
        @pl.when(last_step())
        def _():
            for item in self.items(ins, outs, scratch):
                item.finish()


class Reduce:
    def __init__(self, index, part, src, out, bufs, sems):
        self.index, self.part, self.src, self.out = index, part, src, out
        self.acc, self.mate, self.inbox = bufs
        self.load_sem, self.send_sem, self.mate_sem, self.recv_sem = sems

    def load(self, rel):
        return pltpu.make_async_copy(self.part.of_chip(self.src, rel), self.acc.at[rel], self.load_sem.at[self.index, rel])

    def to_mate(self, rel):
        return pltpu.make_async_remote_copy(
            src_ref=self.part.of_chip(self.src, rel | 16), dst_ref=self.mate.at[rel],
            send_sem=self.send_sem.at[self.index, 16 + rel], recv_sem=self.mate_sem.at[self.index, rel],
            device_id=chip(self.part.order, 16), device_id_type=MESH_ID,
        )

    def onward(self, rel):
        return pltpu.make_async_remote_copy(
            src_ref=self.acc.at[rel], dst_ref=self.inbox.at[rel - 1], send_sem=self.send_sem.at[self.index, rel],
            recv_sem=self.recv_sem.at[self.index, rel], device_id=chip(self.part.order, 1 << highest(rel)),
            device_id_type=MESH_ID,
        )

    def begin(self, rel):
        self.to_mate(rel).start()
        self.load(rel).start()

    def stage(self, rel):
        self.load(rel).wait()
        self.to_mate(rel).wait_recv()
        total = self.acc[rel].astype(F32) + self.mate[rel].astype(F32)
        for axis in range(highest(rel) + 1, 4):
            came = rel | (1 << axis)
            self.onward(came).wait_recv()
            total = total + self.inbox[came - 1].astype(F32)
        if rel == 0:
            self.out[pl.ds(self.part.start, self.part.size), :] = total
        else:
            self.acc[rel] = total.astype(BF16)
            self.onward(rel).start()

    def finish(self):
        for rel in range(16):
            self.to_mate(rel).wait_send()
            if rel:
                self.onward(rel).wait_send()


class Behind:
    def __init__(self, ident, args, parts):
        self.ident, self.args, self.parts = ident, list(args), parts
        shapes = {p.operand: p.shape for p in parts}
        self.outs = [(shapes[k], F32) for k in range(len(self.args))]
        self.out_spec = None
        self.scratch = []
        for p in parts:
            block = (p.size, p.shape[1])
            self.scratch += [pltpu.VMEM((16,) + block, BF16), pltpu.VMEM((16,) + block, BF16), pltpu.VMEM((15,) + block, BF16)]
        count = len(parts)
        self.scratch += [
            pltpu.SemaphoreType.DMA((count, 16)), pltpu.SemaphoreType.DMA((count, 32)),
            pltpu.SemaphoreType.DMA((count, 16)), pltpu.SemaphoreType.DMA((count, 16)),
        ]

    def items(self, ins, outs, scratch):
        bufs, sems = scratch[: 3 * len(self.parts)], scratch[3 * len(self.parts) :]
        return [
            Reduce(i, p, ins[p.operand], outs[p.operand], bufs[3 * i : 3 * i + 3], sems)
            for i, p in enumerate(self.parts)
        ]

    def run(self, ins, outs, scratch):
        items = self.items(ins, outs, scratch)
        for s, rels in enumerate(REDUCE_STEPS):

            @pl.when(pl.program_id(0) == s)
            def _(s=s, rels=rels):
                if s == 0:
                    meet(chip_peers())
                    for rel in reversed(STAGES):
                        for item in items:
                            item.begin(rel)
                for rel in rels:
                    for item in items:
                        item.stage(rel)

    def end(self, ins, outs, scratch):
        @pl.when(last_step())
        def _():
            for item in self.items(ins, outs, scratch):
                item.finish()


def reduce_kernel(plan, *refs):
    ins, refs = refs[: len(plan.args)], refs[len(plan.args) :]
    outs, scratch = refs[: len(plan.outs)], refs[len(plan.outs) :]
    items = plan.items(ins, outs, scratch)
    meet(chip_peers())
    for rel in reversed(STAGES):
        for item in items:
            item.begin(rel)
    for rel in reversed(STAGES):
        for item in items:
            item.stage(rel)
    for item in items:
        item.finish()


def reduce_now(name, plan):
    return pl.pallas_call(
        functools.partial(reduce_kernel, plan),
        in_specs=[pl.BlockSpec(memory_space=pl.ANY)] * len(plan.args),
        out_specs=[pl.BlockSpec(memory_space=pltpu.VMEM)] * len(plan.outs),
        out_shape=[jax.ShapeDtypeStruct(s, d) for s, d in plan.outs],
        scratch_shapes=plan.scratch,
        compiler_params=pltpu.CompilerParams(
            collective_id=plan.ident, has_side_effects=True, vmem_limit_bytes=VMEM_LIMIT
        ),
        cost_estimate=cost(0, [(a.shape, a.dtype) for a in plan.args]),
        name=name,
    )(*plan.args)


def copy_attention(src, start, dst):
    cn = dst.shape[0]
    cw = src.shape[2] // 4
    c = WIDE * cw
    for w in range(WIDE):
        dst[:, pl.ds(3 * cw * w, 3 * cw)] = src[w, pl.ds(start, cn), pl.ds(0, 3 * cw)]
        dst[:, pl.ds(3 * c + cw * w, cw)] = src[w, pl.ds(start, cn), pl.ds(3 * cw, cw)]


def unpack_first_kernel(got, watt, lay, sh, hid):
    copy_attention(got, 16, watt)
    cw = got.shape[2] // 4
    for w in range(WIDE):
        lay[0, :, pl.ds(cw * w, cw)] = got[w, pl.ds(0, 16), pl.ds(0, cw)].astype(F32)

    @pl.when(pl.program_id(0) == 0)
    def _():
        for w in range(WIDE):
            part = got[w, pl.ds(0, 16), pl.ds(LANES, cw)].astype(F32)
            sh[:, pl.ds(cw * w, cw)] = part
            for j in range(2):
                for q in range(4):
                    row = 5 + 4 * j + q
                    hid[j, :, pl.ds(4 * cw * w + cw * q, cw)] = part[row : row + 1]


def unpack_first(got):
    rows, lanes = got.shape[1:]
    c = 2 * lanes
    cn = c // NARROW
    outs = [((c, 4 * c), BF16), ((NARROW, 16, c), F32), ((16, c), F32), ((2, 1, 4 * c), F32)]
    return pl.pallas_call(
        unpack_first_kernel,
        grid=(NARROW,),
        in_specs=[pl.BlockSpec((WIDE, rows, lanes), lambda n: (n, 0, 0))],
        out_specs=[
            pl.BlockSpec((cn, 4 * c), lambda n: (n, 0)), pl.BlockSpec((1, 16, c), lambda n: (n, 0, 0)),
            pl.BlockSpec((16, c), lambda n: (0, 0)), pl.BlockSpec((2, 1, 4 * c), lambda n: (0, 0, 0)),
        ],
        out_shape=[jax.ShapeDtypeStruct(s, d) for s, d in outs],
        compiler_params=params(),
        cost_estimate=cost(0, [(got.shape, BF16)] + outs),
        name="unpack_first",
    )(got)


def unpack_attention_kernel(got, watt):
    copy_attention(got, 0, watt)


def unpack_attention(got):
    rows, lanes = got.shape[1:]
    c = 2 * lanes
    shape = (c, 4 * c)
    return pl.pallas_call(
        unpack_attention_kernel,
        grid=(NARROW,),
        in_specs=[pl.BlockSpec((WIDE, rows, lanes), lambda n: (n, 0, 0))],
        out_specs=pl.BlockSpec((c // NARROW, 4 * c), lambda n: (n, 0)),
        out_shape=jax.ShapeDtypeStruct(shape, BF16),
        compiler_params=params(),
        cost_estimate=cost(0, [(shape, BF16)] * 2),
        name="unpack_attention",
    )(got)


def grad_attention_kernel(start, left0, right0, left1, right1, *refs):
    *head, out, result = refs[:-1] if len(refs) > 2 else refs
    step = pl.program_id(0)
    c = right0.shape[1]
    cn, cw = c // NARROW, c // WIDE

    def spread(s, w, low, high):
        for n in range(NARROW):
            at = pl.ds(low - 3 * cw * w, high - low)
            out[n * WIDE + w, pl.ds(start, cn), at] = result[pl.ds(cn * n, cn), pl.ds(low - c * s, high - low)]

    for s in range(4):

        @pl.when(step == s)
        def _(s=s):
            if s < 3:
                result[...] = dot(left0[...], right0[...], DIMS_TN).astype(BF16)
                for w in range(WIDE):
                    low, high = max(3 * cw * w, c * s), min(3 * cw * (w + 1), c * (s + 1))
                    if low < high:
                        spread(s, w, low, high)
            else:
                result[...] = dot(left1[...], right1[...], DIMS_TN).astype(BF16)
                for w in range(WIDE):
                    for n in range(NARROW):
                        at = pl.ds(3 * cw, cw)
                        out[n * WIDE + w, pl.ds(start, cn), at] = result[pl.ds(cn * n, cn), pl.ds(cw * w, cw)]
                if head:
                    pack_small(*head, out, refs[-1])


def pack_small(small, sb, cb, hid0, hid1, out, shared):
    c = small.shape[2]
    cw = c // WIDE
    shared[...] = jnp.zeros_like(shared)
    shared[pl.ds(0, 1), :] = sb[:, pl.ds(0, c)]
    shared[pl.ds(1, 1), :] = sb[:, pl.ds(2 * c, c)]
    for k in range(3):
        shared[pl.ds(2 + k, 1), :] = cb[:, pl.ds(k * c, c)]
    for j, hid in enumerate((hid0, hid1)):
        for w in range(WIDE):
            for q in range(4):
                shared[pl.ds(5 + 4 * j + q, 1), pl.ds(cw * w, cw)] = hid[:, pl.ds(4 * cw * w + cw * q, cw)]
    out[:, pl.ds(0, 16), :] = jnp.zeros((WIDE * NARROW, 16, out.shape[2]), BF16)
    for w in range(WIDE):
        for n in range(NARROW):
            out[n * WIDE + w, pl.ds(0, 16), pl.ds(0, cw)] = small[n, :, pl.ds(cw * w, cw)].astype(BF16)
            out[n * WIDE + w, pl.ds(0, 16), pl.ds(LANES, cw)] = shared[:, pl.ds(cw * w, cw)].astype(BF16)


def grad_attention(name, left0, right0, left1, right1, head=()):
    flat = [a.reshape(-1, a.shape[-1]) for a in (left0, right0, left1, right1)]
    rows, c = flat[0].shape
    cn = c // NARROW
    start = 16 if head else 0
    shape = (WIDE * NARROW, start + cn, c // 2)
    scratch = [pltpu.VMEM((c, c), BF16)] + ([pltpu.VMEM((16, c), F32)] if head else [])
    return pl.pallas_call(
        functools.partial(grad_attention_kernel, start),
        grid=(4,),
        in_specs=[
            whole((rows, c)), pl.BlockSpec((rows, c), lambda i: (0, jnp.minimum(i, 2))), whole((rows, c)), whole((rows, c)),
        ] + [whole(a.shape) for a in head],
        out_specs=pl.BlockSpec(shape, lambda i: (0, 0, 0)),
        out_shape=jax.ShapeDtypeStruct(shape, BF16),
        scratch_shapes=scratch,
        compiler_params=params(),
        cost_estimate=cost(8 * rows * c * c, [(a.shape, BF16) for a in flat] + [(shape, BF16)]),
        name=name,
    )(*flat, *head)


def attention_piece(qkv, proj):
    return jnp.concatenate([qkv.T, proj.T], axis=1)


def turned(value):
    return value.astype(F32).T.astype(BF16)


def gather_first_kernel(
    plan, conv_weight, conv_bias, norm_gain, norm_bias, qkv0, qkv1, proj, attn_bias, hidden_bias, out_bias,
    got, chan, piece, *sems,
):
    cw = conv_bias.shape[1]
    cn = qkv0.shape[1]
    piece[pl.ds(0, 16), :] = jnp.zeros((16, piece.shape[1]), BF16)
    taps_now = conv_weight[0].astype(F32)
    rows = [taps_now] + [r[...].astype(F32) for r in (conv_bias, norm_gain, norm_bias, out_bias)]
    rows.append(jnp.zeros((3, cw), F32))
    piece[pl.ds(0, 16), pl.ds(0, cw)] = jnp.concatenate(rows, axis=0).astype(BF16)
    hidden = hidden_bias[...].astype(F32)
    rows = [attn_bias[...].astype(F32)]
    rows += [hidden[j : j + 1, cw * q : cw * (q + 1)] for j in range(2) for q in range(4)]
    rows.append(jnp.zeros((3, cw), F32))
    piece[pl.ds(0, 16), pl.ds(LANES, cw)] = jnp.concatenate(rows, axis=0).astype(BF16)
    piece[pl.ds(16, cn), pl.ds(0, 3 * cw)] = turned(qkv0[...])
    piece[pl.ds(16, cn), pl.ds(3 * cw, cw)] = turned(proj[0])
    items = plan.items([piece], [got], sems)
    meet(ring_peers())
    gather_step(items, (0,), ())
    chan[:, pl.ds(0, 3 * cw)] = turned(qkv1[...])
    chan[:, pl.ds(3 * cw, cw)] = turned(proj[1])
    for rings, crosses in GATHER_STEPS[1:]:
        gather_step(items, rings, crosses)
    for item in items:
        item.finish()


def gather_first(p):
    rows, cn = p["spatial_qkv"].shape
    lanes = rows * 4 // 3
    shape = (16 + cn, lanes)
    plan = Beside(1, [None], halves(0, "slot", shape))
    outs = plan.outs + [((cn, lanes), BF16)]
    args = [p[k] for k in NAMES if not k.startswith("mlp")]
    vmem = pl.BlockSpec(memory_space=pltpu.VMEM)
    return pl.pallas_call(
        functools.partial(gather_first_kernel, plan),
        in_specs=[vmem] * len(args),
        out_specs=[plan.out_spec, vmem],
        out_shape=[jax.ShapeDtypeStruct(s, d) for s, d in outs],
        scratch_shapes=[pltpu.VMEM(shape, BF16)] + plan.scratch,
        compiler_params=pltpu.CompilerParams(collective_id=1, has_side_effects=True, vmem_limit_bytes=VMEM_LIMIT),
        cost_estimate=cost(0, outs),
        name="gather_first",
    )(*args)


def finish_kernel(
    att0, att1, in0, in1, out0, out1,
    conv_weight, conv_bias, norm_gain, norm_bias, qkv0, qkv1, proj, mlp_in, mlp_out, attn_bias, hidden_bias, out_bias,
):
    cw = conv_bias.shape[1]
    cn = qkv0.shape[1]
    for k in range(9):
        conv_weight[k] = att0[pl.ds(k, 1), pl.ds(0, cw)]
    for k, row in enumerate((conv_bias, norm_gain, norm_bias, out_bias)):
        row[...] = att0[pl.ds(9 + k, 1), pl.ds(0, cw)]
    attn_bias[...] = att0[pl.ds(0, 5), pl.ds(LANES, cw)]
    for j in range(2):
        for q in range(4):
            hidden_bias[pl.ds(j, 1), pl.ds(cw * q, cw)] = att0[pl.ds(5 + 4 * j + q, 1), pl.ds(LANES, cw)]
    qkv0[...] = att0[pl.ds(16, cn), pl.ds(0, 3 * cw)].T
    proj[0] = att0[pl.ds(16, cn), pl.ds(3 * cw, cw)].T
    qkv1[...] = att1[:, pl.ds(0, 3 * cw)].T
    proj[1] = att1[:, pl.ds(3 * cw, cw)].T
    mlp_in[0] = in0[...]
    mlp_in[1] = in1[...]
    mlp_out[0] = out0[...]
    mlp_out[1] = out1[...]


def finish(*reduced):
    att0 = reduced[0]
    cn, lanes = att0.shape[0] - 16, att0.shape[1]
    cw = lanes // 4
    row = (1, cw)
    shapes = [
        (9, 1, cw), row, row, row, (3 * cw, cn), (3 * cw, cn), (2, cw, cn), (2, cn, lanes), (2, cw, 2 * lanes),
        (5, cw), (2, lanes), row,
    ]
    vmem = pl.BlockSpec(memory_space=pltpu.VMEM)
    outs = pl.pallas_call(
        finish_kernel,
        in_specs=[vmem] * 6,
        out_specs=[vmem] * len(shapes),
        out_shape=[jax.ShapeDtypeStruct(s, F32) for s in shapes],
        compiler_params=pltpu.CompilerParams(vmem_limit_bytes=VMEM_LIMIT),
        cost_estimate=cost(0, [(s, F32) for s in shapes]),
        name="finish",
    )(*reduced)
    outs = list(outs)
    outs[0] = outs[0].transpose(1, 0, 2)
    outs[7] = outs[7].transpose(0, 2, 1)
    return outs


class Direct:
    def __init__(self, p):
        got, self.chan = gather_first(p)
        self.first, self.second = p["mlp_in"].transpose(0, 2, 1), p["mlp_out"]
        watt0, self.lay, self.sh, self.hid = unpack_first(got)
        self.watt, self.w_in, self.w_out = [watt0, None], [None, None], [None, None]

    def forward_window(self, *args):
        parts = pair(0, 1, self.first.shape[1:], self.second.shape[1:])
        carry = Beside(3, [self.first, self.second], parts, {0: 0, 1: 0})
        *outs, self.w_in[0], self.w_out[0] = forward_window(*args, carry=carry)
        return outs

    def forward_mlp(self, *args):
        parts = halves(0, "slot", self.chan.shape) + halves(1, "in", self.first.shape[1:])
        carry = Beside(4, [self.chan, self.first], parts, {1: 1})
        *outs, chan, self.w_in[1] = forward_mlp(*args, carry=carry)
        self.watt[1] = unpack_attention(chan)
        return outs

    def forward_channel(self, *args):
        parts = halves(0, "out", self.second.shape[1:])
        *outs, self.w_out[1] = forward_channel(*args, carry=Beside(5, [self.second], parts, {0: 1}))
        return outs

    def backward_channel(self, grads, *args):
        self.go1 = grads[1]
        parts = halves(0, "in", self.first.shape[1:])
        *outs, self.gi1 = backward_channel(*args, carry=Behind(6, grads[:1], parts))
        return outs

    def channel_grads(self, *args):
        return grad_attention("channel_grads", *args)

    def backward_mlp(self, grads, *args):
        self.att1 = grads
        parts = halves(0, "out", self.second.shape[1:])
        *outs, self.go1 = backward_mlp(*args, carry=Behind(7, [self.go1], parts))
        return outs

    def backward_window(self, grads, *args):
        parts = pair(0, 1, self.first.shape[1:], self.second.shape[1:]) + halves(2, "slot", self.chan.shape)
        *outs, self.gi0, self.go0, self.att1 = backward_window(*args, carry=Behind(8, list(grads) + [self.att1], parts))
        return outs

    def reduce_last(self, grads, smalls, sb, cb, hid0, hid1):
        packed = grad_attention("window_grads", *grads, (jnp.stack(smalls), sb, cb, hid0, hid1))
        (att0,) = reduce_now("reduce_last", Behind(2, [packed], halves(0, "slot", packed.shape[1:])))
        return tuple(finish(att0, self.att1, self.gi0, self.gi1, self.go0, self.go1))


class Plain:
    def __init__(self, p):
        self.layers, self.cw = p["conv_bias"].shape
        wide = p["attn_bias"].shape
        self.narrow = 4 // self.layers
        self.cn = p["spatial_qkv"].shape[1]
        self.c = self.cn * self.narrow
        self.wide = self.c // self.cw
        self.fw = p["hidden_bias"].shape[1]
        c, cn, cw, fw, n, w = self.c, self.cn, self.cw, self.fw, self.narrow, self.wide

        def spread(v):
            return lax.all_gather(v, BOTH, axis=0, tiled=False).reshape((n, w) + v.shape)

        def attention(qkv, proj):
            got = spread(attention_piece(qkv, proj)).transpose(0, 2, 1, 3)
            return jnp.concatenate([got[..., : 3 * cw].reshape(c, 3 * c), got[..., 3 * cw :].reshape(c, c)], axis=1)

        self.watt = tuple(attention(p[k], p["projection"][i]) for i, k in enumerate(("spatial_qkv", "channel_qkv")))
        self.w_in = tuple(spread(p["mlp_in"][i].T).transpose(0, 2, 1, 3).reshape(c, -1) for i in range(2))
        self.w_out = tuple(spread(p["mlp_out"][i]).transpose(1, 2, 0, 3).reshape(c, -1) for i in range(2))

        def layer(v):
            return spread(v).transpose(0, 2, 3, 1, 4).reshape(4, -1, c)

        rows = [layer(p["conv_weight"])]
        rows += [layer(p[k][:, None]) for k in ("conv_bias", "norm_gain", "norm_bias", "out_bias")]
        self.lay = jnp.pad(jnp.concatenate(rows, axis=1).astype(F32), ((0, 0), (0, 3), (0, 0)))
        attn = spread(p["attn_bias"])[0].transpose(1, 0, 2).reshape(5, c)
        self.sh = jnp.pad(attn.astype(F32), ((0, 11), (0, 0)))
        self.hid = spread(p["hidden_bias"])[0].transpose(1, 0, 2).reshape(2, 1, -1).astype(F32)

    def forward_window(self, *args):
        return forward_window(*args)

    def forward_mlp(self, *args):
        return forward_mlp(*args)

    def forward_channel(self, *args):
        return forward_channel(*args)

    def backward_channel(self, grads, *args):
        self.mlp1 = (self.matrix(grads[0], False), self.matrix(grads[1], True))
        return backward_channel(*args)

    def backward_mlp(self, grads, *args):
        self.att1 = (self.matrix(grads[0], False), self.matrix(grads[1], False))
        return backward_mlp(*args)

    def backward_window(self, grads, *args):
        self.mlp0 = (self.matrix(grads[0], False), self.matrix(grads[1], True))
        return backward_window(*args)

    def channel_grads(self, *args):
        return grad_pair("channel_grads", *args)

    def matrix(self, grad, rows_wide):
        n, w = self.narrow, self.wide
        a, b = (w, n) if rows_wide else (n, w)
        grad = grad.reshape(a, grad.shape[0] // a, b, grad.shape[1] // b)
        grad = grad.transpose(2, 0, 1, 3) if rows_wide else grad.transpose(0, 2, 1, 3)
        grad = grad.astype(BF16).reshape(n * w * grad.shape[2], grad.shape[3])
        return lax.psum_scatter(grad, BOTH, scatter_dimension=0, tiled=True).astype(F32)

    def reduce_last(self, grads, smalls, sb, cb, hid0, hid1):
        c, cw, fw, n, w = self.c, self.cw, self.fw, self.narrow, self.wide
        grads = grad_pair("window_grads", *grads)
        first = (self.matrix(grads[0], False), self.matrix(grads[1], False)) + self.mlp0
        rest = self.att1 + self.mlp1
        small = jnp.stack(smalls).reshape(n, self.layers * 16, w, cw).transpose(0, 2, 1, 3)
        attn = jnp.concatenate([sb[:, :c], sb[:, 2 * c :], cb.reshape(3, c)]).reshape(5, w, cw).transpose(1, 0, 2)
        hid = jnp.concatenate([hid0, hid1]).reshape(2, w, fw).transpose(1, 0, 2).reshape(w, -1, cw)
        common = jnp.concatenate([attn, hid], axis=1)
        common = jnp.broadcast_to(common[None], (n,) + common.shape)
        flat = jnp.concatenate([small, common], axis=2).astype(BF16).reshape(-1, cw)
        got = lax.psum_scatter(flat, BOTH, scatter_dimension=0, tiled=True).astype(F32)
        small = got[: self.layers * 16].reshape(self.layers, 16, cw)
        shared = got[self.layers * 16 :]
        return (
            small[:, :9], small[:, 9], small[:, 10], small[:, 11], first[0].T, rest[0].T,
            jnp.stack([first[1].T, rest[1].T]), jnp.stack([first[2].T, rest[2].T]), jnp.stack([first[3], rest[3]]),
            shared[:5], shared[5:].reshape(2, fw), small[:, 12],
        )


NAMES = (
    "conv_weight", "conv_bias", "norm_gain", "norm_bias", "spatial_qkv", "channel_qkv", "projection", "mlp_in",
    "mlp_out", "attn_bias", "hidden_bias", "out_bias",
)


def local(plan, inputs, heights, widths, *rest):
    if inputs.shape[0] != CARRY_STEPS:
        plan = Plain
    weights = plan(dict(zip(NAMES, rest[:-1])))
    cotangent = rest[-1]
    lay, sh, hid = weights.lay, weights.sh, weights.hid
    mask = token_mask(heights, widths)
    inputs, cotangent = cells_first(inputs), cells_first(cotangent)
    n1, z1, r1, q1, o1, p1, x2 = weights.forward_window(inputs, mask, lay, sh, weights.watt[0])
    n2, z2, r2, u1, d1, x4 = weights.forward_mlp(x2, mask, lay, hid, weights.w_in[0], weights.w_out[0])
    n3, z3, r3, q3, o3, a3, x6 = weights.forward_channel(x4, mask, lay, sh, weights.watt[1])
    out, g6, n4, u2, gy2, gh2, small3, hid1 = last_mlp(
        x6, cotangent, mask, lay, hid, weights.w_in[1], weights.w_out[1])
    grads = grad_pair("last_mlp_grads", n4, gh2, gy2, u2)
    g4, ga3, dq3, small2, cb = weights.backward_channel(
        grads, g6, x4, z3, r3, q3, a3, mask, lay, weights.watt[1])
    grads = weights.channel_grads(n3, dq3, o3, ga3)
    g2, gy1, gh1, small1, hid0 = weights.backward_mlp(
        grads, g4, x2, z2, r2, d1, mask, lay, weights.w_in[0], weights.w_out[0])
    grads = grad_pair("mlp_grads", n2, gh1, gy1, u1)
    input_grad, ga1, dq1, small0, sb = weights.backward_window(
        grads, g2, inputs, z1, r1, q1, p1, mask, lay, weights.watt[0])
    last = weights.reduce_last((n1, dq1, o1, ga1), (small0, small1, small2, small3), sb, cb, hid0, hid1)
    return (images_first(out), images_first(input_grad)) + tuple(last)


def solution(mesh):
    matrix = P("wide", "narrow")
    cells = P(("wide", "narrow"), None, None, None)
    stacked = P(None, "wide", "narrow")
    row = P("narrow", "wide")
    shared = P(None, "wide")
    images = P(("wide", "narrow"))
    kernels = P("narrow", None, "wide")
    in_specs = (
        cells, images, images, kernels, row, row, row, matrix, matrix,
        stacked, stacked, stacked, shared, shared, row, cells,
    )
    out_specs = (
        cells, cells, kernels, row, row, row, matrix, matrix, stacked, stacked, stacked, shared, shared, row,
    )
    plan = Direct if (mesh.shape["wide"], mesh.shape["narrow"]) == (WIDE, NARROW) else Plain
    body = functools.partial(local, plan)
    return jax.shard_map(body, mesh=mesh, in_specs=in_specs, out_specs=out_specs, check_vma=False)
```

```python
import functools

import jax
import jax.numpy as jnp
from jax import lax
from jax.experimental import pallas as pl
from jax.experimental.pallas import tpu as pltpu
from jax.sharding import PartitionSpec as P

HD = 32
WIN = 7
LANES = 128
SUB = 8
GROUP = 256
WTOK = WIN * SUB
FFC = 1024
NROWS = 112
SCALE = HD ** (-0.5)
EPS = 1e-05
NEG = -1e30
F32 = jnp.float32
BF16 = jnp.bfloat16
VMEM_LIMIT = 60 * 1024 * 1024
DIMS_NN = (((1,), (0,)), ((), ()))
DIMS_NT = (((1,), (1,)), ((), ()))
DIMS_TN = (((0,), (0,)), ((), ()))


def dot(a, b, dims):
    return lax.dot_general(a, b, dims, preferred_element_type=F32)


def tok(r, half):
    return ((r // WIN) * 2 + half) * WTOK + (r % WIN) * SUB


def fill_cells(src, cells):
    for j in range(cells.shape[0]):
        cells[j] = src[:, pl.ds(j * LANES, LANES)].astype(F32)


def drain_cells(cells, dst):
    for j in range(cells.shape[0]):
        dst[:, pl.ds(j * LANES, LANES)] = cells[j].astype(BF16)


def cell_rows(cells, r, half):
    images = cells.shape[1] // (4 * WIN * WIN)
    start = (r * 2 * WIN + WIN * half) * images
    if images == 1:
        return pl.ds(start, WIN)
    return pl.ds(start + pl.program_id(0), WIN, stride=images)


def load_cells(cells, dst):
    for r in range(2 * WIN):
        for half in range(2):
            for j in range(cells.shape[0]):
                dst[pl.ds(tok(r, half), WIN), pl.ds(j * LANES, LANES)] = cells.at[j][cell_rows(cells, r, half), :]


def store_cells(src, cells):
    for r in range(2 * WIN):
        for half in range(2):
            for j in range(cells.shape[0]):
                cells.at[j][cell_rows(cells, r, half), :] = src[pl.ds(tok(r, half), WIN), pl.ds(j * LANES, LANES)]


def cells_first(images):
    return images.transpose(1, 2, 0, 3).reshape(-1, images.shape[3])


def images_first(cells):
    return cells.reshape(2 * WIN, 2 * WIN, -1, cells.shape[1]).transpose(2, 0, 1, 3)


def neighbours(left, right):
    last = lax.broadcasted_iota(jnp.int32, (SUB, LANES), 0) == SUB - 1
    up_right = pltpu.roll(right, SUB - 1, 0)
    up_left = pltpu.roll(jnp.where(last, up_right, left), SUB - 1, 0)
    down_left = pltpu.roll(left, 1, 0)
    down_right = pltpu.roll(jnp.where(last, down_left, right), 1, 0)
    return ((down_left, left, up_left), (down_right, right, up_right))


def masked_row(src, mask, r, lanes):
    pair = []
    for half in range(2):
        rows = pl.ds(tok(r, half), SUB)
        pair.append(src[rows, lanes] * mask[0, rows, :])
    return neighbours(*pair)


def plain_row(src, r, lanes):
    return neighbours(*[src[pl.ds(tok(r, half), SUB), lanes] for half in range(2)])


def lay_row(lay, k):
    return lay[0, pl.ds(k, 1), :]


def taps(lay, lanes):
    return [jnp.broadcast_to(lay[0, pl.ds(k, 1), lanes], (SUB, LANES)) for k in range(10)]


def conv_forward(src, mask, lay, dst):
    rows = 2 * WIN

    @pl.loop(0, src.shape[1] // LANES)
    def _(j):
        lanes = pl.ds(pl.multiple_of(j * LANES, LANES), LANES)
        w = taps(lay, lanes)
        shift = w[9]
        window = [None, masked_row(src, mask, 0, lanes), masked_row(src, mask, 1, lanes)]
        for r in range(rows):
            for half in range(2):
                total = shift
                for a in range(3):
                    if window[a] is None:
                        continue
                    for b in range(3):
                        total = total + w[3 * a + b] * window[a][half][b]
                at = pl.ds(tok(r, half), SUB)
                dst[at, lanes] = src[at, lanes] + total
            following = masked_row(src, mask, r + 2, lanes) if r + 2 < rows else None
            window = [window[1], window[2], following]


def conv_backward(x_src, g_src, mask, lay, sums, dst):
    rows = 2 * WIN

    @pl.loop(0, x_src.shape[1] // LANES)
    def _(j):
        lanes = pl.ds(pl.multiple_of(j * LANES, LANES), LANES)
        w = taps(lay, lanes)
        g_win = [None, plain_row(g_src, 0, lanes), plain_row(g_src, 1, lanes)]
        x_win = [None, masked_row(x_src, mask, 0, lanes), masked_row(x_src, mask, 1, lanes)]
        grads = [sums[pl.ds(SUB * k, SUB), lanes] for k in range(10)]
        for r in range(rows):
            for half in range(2):
                center = g_win[1][half][1]
                total = None
                for a in range(3):
                    for b in range(3):
                        if x_win[a] is not None:
                            grads[3 * a + b] = grads[3 * a + b] + center * x_win[a][half][b]
                        if g_win[2 - a] is not None:
                            term = w[3 * a + b] * g_win[2 - a][half][2 - b]
                            total = term if total is None else total + term
                grads[9] = grads[9] + center
                at = pl.ds(tok(r, half), SUB)
                dst[at, lanes] = center + mask[0, at, :] * total
            more = r + 2 < rows
            g_win = [g_win[1], g_win[2], plain_row(g_src, r + 2, lanes) if more else None]
            x_win = [x_win[1], x_win[2], masked_row(x_src, mask, r + 2, lanes) if more else None]
        for k in range(10):
            sums[pl.ds(SUB * k, SUB), lanes] = grads[k]


def norm_forward(src, lay, z_out, r_out, n_out):
    features = src.shape[1]

    @pl.loop(0, src.shape[0] // (2 * NROWS))
    def _(i):
        for j in range(2):
            rows = pl.ds(pl.multiple_of(i * (2 * NROWS) + j * NROWS, NROWS), NROWS)
            x = src[rows, :]
            center = x - jnp.sum(x, axis=1, keepdims=True) * (1.0 / features)
            var = jnp.sum(center * center, axis=1, keepdims=True) * (1.0 / features)
            rstd = lax.rsqrt(var + EPS)
            z = center * rstd
            z_out[rows, :] = z
            r_out[rows, :] = jnp.broadcast_to(rstd, (NROWS, LANES))
            n_out[rows, :] = (z * lay_row(lay, 10) + lay_row(lay, 11)).astype(BF16)


def norm_backward(dn, z_src, r_src, lay, g_src, sums, first, dst):
    features = dn.shape[1]

    @pl.loop(0, dn.shape[0] // (2 * NROWS))
    def _(i):
        for j in range(2):
            rows = pl.ds(pl.multiple_of(i * (2 * NROWS) + j * NROWS, NROWS), NROWS)
            d = dn[rows, :]
            z = z_src[rows, :]
            t = d * lay_row(lay, 10)
            m1 = jnp.sum(t, axis=1, keepdims=True) * (1.0 / features)
            m2 = jnp.sum(t * z, axis=1, keepdims=True) * (1.0 / features)
            dst[rows, :] = g_src[rows, :] + (t - m1 - z * m2) * r_src[rows, 0:1]
            at = pl.ds(first, SUB)
            sums[at, :] = sums[at, :] + fold_rows(d * z)
            at = pl.ds(first + SUB, SUB)
            sums[at, :] = sums[at, :] + fold_rows(d)


def fold_rows(value):
    total = value[:SUB]
    for i in range(1, value.shape[0] // SUB):
        total = total + value[SUB * i : SUB * (i + 1)]
    return total


def finish_sums(sums, out):
    for k in range(sums.shape[0] // SUB):
        out[pl.ds(k, 1), :] = jnp.sum(sums[pl.ds(SUB * k, SUB), :], axis=0, keepdims=True)


def head_masks():
    lane = lax.broadcasted_iota(jnp.int32, (WTOK, GROUP), 1) // HD
    return [lane == h for h in range(GROUP // HD)]


def spread_heads(value, masks):
    return jnp.concatenate([jnp.where(m, value, 0.0) for m in masks], axis=0).astype(BF16)


def collect_heads(full, masks):
    total = full[:WTOK]
    for h in range(1, len(masks)):
        total = jnp.where(masks[h], full[WTOK * h : WTOK * (h + 1)], total)
    return total


def rounded(value):
    return value.astype(BF16).astype(F32)


def gelu_pair(h):
    cdf = 0.5 * (1.0 + lax.erf(h * 0.7071067811865476))
    pdf = jnp.exp(h * h * -0.5) * 0.3989422804014327
    return h * cdf, cdf + h * pdf


def first_step():
    return pl.program_id(0) == 0


def last_step():
    return pl.program_id(0) == pl.num_programs(0) - 1


def window_forward_kernel(
    inp, mask, lay, sh, watt,
    n_out, z_out, r_out, q_out, o_out, p_out, x_out,
    cells, x0, x1, qf, of,
):
    features = x0.shape[1]

    @pl.when(first_step())
    def _():
        x0[...] = jnp.zeros_like(x0)
        fill_cells(inp, cells)

    load_cells(cells, x0)
    conv_forward(x0, mask, lay, x1)
    norm_forward(x1, lay, z_out.at[0], r_out.at[0], n_out.at[0])
    chunk = features
    for c in range(3):
        lanes = pl.ds(c * chunk, chunk)
        part = dot(n_out[0], watt[:, lanes], DIMS_NN)
        if c != 1:
            part = part + sh[pl.ds(c // 2, 1), :]
        part = part.astype(BF16)
        q_out[0, :, lanes] = part
        qf[:, lanes] = part.astype(F32)

    @pl.loop(0, 4)
    def _(w):
        rows = pl.ds(pl.multiple_of(w * WTOK, SUB), WTOK)
        valid = mask[0, rows, 0:1] > 0.0
        masks = head_masks()
        for g in range(features // GROUP):
            q = qf[rows, pl.ds(g * GROUP, GROUP)]
            k = qf[rows, pl.ds(features + g * GROUP, GROUP)].astype(BF16)
            v = qf[rows, pl.ds(2 * features + g * GROUP, GROUP)].astype(BF16)
            s = dot(k, spread_heads(q, masks), DIMS_NT) * SCALE
            s = jnp.where(valid, s, NEG)
            e = jnp.exp(s - jnp.max(s, axis=0, keepdims=True))
            p = (e / jnp.sum(e, axis=0, keepdims=True)).astype(BF16)
            p_out[0, w, g] = p
            of[rows, pl.ds(g * GROUP, GROUP)] = collect_heads(dot(p, v, DIMS_TN), masks)

    o_out[0] = of[...].astype(BF16)
    x_out[0] = x1[...] + (dot(o_out[0], watt[:, pl.ds(3 * features, features)], DIMS_NN) + lay_row(lay, 12))


def mlp_forward_kernel(
    x_in, mask, lay, hb, w_in, w_out,
    n_out, z_out, r_out, u_out, d_out, x_out,
    x1, acc,
):
    conv_forward(x_in.at[0], mask, lay, x1)
    norm_forward(x1, lay, z_out.at[0], r_out.at[0], n_out.at[0])
    for c in range(w_in.shape[1] // FFC):
        lanes = pl.ds(c * FFC, FFC)
        h = dot(n_out[0], w_in[:, lanes], DIMS_NN) + hb[0, :, lanes]
        u, d = gelu_pair(h)
        u = u.astype(BF16)
        u_out[0, :, lanes] = u
        d_out[0, :, lanes] = d.astype(BF16)
        y = dot(u, w_out[:, lanes], DIMS_NT)
        acc[...] = y if c == 0 else acc[...] + y
    x_out[0] = x1[...] + (acc[...] + lay_row(lay, 12))


def group_mask():
    row = lax.broadcasted_iota(jnp.int32, (GROUP, GROUP), 0) // HD
    col = lax.broadcasted_iota(jnp.int32, (GROUP, GROUP), 1) // HD
    return row == col


def channel_forward_kernel(
    x_in, mask, lay, sh, watt,
    n_out, z_out, r_out, q_out, o_out, a_out, x_out,
    x1,
):
    features = x1.shape[1]
    conv_forward(x_in.at[0], mask, lay, x1)
    norm_forward(x1, lay, z_out.at[0], r_out.at[0], n_out.at[0])
    for c in range(3):
        lanes = pl.ds(c * features, features)
        part = dot(n_out[0], watt[:, lanes], DIMS_NN) + sh[pl.ds(2 + c, 1), :]
        if c == 1:
            part = part * mask[0, :, 0:1]
        q_out[0, :, lanes] = part.astype(BF16)
    same = group_mask()
    for g in range(features // GROUP):
        q = q_out[0, :, pl.ds(g * GROUP, GROUP)]
        k = q_out[0, :, pl.ds(features + g * GROUP, GROUP)]
        v = q_out[0, :, pl.ds(2 * features + g * GROUP, GROUP)]
        s = jnp.where(same, dot(k, q, DIMS_TN) * SCALE, -jnp.inf)
        e = jnp.exp(s - jnp.max(s, axis=0, keepdims=True))
        a = (e / jnp.sum(e, axis=0, keepdims=True)).astype(BF16)
        a_out[0, g] = a
        o_out[0, :, pl.ds(g * GROUP, GROUP)] = dot(v, a, DIMS_NN).astype(BF16)
    x_out[0] = x1[...] + (dot(o_out[0], watt[:, pl.ds(3 * features, features)], DIMS_NN) + lay_row(lay, 12))


def last_mlp_kernel(
    x_in, cot, mask, lay, hb, w_in, w_out,
    out, g_out, n_out, u_out, gy_out, gh_out, small_out, hidden_out,
    cells, x1, z, r, acc, dn, g8, sums, hsums,
):
    @pl.when(first_step())
    def _():
        g8[...] = jnp.zeros_like(g8)
        sums[...] = jnp.zeros_like(sums)
        hsums[...] = jnp.zeros_like(hsums)
        fill_cells(cot, cells)

    x6 = x_in.at[0]
    load_cells(cells, g8)
    conv_forward(x6, mask, lay, x1)
    norm_forward(x1, lay, z, r, n_out.at[0])
    g8[...] = g8[...] * mask[0, :, 0:1]
    gy_out[0] = g8[...].astype(BF16)
    sums[pl.ds(12 * SUB, SUB), :] = sums[pl.ds(12 * SUB, SUB), :] + fold_rows(gy_out[0].astype(F32))
    for c in range(1):
        lanes = pl.ds(0, w_in.shape[1])
        h = dot(n_out[0], w_in[:, lanes], DIMS_NN) + hb[0, :, lanes]
        du = dot(gy_out[0], w_out[:, lanes], DIMS_NN)
        u, d = gelu_pair(h)
        u = u.astype(BF16)
        u_out[0, :, lanes] = u
        gh = (du * d).astype(BF16)
        gh_out[0, :, lanes] = gh
        hsums[:, lanes] = hsums[:, lanes] + fold_rows(gh.astype(F32))
        y = dot(u, w_out[:, lanes], DIMS_NT)
        dx = dot(gh, w_in[:, lanes], DIMS_NT)
        acc[...] = y if c == 0 else acc[...] + y
        dn[...] = dx if c == 0 else dn[...] + dx
    acc[...] = (x1[...] + (acc[...] + lay_row(lay, 12))) * mask[0, :, 0:1]
    store_cells(acc, cells)
    norm_backward(dn, z, r, lay, g8, sums, 10 * SUB, x1)
    conv_backward(x6, x1, mask, lay, sums, g_out.at[0])

    @pl.when(last_step())
    def _():
        drain_cells(cells, out)
        finish_sums(sums, small_out)
        finish_sums(hsums, hidden_out)


def mlp_backward_kernel(
    g_in, x_in, z_in, r_in, d_in, mask, lay, w_in, w_out,
    g_out, gy_out, gh_out, small_out, hidden_out,
    dn, g1, sums, hsums,
):
    @pl.when(first_step())
    def _():
        sums[...] = jnp.zeros_like(sums)
        hsums[...] = jnp.zeros_like(hsums)

    gy_out[0] = g_in[0].astype(BF16)
    sums[pl.ds(12 * SUB, SUB), :] = sums[pl.ds(12 * SUB, SUB), :] + fold_rows(gy_out[0].astype(F32))
    for c in range(w_in.shape[1] // FFC):
        lanes = pl.ds(c * FFC, FFC)
        du = dot(gy_out[0], w_out[:, lanes], DIMS_NN)
        gh = (du * d_in[0, :, lanes].astype(F32)).astype(BF16)
        gh_out[0, :, lanes] = gh
        hsums[:, lanes] = hsums[:, lanes] + fold_rows(gh.astype(F32))
        dx = dot(gh, w_in[:, lanes], DIMS_NT)
        dn[...] = dx if c == 0 else dn[...] + dx
    norm_backward(dn, z_in.at[0], r_in.at[0], lay, g_in.at[0], sums, 10 * SUB, g1)
    conv_backward(x_in.at[0], g1, mask, lay, sums, g_out.at[0])

    @pl.when(last_step())
    def _():
        finish_sums(sums, small_out)
        finish_sums(hsums, hidden_out)


def channel_backward_kernel(
    g_in, x_in, z_in, r_in, q_in, a_in, mask, lay, watt,
    g_out, ga_out, dq_out, small_out, bias_out,
    dn, g1, sums, bsums,
):
    features = dn.shape[1]

    @pl.when(first_step())
    def _():
        sums[...] = jnp.zeros_like(sums)
        bsums[...] = jnp.zeros_like(bsums)

    ga_out[0] = g_in[0].astype(BF16)
    sums[pl.ds(12 * SUB, SUB), :] = sums[pl.ds(12 * SUB, SUB), :] + fold_rows(ga_out[0].astype(F32))
    go = dot(ga_out[0], watt[:, pl.ds(3 * features, features)], DIMS_NT).astype(BF16)
    for g in range(features // GROUP):
        at = [pl.ds(i * features + g * GROUP, GROUP) for i in range(3)]
        q, k, v = (q_in[0, :, lanes] for lanes in at)
        gog = go[:, g * GROUP : (g + 1) * GROUP]
        a = a_in[0, g]
        af = a.astype(F32)
        dp = dot(v, gog, DIMS_TN)
        ds = (af * (dp - jnp.sum(dp * af, axis=0, keepdims=True))).astype(BF16)
        dq_out[0, :, at[0]] = (dot(k, ds, DIMS_NN) * SCALE).astype(BF16)
        dq_out[0, :, at[1]] = (dot(q, ds, DIMS_NT) * SCALE * mask[0, :, 0:1]).astype(BF16)
        dq_out[0, :, at[2]] = dot(gog, a, DIMS_NT).astype(BF16)
    bsums[...] = bsums[...] + fold_rows(dq_out[0].astype(F32))
    dn[...] = dot(dq_out[0], watt[:, pl.ds(0, 3 * features)], DIMS_NT)
    norm_backward(dn, z_in.at[0], r_in.at[0], lay, g_in.at[0], sums, 10 * SUB, g1)
    conv_backward(x_in.at[0], g1, mask, lay, sums, g_out.at[0])

    @pl.when(last_step())
    def _():
        finish_sums(sums, small_out)
        finish_sums(bsums, bias_out)


def window_backward_kernel(
    g_in, inp, z_in, r_in, q_in, p_in, mask, lay, watt,
    g_out, ga_out, dq_out, small_out, bias_out,
    cells, x0, qf, gof, dqf, dn, g1, sums, bsums,
):
    features = dn.shape[1]

    @pl.when(first_step())
    def _():
        x0[...] = jnp.zeros_like(x0)
        sums[...] = jnp.zeros_like(sums)
        bsums[...] = jnp.zeros_like(bsums)
        fill_cells(inp, cells)

    load_cells(cells, x0)
    ga_out[0] = g_in[0].astype(BF16)
    sums[pl.ds(12 * SUB, SUB), :] = sums[pl.ds(12 * SUB, SUB), :] + fold_rows(ga_out[0].astype(F32))
    gof[...] = rounded(dot(ga_out[0], watt[:, pl.ds(3 * features, features)], DIMS_NT))
    qf[...] = q_in[0].astype(F32)

    @pl.loop(0, 4)
    def _(w):
        rows = pl.ds(pl.multiple_of(w * WTOK, SUB), WTOK)
        masks = head_masks()
        for g in range(features // GROUP):
            at = [pl.ds(i * features + g * GROUP, GROUP) for i in range(3)]
            qe = spread_heads(qf[rows, at[0]], masks)
            k = qf[rows, at[1]].astype(BF16)
            v = qf[rows, at[2]].astype(BF16)
            goe = spread_heads(gof[rows, at[0]], masks)
            p = p_in[0, w, g]
            pf = p.astype(F32)
            dp = dot(v, goe, DIMS_NT)
            ds = (pf * (dp - jnp.sum(dp * pf, axis=0, keepdims=True))).astype(BF16)
            dqf[rows, at[0]] = collect_heads(dot(ds, k, DIMS_TN), masks) * SCALE
            dqf[rows, at[1]] = dot(ds, qe, DIMS_NN) * SCALE
            dqf[rows, at[2]] = dot(p, goe, DIMS_NN)

    dq_out[0] = dqf[...].astype(BF16)
    bsums[...] = bsums[...] + fold_rows(dq_out[0].astype(F32))
    dn[...] = dot(dq_out[0], watt[:, pl.ds(0, 3 * features)], DIMS_NT)
    norm_backward(dn, z_in.at[0], r_in.at[0], lay, g_in.at[0], sums, 10 * SUB, g1)
    conv_backward(x0, g1, mask, lay, sums, dn)
    store_cells(dn, cells)

    @pl.when(last_step())
    def _():
        drain_cells(cells, g_out)
        finish_sums(sums, small_out)
        finish_sums(bsums, bias_out)


def per_image(shape):
    if len(shape) == 2:
        return whole(shape)
    rest = (0,) * (len(shape) - 1)
    return pl.BlockSpec((1,) + tuple(shape[1:]), lambda i: (i,) + rest)


def whole(shape):
    zeros = (0,) * len(shape)
    return pl.BlockSpec(tuple(shape), lambda i: zeros, pipeline_mode=pl.Buffered(1))


def one_layer(shape, layer):
    return pl.BlockSpec((1,) + tuple(shape[1:]), lambda i: (layer, 0, 0), pipeline_mode=pl.Buffered(1))


def cost(flops, arrays):
    size = sum(jnp.dtype(d).itemsize * functools.reduce(lambda p, q: p * q, s) for s, d in arrays)
    return pl.CostEstimate(flops=int(flops), bytes_accessed=int(size), transcendentals=0)


def params():
    return pltpu.CompilerParams(dimension_semantics=("arbitrary",), vmem_limit_bytes=VMEM_LIMIT)


def carrier(kernel, carry, ins, outs, scratch, refs):
    extra_in, extra_out = len(carry.args), len(carry.outs)
    base_in, refs = refs[:ins], refs[ins:]
    carry_in, refs = refs[:extra_in], refs[extra_in:]
    base_out, refs = refs[:outs], refs[outs:]
    carry_out, refs = refs[:extra_out], refs[extra_out:]
    base_scratch, carry_scratch = refs[:scratch], refs[scratch:]
    carry.run(carry_in, carry_out, carry_scratch)
    kernel(*base_in, *base_out, *base_scratch)
    carry.end(carry_in, carry_out, carry_scratch)


def image_call(kernel, name, layer, batched, lay, shared, outs, sums, scratch, flops, carry=None):
    images = next(a.shape[0] for a in batched if a.ndim > 2)
    ins = [per_image(a.shape) for a in batched] + [one_layer(lay.shape, layer)]
    args = list(batched) + [lay]
    for item in shared:
        if isinstance(item, tuple):
            ins.append(one_layer(item[0].shape, item[1]))
            args.append(item[0])
        else:
            ins.append(whole(item.shape))
            args.append(item)
    out_specs = [per_image(s) for s, _ in outs]
    out_specs += [pl.BlockSpec(tuple(s), lambda i: (0, 0)) for s, _ in sums]
    results = outs + sums
    buffers = [pltpu.VMEM(s, d) for s, d in scratch]
    options = params()
    body = kernel
    if carry is not None:
        counts = (len(args), len(results), len(scratch))

        def body(*refs):
            carrier(kernel, carry, *counts, refs)

        args = args + carry.args
        ins = ins + [pl.BlockSpec(memory_space=pl.ANY)] * len(carry.args)
        out_specs += [carry.out_spec or pl.BlockSpec(tuple(s), lambda i: (0, 0)) for s, _ in carry.outs]
        results = results + carry.outs
        buffers += carry.scratch
        options = pltpu.CompilerParams(
            dimension_semantics=("arbitrary",), vmem_limit_bytes=VMEM_LIMIT, collective_id=carry.ident,
            has_side_effects=True,
        )
    arrays = [(a.shape, a.dtype) for a in args] + results
    return pl.pallas_call(
        body,
        grid=(images,),
        in_specs=ins,
        out_specs=out_specs,
        out_shape=[jax.ShapeDtypeStruct(s, d) for s, d in results],
        scratch_shapes=buffers,
        compiler_params=options,
        cost_estimate=cost(flops, arrays),
        name=name,
    )(*args)


def token_mask(heights, widths):
    t = jnp.arange(4 * WTOK, dtype=jnp.int32)
    window = t // WTOK
    row = (window // 2) * WIN + (t % WTOK) // SUB
    col8 = t % SUB
    col = (window % 2) * WIN + col8
    valid = (row[None] < heights[:, None]) & (col[None] < widths[:, None]) & (col8 < WIN)[None]
    return jnp.broadcast_to(valid.astype(F32)[..., None], valid.shape + (LANES,))


def forward_window(inputs, mask, lay, sh, watt, carry=None):
    (rows, c), images, t = inputs.shape, mask.shape[0], mask.shape[1]
    outs = [
        ((images, t, c), BF16), ((images, t, c), F32), ((images, t, LANES), F32),
        ((images, t, 3 * c), BF16), ((images, t, c), BF16),
        ((images, 4, c // GROUP, WTOK, WTOK * GROUP // HD), BF16), ((images, t, c), F32),
    ]
    scratch = [((c // LANES, rows, LANES), F32), ((t, c), F32), ((t, c), F32), ((t, 3 * c), F32), ((t, c), F32)]
    return image_call(window_forward_kernel, "window_forward", 0, [inputs, mask], lay, [sh, watt],
                      outs, [], scratch, 10 * images * t * c * c, carry)


def forward_mlp(x, mask, lay, hid, w_in, w_out, carry=None):
    images, t, c = x.shape
    ff = w_in.shape[1]
    outs = [
        ((images, t, c), BF16), ((images, t, c), F32), ((images, t, LANES), F32),
        ((images, t, ff), BF16), ((images, t, ff), BF16), ((images, t, c), F32),
    ]
    scratch = [((t, c), F32), ((t, c), F32)]
    return image_call(mlp_forward_kernel, "mlp_forward", 1, [x, mask], lay, [(hid, 0), w_in, w_out],
                      outs, [], scratch, 4 * images * t * c * ff, carry)


def forward_channel(x, mask, lay, sh, watt, carry=None):
    images, t, c = x.shape
    outs = [
        ((images, t, c), BF16), ((images, t, c), F32), ((images, t, LANES), F32),
        ((images, t, 3 * c), BF16), ((images, t, c), BF16),
        ((images, c // GROUP, GROUP, GROUP), BF16), ((images, t, c), F32),
    ]
    return image_call(channel_forward_kernel, "channel_forward", 2, [x, mask], lay, [sh, watt],
                      outs, [], [((t, c), F32)], 9 * images * t * c * c, carry)


def last_mlp(x, cot, mask, lay, hid, w_in, w_out):
    images, t, c = x.shape
    ff = w_in.shape[1]
    outs = [
        (cot.shape, BF16), ((images, t, c), F32), ((images, t, c), BF16), ((images, t, ff), BF16),
        ((images, t, c), BF16), ((images, t, ff), BF16),
    ]
    scratch = [
        ((c // LANES, cot.shape[0], LANES), F32), ((t, c), F32), ((t, c), F32), ((t, LANES), F32), ((t, c), F32),
        ((t, c), F32), ((t, c), F32), ((16 * SUB, c), F32), ((SUB, ff), F32),
    ]
    return image_call(last_mlp_kernel, "last_mlp", 3, [x, cot, mask], lay, [(hid, 1), w_in, w_out],
                      outs, [((16, c), F32), ((1, ff), F32)], scratch, 8 * images * t * c * ff)


def backward_mlp(g, x, z, r, d, mask, lay, w_in, w_out, carry=None):
    images, t, c = x.shape
    ff = w_in.shape[1]
    outs = [((images, t, c), F32), ((images, t, c), BF16), ((images, t, ff), BF16)]
    scratch = [((t, c), F32), ((t, c), F32), ((16 * SUB, c), F32), ((SUB, ff), F32)]
    return image_call(mlp_backward_kernel, "mlp_backward", 1, [g, x, z, r, d, mask], lay, [w_in, w_out],
                      outs, [((16, c), F32), ((1, ff), F32)], scratch, 4 * images * t * c * ff, carry)


def backward_channel(g, x, z, r, q, a, mask, lay, watt, carry=None):
    images, t, c = x.shape
    outs = [((images, t, c), F32), ((images, t, c), BF16), ((images, t, 3 * c), BF16)]
    scratch = [((t, c), F32), ((t, c), F32), ((16 * SUB, c), F32), ((SUB, 3 * c), F32)]
    return image_call(channel_backward_kernel, "channel_backward", 2, [g, x, z, r, q, a, mask], lay, [watt],
                      outs, [((16, c), F32), ((1, 3 * c), F32)], scratch, 10 * images * t * c * c, carry)


def backward_window(g, inputs, z, r, q, p, mask, lay, watt, carry=None):
    images, t, c = g.shape
    outs = [(inputs.shape, BF16), ((images, t, c), BF16), ((images, t, 3 * c), BF16)]
    scratch = [
        ((c // LANES, inputs.shape[0], LANES), F32), ((t, c), F32), ((t, 3 * c), F32), ((t, c), F32),
        ((t, 3 * c), F32), ((t, c), F32), ((t, c), F32), ((16 * SUB, c), F32), ((SUB, 3 * c), F32),
    ]
    return image_call(window_backward_kernel, "window_backward", 0, [g, inputs, z, r, q, p, mask], lay, [watt],
                      outs, [((16, c), F32), ((1, 3 * c), F32)], scratch, 12 * images * t * c * c, carry)


def grad_pair_kernel(first, left0, right0, left1, right1, out0, out1):
    step = pl.program_id(0)

    @pl.when(step < first)
    def _():
        out0[...] = dot(left0[...], right0[...], DIMS_TN).astype(BF16)

    @pl.when(step >= first)
    def _():
        out1[...] = dot(left1[...], right1[...], DIMS_TN).astype(BF16)


def grad_pair(name, left0, right0, left1, right1):
    flat = [a.reshape(-1, a.shape[-1]) for a in (left0, right0, left1, right1)]
    rows, c = flat[0].shape
    first, second = flat[1].shape[1] // c, flat[3].shape[1] // c

    def at_first(i):
        return (0, jnp.minimum(i, first - 1))

    def at_second(i):
        return (0, jnp.maximum(i - first, 0))

    outs = [((c, flat[1].shape[1]), BF16), ((c, flat[3].shape[1]), BF16)]
    return pl.pallas_call(
        functools.partial(grad_pair_kernel, first),
        grid=(first + second,),
        in_specs=[
            whole((rows, c)), pl.BlockSpec((rows, c), at_first),
            whole((rows, c)), pl.BlockSpec((rows, c), at_second),
        ],
        out_specs=[pl.BlockSpec((c, c), at_first), pl.BlockSpec((c, c), at_second)],
        out_shape=[jax.ShapeDtypeStruct(s, d) for s, d in outs],
        compiler_params=params(),
        cost_estimate=cost(2 * rows * c * c * (first + second), [(a.shape, BF16) for a in flat] + outs),
        name=name,
    )(*flat)


WIDE = 8
NARROW = 4
BOTH = ("narrow", "wide")
MESH_ID = pl.DeviceIdType.MESH
RING = (0, 1, -1, 2, -2, 3, -3, 4)
AFAR = RING[::-1]
GATHER_STEPS = (((0,), ()), ((1, -1), (0,)), ((2, -2), (1, -1)), ((3, -3), (2, -2)), ((4,), (3, -3)), ((), (4,)))
REDUCE_STEPS = ((), (15, 11), (7, 14, 10), (3, 6, 13), (2, 9), (5, 12), (1, 8, 4), (0,))
STAGES = (0, 4, 8, 12, 1, 5, 9, 13, 2, 6, 10, 14, 3, 7, 11, 15)
CARRY_STEPS = 8


def whole_part(condition):
    return jnp.where(condition, jnp.int32(1), jnp.int32(0))


def place(order, ring, cross=0, core=0):
    n, w = lax.axis_index("narrow"), lax.axis_index("wide")
    z = whole_part(w >= 2) + whole_part(w >= 4) + whole_part(w >= 6)
    y = whole_part(n >= 2)
    x, c = w - 2 * z, n - 2 * y
    a, b = (x, y) if order == 0 else (y, x)
    if ring:
        at = z + a * (7 - 2 * z) + ring
        at = at - 8 * whole_part(at >= 8) if ring > 0 else at + 8 * whole_part(at < 0)
        a = whole_part(at >= 4)
        z = at + a * (7 - 2 * at)
    if cross:
        b = 1 - b
    if core:
        c = 1 - c
    x, y = (a, b) if order == 0 else (b, a)
    return {"narrow": 2 * y + c, "wide": 2 * z + x}


def chip(order, rel):
    n, w = lax.axis_index("narrow"), lax.axis_index("wide")
    z1 = whole_part(w >= 4)
    z0 = whole_part(w - 4 * z1 >= 2)
    y = whole_part(n >= 2)
    x, c = w - 4 * z1 - 2 * z0, n - 2 * y
    first, second = (4, 8) if order == 0 else (8, 4)
    bits = (1, 2, first, second, 16)
    z0, z1, x, y, c = (1 - v if rel & bit else v for v, bit in zip((z0, z1, x, y, c), bits))
    return {"narrow": 2 * y + c, "wide": 4 * z1 + 2 * z0 + x}


def highest(rel):
    return rel.bit_length() - 1


def number(ring, cross=0, core=0):
    return ring % 8 + 8 * cross + 16 * core


def ring_peers():
    return [place(0, 1), place(0, -1), place(1, 1), place(1, -1), place(0, 0, 1), place(1, 0, 1), place(0, 0, 0, 1)]


def chip_peers():
    return [chip(0, 1 << k) for k in range(5)]


def meet(peers):
    barrier = pltpu.get_barrier_semaphore()
    for at in peers:
        pl.semaphore_signal(barrier, inc=1, device_id=at, device_id_type=MESH_ID)
    pl.semaphore_wait(barrier, len(peers))


class Part:
    def __init__(self, operand, kind, shape, start, size, order):
        self.operand, self.kind, self.shape, self.start, self.size, self.order = operand, kind, shape, start, size, order

    def whole(self):
        rows, cols = self.shape
        return {
            "slot": (WIDE * NARROW, rows, cols), "in": (NARROW * rows, WIDE * cols), "out": (WIDE * rows, NARROW * cols),
        }[self.kind]

    def view(self, ref, n, w):
        rows, cols = self.shape
        if self.kind == "slot":
            return ref.at[n * WIDE + w, pl.ds(self.start, self.size), :]
        a, b = (n, w) if self.kind == "in" else (w, n)
        step = 16
        while step < 128 and rows % (2 * step) == 0 and self.start % (2 * step) == 0:
            step *= 2
        at = pl.multiple_of(a * rows + self.start, step)
        return ref.at[pl.ds(at, self.size), pl.ds(pl.multiple_of(b * cols, cols), cols)]

    def of(self, ref, *where):
        at = place(self.order, *where)
        return self.view(ref, at["narrow"], at["wide"])


    def of_chip(self, ref, rel):
        at = chip(self.order, rel)
        return self.view(ref, at["narrow"], at["wide"])


def halves(operand, kind, shape):
    low = shape[0] // 32 * 16
    return [Part(operand, kind, shape, 0, low, 0), Part(operand, kind, shape, low, shape[0] - low, 1)]


def pair(first, second, shape_in, shape_out):
    return [Part(first, "in", shape_in, 0, shape_in[0], 0), Part(second, "out", shape_out, 0, shape_out[0], 1)]


class Gather:
    def __init__(self, index, part, own, dest, sems):
        self.index, self.part, self.dest = index, part, dest
        self.own = own.at[pl.ds(part.start, part.size), :]
        self.send, self.recv, self.keep = sems

    def copy(self, ring, cross, step):
        target = self.part.of(self.dest, ring, cross)
        if step is None:
            to, slot = place(self.part.order, 0, 0, 1), number(ring, cross, 1)
        elif step == 0:
            to, slot = place(self.part.order, 0, 1), number(ring, 1)
        else:
            to, slot = place(self.part.order, step), number(ring - step)
        return pltpu.make_async_remote_copy(
            src_ref=self.own if ring == 0 and cross == 0 else target, dst_ref=target,
            send_sem=self.send.at[self.index, slot], recv_sem=self.recv.at[self.index, slot],
            device_id=to, device_id_type=MESH_ID,
        )

    def arrival(self, ring, cross=0, core=0):
        target = self.part.of(self.dest, ring, cross, core)
        return pltpu.make_async_remote_copy(
            src_ref=target, dst_ref=target, send_sem=self.send.at[self.index, 0],
            recv_sem=self.recv.at[self.index, number(ring, cross, core)], device_id=place(self.part.order, 1),
            device_id_type=MESH_ID,
        )

    def stay(self):
        return pltpu.make_async_copy(self.own, self.part.of(self.dest, 0), self.keep.at[self.index])

    def sends(self, ring):
        steps = []
        if 0 <= ring < 4:
            steps.append(-1)
        if -3 < ring <= 0:
            steps.append(1)
        return steps + [0, None]

    def stage(self, ring):
        if ring == 0:
            self.stay().start()
        else:
            self.arrival(ring).wait_recv()
        for step in self.sends(ring):
            self.copy(ring, 0, step).start()

    def crossed(self, ring):
        self.arrival(ring, 1).wait_recv()
        self.copy(ring, 1, None).start()

    def finish(self):
        for ring in RING:
            self.arrival(ring, 0, 1).wait_recv()
            self.arrival(ring, 1, 1).wait_recv()
        for ring in RING:
            for step in self.sends(ring):
                self.copy(ring, 0, step).wait_send()
            self.copy(ring, 1, None).wait_send()
        self.stay().wait()


def gather_step(items, rings, crosses):
    for ring in rings:
        for item in items:
            item.stage(ring)
    for ring in crosses:
        for item in items:
            item.crossed(ring)


def gather_sems(count):
    return [pltpu.SemaphoreType.DMA((count, 32)), pltpu.SemaphoreType.DMA((count, 32)), pltpu.SemaphoreType.DMA((count,))]


class Beside:
    def __init__(self, ident, args, parts, pick=None):
        self.ident, self.args, self.parts = ident, list(args), parts
        self.pick = pick or {}
        shapes = {p.operand: p.whole() for p in parts}
        self.outs = [(shapes[k], BF16) for k in range(len(self.args))]
        self.out_spec = pl.BlockSpec(memory_space=pl.ANY)
        self.scratch = gather_sems(len(parts))

    def items(self, ins, outs, scratch):
        ins = [ref.at[self.pick[k]] if k in self.pick else ref for k, ref in enumerate(ins)]
        return [Gather(i, p, ins[p.operand], outs[p.operand], scratch) for i, p in enumerate(self.parts)]

    def run(self, ins, outs, scratch):
        items = self.items(ins, outs, scratch)
        for s, (rings, crosses) in enumerate(GATHER_STEPS):

            @pl.when(pl.program_id(0) == s)
            def _(s=s, rings=rings, crosses=crosses):
                if s == 0:
                    meet(ring_peers())
                gather_step(items, rings, crosses)

    def end(self, ins, outs, scratch):
        @pl.when(last_step())
        def _():
            for item in self.items(ins, outs, scratch):
                item.finish()


PHASE_STEPS = ((0, 1, 2, 3, 4, 5), (4, 5, 7, 8, 9, 10), (8, 9, 11, 12, 14, 15))


def two_phase_kernel(plans, counts, *refs):
    ins, outs, refs = refs[: counts[0]], refs[counts[0] : counts[0] + counts[1]], refs[counts[0] + counts[1] :]
    x_in, mask, lay1, lay2, hb, w_in, w_out, sh, chan, first, second = ins
    n1, z1, r1, u1, d1, x4, n2, z2, r2, q2, o2, a2, x6, watt, got, in1, out1 = outs
    x1, acc, xs, stage, sem, refs = *refs[:5], refs[5:]
    step = pl.program_id(0)
    sets = []
    for i, (plan, own, dest) in enumerate(zip(plans, (chan, first, second), (got, in1, out1))):
        sets.append(plan.items([own], [dest], refs[3 * i : 3 * i + 3]))
    for s in range(2 * CARRY_STEPS):
        due = [(items, steps.index(s)) for items, steps in zip(sets, PHASE_STEPS) if s in steps]

        @pl.when(step == s)
        def _(s=s, due=due):
            if s == 0:
                meet(ring_peers())
            for items, k in due:
                gather_step(items, *GATHER_STEPS[k])
            if s == CARRY_STEPS:
                for item in sets[0]:
                    item.finish()
                copy = pltpu.make_async_copy(got, stage, sem.at[0])
                copy.start()
                copy.wait()
                cn = chan.shape[0]
                for n in range(NARROW):
                    copy_attention(stage.at[pl.ds(n * WIDE, WIDE)], 0, watt.at[pl.ds(n * cn, cn)])

    @pl.when(step < CARRY_STEPS)
    def _():
        mlp_forward_kernel(x_in, mask, lay1, hb, w_in, w_out, n1, z1, r1, u1, d1, x4, x1, acc)
        xs[pl.ds(step, 1)] = x4[...]

    @pl.when(step >= CARRY_STEPS)
    def _():
        x = xs.at[pl.ds(step - CARRY_STEPS, 1)]
        channel_forward_kernel(x, mask, lay2, sh, watt, n2, z2, r2, q2, o2, a2, x6, x1)

    @pl.when(last_step())
    def _():
        for items in sets[1:]:
            for item in items:
                item.finish()


def forward_two(ident, x, mask, lay, hid, w_in, w_out, sh, chan, first, second):
    images, t, c = x.shape
    ff = w_in.shape[1]
    plans = [
        Beside(ident, [chan], halves(0, "slot", chan.shape)),
        Beside(ident, [first], halves(0, "in", first.shape[1:]), {0: 1}),
        Beside(ident, [second], halves(0, "out", second.shape[1:]), {0: 1}),
    ]

    def before(shape):
        rest = (0,) * (len(shape) - 1)
        return pl.BlockSpec((1,) + tuple(shape[1:]), lambda i: (jnp.minimum(i, images - 1),) + rest)

    def after(shape):
        rest = (0,) * (len(shape) - 1)
        return pl.BlockSpec((1,) + tuple(shape[1:]), lambda i: (jnp.maximum(i - images, 0),) + rest)

    each = pl.BlockSpec((1, t, LANES), lambda i: (lax.rem(i, images), 0, 0))
    anywhere = pl.BlockSpec(memory_space=pl.ANY)
    args = [x, mask, lay, lay, hid, w_in, w_out, sh, chan, first, second]
    in_specs = [
        before(x.shape), each, one_layer(lay.shape, 1), one_layer(lay.shape, 2), one_layer(hid.shape, 0),
        whole(w_in.shape), whole(w_out.shape), whole(sh.shape), anywhere, anywhere, anywhere,
    ]
    low = [
        ((images, t, c), BF16), ((images, t, c), F32), ((images, t, LANES), F32), ((images, t, ff), BF16),
        ((images, t, ff), BF16), ((images, t, c), F32),
    ]
    high = [
        ((images, t, c), BF16), ((images, t, c), F32), ((images, t, LANES), F32), ((images, t, 3 * c), BF16),
        ((images, t, c), BF16), ((images, c // GROUP, GROUP, GROUP), BF16), ((images, t, c), F32),
    ]
    outs = low + high + [((c, 4 * c), BF16)] + [o for plan in plans for o in plan.outs]
    out_specs = [before(s) for s, _ in low] + [after(s) for s, _ in high] + [whole((c, 4 * c))] + [anywhere] * 3
    scratch = [
        pltpu.VMEM((t, c), F32), pltpu.VMEM((t, c), F32), pltpu.VMEM((images, t, c), F32),
        pltpu.VMEM(plans[0].outs[0][0], BF16), pltpu.SemaphoreType.DMA((1,)),
    ]
    scratch += [item for plan in plans for item in plan.scratch]
    return pl.pallas_call(
        functools.partial(two_phase_kernel, plans, (len(args), len(outs))),
        grid=(2 * images,),
        in_specs=in_specs,
        out_specs=out_specs,
        out_shape=[jax.ShapeDtypeStruct(s, d) for s, d in outs],
        scratch_shapes=scratch,
        compiler_params=pltpu.CompilerParams(
            dimension_semantics=("arbitrary",), vmem_limit_bytes=VMEM_LIMIT, collective_id=ident, has_side_effects=True,
        ),
        cost_estimate=cost(4 * images * t * c * ff + 9 * images * t * c * c, [(a.shape, a.dtype) for a in args] + outs),
        name="mlp_channel_forward",
    )(*args)


class Reduce:
    def __init__(self, index, part, src, out, bufs, sems):
        self.index, self.part, self.src, self.out = index, part, src, out
        self.acc, self.mate, self.inbox = bufs
        self.load_sem, self.send_sem, self.mate_sem, self.recv_sem = sems

    def load(self, rel):
        return pltpu.make_async_copy(self.part.of_chip(self.src, rel), self.acc.at[rel], self.load_sem.at[self.index, rel])

    def to_mate(self, rel):
        return pltpu.make_async_remote_copy(
            src_ref=self.part.of_chip(self.src, rel | 16), dst_ref=self.mate.at[rel],
            send_sem=self.send_sem.at[self.index, 16 + rel], recv_sem=self.mate_sem.at[self.index, rel],
            device_id=chip(self.part.order, 16), device_id_type=MESH_ID,
        )

    def onward(self, rel):
        return pltpu.make_async_remote_copy(
            src_ref=self.acc.at[rel], dst_ref=self.inbox.at[rel - 1], send_sem=self.send_sem.at[self.index, rel],
            recv_sem=self.recv_sem.at[self.index, rel], device_id=chip(self.part.order, 1 << highest(rel)),
            device_id_type=MESH_ID,
        )

    def begin(self, rel):
        self.to_mate(rel).start()
        self.load(rel).start()

    def stage(self, rel):
        self.load(rel).wait()
        self.to_mate(rel).wait_recv()
        total = self.acc[rel].astype(F32) + self.mate[rel].astype(F32)
        for axis in range(highest(rel) + 1, 4):
            came = rel | (1 << axis)
            self.onward(came).wait_recv()
            total = total + self.inbox[came - 1].astype(F32)
        if rel == 0:
            self.out[pl.ds(self.part.start, self.part.size), :] = total
        else:
            self.acc[rel] = total.astype(BF16)
            self.onward(rel).start()

    def finish(self):
        for rel in range(16):
            self.to_mate(rel).wait_send()
            if rel:
                self.onward(rel).wait_send()


class Behind:
    def __init__(self, ident, args, parts):
        self.ident, self.args, self.parts = ident, list(args), parts
        shapes = {p.operand: p.shape for p in parts}
        self.outs = [(shapes[k], F32) for k in range(len(self.args))]
        self.out_spec = None
        self.scratch = []
        for p in parts:
            block = (p.size, p.shape[1])
            self.scratch += [pltpu.VMEM((16,) + block, BF16), pltpu.VMEM((16,) + block, BF16), pltpu.VMEM((15,) + block, BF16)]
        count = len(parts)
        self.scratch += [
            pltpu.SemaphoreType.DMA((count, 16)), pltpu.SemaphoreType.DMA((count, 32)),
            pltpu.SemaphoreType.DMA((count, 16)), pltpu.SemaphoreType.DMA((count, 16)),
        ]

    def items(self, ins, outs, scratch):
        bufs, sems = scratch[: 3 * len(self.parts)], scratch[3 * len(self.parts) :]
        return [
            Reduce(i, p, ins[p.operand], outs[p.operand], bufs[3 * i : 3 * i + 3], sems)
            for i, p in enumerate(self.parts)
        ]

    def run(self, ins, outs, scratch):
        items = self.items(ins, outs, scratch)
        for s, rels in enumerate(REDUCE_STEPS):

            @pl.when(pl.program_id(0) == s)
            def _(s=s, rels=rels):
                if s == 0:
                    meet(chip_peers())
                    for rel in reversed(STAGES):
                        for item in items:
                            item.begin(rel)
                for rel in rels:
                    for item in items:
                        item.stage(rel)

    def end(self, ins, outs, scratch):
        @pl.when(last_step())
        def _():
            for item in self.items(ins, outs, scratch):
                item.finish()


def reduce_kernel(plan, *refs):
    ins, refs = refs[: len(plan.args)], refs[len(plan.args) :]
    outs, scratch = refs[: len(plan.outs)], refs[len(plan.outs) :]
    items = plan.items(ins, outs, scratch)
    meet(chip_peers())
    for rel in reversed(STAGES):
        for item in items:
            item.begin(rel)
    for rel in reversed(STAGES):
        for item in items:
            item.stage(rel)
    for item in items:
        item.finish()


def reduce_now(name, plan):
    return pl.pallas_call(
        functools.partial(reduce_kernel, plan),
        in_specs=[pl.BlockSpec(memory_space=pl.ANY)] * len(plan.args),
        out_specs=[pl.BlockSpec(memory_space=pltpu.VMEM)] * len(plan.outs),
        out_shape=[jax.ShapeDtypeStruct(s, d) for s, d in plan.outs],
        scratch_shapes=plan.scratch,
        compiler_params=pltpu.CompilerParams(
            collective_id=plan.ident, has_side_effects=True, vmem_limit_bytes=VMEM_LIMIT
        ),
        cost_estimate=cost(0, [(a.shape, a.dtype) for a in plan.args]),
        name=name,
    )(*plan.args)


def copy_attention(src, start, dst):
    cn = dst.shape[0]
    cw = src.shape[2] // 4
    c = WIDE * cw
    for w in range(WIDE):
        dst[:, pl.ds(3 * cw * w, 3 * cw)] = src[w, pl.ds(start, cn), pl.ds(0, 3 * cw)]
        dst[:, pl.ds(3 * c + cw * w, cw)] = src[w, pl.ds(start, cn), pl.ds(3 * cw, cw)]


def unpack_first_kernel(got, heights, widths, watt, lay, sh, hid, mask):
    copy_attention(got, 16, watt)
    cw = got.shape[2] // 4
    for w in range(WIDE):
        lay[0, :, pl.ds(cw * w, cw)] = got[w, pl.ds(0, 16), pl.ds(0, cw)].astype(F32)

    @pl.when(pl.program_id(0) == 0)
    def _():
        for w in range(WIDE):
            part = got[w, pl.ds(0, 16), pl.ds(LANES, cw)].astype(F32)
            sh[:, pl.ds(cw * w, cw)] = part
            for j in range(2):
                for q in range(4):
                    row = 5 + 4 * j + q
                    hid[j, :, pl.ds(4 * cw * w + cw * q, cw)] = part[row : row + 1]

    @pl.when(pl.program_id(0) == 1)
    def _():
        t = lax.broadcasted_iota(jnp.int32, mask.shape[1:], 0)
        window = whole_part(t >= WTOK) + whole_part(t >= 2 * WTOK) + whole_part(t >= 3 * WTOK)
        rest = t - window * WTOK
        low = lax.shift_right_logical(rest, 3)
        col8 = rest - low * SUB
        lower = whole_part(window >= 2)
        row = lower * WIN + low
        col = (window - 2 * lower) * WIN + col8
        for i in range(mask.shape[0]):
            valid = (row < heights[i]) & (col < widths[i]) & (col8 < WIN)
            mask[i] = jnp.where(valid, 1.0, 0.0)


def unpack_first(got, heights, widths):
    rows, lanes = got.shape[1:]
    c = 2 * lanes
    cn = c // NARROW
    images = heights.shape[0]
    outs = [
        ((c, 4 * c), BF16), ((NARROW, 16, c), F32), ((16, c), F32), ((2, 1, 4 * c), F32), ((images, 4 * WTOK, LANES), F32),
    ]
    return pl.pallas_call(
        unpack_first_kernel,
        grid=(NARROW,),
        in_specs=[pl.BlockSpec((WIDE, rows, lanes), lambda n: (n, 0, 0))] + [pl.BlockSpec(memory_space=pltpu.SMEM)] * 2,
        out_specs=[
            pl.BlockSpec((cn, 4 * c), lambda n: (n, 0)), pl.BlockSpec((1, 16, c), lambda n: (n, 0, 0)),
            pl.BlockSpec((16, c), lambda n: (0, 0)), pl.BlockSpec((2, 1, 4 * c), lambda n: (0, 0, 0)),
            pl.BlockSpec((images, 4 * WTOK, LANES), lambda n: (0, 0, 0)),
        ],
        out_shape=[jax.ShapeDtypeStruct(s, d) for s, d in outs],
        compiler_params=params(),
        cost_estimate=cost(0, [(got.shape, BF16)] + outs),
        name="unpack_first",
    )(got, heights, widths)


def grad_attention_kernel(start, left0, right0, left1, right1, *refs):
    *head, out, result = refs[:-1] if len(refs) > 2 else refs
    step = pl.program_id(0)
    c = right0.shape[1]
    cn, cw = c // NARROW, c // WIDE

    def spread(s, w, low, high):
        for n in range(NARROW):
            at = pl.ds(low - 3 * cw * w, high - low)
            out[n * WIDE + w, pl.ds(start, cn), at] = result[pl.ds(cn * n, cn), pl.ds(low - c * s, high - low)]

    for s in range(4):

        @pl.when(step == s)
        def _(s=s):
            if s < 3:
                result[...] = dot(left0[...], right0[...], DIMS_TN).astype(BF16)
                for w in range(WIDE):
                    low, high = max(3 * cw * w, c * s), min(3 * cw * (w + 1), c * (s + 1))
                    if low < high:
                        spread(s, w, low, high)
            else:
                result[...] = dot(left1[...], right1[...], DIMS_TN).astype(BF16)
                for w in range(WIDE):
                    for n in range(NARROW):
                        at = pl.ds(3 * cw, cw)
                        out[n * WIDE + w, pl.ds(start, cn), at] = result[pl.ds(cn * n, cn), pl.ds(cw * w, cw)]
                if head:
                    pack_small(*head, out, refs[-1])


def pack_small(small0, small1, small2, small3, sb, cb, hid0, hid1, out, shared):
    smalls = (small0, small1, small2, small3)
    c = small0.shape[1]
    cw = c // WIDE
    shared[...] = jnp.zeros_like(shared)
    shared[pl.ds(0, 1), :] = sb[:, pl.ds(0, c)]
    shared[pl.ds(1, 1), :] = sb[:, pl.ds(2 * c, c)]
    for k in range(3):
        shared[pl.ds(2 + k, 1), :] = cb[:, pl.ds(k * c, c)]
    for j, hid in enumerate((hid0, hid1)):
        for w in range(WIDE):
            for q in range(4):
                shared[pl.ds(5 + 4 * j + q, 1), pl.ds(cw * w, cw)] = hid[:, pl.ds(4 * cw * w + cw * q, cw)]
    out[:, pl.ds(0, 16), :] = jnp.zeros((WIDE * NARROW, 16, out.shape[2]), BF16)
    for w in range(WIDE):
        for n in range(NARROW):
            out[n * WIDE + w, pl.ds(0, 16), pl.ds(0, cw)] = smalls[n][:, pl.ds(cw * w, cw)].astype(BF16)
            out[n * WIDE + w, pl.ds(0, 16), pl.ds(LANES, cw)] = shared[:, pl.ds(cw * w, cw)].astype(BF16)


def grad_attention(name, left0, right0, left1, right1, head=()):
    flat = [a.reshape(-1, a.shape[-1]) for a in (left0, right0, left1, right1)]
    rows, c = flat[0].shape
    cn = c // NARROW
    start = 16 if head else 0
    shape = (WIDE * NARROW, start + cn, c // 2)
    scratch = [pltpu.VMEM((c, c), BF16)] + ([pltpu.VMEM((16, c), F32)] if head else [])
    return pl.pallas_call(
        functools.partial(grad_attention_kernel, start),
        grid=(4,),
        in_specs=[
            whole((rows, c)), pl.BlockSpec((rows, c), lambda i: (0, jnp.minimum(i, 2))), whole((rows, c)), whole((rows, c)),
        ] + [whole(a.shape) for a in head],
        out_specs=pl.BlockSpec(shape, lambda i: (0, 0, 0)),
        out_shape=jax.ShapeDtypeStruct(shape, BF16),
        scratch_shapes=scratch,
        compiler_params=params(),
        cost_estimate=cost(8 * rows * c * c, [(a.shape, BF16) for a in flat] + [(shape, BF16)]),
        name=name,
    )(*flat, *head)


def attention_piece(qkv, proj):
    return jnp.concatenate([qkv.T, proj.T], axis=1)


def turned(value):
    return value.astype(F32).T.astype(BF16)


def gather_first_kernel(
    plan, conv_weight, conv_bias, norm_gain, norm_bias, qkv0, qkv1, proj, attn_bias, hidden_bias, out_bias,
    got, chan, piece, *sems,
):
    cw = conv_bias.shape[1]
    cn = qkv0.shape[1]
    piece[pl.ds(0, 16), :] = jnp.zeros((16, piece.shape[1]), BF16)
    taps_now = conv_weight[0].astype(F32)
    rows = [taps_now] + [r[...].astype(F32) for r in (conv_bias, norm_gain, norm_bias, out_bias)]
    rows.append(jnp.zeros((3, cw), F32))
    piece[pl.ds(0, 16), pl.ds(0, cw)] = jnp.concatenate(rows, axis=0).astype(BF16)
    hidden = hidden_bias[...].astype(F32)
    rows = [attn_bias[...].astype(F32)]
    rows += [hidden[j : j + 1, cw * q : cw * (q + 1)] for j in range(2) for q in range(4)]
    rows.append(jnp.zeros((3, cw), F32))
    piece[pl.ds(0, 16), pl.ds(LANES, cw)] = jnp.concatenate(rows, axis=0).astype(BF16)
    piece[pl.ds(16, cn), pl.ds(0, 3 * cw)] = turned(qkv0[...])
    piece[pl.ds(16, cn), pl.ds(3 * cw, cw)] = turned(proj[0])
    items = plan.items([piece], [got], sems)
    meet(ring_peers())
    gather_step(items, (0,), ())
    chan[:, pl.ds(0, 3 * cw)] = turned(qkv1[...])
    chan[:, pl.ds(3 * cw, cw)] = turned(proj[1])
    for rings, crosses in GATHER_STEPS[1:]:
        gather_step(items, rings, crosses)
    for item in items:
        item.finish()


def gather_first(p):
    rows, cn = p["spatial_qkv"].shape
    lanes = rows * 4 // 3
    shape = (16 + cn, lanes)
    plan = Beside(1, [None], halves(0, "slot", shape))
    outs = plan.outs + [((cn, lanes), BF16)]
    args = [p[k] for k in NAMES if not k.startswith("mlp")]
    vmem = pl.BlockSpec(memory_space=pltpu.VMEM)
    return pl.pallas_call(
        functools.partial(gather_first_kernel, plan),
        in_specs=[vmem] * len(args),
        out_specs=[plan.out_spec, vmem],
        out_shape=[jax.ShapeDtypeStruct(s, d) for s, d in outs],
        scratch_shapes=[pltpu.VMEM(shape, BF16)] + plan.scratch,
        compiler_params=pltpu.CompilerParams(collective_id=1, has_side_effects=True, vmem_limit_bytes=VMEM_LIMIT),
        cost_estimate=cost(0, outs),
        name="gather_first",
    )(*args)


def finish_kernel(
    att0, att1, in0, in1, out0, out1,
    conv_weight, conv_bias, norm_gain, norm_bias, qkv0, qkv1, proj, mlp_in, mlp_out, attn_bias, hidden_bias, out_bias,
):
    cw = conv_bias.shape[1]
    cn = qkv0.shape[1]
    for k in range(9):
        conv_weight[k] = att0[pl.ds(k, 1), pl.ds(0, cw)]
    for k, row in enumerate((conv_bias, norm_gain, norm_bias, out_bias)):
        row[...] = att0[pl.ds(9 + k, 1), pl.ds(0, cw)]
    attn_bias[...] = att0[pl.ds(0, 5), pl.ds(LANES, cw)]
    for j in range(2):
        for q in range(4):
            hidden_bias[pl.ds(j, 1), pl.ds(cw * q, cw)] = att0[pl.ds(5 + 4 * j + q, 1), pl.ds(LANES, cw)]
    qkv0[...] = att0[pl.ds(16, cn), pl.ds(0, 3 * cw)].T
    proj[0] = att0[pl.ds(16, cn), pl.ds(3 * cw, cw)].T
    qkv1[...] = att1[:, pl.ds(0, 3 * cw)].T
    proj[1] = att1[:, pl.ds(3 * cw, cw)].T
    mlp_in[0] = in0[...]
    mlp_in[1] = in1[...]
    mlp_out[0] = out0[...]
    mlp_out[1] = out1[...]


def finish(*reduced):
    att0 = reduced[0]
    cn, lanes = att0.shape[0] - 16, att0.shape[1]
    cw = lanes // 4
    row = (1, cw)
    shapes = [
        (9, 1, cw), row, row, row, (3 * cw, cn), (3 * cw, cn), (2, cw, cn), (2, cn, lanes), (2, cw, 2 * lanes),
        (5, cw), (2, lanes), row,
    ]
    vmem = pl.BlockSpec(memory_space=pltpu.VMEM)
    outs = pl.pallas_call(
        finish_kernel,
        in_specs=[vmem] * 6,
        out_specs=[vmem] * len(shapes),
        out_shape=[jax.ShapeDtypeStruct(s, F32) for s in shapes],
        compiler_params=pltpu.CompilerParams(vmem_limit_bytes=VMEM_LIMIT),
        cost_estimate=cost(0, [(s, F32) for s in shapes]),
        name="finish",
    )(*reduced)
    outs = list(outs)
    outs[0] = outs[0].transpose(1, 0, 2)
    outs[7] = outs[7].transpose(0, 2, 1)
    return outs


class Direct:
    def __init__(self, p, heights, widths):
        got, self.chan = gather_first(p)
        self.first, self.second = p["mlp_in"].transpose(0, 2, 1), p["mlp_out"]
        watt0, self.lay, self.sh, self.hid, self.mask = unpack_first(got, heights, widths)
        self.watt, self.w_in, self.w_out = [watt0, None], [None, None], [None, None]

    def forward_window(self, *args):
        parts = pair(0, 1, self.first.shape[1:], self.second.shape[1:])
        carry = Beside(3, [self.first, self.second], parts, {0: 0, 1: 0})
        *outs, self.w_in[0], self.w_out[0] = forward_window(*args, carry=carry)
        return outs

    def forward_two(self, *args):
        *outs, self.watt[1], _, self.w_in[1], self.w_out[1] = forward_two(
            4, *args, self.sh, self.chan, self.first, self.second)
        return outs

    def backward_channel(self, grads, *args):
        self.go1 = grads[1]
        parts = halves(0, "in", self.first.shape[1:])
        *outs, self.gi1 = backward_channel(*args, carry=Behind(6, grads[:1], parts))
        return outs

    def channel_grads(self, *args):
        return grad_attention("channel_grads", *args)

    def backward_mlp(self, grads, *args):
        self.att1 = grads
        parts = halves(0, "out", self.second.shape[1:])
        *outs, self.go1 = backward_mlp(*args, carry=Behind(7, [self.go1], parts))
        return outs

    def backward_window(self, grads, *args):
        parts = pair(0, 1, self.first.shape[1:], self.second.shape[1:]) + halves(2, "slot", self.chan.shape)
        *outs, self.gi0, self.go0, self.att1 = backward_window(*args, carry=Behind(8, list(grads) + [self.att1], parts))
        return outs

    def reduce_last(self, grads, smalls, sb, cb, hid0, hid1):
        packed = grad_attention("window_grads", *grads, (*smalls, sb, cb, hid0, hid1))
        (att0,) = reduce_now("reduce_last", Behind(2, [packed], halves(0, "slot", packed.shape[1:])))
        return tuple(finish(att0, self.att1, self.gi0, self.gi1, self.go0, self.go1))


class Plain:
    def __init__(self, p, heights, widths):
        self.mask = token_mask(heights, widths)
        self.layers, self.cw = p["conv_bias"].shape
        wide = p["attn_bias"].shape
        self.narrow = 4 // self.layers
        self.cn = p["spatial_qkv"].shape[1]
        self.c = self.cn * self.narrow
        self.wide = self.c // self.cw
        self.fw = p["hidden_bias"].shape[1]
        c, cn, cw, fw, n, w = self.c, self.cn, self.cw, self.fw, self.narrow, self.wide

        def spread(v):
            return lax.all_gather(v, BOTH, axis=0, tiled=False).reshape((n, w) + v.shape)

        def attention(qkv, proj):
            got = spread(attention_piece(qkv, proj)).transpose(0, 2, 1, 3)
            return jnp.concatenate([got[..., : 3 * cw].reshape(c, 3 * c), got[..., 3 * cw :].reshape(c, c)], axis=1)

        self.watt = tuple(attention(p[k], p["projection"][i]) for i, k in enumerate(("spatial_qkv", "channel_qkv")))
        self.w_in = tuple(spread(p["mlp_in"][i].T).transpose(0, 2, 1, 3).reshape(c, -1) for i in range(2))
        self.w_out = tuple(spread(p["mlp_out"][i]).transpose(1, 2, 0, 3).reshape(c, -1) for i in range(2))

        def layer(v):
            return spread(v).transpose(0, 2, 3, 1, 4).reshape(4, -1, c)

        rows = [layer(p["conv_weight"])]
        rows += [layer(p[k][:, None]) for k in ("conv_bias", "norm_gain", "norm_bias", "out_bias")]
        self.lay = jnp.pad(jnp.concatenate(rows, axis=1).astype(F32), ((0, 0), (0, 3), (0, 0)))
        attn = spread(p["attn_bias"])[0].transpose(1, 0, 2).reshape(5, c)
        self.sh = jnp.pad(attn.astype(F32), ((0, 11), (0, 0)))
        self.hid = spread(p["hidden_bias"])[0].transpose(1, 0, 2).reshape(2, 1, -1).astype(F32)

    def forward_window(self, *args):
        return forward_window(*args)

    def forward_two(self, x, mask, lay, hid, w_in, w_out):
        low = forward_mlp(x, mask, lay, hid, w_in, w_out)
        return list(low) + list(forward_channel(low[-1], mask, lay, self.sh, self.watt[1]))

    def backward_channel(self, grads, *args):
        self.mlp1 = (self.matrix(grads[0], False), self.matrix(grads[1], True))
        return backward_channel(*args)

    def backward_mlp(self, grads, *args):
        self.att1 = (self.matrix(grads[0], False), self.matrix(grads[1], False))
        return backward_mlp(*args)

    def backward_window(self, grads, *args):
        self.mlp0 = (self.matrix(grads[0], False), self.matrix(grads[1], True))
        return backward_window(*args)

    def channel_grads(self, *args):
        return grad_pair("channel_grads", *args)

    def matrix(self, grad, rows_wide):
        n, w = self.narrow, self.wide
        a, b = (w, n) if rows_wide else (n, w)
        grad = grad.reshape(a, grad.shape[0] // a, b, grad.shape[1] // b)
        grad = grad.transpose(2, 0, 1, 3) if rows_wide else grad.transpose(0, 2, 1, 3)
        grad = grad.astype(BF16).reshape(n * w * grad.shape[2], grad.shape[3])
        return lax.psum_scatter(grad, BOTH, scatter_dimension=0, tiled=True).astype(F32)

    def reduce_last(self, grads, smalls, sb, cb, hid0, hid1):
        c, cw, fw, n, w = self.c, self.cw, self.fw, self.narrow, self.wide
        grads = grad_pair("window_grads", *grads)
        first = (self.matrix(grads[0], False), self.matrix(grads[1], False)) + self.mlp0
        rest = self.att1 + self.mlp1
        small = jnp.stack(smalls).reshape(n, self.layers * 16, w, cw).transpose(0, 2, 1, 3)
        attn = jnp.concatenate([sb[:, :c], sb[:, 2 * c :], cb.reshape(3, c)]).reshape(5, w, cw).transpose(1, 0, 2)
        hid = jnp.concatenate([hid0, hid1]).reshape(2, w, fw).transpose(1, 0, 2).reshape(w, -1, cw)
        common = jnp.concatenate([attn, hid], axis=1)
        common = jnp.broadcast_to(common[None], (n,) + common.shape)
        flat = jnp.concatenate([small, common], axis=2).astype(BF16).reshape(-1, cw)
        got = lax.psum_scatter(flat, BOTH, scatter_dimension=0, tiled=True).astype(F32)
        small = got[: self.layers * 16].reshape(self.layers, 16, cw)
        shared = got[self.layers * 16 :]
        return (
            small[:, :9], small[:, 9], small[:, 10], small[:, 11], first[0].T, rest[0].T,
            jnp.stack([first[1].T, rest[1].T]), jnp.stack([first[2].T, rest[2].T]), jnp.stack([first[3], rest[3]]),
            shared[:5], shared[5:].reshape(2, fw), small[:, 12],
        )


NAMES = (
    "conv_weight", "conv_bias", "norm_gain", "norm_bias", "spatial_qkv", "channel_qkv", "projection", "mlp_in",
    "mlp_out", "attn_bias", "hidden_bias", "out_bias",
)


def local(plan, inputs, heights, widths, *rest):
    if inputs.shape[0] != CARRY_STEPS:
        plan = Plain
    weights = plan(dict(zip(NAMES, rest[:-1])), heights, widths)
    cotangent = rest[-1]
    lay, sh, hid = weights.lay, weights.sh, weights.hid
    mask = weights.mask
    inputs, cotangent = cells_first(inputs), cells_first(cotangent)
    n1, z1, r1, q1, o1, p1, x2 = weights.forward_window(inputs, mask, lay, sh, weights.watt[0])
    n2, z2, r2, u1, d1, x4, n3, z3, r3, q3, o3, a3, x6 = weights.forward_two(
        x2, mask, lay, hid, weights.w_in[0], weights.w_out[0])
    out, g6, n4, u2, gy2, gh2, small3, hid1 = last_mlp(
        x6, cotangent, mask, lay, hid, weights.w_in[1], weights.w_out[1])
    grads = grad_pair("last_mlp_grads", n4, gh2, gy2, u2)
    g4, ga3, dq3, small2, cb = weights.backward_channel(
        grads, g6, x4, z3, r3, q3, a3, mask, lay, weights.watt[1])
    grads = weights.channel_grads(n3, dq3, o3, ga3)
    g2, gy1, gh1, small1, hid0 = weights.backward_mlp(
        grads, g4, x2, z2, r2, d1, mask, lay, weights.w_in[0], weights.w_out[0])
    grads = grad_pair("mlp_grads", n2, gh1, gy1, u1)
    input_grad, ga1, dq1, small0, sb = weights.backward_window(
        grads, g2, inputs, z1, r1, q1, p1, mask, lay, weights.watt[0])
    last = weights.reduce_last((n1, dq1, o1, ga1), (small0, small1, small2, small3), sb, cb, hid0, hid1)
    return (images_first(out), images_first(input_grad)) + tuple(last)


def solution(mesh):
    matrix = P("wide", "narrow")
    cells = P(("wide", "narrow"), None, None, None)
    stacked = P(None, "wide", "narrow")
    row = P("narrow", "wide")
    shared = P(None, "wide")
    images = P(("wide", "narrow"))
    kernels = P("narrow", None, "wide")
    in_specs = (
        cells, images, images, kernels, row, row, row, matrix, matrix,
        stacked, stacked, stacked, shared, shared, row, cells,
    )
    out_specs = (
        cells, cells, kernels, row, row, row, matrix, matrix, stacked, stacked, stacked, shared, shared, row,
    )
    plan = Direct if (mesh.shape["wide"], mesh.shape["narrow"]) == (WIDE, NARROW) else Plain
    body = functools.partial(local, plan)
    return jax.shard_map(body, mesh=mesh, in_specs=in_specs, out_specs=out_specs, check_vma=False)
```

```python
import functools

import jax
import jax.numpy as jnp
from jax import lax
from jax.experimental import pallas as pl
from jax.experimental.pallas import tpu as pltpu
from jax.sharding import PartitionSpec as P

HD = 32
WIN = 7
LANES = 128
SUB = 8
GROUP = 256
WTOK = WIN * SUB
FFC = 1024
NROWS = 112
SCALE = HD ** (-0.5)
EPS = 1e-05
NEG = -1e30
F32 = jnp.float32
BF16 = jnp.bfloat16
VMEM_LIMIT = 60 * 1024 * 1024
DIMS_NN = (((1,), (0,)), ((), ()))
DIMS_NT = (((1,), (1,)), ((), ()))
DIMS_TN = (((0,), (0,)), ((), ()))


def dot(a, b, dims):
    return lax.dot_general(a, b, dims, preferred_element_type=F32)


def tok(r, half):
    return ((r // WIN) * 2 + half) * WTOK + (r % WIN) * SUB


def fill_cells(src, cells):
    for j in range(cells.shape[0]):
        cells[j] = src[:, pl.ds(j * LANES, LANES)].astype(F32)


def drain_cells(cells, dst):
    for j in range(cells.shape[0]):
        dst[:, pl.ds(j * LANES, LANES)] = cells[j].astype(BF16)


def cell_rows(cells, r, half):
    images = cells.shape[1] // (4 * WIN * WIN)
    start = (r * 2 * WIN + WIN * half) * images
    if images == 1:
        return pl.ds(start, WIN)
    return pl.ds(start + pl.program_id(0), WIN, stride=images)


def load_cells(cells, dst):
    for r in range(2 * WIN):
        for half in range(2):
            for j in range(cells.shape[0]):
                dst[pl.ds(tok(r, half), WIN), pl.ds(j * LANES, LANES)] = cells.at[j][cell_rows(cells, r, half), :]


def store_cells(src, cells):
    for r in range(2 * WIN):
        for half in range(2):
            for j in range(cells.shape[0]):
                cells.at[j][cell_rows(cells, r, half), :] = src[pl.ds(tok(r, half), WIN), pl.ds(j * LANES, LANES)]


def cells_first(images):
    return images.transpose(1, 2, 0, 3).reshape(-1, images.shape[3])


def images_first(cells):
    return cells.reshape(2 * WIN, 2 * WIN, -1, cells.shape[1]).transpose(2, 0, 1, 3)


def neighbours(left, right):
    last = lax.broadcasted_iota(jnp.int32, (SUB, LANES), 0) == SUB - 1
    up_right = pltpu.roll(right, SUB - 1, 0)
    up_left = pltpu.roll(jnp.where(last, up_right, left), SUB - 1, 0)
    down_left = pltpu.roll(left, 1, 0)
    down_right = pltpu.roll(jnp.where(last, down_left, right), 1, 0)
    return ((down_left, left, up_left), (down_right, right, up_right))


def masked_row(src, mask, r, lanes):
    pair = []
    for half in range(2):
        rows = pl.ds(tok(r, half), SUB)
        pair.append(src[rows, lanes] * mask[0, rows, :])
    return neighbours(*pair)


def plain_row(src, r, lanes):
    return neighbours(*[src[pl.ds(tok(r, half), SUB), lanes] for half in range(2)])


def lay_row(lay, k):
    return lay[0, pl.ds(k, 1), :]


def taps(lay, lanes):
    return [jnp.broadcast_to(lay[0, pl.ds(k, 1), lanes], (SUB, LANES)) for k in range(10)]


def conv_forward(src, mask, lay, dst):
    rows = 2 * WIN

    @pl.loop(0, src.shape[1] // LANES)
    def _(j):
        lanes = pl.ds(pl.multiple_of(j * LANES, LANES), LANES)
        w = taps(lay, lanes)
        shift = w[9]
        window = [None, masked_row(src, mask, 0, lanes), masked_row(src, mask, 1, lanes)]
        for r in range(rows):
            for half in range(2):
                total = shift
                for a in range(3):
                    if window[a] is None:
                        continue
                    for b in range(3):
                        total = total + w[3 * a + b] * window[a][half][b]
                at = pl.ds(tok(r, half), SUB)
                dst[at, lanes] = src[at, lanes] + total
            following = masked_row(src, mask, r + 2, lanes) if r + 2 < rows else None
            window = [window[1], window[2], following]


def conv_backward(x_src, g_src, mask, lay, sums, dst):
    rows = 2 * WIN

    @pl.loop(0, x_src.shape[1] // LANES)
    def _(j):
        lanes = pl.ds(pl.multiple_of(j * LANES, LANES), LANES)
        w = taps(lay, lanes)
        g_win = [None, plain_row(g_src, 0, lanes), plain_row(g_src, 1, lanes)]
        x_win = [None, masked_row(x_src, mask, 0, lanes), masked_row(x_src, mask, 1, lanes)]
        grads = [sums[pl.ds(SUB * k, SUB), lanes] for k in range(10)]
        for r in range(rows):
            for half in range(2):
                center = g_win[1][half][1]
                total = None
                for a in range(3):
                    for b in range(3):
                        if x_win[a] is not None:
                            grads[3 * a + b] = grads[3 * a + b] + center * x_win[a][half][b]
                        if g_win[2 - a] is not None:
                            term = w[3 * a + b] * g_win[2 - a][half][2 - b]
                            total = term if total is None else total + term
                grads[9] = grads[9] + center
                at = pl.ds(tok(r, half), SUB)
                dst[at, lanes] = center + mask[0, at, :] * total
            more = r + 2 < rows
            g_win = [g_win[1], g_win[2], plain_row(g_src, r + 2, lanes) if more else None]
            x_win = [x_win[1], x_win[2], masked_row(x_src, mask, r + 2, lanes) if more else None]
        for k in range(10):
            sums[pl.ds(SUB * k, SUB), lanes] = grads[k]


def norm_forward(src, lay, z_out, r_out, n_out):
    features = src.shape[1]

    @pl.loop(0, src.shape[0] // (2 * NROWS))
    def _(i):
        for j in range(2):
            rows = pl.ds(pl.multiple_of(i * (2 * NROWS) + j * NROWS, NROWS), NROWS)
            x = src[rows, :]
            center = x - jnp.sum(x, axis=1, keepdims=True) * (1.0 / features)
            var = jnp.sum(center * center, axis=1, keepdims=True) * (1.0 / features)
            rstd = lax.rsqrt(var + EPS)
            z = center * rstd
            z_out[rows, :] = z
            r_out[rows, :] = jnp.broadcast_to(rstd, (NROWS, LANES))
            n_out[rows, :] = (z * lay_row(lay, 10) + lay_row(lay, 11)).astype(BF16)


def norm_backward(dn, z_src, r_src, lay, g_src, sums, first, dst):
    features = dn.shape[1]

    @pl.loop(0, dn.shape[0] // (2 * NROWS))
    def _(i):
        for j in range(2):
            rows = pl.ds(pl.multiple_of(i * (2 * NROWS) + j * NROWS, NROWS), NROWS)
            d = dn[rows, :]
            z = z_src[rows, :]
            t = d * lay_row(lay, 10)
            m1 = jnp.sum(t, axis=1, keepdims=True) * (1.0 / features)
            m2 = jnp.sum(t * z, axis=1, keepdims=True) * (1.0 / features)
            dst[rows, :] = g_src[rows, :] + (t - m1 - z * m2) * r_src[rows, 0:1]
            at = pl.ds(first, SUB)
            sums[at, :] = sums[at, :] + fold_rows(d * z)
            at = pl.ds(first + SUB, SUB)
            sums[at, :] = sums[at, :] + fold_rows(d)


def fold_rows(value):
    total = value[:SUB]
    for i in range(1, value.shape[0] // SUB):
        total = total + value[SUB * i : SUB * (i + 1)]
    return total


def finish_sums(sums, out):
    for k in range(sums.shape[0] // SUB):
        out[pl.ds(k, 1), :] = jnp.sum(sums[pl.ds(SUB * k, SUB), :], axis=0, keepdims=True)


def head_masks():
    lane = lax.broadcasted_iota(jnp.int32, (WTOK, GROUP), 1) // HD
    return [lane == h for h in range(GROUP // HD)]


def spread_heads(value, masks):
    return jnp.concatenate([jnp.where(m, value, 0.0) for m in masks], axis=0).astype(BF16)


def collect_heads(full, masks):
    total = full[:WTOK]
    for h in range(1, len(masks)):
        total = jnp.where(masks[h], full[WTOK * h : WTOK * (h + 1)], total)
    return total


def rounded(value):
    return value.astype(BF16).astype(F32)


def gelu_pair(h):
    cdf = 0.5 * (1.0 + lax.erf(h * 0.7071067811865476))
    pdf = jnp.exp(h * h * -0.5) * 0.3989422804014327
    return h * cdf, cdf + h * pdf


def first_step(steps=None):
    return pl.program_id(0) == (steps[0] if steps else 0)


def last_step(steps=None):
    return pl.program_id(0) == (steps[1] if steps else pl.num_programs(0)) - 1


def window_forward_kernel(
    inp, mask, lay, sh, watt,
    n_out, z_out, r_out, q_out, o_out, p_out, x_out,
    cells, x0, x1, qf, of,
):
    features = x0.shape[1]

    @pl.when(first_step())
    def _():
        x0[...] = jnp.zeros_like(x0)
        fill_cells(inp, cells)

    load_cells(cells, x0)
    conv_forward(x0, mask, lay, x1)
    norm_forward(x1, lay, z_out.at[0], r_out.at[0], n_out.at[0])
    chunk = features
    for c in range(3):
        lanes = pl.ds(c * chunk, chunk)
        part = dot(n_out[0], watt[:, lanes], DIMS_NN)
        if c != 1:
            part = part + sh[pl.ds(c // 2, 1), :]
        part = part.astype(BF16)
        q_out[0, :, lanes] = part
        qf[:, lanes] = part.astype(F32)

    @pl.loop(0, 4)
    def _(w):
        rows = pl.ds(pl.multiple_of(w * WTOK, SUB), WTOK)
        valid = mask[0, rows, 0:1] > 0.0
        masks = head_masks()
        for g in range(features // GROUP):
            q = qf[rows, pl.ds(g * GROUP, GROUP)]
            k = qf[rows, pl.ds(features + g * GROUP, GROUP)].astype(BF16)
            v = qf[rows, pl.ds(2 * features + g * GROUP, GROUP)].astype(BF16)
            s = dot(k, spread_heads(q, masks), DIMS_NT) * SCALE
            s = jnp.where(valid, s, NEG)
            e = jnp.exp(s - jnp.max(s, axis=0, keepdims=True))
            p = (e / jnp.sum(e, axis=0, keepdims=True)).astype(BF16)
            p_out[0, w, g] = p
            of[rows, pl.ds(g * GROUP, GROUP)] = collect_heads(dot(p, v, DIMS_TN), masks)

    o_out[0] = of[...].astype(BF16)
    x_out[0] = x1[...] + (dot(o_out[0], watt[:, pl.ds(3 * features, features)], DIMS_NN) + lay_row(lay, 12))


def mlp_forward_kernel(
    x_in, mask, lay, hb, w_in, w_out,
    n_out, z_out, r_out, u_out, d_out, x_out,
    x1, acc,
):
    conv_forward(x_in.at[0], mask, lay, x1)
    norm_forward(x1, lay, z_out.at[0], r_out.at[0], n_out.at[0])
    for c in range(w_in.shape[1] // FFC):
        lanes = pl.ds(c * FFC, FFC)
        h = dot(n_out[0], w_in[:, lanes], DIMS_NN) + hb[0, :, lanes]
        u, d = gelu_pair(h)
        u = u.astype(BF16)
        u_out[0, :, lanes] = u
        d_out[0, :, lanes] = d.astype(BF16)
        y = dot(u, w_out[:, lanes], DIMS_NT)
        acc[...] = y if c == 0 else acc[...] + y
    x_out[0] = x1[...] + (acc[...] + lay_row(lay, 12))


def group_mask():
    row = lax.broadcasted_iota(jnp.int32, (GROUP, GROUP), 0) // HD
    col = lax.broadcasted_iota(jnp.int32, (GROUP, GROUP), 1) // HD
    return row == col


def channel_forward_kernel(
    x_in, mask, lay, sh, watt,
    n_out, z_out, r_out, q_out, o_out, a_out, x_out,
    x1,
):
    features = x1.shape[1]
    conv_forward(x_in.at[0], mask, lay, x1)
    norm_forward(x1, lay, z_out.at[0], r_out.at[0], n_out.at[0])
    for c in range(3):
        lanes = pl.ds(c * features, features)
        part = dot(n_out[0], watt[:, lanes], DIMS_NN) + sh[pl.ds(2 + c, 1), :]
        if c == 1:
            part = part * mask[0, :, 0:1]
        q_out[0, :, lanes] = part.astype(BF16)
    same = group_mask()
    for g in range(features // GROUP):
        q = q_out[0, :, pl.ds(g * GROUP, GROUP)]
        k = q_out[0, :, pl.ds(features + g * GROUP, GROUP)]
        v = q_out[0, :, pl.ds(2 * features + g * GROUP, GROUP)]
        s = jnp.where(same, dot(k, q, DIMS_TN) * SCALE, -jnp.inf)
        e = jnp.exp(s - jnp.max(s, axis=0, keepdims=True))
        a = (e / jnp.sum(e, axis=0, keepdims=True)).astype(BF16)
        a_out[0, g] = a
        o_out[0, :, pl.ds(g * GROUP, GROUP)] = dot(v, a, DIMS_NN).astype(BF16)
    x_out[0] = x1[...] + (dot(o_out[0], watt[:, pl.ds(3 * features, features)], DIMS_NN) + lay_row(lay, 12))


def last_mlp_kernel(
    x_in, cot, mask, lay, hb, w_in, w_out,
    out, g_out, n_out, u_out, gy_out, gh_out, small_out, hidden_out,
    cells, x1, z, r, acc, dn, g8, sums, hsums,
):
    @pl.when(first_step())
    def _():
        g8[...] = jnp.zeros_like(g8)
        sums[...] = jnp.zeros_like(sums)
        hsums[...] = jnp.zeros_like(hsums)
        fill_cells(cot, cells)

    x6 = x_in.at[0]
    load_cells(cells, g8)
    conv_forward(x6, mask, lay, x1)
    norm_forward(x1, lay, z, r, n_out.at[0])
    g8[...] = g8[...] * mask[0, :, 0:1]
    gy_out[0] = g8[...].astype(BF16)
    sums[pl.ds(12 * SUB, SUB), :] = sums[pl.ds(12 * SUB, SUB), :] + fold_rows(gy_out[0].astype(F32))
    for c in range(1):
        lanes = pl.ds(0, w_in.shape[1])
        h = dot(n_out[0], w_in[:, lanes], DIMS_NN) + hb[0, :, lanes]
        du = dot(gy_out[0], w_out[:, lanes], DIMS_NN)
        u, d = gelu_pair(h)
        u = u.astype(BF16)
        u_out[0, :, lanes] = u
        gh = (du * d).astype(BF16)
        gh_out[0, :, lanes] = gh
        hsums[:, lanes] = hsums[:, lanes] + fold_rows(gh.astype(F32))
        y = dot(u, w_out[:, lanes], DIMS_NT)
        dx = dot(gh, w_in[:, lanes], DIMS_NT)
        acc[...] = y if c == 0 else acc[...] + y
        dn[...] = dx if c == 0 else dn[...] + dx
    acc[...] = (x1[...] + (acc[...] + lay_row(lay, 12))) * mask[0, :, 0:1]
    store_cells(acc, cells)
    norm_backward(dn, z, r, lay, g8, sums, 10 * SUB, x1)
    conv_backward(x6, x1, mask, lay, sums, g_out.at[0])

    @pl.when(last_step())
    def _():
        drain_cells(cells, out)
        finish_sums(sums, small_out)
        finish_sums(hsums, hidden_out)


def mlp_backward_kernel(
    g_in, x_in, z_in, r_in, d_in, mask, lay, w_in, w_out,
    g_out, gy_out, gh_out, small_out, hidden_out,
    dn, g1, sums, hsums,
    steps=None,
):
    @pl.when(first_step(steps))
    def _():
        sums[...] = jnp.zeros_like(sums)
        hsums[...] = jnp.zeros_like(hsums)

    gy_out[0] = g_in[0].astype(BF16)
    sums[pl.ds(12 * SUB, SUB), :] = sums[pl.ds(12 * SUB, SUB), :] + fold_rows(gy_out[0].astype(F32))
    for c in range(w_in.shape[1] // FFC):
        lanes = pl.ds(c * FFC, FFC)
        du = dot(gy_out[0], w_out[:, lanes], DIMS_NN)
        gh = (du * d_in[0, :, lanes].astype(F32)).astype(BF16)
        gh_out[0, :, lanes] = gh
        hsums[:, lanes] = hsums[:, lanes] + fold_rows(gh.astype(F32))
        dx = dot(gh, w_in[:, lanes], DIMS_NT)
        dn[...] = dx if c == 0 else dn[...] + dx
    norm_backward(dn, z_in.at[0], r_in.at[0], lay, g_in.at[0], sums, 10 * SUB, g1)
    conv_backward(x_in.at[0], g1, mask, lay, sums, g_out.at[0])

    @pl.when(last_step(steps))
    def _():
        finish_sums(sums, small_out)
        finish_sums(hsums, hidden_out)


def channel_backward_kernel(
    g_in, x_in, z_in, r_in, q_in, a_in, mask, lay, watt,
    g_out, ga_out, dq_out, small_out, bias_out,
    dn, g1, sums, bsums,
    steps=None,
):
    features = dn.shape[1]

    @pl.when(first_step(steps))
    def _():
        sums[...] = jnp.zeros_like(sums)
        bsums[...] = jnp.zeros_like(bsums)

    ga_out[0] = g_in[0].astype(BF16)
    sums[pl.ds(12 * SUB, SUB), :] = sums[pl.ds(12 * SUB, SUB), :] + fold_rows(ga_out[0].astype(F32))
    go = dot(ga_out[0], watt[:, pl.ds(3 * features, features)], DIMS_NT).astype(BF16)
    for g in range(features // GROUP):
        at = [pl.ds(i * features + g * GROUP, GROUP) for i in range(3)]
        q, k, v = (q_in[0, :, lanes] for lanes in at)
        gog = go[:, g * GROUP : (g + 1) * GROUP]
        a = a_in[0, g]
        af = a.astype(F32)
        dp = dot(v, gog, DIMS_TN)
        ds = (af * (dp - jnp.sum(dp * af, axis=0, keepdims=True))).astype(BF16)
        dq_out[0, :, at[0]] = (dot(k, ds, DIMS_NN) * SCALE).astype(BF16)
        dq_out[0, :, at[1]] = (dot(q, ds, DIMS_NT) * SCALE * mask[0, :, 0:1]).astype(BF16)
        dq_out[0, :, at[2]] = dot(gog, a, DIMS_NT).astype(BF16)
    bsums[...] = bsums[...] + fold_rows(dq_out[0].astype(F32))
    dn[...] = dot(dq_out[0], watt[:, pl.ds(0, 3 * features)], DIMS_NT)
    norm_backward(dn, z_in.at[0], r_in.at[0], lay, g_in.at[0], sums, 10 * SUB, g1)
    conv_backward(x_in.at[0], g1, mask, lay, sums, g_out.at[0])

    @pl.when(last_step(steps))
    def _():
        finish_sums(sums, small_out)
        finish_sums(bsums, bias_out)


def window_backward_kernel(
    g_in, inp, z_in, r_in, q_in, p_in, mask, lay, watt,
    g_out, ga_out, dq_out, small_out, bias_out,
    cells, x0, qf, gof, dqf, dn, g1, sums, bsums,
):
    features = dn.shape[1]

    @pl.when(first_step())
    def _():
        x0[...] = jnp.zeros_like(x0)
        sums[...] = jnp.zeros_like(sums)
        bsums[...] = jnp.zeros_like(bsums)
        fill_cells(inp, cells)

    load_cells(cells, x0)
    ga_out[0] = g_in[0].astype(BF16)
    sums[pl.ds(12 * SUB, SUB), :] = sums[pl.ds(12 * SUB, SUB), :] + fold_rows(ga_out[0].astype(F32))
    gof[...] = rounded(dot(ga_out[0], watt[:, pl.ds(3 * features, features)], DIMS_NT))
    qf[...] = q_in[0].astype(F32)

    @pl.loop(0, 4)
    def _(w):
        rows = pl.ds(pl.multiple_of(w * WTOK, SUB), WTOK)
        masks = head_masks()
        for g in range(features // GROUP):
            at = [pl.ds(i * features + g * GROUP, GROUP) for i in range(3)]
            qe = spread_heads(qf[rows, at[0]], masks)
            k = qf[rows, at[1]].astype(BF16)
            v = qf[rows, at[2]].astype(BF16)
            goe = spread_heads(gof[rows, at[0]], masks)
            p = p_in[0, w, g]
            pf = p.astype(F32)
            dp = dot(v, goe, DIMS_NT)
            ds = (pf * (dp - jnp.sum(dp * pf, axis=0, keepdims=True))).astype(BF16)
            dqf[rows, at[0]] = collect_heads(dot(ds, k, DIMS_TN), masks) * SCALE
            dqf[rows, at[1]] = dot(ds, qe, DIMS_NN) * SCALE
            dqf[rows, at[2]] = dot(p, goe, DIMS_NN)

    dq_out[0] = dqf[...].astype(BF16)
    bsums[...] = bsums[...] + fold_rows(dq_out[0].astype(F32))
    dn[...] = dot(dq_out[0], watt[:, pl.ds(0, 3 * features)], DIMS_NT)
    norm_backward(dn, z_in.at[0], r_in.at[0], lay, g_in.at[0], sums, 10 * SUB, g1)
    conv_backward(x0, g1, mask, lay, sums, dn)
    store_cells(dn, cells)

    @pl.when(last_step())
    def _():
        drain_cells(cells, g_out)
        finish_sums(sums, small_out)
        finish_sums(bsums, bias_out)


def per_image(shape):
    if len(shape) == 2:
        return whole(shape)
    rest = (0,) * (len(shape) - 1)
    return pl.BlockSpec((1,) + tuple(shape[1:]), lambda i: (i,) + rest)


def whole(shape):
    zeros = (0,) * len(shape)
    return pl.BlockSpec(tuple(shape), lambda i: zeros, pipeline_mode=pl.Buffered(1))


def one_layer(shape, layer):
    return pl.BlockSpec((1,) + tuple(shape[1:]), lambda i: (layer, 0, 0), pipeline_mode=pl.Buffered(1))


def cost(flops, arrays):
    size = sum(jnp.dtype(d).itemsize * functools.reduce(lambda p, q: p * q, s) for s, d in arrays)
    return pl.CostEstimate(flops=int(flops), bytes_accessed=int(size), transcendentals=0)


def params():
    return pltpu.CompilerParams(dimension_semantics=("arbitrary",), vmem_limit_bytes=VMEM_LIMIT)


def carrier(kernel, carry, ins, outs, scratch, refs):
    extra_in, extra_out = len(carry.args), len(carry.outs)
    base_in, refs = refs[:ins], refs[ins:]
    carry_in, refs = refs[:extra_in], refs[extra_in:]
    base_out, refs = refs[:outs], refs[outs:]
    carry_out, refs = refs[:extra_out], refs[extra_out:]
    base_scratch, carry_scratch = refs[:scratch], refs[scratch:]
    carry.run(carry_in, carry_out, carry_scratch)
    kernel(*base_in, *base_out, *base_scratch)
    carry.end(carry_in, carry_out, carry_scratch)


def image_call(kernel, name, layer, batched, lay, shared, outs, sums, scratch, flops, carry=None):
    images = next(a.shape[0] for a in batched if a.ndim > 2)
    ins = [per_image(a.shape) for a in batched] + [one_layer(lay.shape, layer)]
    args = list(batched) + [lay]
    for item in shared:
        if isinstance(item, tuple):
            ins.append(one_layer(item[0].shape, item[1]))
            args.append(item[0])
        else:
            ins.append(whole(item.shape))
            args.append(item)
    out_specs = [per_image(s) for s, _ in outs]
    out_specs += [pl.BlockSpec(tuple(s), lambda i: (0, 0)) for s, _ in sums]
    results = outs + sums
    buffers = [pltpu.VMEM(s, d) for s, d in scratch]
    options = params()
    body = kernel
    if carry is not None:
        counts = (len(args), len(results), len(scratch))

        def body(*refs):
            carrier(kernel, carry, *counts, refs)

        args = args + carry.args
        ins = ins + [pl.BlockSpec(memory_space=pl.ANY)] * len(carry.args)
        out_specs += [carry.out_spec or pl.BlockSpec(tuple(s), lambda i: (0, 0)) for s, _ in carry.outs]
        results = results + carry.outs
        buffers += carry.scratch
        options = pltpu.CompilerParams(
            dimension_semantics=("arbitrary",), vmem_limit_bytes=VMEM_LIMIT, collective_id=carry.ident,
            has_side_effects=True,
        )
    arrays = [(a.shape, a.dtype) for a in args] + results
    return pl.pallas_call(
        body,
        grid=(images,),
        in_specs=ins,
        out_specs=out_specs,
        out_shape=[jax.ShapeDtypeStruct(s, d) for s, d in results],
        scratch_shapes=buffers,
        compiler_params=options,
        cost_estimate=cost(flops, arrays),
        name=name,
    )(*args)


def token_mask(heights, widths):
    t = jnp.arange(4 * WTOK, dtype=jnp.int32)
    window = t // WTOK
    row = (window // 2) * WIN + (t % WTOK) // SUB
    col8 = t % SUB
    col = (window % 2) * WIN + col8
    valid = (row[None] < heights[:, None]) & (col[None] < widths[:, None]) & (col8 < WIN)[None]
    return jnp.broadcast_to(valid.astype(F32)[..., None], valid.shape + (LANES,))


def forward_window(inputs, mask, lay, sh, watt, carry=None):
    (rows, c), images, t = inputs.shape, mask.shape[0], mask.shape[1]
    outs = [
        ((images, t, c), BF16), ((images, t, c), F32), ((images, t, LANES), F32),
        ((images, t, 3 * c), BF16), ((images, t, c), BF16),
        ((images, 4, c // GROUP, WTOK, WTOK * GROUP // HD), BF16), ((images, t, c), F32),
    ]
    scratch = [((c // LANES, rows, LANES), F32), ((t, c), F32), ((t, c), F32), ((t, 3 * c), F32), ((t, c), F32)]
    return image_call(window_forward_kernel, "window_forward", 0, [inputs, mask], lay, [sh, watt],
                      outs, [], scratch, 10 * images * t * c * c, carry)


def forward_mlp(x, mask, lay, hid, w_in, w_out, carry=None):
    images, t, c = x.shape
    ff = w_in.shape[1]
    outs = [
        ((images, t, c), BF16), ((images, t, c), F32), ((images, t, LANES), F32),
        ((images, t, ff), BF16), ((images, t, ff), BF16), ((images, t, c), F32),
    ]
    scratch = [((t, c), F32), ((t, c), F32)]
    return image_call(mlp_forward_kernel, "mlp_forward", 1, [x, mask], lay, [(hid, 0), w_in, w_out],
                      outs, [], scratch, 4 * images * t * c * ff, carry)


def forward_channel(x, mask, lay, sh, watt, carry=None):
    images, t, c = x.shape
    outs = [
        ((images, t, c), BF16), ((images, t, c), F32), ((images, t, LANES), F32),
        ((images, t, 3 * c), BF16), ((images, t, c), BF16),
        ((images, c // GROUP, GROUP, GROUP), BF16), ((images, t, c), F32),
    ]
    return image_call(channel_forward_kernel, "channel_forward", 2, [x, mask], lay, [sh, watt],
                      outs, [], [((t, c), F32)], 9 * images * t * c * c, carry)


def last_mlp(x, cot, mask, lay, hid, w_in, w_out):
    images, t, c = x.shape
    ff = w_in.shape[1]
    outs = [
        (cot.shape, BF16), ((images, t, c), F32), ((images, t, c), BF16), ((images, t, ff), BF16),
        ((images, t, c), BF16), ((images, t, ff), BF16),
    ]
    scratch = [
        ((c // LANES, cot.shape[0], LANES), F32), ((t, c), F32), ((t, c), F32), ((t, LANES), F32), ((t, c), F32),
        ((t, c), F32), ((t, c), F32), ((16 * SUB, c), F32), ((SUB, ff), F32),
    ]
    return image_call(last_mlp_kernel, "last_mlp", 3, [x, cot, mask], lay, [(hid, 1), w_in, w_out],
                      outs, [((16, c), F32), ((1, ff), F32)], scratch, 8 * images * t * c * ff)


def backward_mlp(g, x, z, r, d, mask, lay, w_in, w_out, carry=None):
    images, t, c = x.shape
    ff = w_in.shape[1]
    outs = [((images, t, c), F32), ((images, t, c), BF16), ((images, t, ff), BF16)]
    scratch = [((t, c), F32), ((t, c), F32), ((16 * SUB, c), F32), ((SUB, ff), F32)]
    return image_call(mlp_backward_kernel, "mlp_backward", 1, [g, x, z, r, d, mask], lay, [w_in, w_out],
                      outs, [((16, c), F32), ((1, ff), F32)], scratch, 4 * images * t * c * ff, carry)


def backward_channel(g, x, z, r, q, a, mask, lay, watt, carry=None):
    images, t, c = x.shape
    outs = [((images, t, c), F32), ((images, t, c), BF16), ((images, t, 3 * c), BF16)]
    scratch = [((t, c), F32), ((t, c), F32), ((16 * SUB, c), F32), ((SUB, 3 * c), F32)]
    return image_call(channel_backward_kernel, "channel_backward", 2, [g, x, z, r, q, a, mask], lay, [watt],
                      outs, [((16, c), F32), ((1, 3 * c), F32)], scratch, 10 * images * t * c * c, carry)


def backward_window(g, inputs, z, r, q, p, mask, lay, watt, carry=None):
    images, t, c = g.shape
    outs = [(inputs.shape, BF16), ((images, t, c), BF16), ((images, t, 3 * c), BF16)]
    scratch = [
        ((c // LANES, inputs.shape[0], LANES), F32), ((t, c), F32), ((t, 3 * c), F32), ((t, c), F32),
        ((t, 3 * c), F32), ((t, c), F32), ((t, c), F32), ((16 * SUB, c), F32), ((SUB, 3 * c), F32),
    ]
    return image_call(window_backward_kernel, "window_backward", 0, [g, inputs, z, r, q, p, mask], lay, [watt],
                      outs, [((16, c), F32), ((1, 3 * c), F32)], scratch, 12 * images * t * c * c, carry)


def grad_pair_kernel(first, left0, right0, left1, right1, out0, out1):
    step = pl.program_id(0)

    @pl.when(step < first)
    def _():
        out0[...] = dot(left0[...], right0[...], DIMS_TN).astype(BF16)

    @pl.when(step >= first)
    def _():
        out1[...] = dot(left1[...], right1[...], DIMS_TN).astype(BF16)


def grad_pair(name, left0, right0, left1, right1):
    flat = [a.reshape(-1, a.shape[-1]) for a in (left0, right0, left1, right1)]
    rows, c = flat[0].shape
    first, second = flat[1].shape[1] // c, flat[3].shape[1] // c

    def at_first(i):
        return (0, jnp.minimum(i, first - 1))

    def at_second(i):
        return (0, jnp.maximum(i - first, 0))

    outs = [((c, flat[1].shape[1]), BF16), ((c, flat[3].shape[1]), BF16)]
    return pl.pallas_call(
        functools.partial(grad_pair_kernel, first),
        grid=(first + second,),
        in_specs=[
            whole((rows, c)), pl.BlockSpec((rows, c), at_first),
            whole((rows, c)), pl.BlockSpec((rows, c), at_second),
        ],
        out_specs=[pl.BlockSpec((c, c), at_first), pl.BlockSpec((c, c), at_second)],
        out_shape=[jax.ShapeDtypeStruct(s, d) for s, d in outs],
        compiler_params=params(),
        cost_estimate=cost(2 * rows * c * c * (first + second), [(a.shape, BF16) for a in flat] + outs),
        name=name,
    )(*flat)


WIDE = 8
NARROW = 4
BOTH = ("narrow", "wide")
MESH_ID = pl.DeviceIdType.MESH
RING = (0, 1, -1, 2, -2, 3, -3, 4)
AFAR = RING[::-1]
GATHER_STEPS = (((0,), ()), ((1, -1), (0,)), ((2, -2), (1, -1)), ((3, -3), (2, -2)), ((4,), (3, -3)), ((), (4,)))
REDUCE_STEPS = ((), (15, 11), (7, 14, 10), (3, 6, 13), (2, 9), (5, 12), (1, 8, 4), (0,))
STAGES = (0, 4, 8, 12, 1, 5, 9, 13, 2, 6, 10, 14, 3, 7, 11, 15)
CARRY_STEPS = 8


def whole_part(condition):
    return jnp.where(condition, jnp.int32(1), jnp.int32(0))


def place(order, ring, cross=0, core=0):
    n, w = lax.axis_index("narrow"), lax.axis_index("wide")
    z = whole_part(w >= 2) + whole_part(w >= 4) + whole_part(w >= 6)
    y = whole_part(n >= 2)
    x, c = w - 2 * z, n - 2 * y
    a, b = (x, y) if order == 0 else (y, x)
    if ring:
        at = z + a * (7 - 2 * z) + ring
        at = at - 8 * whole_part(at >= 8) if ring > 0 else at + 8 * whole_part(at < 0)
        a = whole_part(at >= 4)
        z = at + a * (7 - 2 * at)
    if cross:
        b = 1 - b
    if core:
        c = 1 - c
    x, y = (a, b) if order == 0 else (b, a)
    return {"narrow": 2 * y + c, "wide": 2 * z + x}


def chip(order, rel):
    n, w = lax.axis_index("narrow"), lax.axis_index("wide")
    z1 = whole_part(w >= 4)
    z0 = whole_part(w - 4 * z1 >= 2)
    y = whole_part(n >= 2)
    x, c = w - 4 * z1 - 2 * z0, n - 2 * y
    first, second = (4, 8) if order == 0 else (8, 4)
    bits = (1, 2, first, second, 16)
    z0, z1, x, y, c = (1 - v if rel & bit else v for v, bit in zip((z0, z1, x, y, c), bits))
    return {"narrow": 2 * y + c, "wide": 4 * z1 + 2 * z0 + x}


def highest(rel):
    return rel.bit_length() - 1


def number(ring, cross=0, core=0):
    return ring % 8 + 8 * cross + 16 * core


def ring_peers():
    return [place(0, 1), place(0, -1), place(1, 1), place(1, -1), place(0, 0, 1), place(1, 0, 1), place(0, 0, 0, 1)]


def chip_peers():
    return [chip(0, 1 << k) for k in range(5)]


def meet(peers):
    barrier = pltpu.get_barrier_semaphore()
    for at in peers:
        pl.semaphore_signal(barrier, inc=1, device_id=at, device_id_type=MESH_ID)
    pl.semaphore_wait(barrier, len(peers))


class Part:
    def __init__(self, operand, kind, shape, start, size, order):
        self.operand, self.kind, self.shape, self.start, self.size, self.order = operand, kind, shape, start, size, order

    def whole(self):
        rows, cols = self.shape
        return {
            "slot": (WIDE * NARROW, rows, cols), "in": (NARROW * rows, WIDE * cols), "out": (WIDE * rows, NARROW * cols),
        }[self.kind]

    def view(self, ref, n, w):
        rows, cols = self.shape
        if self.kind == "slot":
            return ref.at[n * WIDE + w, pl.ds(self.start, self.size), :]
        a, b = (n, w) if self.kind == "in" else (w, n)
        step = 16
        while step < 128 and rows % (2 * step) == 0 and self.start % (2 * step) == 0:
            step *= 2
        at = pl.multiple_of(a * rows + self.start, step)
        return ref.at[pl.ds(at, self.size), pl.ds(pl.multiple_of(b * cols, cols), cols)]

    def of(self, ref, *where):
        at = place(self.order, *where)
        return self.view(ref, at["narrow"], at["wide"])


    def of_chip(self, ref, rel):
        at = chip(self.order, rel)
        return self.view(ref, at["narrow"], at["wide"])


def halves(operand, kind, shape):
    low = shape[0] // 32 * 16
    return [Part(operand, kind, shape, 0, low, 0), Part(operand, kind, shape, low, shape[0] - low, 1)]


def pair(first, second, shape_in, shape_out):
    return [Part(first, "in", shape_in, 0, shape_in[0], 0), Part(second, "out", shape_out, 0, shape_out[0], 1)]


class Gather:
    def __init__(self, index, part, own, dest, sems):
        self.index, self.part, self.dest = index, part, dest
        self.own = own.at[pl.ds(part.start, part.size), :]
        self.send, self.recv, self.keep = sems

    def copy(self, ring, cross, step):
        target = self.part.of(self.dest, ring, cross)
        if step is None:
            to, slot = place(self.part.order, 0, 0, 1), number(ring, cross, 1)
        elif step == 0:
            to, slot = place(self.part.order, 0, 1), number(ring, 1)
        else:
            to, slot = place(self.part.order, step), number(ring - step)
        return pltpu.make_async_remote_copy(
            src_ref=self.own if ring == 0 and cross == 0 else target, dst_ref=target,
            send_sem=self.send.at[self.index, slot], recv_sem=self.recv.at[self.index, slot],
            device_id=to, device_id_type=MESH_ID,
        )

    def arrival(self, ring, cross=0, core=0):
        target = self.part.of(self.dest, ring, cross, core)
        return pltpu.make_async_remote_copy(
            src_ref=target, dst_ref=target, send_sem=self.send.at[self.index, 0],
            recv_sem=self.recv.at[self.index, number(ring, cross, core)], device_id=place(self.part.order, 1),
            device_id_type=MESH_ID,
        )

    def stay(self):
        return pltpu.make_async_copy(self.own, self.part.of(self.dest, 0), self.keep.at[self.index])

    def sends(self, ring):
        steps = []
        if 0 <= ring < 4:
            steps.append(-1)
        if -3 < ring <= 0:
            steps.append(1)
        return steps + [0, None]

    def stage(self, ring):
        if ring == 0:
            self.stay().start()
        else:
            self.arrival(ring).wait_recv()
        for step in self.sends(ring):
            self.copy(ring, 0, step).start()

    def crossed(self, ring):
        self.arrival(ring, 1).wait_recv()
        self.copy(ring, 1, None).start()

    def finish(self):
        for ring in RING:
            self.arrival(ring, 0, 1).wait_recv()
            self.arrival(ring, 1, 1).wait_recv()
        for ring in RING:
            for step in self.sends(ring):
                self.copy(ring, 0, step).wait_send()
            self.copy(ring, 1, None).wait_send()
        self.stay().wait()


def gather_step(items, rings, crosses):
    for ring in rings:
        for item in items:
            item.stage(ring)
    for ring in crosses:
        for item in items:
            item.crossed(ring)


def gather_sems(count):
    return [pltpu.SemaphoreType.DMA((count, 32)), pltpu.SemaphoreType.DMA((count, 32)), pltpu.SemaphoreType.DMA((count,))]


class Beside:
    def __init__(self, ident, args, parts, pick=None):
        self.ident, self.args, self.parts = ident, list(args), parts
        self.pick = pick or {}
        shapes = {p.operand: p.whole() for p in parts}
        self.outs = [(shapes[k], BF16) for k in range(len(self.args))]
        self.out_spec = pl.BlockSpec(memory_space=pl.ANY)
        self.scratch = gather_sems(len(parts))

    def items(self, ins, outs, scratch):
        ins = [ref.at[self.pick[k]] if k in self.pick else ref for k, ref in enumerate(ins)]
        return [Gather(i, p, ins[p.operand], outs[p.operand], scratch) for i, p in enumerate(self.parts)]

    def run(self, ins, outs, scratch):
        items = self.items(ins, outs, scratch)
        for s, (rings, crosses) in enumerate(GATHER_STEPS):

            @pl.when(pl.program_id(0) == s)
            def _(s=s, rings=rings, crosses=crosses):
                if s == 0:
                    meet(ring_peers())
                gather_step(items, rings, crosses)

    def end(self, ins, outs, scratch):
        @pl.when(last_step())
        def _():
            for item in self.items(ins, outs, scratch):
                item.finish()


PHASE_STEPS = ((0, 1, 2, 3, 4, 5), (4, 5, 7, 8, 9, 10), (8, 9, 11, 12, 14, 15))


def two_phase_kernel(plans, counts, *refs):
    ins, outs, refs = refs[: counts[0]], refs[counts[0] : counts[0] + counts[1]], refs[counts[0] + counts[1] :]
    x_in, mask, lay1, lay2, hb, w_in, w_out, sh, chan, first, second = ins
    n1, z1, r1, u1, d1, x4, n2, z2, r2, q2, o2, a2, x6, watt, got, in1, out1 = outs
    x1, acc, xs, stage, sem, refs = *refs[:5], refs[5:]
    step = pl.program_id(0)
    sets = []
    for i, (plan, own, dest) in enumerate(zip(plans, (chan, first, second), (got, in1, out1))):
        sets.append(plan.items([own], [dest], refs[3 * i : 3 * i + 3]))
    for s in range(2 * CARRY_STEPS):
        due = [(items, steps.index(s)) for items, steps in zip(sets, PHASE_STEPS) if s in steps]

        @pl.when(step == s)
        def _(s=s, due=due):
            if s == 0:
                meet(ring_peers())
            for items, k in due:
                gather_step(items, *GATHER_STEPS[k])
            if s == CARRY_STEPS:
                for item in sets[0]:
                    item.finish()
                copy = pltpu.make_async_copy(got, stage, sem.at[0])
                copy.start()
                copy.wait()
                cn = chan.shape[0]
                for n in range(NARROW):
                    copy_attention(stage.at[pl.ds(n * WIDE, WIDE)], 0, watt.at[pl.ds(n * cn, cn)])

    @pl.when(step < CARRY_STEPS)
    def _():
        mlp_forward_kernel(x_in, mask, lay1, hb, w_in, w_out, n1, z1, r1, u1, d1, x4, x1, acc)
        xs[pl.ds(step, 1)] = x4[...]

    @pl.when(step >= CARRY_STEPS)
    def _():
        x = xs.at[pl.ds(step - CARRY_STEPS, 1)]
        channel_forward_kernel(x, mask, lay2, sh, watt, n2, z2, r2, q2, o2, a2, x6, x1)

    @pl.when(last_step())
    def _():
        for items in sets[1:]:
            for item in items:
                item.finish()


def forward_two(ident, x, mask, lay, hid, w_in, w_out, sh, chan, first, second):
    images, t, c = x.shape
    ff = w_in.shape[1]
    plans = [
        Beside(ident, [chan], halves(0, "slot", chan.shape)),
        Beside(ident, [first], halves(0, "in", first.shape[1:]), {0: 1}),
        Beside(ident, [second], halves(0, "out", second.shape[1:]), {0: 1}),
    ]

    def before(shape):
        rest = (0,) * (len(shape) - 1)
        return pl.BlockSpec((1,) + tuple(shape[1:]), lambda i: (jnp.minimum(i, images - 1),) + rest)

    def after(shape):
        rest = (0,) * (len(shape) - 1)
        return pl.BlockSpec((1,) + tuple(shape[1:]), lambda i: (jnp.maximum(i - images, 0),) + rest)

    each = pl.BlockSpec((1, t, LANES), lambda i: (lax.rem(i, images), 0, 0))
    anywhere = pl.BlockSpec(memory_space=pl.ANY)
    args = [x, mask, lay, lay, hid, w_in, w_out, sh, chan, first, second]
    in_specs = [
        before(x.shape), each, one_layer(lay.shape, 1), one_layer(lay.shape, 2), one_layer(hid.shape, 0),
        whole(w_in.shape), whole(w_out.shape), whole(sh.shape), anywhere, anywhere, anywhere,
    ]
    low = [
        ((images, t, c), BF16), ((images, t, c), F32), ((images, t, LANES), F32), ((images, t, ff), BF16),
        ((images, t, ff), BF16), ((images, t, c), F32),
    ]
    high = [
        ((images, t, c), BF16), ((images, t, c), F32), ((images, t, LANES), F32), ((images, t, 3 * c), BF16),
        ((images, t, c), BF16), ((images, c // GROUP, GROUP, GROUP), BF16), ((images, t, c), F32),
    ]
    outs = low + high + [((c, 4 * c), BF16)] + [o for plan in plans for o in plan.outs]
    out_specs = [before(s) for s, _ in low] + [after(s) for s, _ in high] + [whole((c, 4 * c))] + [anywhere] * 3
    scratch = [
        pltpu.VMEM((t, c), F32), pltpu.VMEM((t, c), F32), pltpu.VMEM((images, t, c), F32),
        pltpu.VMEM(plans[0].outs[0][0], BF16), pltpu.SemaphoreType.DMA((1,)),
    ]
    scratch += [item for plan in plans for item in plan.scratch]
    return pl.pallas_call(
        functools.partial(two_phase_kernel, plans, (len(args), len(outs))),
        grid=(2 * images,),
        in_specs=in_specs,
        out_specs=out_specs,
        out_shape=[jax.ShapeDtypeStruct(s, d) for s, d in outs],
        scratch_shapes=scratch,
        compiler_params=pltpu.CompilerParams(
            dimension_semantics=("arbitrary",), vmem_limit_bytes=VMEM_LIMIT, collective_id=ident, has_side_effects=True,
        ),
        cost_estimate=cost(4 * images * t * c * ff + 9 * images * t * c * c, [(a.shape, a.dtype) for a in args] + outs),
        name="mlp_channel_forward",
    )(*args)


class Reduce:
    def __init__(self, index, part, src, out, bufs, sems):
        self.index, self.part, self.src, self.out = index, part, src, out
        self.acc, self.mate, self.inbox = bufs
        self.load_sem, self.send_sem, self.mate_sem, self.recv_sem = sems

    def load(self, rel):
        return pltpu.make_async_copy(self.part.of_chip(self.src, rel), self.acc.at[rel], self.load_sem.at[self.index, rel])

    def to_mate(self, rel):
        return pltpu.make_async_remote_copy(
            src_ref=self.part.of_chip(self.src, rel | 16), dst_ref=self.mate.at[rel],
            send_sem=self.send_sem.at[self.index, 16 + rel], recv_sem=self.mate_sem.at[self.index, rel],
            device_id=chip(self.part.order, 16), device_id_type=MESH_ID,
        )

    def onward(self, rel):
        return pltpu.make_async_remote_copy(
            src_ref=self.acc.at[rel], dst_ref=self.inbox.at[rel - 1], send_sem=self.send_sem.at[self.index, rel],
            recv_sem=self.recv_sem.at[self.index, rel], device_id=chip(self.part.order, 1 << highest(rel)),
            device_id_type=MESH_ID,
        )

    def begin(self, rel):
        self.to_mate(rel).start()
        self.load(rel).start()

    def stage(self, rel):
        self.load(rel).wait()
        self.to_mate(rel).wait_recv()
        total = self.acc[rel].astype(F32) + self.mate[rel].astype(F32)
        for axis in range(highest(rel) + 1, 4):
            came = rel | (1 << axis)
            self.onward(came).wait_recv()
            total = total + self.inbox[came - 1].astype(F32)
        if rel == 0:
            self.out[pl.ds(self.part.start, self.part.size), :] = total
        else:
            self.acc[rel] = total.astype(BF16)
            self.onward(rel).start()

    def finish(self):
        for rel in range(16):
            self.to_mate(rel).wait_send()
            if rel:
                self.onward(rel).wait_send()


class Behind:
    def __init__(self, ident, args, parts):
        self.ident, self.args, self.parts = ident, list(args), parts
        shapes = {p.operand: p.shape for p in parts}
        self.outs = [(shapes[k], F32) for k in range(len(self.args))]
        self.out_spec = None
        self.scratch = []
        for p in parts:
            block = (p.size, p.shape[1])
            self.scratch += [pltpu.VMEM((16,) + block, BF16), pltpu.VMEM((16,) + block, BF16), pltpu.VMEM((15,) + block, BF16)]
        count = len(parts)
        self.scratch += [
            pltpu.SemaphoreType.DMA((count, 16)), pltpu.SemaphoreType.DMA((count, 32)),
            pltpu.SemaphoreType.DMA((count, 16)), pltpu.SemaphoreType.DMA((count, 16)),
        ]

    def items(self, ins, outs, scratch):
        bufs, sems = scratch[: 3 * len(self.parts)], scratch[3 * len(self.parts) :]
        return [
            Reduce(i, p, ins[p.operand], outs[p.operand], bufs[3 * i : 3 * i + 3], sems)
            for i, p in enumerate(self.parts)
        ]

    def run(self, ins, outs, scratch):
        items = self.items(ins, outs, scratch)
        for s, rels in enumerate(REDUCE_STEPS):

            @pl.when(pl.program_id(0) == s)
            def _(s=s, rels=rels):
                if s == 0:
                    meet(chip_peers())
                    for rel in reversed(STAGES):
                        for item in items:
                            item.begin(rel)
                for rel in rels:
                    for item in items:
                        item.stage(rel)

    def end(self, ins, outs, scratch):
        @pl.when(last_step())
        def _():
            for item in self.items(ins, outs, scratch):
                item.finish()


BACK_STEPS = ((0, 1, 2, 3, 4, 5, 6, 7), (4, 6, 7, 8, 10, 11, 13, 15))


def two_phase_back_kernel(plans, counts, *refs):
    ins, outs, refs = refs[: counts[0]], refs[counts[0] : counts[0] + counts[1]], refs[counts[0] + counts[1] :]
    g_in, xa, za, ra, q, a, mask, lay2, watt, xb, zb, rb, d, lay1, w_in, w_out, src0, src1 = ins
    ga, dq, small2, cb, g_out, gy, gh, small1, hid, red0, red1 = outs
    dn, g1, gs, sums_a, bsums, sums_b, hsums, refs = *refs[:7], refs[7:]
    step = pl.program_id(0)
    first = len(plans[0].scratch)
    sets = [plans[0].items([src0], [red0], refs[:first]), plans[1].items([src1], [red1], refs[first:])]
    for s in range(2 * CARRY_STEPS):
        due = [(items, steps.index(s)) for items, steps in zip(sets, BACK_STEPS) if s in steps]
        if not due:
            continue

        @pl.when(step == s)
        def _(s=s, due=due):
            if s == 0:
                meet(chip_peers())
            for items, k in due:
                if k == 0:
                    for rel in reversed(STAGES):
                        for item in items:
                            item.begin(rel)
                for rel in REDUCE_STEPS[k]:
                    for item in items:
                        item.stage(rel)

    @pl.when(step < CARRY_STEPS)
    def _():
        middle = gs.at[pl.ds(step, 1)]
        channel_backward_kernel(
            g_in, xa, za, ra, q, a, mask, lay2, watt, middle, ga, dq, small2, cb, dn, g1, sums_a, bsums,
            steps=(0, CARRY_STEPS),
        )

    @pl.when(step >= CARRY_STEPS)
    def _():
        middle = gs.at[pl.ds(step - CARRY_STEPS, 1)]
        mlp_backward_kernel(
            middle, xb, zb, rb, d, mask, lay1, w_in, w_out, g_out, gy, gh, small1, hid, dn, g1, sums_b, hsums,
            steps=(CARRY_STEPS, 2 * CARRY_STEPS),
        )

    @pl.when(last_step())
    def _():
        for items in sets:
            for item in items:
                item.finish()


def backward_two(ident, grads, g, xa, za, ra, q, a, mask, lay, watt, xb, zb, rb, d, w_in, w_out):
    images, t, c = g.shape
    ff = w_in.shape[1]
    plans = [
        Behind(ident, grads[:1], halves(0, "in", (grads[0].shape[0] // NARROW, grads[0].shape[1] // WIDE))),
        Behind(ident, grads[1:], halves(0, "out", (grads[1].shape[0] // WIDE, grads[1].shape[1] // NARROW))),
    ]

    def before(shape):
        rest = (0,) * (len(shape) - 1)
        return pl.BlockSpec((1,) + tuple(shape[1:]), lambda i: (jnp.minimum(i, images - 1),) + rest)

    def after(shape):
        rest = (0,) * (len(shape) - 1)
        return pl.BlockSpec((1,) + tuple(shape[1:]), lambda i: (jnp.maximum(i - images, 0),) + rest)

    def still(shape):
        return pl.BlockSpec(tuple(shape), lambda i: (0, 0))

    each = pl.BlockSpec((1, t, LANES), lambda i: (lax.rem(i, images), 0, 0))
    anywhere = pl.BlockSpec(memory_space=pl.ANY)
    args = [g, xa, za, ra, q, a, mask, lay, watt, xb, zb, rb, d, lay, w_in, w_out] + list(grads)
    in_specs = [before(v.shape) for v in (g, xa, za, ra, q, a)]
    in_specs += [each, one_layer(lay.shape, 2), whole(watt.shape)]
    in_specs += [after(v.shape) for v in (xb, zb, rb, d)]
    in_specs += [one_layer(lay.shape, 1), whole(w_in.shape), whole(w_out.shape), anywhere, anywhere]
    outs = [((images, t, c), BF16), ((images, t, 3 * c), BF16), ((16, c), F32), ((1, 3 * c), F32)]
    out_specs = [before(outs[0][0]), before(outs[1][0]), still(outs[2][0]), still(outs[3][0])]
    more = [((images, t, c), F32), ((images, t, c), BF16), ((images, t, ff), BF16), ((16, c), F32), ((1, ff), F32)]
    out_specs += [after(v) for v, _ in more[:3]] + [still(v) for v, _ in more[3:]]
    reds = [o for plan in plans for o in plan.outs]
    out_specs += [still(v) for v, _ in reds]
    outs = outs + more + reds
    scratch = [
        pltpu.VMEM(v, F32) for v in (
            (t, c), (t, c), (images, t, c), (16 * SUB, c), (SUB, 3 * c), (16 * SUB, c), (SUB, ff),
        )
    ]
    scratch += [item for plan in plans for item in plan.scratch]
    return pl.pallas_call(
        functools.partial(two_phase_back_kernel, plans, (len(args), len(outs))),
        grid=(2 * images,),
        in_specs=in_specs,
        out_specs=out_specs,
        out_shape=[jax.ShapeDtypeStruct(s, d) for s, d in outs],
        scratch_shapes=scratch,
        compiler_params=pltpu.CompilerParams(
            dimension_semantics=("arbitrary",), vmem_limit_bytes=VMEM_LIMIT, collective_id=ident, has_side_effects=True,
        ),
        cost_estimate=cost(4 * images * t * c * ff + 10 * images * t * c * c, [(v.shape, v.dtype) for v in args] + outs),
        name="channel_mlp_backward",
    )(*args)


def reduce_kernel(plan, *refs):
    ins, refs = refs[: len(plan.args)], refs[len(plan.args) :]
    outs, scratch = refs[: len(plan.outs)], refs[len(plan.outs) :]
    items = plan.items(ins, outs, scratch)
    meet(chip_peers())
    for rel in reversed(STAGES):
        for item in items:
            item.begin(rel)
    for rel in reversed(STAGES):
        for item in items:
            item.stage(rel)
    for item in items:
        item.finish()


def reduce_now(name, plan):
    return pl.pallas_call(
        functools.partial(reduce_kernel, plan),
        in_specs=[pl.BlockSpec(memory_space=pl.ANY)] * len(plan.args),
        out_specs=[pl.BlockSpec(memory_space=pltpu.VMEM)] * len(plan.outs),
        out_shape=[jax.ShapeDtypeStruct(s, d) for s, d in plan.outs],
        scratch_shapes=plan.scratch,
        compiler_params=pltpu.CompilerParams(
            collective_id=plan.ident, has_side_effects=True, vmem_limit_bytes=VMEM_LIMIT
        ),
        cost_estimate=cost(0, [(a.shape, a.dtype) for a in plan.args]),
        name=name,
    )(*plan.args)


def copy_attention(src, start, dst):
    cn = dst.shape[0]
    cw = src.shape[2] // 4
    c = WIDE * cw
    for w in range(WIDE):
        dst[:, pl.ds(3 * cw * w, 3 * cw)] = src[w, pl.ds(start, cn), pl.ds(0, 3 * cw)]
        dst[:, pl.ds(3 * c + cw * w, cw)] = src[w, pl.ds(start, cn), pl.ds(3 * cw, cw)]


def unpack_first_kernel(got, heights, widths, watt, lay, sh, hid, mask):
    copy_attention(got, 16, watt)
    cw = got.shape[2] // 4
    for w in range(WIDE):
        lay[0, :, pl.ds(cw * w, cw)] = got[w, pl.ds(0, 16), pl.ds(0, cw)].astype(F32)

    @pl.when(pl.program_id(0) == 0)
    def _():
        for w in range(WIDE):
            part = got[w, pl.ds(0, 16), pl.ds(LANES, cw)].astype(F32)
            sh[:, pl.ds(cw * w, cw)] = part
            for j in range(2):
                for q in range(4):
                    row = 5 + 4 * j + q
                    hid[j, :, pl.ds(4 * cw * w + cw * q, cw)] = part[row : row + 1]

    @pl.when(pl.program_id(0) == 1)
    def _():
        t = lax.broadcasted_iota(jnp.int32, mask.shape[1:], 0)
        window = whole_part(t >= WTOK) + whole_part(t >= 2 * WTOK) + whole_part(t >= 3 * WTOK)
        rest = t - window * WTOK
        low = lax.shift_right_logical(rest, 3)
        col8 = rest - low * SUB
        lower = whole_part(window >= 2)
        row = lower * WIN + low
        col = (window - 2 * lower) * WIN + col8
        for i in range(mask.shape[0]):
            valid = (row < heights[i]) & (col < widths[i]) & (col8 < WIN)
            mask[i] = jnp.where(valid, 1.0, 0.0)


def unpack_first(got, heights, widths):
    rows, lanes = got.shape[1:]
    c = 2 * lanes
    cn = c // NARROW
    images = heights.shape[0]
    outs = [
        ((c, 4 * c), BF16), ((NARROW, 16, c), F32), ((16, c), F32), ((2, 1, 4 * c), F32), ((images, 4 * WTOK, LANES), F32),
    ]
    return pl.pallas_call(
        unpack_first_kernel,
        grid=(NARROW,),
        in_specs=[pl.BlockSpec((WIDE, rows, lanes), lambda n: (n, 0, 0))] + [pl.BlockSpec(memory_space=pltpu.SMEM)] * 2,
        out_specs=[
            pl.BlockSpec((cn, 4 * c), lambda n: (n, 0)), pl.BlockSpec((1, 16, c), lambda n: (n, 0, 0)),
            pl.BlockSpec((16, c), lambda n: (0, 0)), pl.BlockSpec((2, 1, 4 * c), lambda n: (0, 0, 0)),
            pl.BlockSpec((images, 4 * WTOK, LANES), lambda n: (0, 0, 0)),
        ],
        out_shape=[jax.ShapeDtypeStruct(s, d) for s, d in outs],
        compiler_params=params(),
        cost_estimate=cost(0, [(got.shape, BF16)] + outs),
        name="unpack_first",
    )(got, heights, widths)


def grad_attention_kernel(start, left0, right0, left1, right1, *refs):
    *head, out, result = refs[:-1] if len(refs) > 2 else refs
    step = pl.program_id(0)
    c = right0.shape[1]
    cn, cw = c // NARROW, c // WIDE

    def spread(s, w, low, high):
        for n in range(NARROW):
            at = pl.ds(low - 3 * cw * w, high - low)
            out[n * WIDE + w, pl.ds(start, cn), at] = result[pl.ds(cn * n, cn), pl.ds(low - c * s, high - low)]

    for s in range(4):

        @pl.when(step == s)
        def _(s=s):
            if s < 3:
                result[...] = dot(left0[...], right0[...], DIMS_TN).astype(BF16)
                for w in range(WIDE):
                    low, high = max(3 * cw * w, c * s), min(3 * cw * (w + 1), c * (s + 1))
                    if low < high:
                        spread(s, w, low, high)
            else:
                result[...] = dot(left1[...], right1[...], DIMS_TN).astype(BF16)
                for w in range(WIDE):
                    for n in range(NARROW):
                        at = pl.ds(3 * cw, cw)
                        out[n * WIDE + w, pl.ds(start, cn), at] = result[pl.ds(cn * n, cn), pl.ds(cw * w, cw)]
                if head:
                    pack_small(*head, out, refs[-1])


def pack_small(small0, small1, small2, small3, sb, cb, hid0, hid1, out, shared):
    smalls = (small0, small1, small2, small3)
    c = small0.shape[1]
    cw = c // WIDE
    shared[...] = jnp.zeros_like(shared)
    shared[pl.ds(0, 1), :] = sb[:, pl.ds(0, c)]
    shared[pl.ds(1, 1), :] = sb[:, pl.ds(2 * c, c)]
    for k in range(3):
        shared[pl.ds(2 + k, 1), :] = cb[:, pl.ds(k * c, c)]
    for j, hid in enumerate((hid0, hid1)):
        for w in range(WIDE):
            for q in range(4):
                shared[pl.ds(5 + 4 * j + q, 1), pl.ds(cw * w, cw)] = hid[:, pl.ds(4 * cw * w + cw * q, cw)]
    out[:, pl.ds(0, 16), :] = jnp.zeros((WIDE * NARROW, 16, out.shape[2]), BF16)
    for w in range(WIDE):
        for n in range(NARROW):
            out[n * WIDE + w, pl.ds(0, 16), pl.ds(0, cw)] = smalls[n][:, pl.ds(cw * w, cw)].astype(BF16)
            out[n * WIDE + w, pl.ds(0, 16), pl.ds(LANES, cw)] = shared[:, pl.ds(cw * w, cw)].astype(BF16)


def grad_attention(name, left0, right0, left1, right1, head=()):
    flat = [a.reshape(-1, a.shape[-1]) for a in (left0, right0, left1, right1)]
    rows, c = flat[0].shape
    cn = c // NARROW
    start = 16 if head else 0
    shape = (WIDE * NARROW, start + cn, c // 2)
    scratch = [pltpu.VMEM((c, c), BF16)] + ([pltpu.VMEM((16, c), F32)] if head else [])
    return pl.pallas_call(
        functools.partial(grad_attention_kernel, start),
        grid=(4,),
        in_specs=[
            whole((rows, c)), pl.BlockSpec((rows, c), lambda i: (0, jnp.minimum(i, 2))), whole((rows, c)), whole((rows, c)),
        ] + [whole(a.shape) for a in head],
        out_specs=pl.BlockSpec(shape, lambda i: (0, 0, 0)),
        out_shape=jax.ShapeDtypeStruct(shape, BF16),
        scratch_shapes=scratch,
        compiler_params=params(),
        cost_estimate=cost(8 * rows * c * c, [(a.shape, BF16) for a in flat] + [(shape, BF16)]),
        name=name,
    )(*flat, *head)


def attention_piece(qkv, proj):
    return jnp.concatenate([qkv.T, proj.T], axis=1)


def turned(value):
    return value.astype(F32).T.astype(BF16)


def gather_first_kernel(
    plan, conv_weight, conv_bias, norm_gain, norm_bias, qkv0, qkv1, proj, attn_bias, hidden_bias, out_bias,
    got, chan, piece, *sems,
):
    cw = conv_bias.shape[1]
    cn = qkv0.shape[1]
    piece[pl.ds(0, 16), :] = jnp.zeros((16, piece.shape[1]), BF16)
    taps_now = conv_weight[0].astype(F32)
    rows = [taps_now] + [r[...].astype(F32) for r in (conv_bias, norm_gain, norm_bias, out_bias)]
    rows.append(jnp.zeros((3, cw), F32))
    piece[pl.ds(0, 16), pl.ds(0, cw)] = jnp.concatenate(rows, axis=0).astype(BF16)
    hidden = hidden_bias[...].astype(F32)
    rows = [attn_bias[...].astype(F32)]
    rows += [hidden[j : j + 1, cw * q : cw * (q + 1)] for j in range(2) for q in range(4)]
    rows.append(jnp.zeros((3, cw), F32))
    piece[pl.ds(0, 16), pl.ds(LANES, cw)] = jnp.concatenate(rows, axis=0).astype(BF16)
    piece[pl.ds(16, cn), pl.ds(0, 3 * cw)] = turned(qkv0[...])
    piece[pl.ds(16, cn), pl.ds(3 * cw, cw)] = turned(proj[0])
    items = plan.items([piece], [got], sems)
    meet(ring_peers())
    gather_step(items, (0,), ())
    chan[:, pl.ds(0, 3 * cw)] = turned(qkv1[...])
    chan[:, pl.ds(3 * cw, cw)] = turned(proj[1])
    for rings, crosses in GATHER_STEPS[1:]:
        gather_step(items, rings, crosses)
    for item in items:
        item.finish()


def gather_first(p):
    rows, cn = p["spatial_qkv"].shape
    lanes = rows * 4 // 3
    shape = (16 + cn, lanes)
    plan = Beside(1, [None], halves(0, "slot", shape))
    outs = plan.outs + [((cn, lanes), BF16)]
    args = [p[k] for k in NAMES if not k.startswith("mlp")]
    vmem = pl.BlockSpec(memory_space=pltpu.VMEM)
    return pl.pallas_call(
        functools.partial(gather_first_kernel, plan),
        in_specs=[vmem] * len(args),
        out_specs=[plan.out_spec, vmem],
        out_shape=[jax.ShapeDtypeStruct(s, d) for s, d in outs],
        scratch_shapes=[pltpu.VMEM(shape, BF16)] + plan.scratch,
        compiler_params=pltpu.CompilerParams(collective_id=1, has_side_effects=True, vmem_limit_bytes=VMEM_LIMIT),
        cost_estimate=cost(0, outs),
        name="gather_first",
    )(*args)


def finish_kernel(
    att0, att1, in0, in1, out0, out1,
    conv_weight, conv_bias, norm_gain, norm_bias, qkv0, qkv1, proj, mlp_in, mlp_out, attn_bias, hidden_bias, out_bias,
):
    cw = conv_bias.shape[1]
    cn = qkv0.shape[1]
    for k in range(9):
        conv_weight[k] = att0[pl.ds(k, 1), pl.ds(0, cw)]
    for k, row in enumerate((conv_bias, norm_gain, norm_bias, out_bias)):
        row[...] = att0[pl.ds(9 + k, 1), pl.ds(0, cw)]
    attn_bias[...] = att0[pl.ds(0, 5), pl.ds(LANES, cw)]
    for j in range(2):
        for q in range(4):
            hidden_bias[pl.ds(j, 1), pl.ds(cw * q, cw)] = att0[pl.ds(5 + 4 * j + q, 1), pl.ds(LANES, cw)]
    qkv0[...] = att0[pl.ds(16, cn), pl.ds(0, 3 * cw)].T
    proj[0] = att0[pl.ds(16, cn), pl.ds(3 * cw, cw)].T
    qkv1[...] = att1[:, pl.ds(0, 3 * cw)].T
    proj[1] = att1[:, pl.ds(3 * cw, cw)].T
    mlp_in[0] = in0[...]
    mlp_in[1] = in1[...]
    mlp_out[0] = out0[...]
    mlp_out[1] = out1[...]


def finish(*reduced):
    att0 = reduced[0]
    cn, lanes = att0.shape[0] - 16, att0.shape[1]
    cw = lanes // 4
    row = (1, cw)
    shapes = [
        (9, 1, cw), row, row, row, (3 * cw, cn), (3 * cw, cn), (2, cw, cn), (2, cn, lanes), (2, cw, 2 * lanes),
        (5, cw), (2, lanes), row,
    ]
    vmem = pl.BlockSpec(memory_space=pltpu.VMEM)
    outs = pl.pallas_call(
        finish_kernel,
        in_specs=[vmem] * 6,
        out_specs=[vmem] * len(shapes),
        out_shape=[jax.ShapeDtypeStruct(s, F32) for s in shapes],
        compiler_params=pltpu.CompilerParams(vmem_limit_bytes=VMEM_LIMIT),
        cost_estimate=cost(0, [(s, F32) for s in shapes]),
        name="finish",
    )(*reduced)
    outs = list(outs)
    outs[0] = outs[0].transpose(1, 0, 2)
    outs[7] = outs[7].transpose(0, 2, 1)
    return outs


class Direct:
    def __init__(self, p, heights, widths):
        got, self.chan = gather_first(p)
        self.first, self.second = p["mlp_in"].transpose(0, 2, 1), p["mlp_out"]
        watt0, self.lay, self.sh, self.hid, self.mask = unpack_first(got, heights, widths)
        self.watt, self.w_in, self.w_out = [watt0, None], [None, None], [None, None]

    def forward_window(self, *args):
        parts = pair(0, 1, self.first.shape[1:], self.second.shape[1:])
        carry = Beside(3, [self.first, self.second], parts, {0: 0, 1: 0})
        *outs, self.w_in[0], self.w_out[0] = forward_window(*args, carry=carry)
        return outs

    def forward_two(self, *args):
        *outs, self.watt[1], _, self.w_in[1], self.w_out[1] = forward_two(
            4, *args, self.sh, self.chan, self.first, self.second)
        return outs

    def backward_two(self, grads, *args):
        *outs, self.gi1, self.go1 = backward_two(6, grads, *args)
        return outs

    def channel_grads(self, *args):
        self.att1 = grad_attention("channel_grads", *args)

    def backward_window(self, grads, *args):
        parts = pair(0, 1, self.first.shape[1:], self.second.shape[1:]) + halves(2, "slot", self.chan.shape)
        *outs, self.gi0, self.go0, self.att1 = backward_window(*args, carry=Behind(8, list(grads) + [self.att1], parts))
        return outs

    def reduce_last(self, grads, smalls, sb, cb, hid0, hid1):
        packed = grad_attention("window_grads", *grads, (*smalls, sb, cb, hid0, hid1))
        (att0,) = reduce_now("reduce_last", Behind(2, [packed], halves(0, "slot", packed.shape[1:])))
        return tuple(finish(att0, self.att1, self.gi0, self.gi1, self.go0, self.go1))


class Plain:
    def __init__(self, p, heights, widths):
        self.mask = token_mask(heights, widths)
        self.layers, self.cw = p["conv_bias"].shape
        wide = p["attn_bias"].shape
        self.narrow = 4 // self.layers
        self.cn = p["spatial_qkv"].shape[1]
        self.c = self.cn * self.narrow
        self.wide = self.c // self.cw
        self.fw = p["hidden_bias"].shape[1]
        c, cn, cw, fw, n, w = self.c, self.cn, self.cw, self.fw, self.narrow, self.wide

        def spread(v):
            return lax.all_gather(v, BOTH, axis=0, tiled=False).reshape((n, w) + v.shape)

        def attention(qkv, proj):
            got = spread(attention_piece(qkv, proj)).transpose(0, 2, 1, 3)
            return jnp.concatenate([got[..., : 3 * cw].reshape(c, 3 * c), got[..., 3 * cw :].reshape(c, c)], axis=1)

        self.watt = tuple(attention(p[k], p["projection"][i]) for i, k in enumerate(("spatial_qkv", "channel_qkv")))
        self.w_in = tuple(spread(p["mlp_in"][i].T).transpose(0, 2, 1, 3).reshape(c, -1) for i in range(2))
        self.w_out = tuple(spread(p["mlp_out"][i]).transpose(1, 2, 0, 3).reshape(c, -1) for i in range(2))

        def layer(v):
            return spread(v).transpose(0, 2, 3, 1, 4).reshape(4, -1, c)

        rows = [layer(p["conv_weight"])]
        rows += [layer(p[k][:, None]) for k in ("conv_bias", "norm_gain", "norm_bias", "out_bias")]
        self.lay = jnp.pad(jnp.concatenate(rows, axis=1).astype(F32), ((0, 0), (0, 3), (0, 0)))
        attn = spread(p["attn_bias"])[0].transpose(1, 0, 2).reshape(5, c)
        self.sh = jnp.pad(attn.astype(F32), ((0, 11), (0, 0)))
        self.hid = spread(p["hidden_bias"])[0].transpose(1, 0, 2).reshape(2, 1, -1).astype(F32)

    def forward_window(self, *args):
        return forward_window(*args)

    def forward_two(self, x, mask, lay, hid, w_in, w_out):
        low = forward_mlp(x, mask, lay, hid, w_in, w_out)
        return list(low) + list(forward_channel(low[-1], mask, lay, self.sh, self.watt[1]))

    def backward_two(self, grads, g, xa, za, ra, q, a, mask, lay, watt, xb, zb, rb, d, w_in, w_out):
        self.mlp1 = (self.matrix(grads[0], False), self.matrix(grads[1], True))
        high = backward_channel(g, xa, za, ra, q, a, mask, lay, watt)
        return list(high[1:]) + list(backward_mlp(high[0], xb, zb, rb, d, mask, lay, w_in, w_out))

    def backward_window(self, grads, *args):
        self.mlp0 = (self.matrix(grads[0], False), self.matrix(grads[1], True))
        return backward_window(*args)

    def channel_grads(self, *args):
        grads = grad_pair("channel_grads", *args)
        self.att1 = (self.matrix(grads[0], False), self.matrix(grads[1], False))

    def matrix(self, grad, rows_wide):
        n, w = self.narrow, self.wide
        a, b = (w, n) if rows_wide else (n, w)
        grad = grad.reshape(a, grad.shape[0] // a, b, grad.shape[1] // b)
        grad = grad.transpose(2, 0, 1, 3) if rows_wide else grad.transpose(0, 2, 1, 3)
        grad = grad.astype(BF16).reshape(n * w * grad.shape[2], grad.shape[3])
        return lax.psum_scatter(grad, BOTH, scatter_dimension=0, tiled=True).astype(F32)

    def reduce_last(self, grads, smalls, sb, cb, hid0, hid1):
        c, cw, fw, n, w = self.c, self.cw, self.fw, self.narrow, self.wide
        grads = grad_pair("window_grads", *grads)
        first = (self.matrix(grads[0], False), self.matrix(grads[1], False)) + self.mlp0
        rest = self.att1 + self.mlp1
        small = jnp.stack(smalls).reshape(n, self.layers * 16, w, cw).transpose(0, 2, 1, 3)
        attn = jnp.concatenate([sb[:, :c], sb[:, 2 * c :], cb.reshape(3, c)]).reshape(5, w, cw).transpose(1, 0, 2)
        hid = jnp.concatenate([hid0, hid1]).reshape(2, w, fw).transpose(1, 0, 2).reshape(w, -1, cw)
        common = jnp.concatenate([attn, hid], axis=1)
        common = jnp.broadcast_to(common[None], (n,) + common.shape)
        flat = jnp.concatenate([small, common], axis=2).astype(BF16).reshape(-1, cw)
        got = lax.psum_scatter(flat, BOTH, scatter_dimension=0, tiled=True).astype(F32)
        small = got[: self.layers * 16].reshape(self.layers, 16, cw)
        shared = got[self.layers * 16 :]
        return (
            small[:, :9], small[:, 9], small[:, 10], small[:, 11], first[0].T, rest[0].T,
            jnp.stack([first[1].T, rest[1].T]), jnp.stack([first[2].T, rest[2].T]), jnp.stack([first[3], rest[3]]),
            shared[:5], shared[5:].reshape(2, fw), small[:, 12],
        )


NAMES = (
    "conv_weight", "conv_bias", "norm_gain", "norm_bias", "spatial_qkv", "channel_qkv", "projection", "mlp_in",
    "mlp_out", "attn_bias", "hidden_bias", "out_bias",
)


def local(plan, inputs, heights, widths, *rest):
    if inputs.shape[0] != CARRY_STEPS:
        plan = Plain
    weights = plan(dict(zip(NAMES, rest[:-1])), heights, widths)
    cotangent = rest[-1]
    lay, sh, hid = weights.lay, weights.sh, weights.hid
    mask = weights.mask
    inputs, cotangent = cells_first(inputs), cells_first(cotangent)
    n1, z1, r1, q1, o1, p1, x2 = weights.forward_window(inputs, mask, lay, sh, weights.watt[0])
    n2, z2, r2, u1, d1, x4, n3, z3, r3, q3, o3, a3, x6 = weights.forward_two(
        x2, mask, lay, hid, weights.w_in[0], weights.w_out[0])
    out, g6, n4, u2, gy2, gh2, small3, hid1 = last_mlp(
        x6, cotangent, mask, lay, hid, weights.w_in[1], weights.w_out[1])
    grads = grad_pair("last_mlp_grads", n4, gh2, gy2, u2)
    ga3, dq3, small2, cb, g2, gy1, gh1, small1, hid0 = weights.backward_two(
        grads, g6, x4, z3, r3, q3, a3, mask, lay, weights.watt[1], x2, z2, r2, d1, weights.w_in[0], weights.w_out[0])
    weights.channel_grads(n3, dq3, o3, ga3)
    grads = grad_pair("mlp_grads", n2, gh1, gy1, u1)
    input_grad, ga1, dq1, small0, sb = weights.backward_window(
        grads, g2, inputs, z1, r1, q1, p1, mask, lay, weights.watt[0])
    last = weights.reduce_last((n1, dq1, o1, ga1), (small0, small1, small2, small3), sb, cb, hid0, hid1)
    return (images_first(out), images_first(input_grad)) + tuple(last)


def solution(mesh):
    matrix = P("wide", "narrow")
    cells = P(("wide", "narrow"), None, None, None)
    stacked = P(None, "wide", "narrow")
    row = P("narrow", "wide")
    shared = P(None, "wide")
    images = P(("wide", "narrow"))
    kernels = P("narrow", None, "wide")
    in_specs = (
        cells, images, images, kernels, row, row, row, matrix, matrix,
        stacked, stacked, stacked, shared, shared, row, cells,
    )
    out_specs = (
        cells, cells, kernels, row, row, row, matrix, matrix, stacked, stacked, stacked, shared, shared, row,
    )
    plan = Direct if (mesh.shape["wide"], mesh.shape["narrow"]) == (WIDE, NARROW) else Plain
    body = functools.partial(local, plan)
    return jax.shard_map(body, mesh=mesh, in_specs=in_specs, out_specs=out_specs, check_vma=False)
```
